32 devices in a mesh: dp: 8 (over y, x, core), mp: 4 (over z).
Axes of the slice: x: 2, y: 2, z: 4, core: 2. Of those that a mesh axis runs over, the one named last changes fastest.
Arguments:
- tokens: bfloat16 [16, 512, 1024], P('dp', 'mp'), may hold values from -6 to 6
- memory: bfloat16 [16, 512, 1024], P('dp', 'mp'), may hold values from -6 to 6
- compressed: bfloat16 [16, 512, 1024], P('dp', 'mp'), may hold values from -6 to 6
- valid_counts: int32 [16], P('dp'), may hold values from 64 to 512, as said below
- attention_norm_gain: float32 [1024], replicated, may hold values from 0.5 to 1.5
- attention_norm_bias: float32 [1024], replicated, may hold values from -1.75 to 1.75
- query_projection: bfloat16 [1024, 1024], P(None, 'mp'), may hold values from -0.1875 to 0.1875
- key_projection: bfloat16 [1024, 1024], P(None, 'mp'), may hold values from -0.1875 to 0.1875
- value_projection: bfloat16 [1024, 1024], P(None, 'mp'), may hold values from -0.1875 to 0.1875
- out_weight: bfloat16 [1024, 1024], P('mp'), may hold values from -2 to 2
- feedforward_norm_gain: float32 [1024], replicated, may hold values from 0.5 to 1.5
- feedforward_norm_bias: float32 [1024], replicated, may hold values from -1.75 to 1.75
- up_weight: bfloat16 [1024, 4096], P(None, 'mp'), may hold values from -0.1875 to 0.1875
- up_bias: float32 [4096], P('mp'), may hold values from -3 to 3
- down_weight: bfloat16 [4096, 1024], P('mp'), may hold values from -0.09375 to 0.09375
- down_bias: float32 [1024], replicated, may hold values from -3 to 3
- squeeze_weight: bfloat16 [3072, 1024], replicated, may hold values from -0.109375 to 0.109375
- cotangent: bfloat16 [16, 512, 1024], P('dp', 'mp'), may hold values from -6 to 6
Outputs:
- output: bfloat16 [16, 512, 1024], P('dp', 'mp')
- tokens_grad: float32 [16, 512, 1024], P('dp', 'mp')
- attention_gain_gradient: float32 [1024], replicated
- first_bias_grad: float32 [1024], replicated
- query_weight_grad: float32 [1024, 1024], P(None, 'mp')
- key_weight_grad: float32 [1024, 1024], P(None, 'mp')
- value_weight_grad: float32 [1024, 1024], P(None, 'mp')
- out_weight_grad: float32 [1024, 1024], P('mp')
- feedforward_gain_gradient: float32 [1024], replicated
- second_bias_grad: float32 [1024], replicated
- up_weight_grad: float32 [1024, 4096], P(None, 'mp')
- up_bias_grad: float32 [4096], P('mp')
- down_weight_grad: float32 [4096, 1024], P('mp')
- down_bias_grad: float32 [1024], replicated
- new_memory: bfloat16 [16, 512, 1024], P('dp', 'mp')
- new_compressed: bfloat16 [16, 512, 1024], P('dp', 'mp')
The draws below stay inside these ranges and needn't reach their ends.
Inputs may be any that keep to these rules, and one draw needn't show every extreme that they name: The first valid_counts tokens of a segment are real, the rest padding.
All inputs are finite; a program needn't handle non-finite values.
Results may differ from the reference program's by a relative error of at most 0.015.
Values may be sent and summed in bfloat16 or wider, within the bound.
A program may use at most 192 MiB of HBM per device.

```python
import jax
import jax.numpy as jnp
from jax import lax

D = 1024
HEAD_DIM = 128
FF = 4096
SEG = 512
MEM = 512
CMEM = 512
RATE = 3
SEGS = 16


def draw_valid_counts(key, part):
    first_key, second_key = jax.random.split(key)
    partial_counts = jax.random.randint(first_key, (SEGS,), SEG // 8, SEG + 1)
    chooser = jax.random.randint(second_key, (SEGS,), 0, 4)
    counts = jnp.where(chooser == 0, partial_counts, SEG)
    counts = counts.at[0].set(SEG).at[SEGS - 1].set(SEG // 8)
    return counts.astype(jnp.int32)


def block_levels(key, extent, cuts, low, top_value):
    level = 1.0
    for axis_at, parts in cuts:
        draws = jax.random.uniform(jax.random.fold_in(jax.random.fold_in(key, 6), axis_at), (parts,), jnp.float32, low / len(cuts), top_value / len(cuts))
        level = level * jnp.repeat(jnp.exp(draws), extent[axis_at] // parts).reshape((-1,) + (1,) * (len(extent) - 1 - axis_at))
    return level


def centred(key, dims, deviation, reach, cuts=(), kind=jnp.bfloat16):
    values = jax.random.normal(key, dims, jnp.float32) * deviation
    if len(cuts) > 0:
        values = block_levels(key, dims, cuts, -0.22, 0.18) * values
    return jnp.clip(values, min=-reach, max=reach).astype(kind)


def setup_inputs(seed: int = 0) -> dict:
    splits = jax.random.split(jax.random.key(seed), 19)
    return {
        "tokens": centred(splits[0], (SEGS, SEG, D), 1.0, 6.0, ((0, 8), (1, 4))),
        "memory": centred(splits[1], (SEGS, MEM, D), 1.0, 6.0, ((0, 8), (1, 4))),
        "compressed": centred(splits[2], (SEGS, CMEM, D), 1.0, 6.0, ((0, 8), (1, 4))),
        "valid_counts": draw_valid_counts(jax.random.fold_in(splits[18], 71), 0),
        "attention_norm_gain": jnp.clip(1.0 + 0.1 * jax.random.normal(splits[4], (D,), jnp.float32), 0.5, 1.5),
        "attention_norm_bias": centred(splits[5], (D,), 0.3, 1.75, (), jnp.float32),
        "query_projection": centred(splits[6], (D, D), D ** -0.5, 0.1875, ((1, 4),)),
        "key_projection": centred(splits[7], (D, D), D ** -0.5, 0.1875, ((1, 4),)),
        "value_projection": centred(splits[8], (D, D), D ** -0.5, 0.1875, ((1, 4),)),
        "out_weight": centred(splits[9], (D, D), 8 ** -0.5, 2.0, ((0, 4),)),
        "feedforward_norm_gain": jnp.clip(1.0 + 0.1 * jax.random.normal(splits[10], (D,), jnp.float32), 0.5, 1.5),
        "feedforward_norm_bias": centred(splits[11], (D,), 0.3, 1.75, (), jnp.float32),
        "up_weight": centred(splits[12], (D, FF), D ** -0.5, 0.1875, ((1, 4),)),
        "up_bias": centred(splits[13], (FF,), 0.5, 3.0, ((0, 4),), jnp.float32),
        "down_weight": centred(splits[14], (FF, D), FF ** -0.5, 0.09375, ((0, 4),)),
        "down_bias": centred(splits[15], (D,), 0.5, 3.0, (), jnp.float32),
        "squeeze_weight": centred(splits[16], (RATE * D, D), (RATE * D) ** -0.5, 0.109375),
        "cotangent": centred(splits[17], (SEGS, SEG, D), 1.0, 6.0, ((0, 8), (1, 4))),
    }


@jax.custom_vjp
def low(v):
    return lax.optimization_barrier(v.astype(jnp.bfloat16)).astype(jnp.float32)

@jax.custom_vjp
def low_back(v):
    return v

def low_keep(v):
    return (low(v), None)

def low_pass(kept, grad):
    return (grad,)

def back_keep(v):
    return (v, None)

def back_low(kept, grad):
    return (low(grad),)
low.defvjp(low_keep, low_pass)
low_back.defvjp(back_keep, back_low)
HIGHEST = lax.Precision.HIGHEST

def layer_norm(rows, scale_factor, shift_by):
    center = lax.optimization_barrier(jnp.mean(rows, axis=-1, keepdims=True))
    centered = rows - center
    spread = lax.optimization_barrier(jnp.mean(centered * centered, axis=-1, keepdims=True))
    return centered * lax.rsqrt(spread + 1e-05) * scale_factor + shift_by

def segment_forward(weights, old_comp, old_mem, fresh, valid_count):
    attention_norm_gain, attention_norm_bias, query_projection, key_projection, value_projection, out_weight, feedforward_norm_gain, feedforward_norm_bias, up_weight, up_bias, down_weight, down_bias = weights
    context_tokens = jnp.concatenate([old_comp, old_mem, fresh], axis=0)
    ctx_len = context_tokens.shape[0]
    seg_len = fresh.shape[0]
    prior_rows = ctx_len - seg_len
    normed_rows = low(layer_norm(context_tokens, attention_norm_gain, attention_norm_bias))
    queries = low(low_back(jnp.dot(normed_rows[prior_rows:], query_projection, precision=HIGHEST)))
    key_rows = low(low_back(jnp.dot(normed_rows, key_projection, precision=HIGHEST)))
    values = low(low_back(jnp.dot(normed_rows, value_projection, precision=HIGHEST)))
    head_count = query_projection.shape[1] // HEAD_DIM
    query_heads = queries.reshape(seg_len, head_count, HEAD_DIM)
    key_heads = key_rows.reshape(ctx_len, head_count, HEAD_DIM)
    value_heads = values.reshape(ctx_len, head_count, HEAD_DIM)
    scores = low_back(jnp.einsum('qhe,khe->hqk', query_heads, key_heads, precision=HIGHEST) * HEAD_DIM ** (-0.5))
    query_pos = jnp.arange(seg_len, dtype=jnp.int32)[:, None]
    key_pos = jnp.arange(ctx_len, dtype=jnp.int32)[None, :] - prior_rows
    allowed = (key_pos < 0) | (key_pos <= query_pos) & (key_pos < valid_count)
    scores = jnp.where(allowed[None], scores, -1e+30)
    attn_probs = low(jax.nn.softmax(scores, axis=-1))
    mixed = low(low_back(jnp.einsum('hqk,khe->qhe', attn_probs, value_heads, precision=HIGHEST)))
    mixed = mixed.reshape(seg_len, head_count * HEAD_DIM)
    attention = low_back(jnp.dot(mixed, out_weight, precision=HIGHEST))
    residual_stream = fresh + attention
    feedforward_input = low(layer_norm(residual_stream, feedforward_norm_gain, feedforward_norm_bias))
    up_in = low_back(jnp.dot(feedforward_input, up_weight, precision=HIGHEST) + up_bias)
    active = low(jax.nn.gelu(up_in))
    down_out = low_back(jnp.dot(active, down_weight, precision=HIGHEST))
    return residual_stream + down_out + down_bias

def memory_update(old_comp, old_mem, fresh, valid_count, squeeze_weight):
    joined = jnp.concatenate([old_mem, fresh], axis=0)
    new_memory = lax.dynamic_slice_in_dim(joined, valid_count.astype(jnp.int32), MEM, 0)
    groups = MEM // RATE
    squeezed = jnp.dot(old_mem[:groups * RATE].reshape(groups, RATE * D), squeeze_weight, precision=HIGHEST)
    evicted = (valid_count // RATE).astype(jnp.int32)
    stacked = jnp.concatenate([old_comp, squeezed], axis=0)
    new_compressed = lax.dynamic_slice_in_dim(stacked, evicted, CMEM, 0)
    return (new_memory, new_compressed)

def reference(tokens, memory, compressed, valid_counts, attention_norm_gain, attention_norm_bias, query_projection, key_projection, value_projection, out_weight, feedforward_norm_gain, feedforward_norm_bias, up_weight, up_bias, down_weight, down_bias, squeeze_weight, cotangent):
    weights = tuple((w.astype(jnp.float32) for w in (attention_norm_gain, attention_norm_bias, query_projection, key_projection, value_projection, out_weight, feedforward_norm_gain, feedforward_norm_bias, up_weight, up_bias, down_weight, down_bias)))
    fresh_all = tokens.astype(jnp.float32)
    mem_all = memory.astype(jnp.float32)
    comp_all = compressed.astype(jnp.float32)
    squeeze_float = squeeze_weight.astype(jnp.float32)
    checked = jax.checkpoint(segment_forward)

    def forward(fresh_in, weight_in):

        def one_segment(item):
            result = checked(weight_in, item[0], item[1], item[2], item[3])
            next_mem, next_comp = memory_update(item[0], item[1], item[2], item[3], squeeze_float)
            return (result, next_mem, next_comp)
        return lax.map(one_segment, (comp_all, mem_all, fresh_in, valid_counts))
    (output, new_memory, new_compressed), backward = jax.vjp(forward, fresh_all, weights)
    tokens_grad, weight_grads = backward((cotangent.astype(jnp.float32), jnp.zeros_like(new_memory), jnp.zeros_like(new_compressed)))
    return (output.astype(jnp.bfloat16), tokens_grad, weight_grads[0], weight_grads[1], weight_grads[2], weight_grads[3], weight_grads[4], weight_grads[5], weight_grads[6], weight_grads[7], weight_grads[8], weight_grads[9], weight_grads[10], weight_grads[11], new_memory.astype(jnp.bfloat16), new_compressed.astype(jnp.bfloat16))
```

```python
import functools

import jax
import jax.numpy as jnp
from jax import lax
from jax.experimental import pallas as pl
from jax.experimental.pallas import tpu as pltpu
from jax.sharding import PartitionSpec as P

HEAD_DIM = 128
RATE = 3


def apply_layer_norm(rows):
    center = jnp.mean(rows, axis=-1, keepdims=True)
    centered = rows - center
    spread = jnp.mean(centered * centered, axis=-1, keepdims=True)
    inverse_deviation = lax.rsqrt(spread + 1e-05)
    return (centered * inverse_deviation, inverse_deviation)


def norm_backward_pass(input_gradient, standardized_rows, inverse_deviation, scale_factor):
    scaled_rows = input_gradient * scale_factor
    attention_norm_mean = jnp.mean(scaled_rows, axis=-1, keepdims=True)
    feedforward_norm_mean = jnp.mean(scaled_rows * standardized_rows, axis=-1, keepdims=True)
    return inverse_deviation * (
        scaled_rows - attention_norm_mean - standardized_rows * feedforward_norm_mean
    )


def squeeze_rows(old_comp, old_mem, fresh, valid_count, offset, own_rows, squeeze_weight):
    features = old_mem.shape[1]
    joined = jnp.concatenate([old_mem, fresh], axis=0)
    new_memory = lax.dynamic_slice_in_dim(joined, valid_count + offset, own_rows, 0)
    comp_len = old_comp.shape[0]
    evicted = valid_count // RATE
    first_row = evicted + offset
    window_start = jnp.maximum(first_row - comp_len, 0)
    padded = jnp.concatenate(
        [old_mem, jnp.zeros((RATE * own_rows, features), jnp.bfloat16)], axis=0
    )
    window = lax.dynamic_slice_in_dim(padded, window_start * RATE, RATE * own_rows, 0)
    squeezed = jnp.dot(
        window.reshape(own_rows, RATE * features),
        squeeze_weight,
        preferred_element_type=jnp.float32,
    ).astype(jnp.bfloat16)
    positions = first_row + jnp.arange(own_rows)
    from_old = jnp.take(old_comp, jnp.clip(positions, 0, comp_len - 1), axis=0)
    from_new = jnp.take(
        squeezed, jnp.clip(positions - comp_len - window_start, 0, own_rows - 1), axis=0
    )
    new_compressed = jnp.where((positions < comp_len)[:, None], from_old, from_new)
    return (new_memory, new_compressed)


def general_device(
    tokens,
    memory,
    compressed,
    valid_counts,
    attention_norm_gain,
    attention_norm_bias,
    query_projection,
    key_projection,
    value_projection,
    out_weight,
    feedforward_norm_gain,
    feedforward_norm_bias,
    up_weight,
    up_bias,
    down_weight,
    down_bias,
    squeeze_weight,
    cotangent,
):
    batch_segs, own_rows, features = tokens.shape
    offset = lax.axis_index("mp") * own_rows
    old_comp, old_mem, fresh = (
        lax.all_gather(compressed, "mp", axis=1, tiled=True),
        lax.all_gather(memory, "mp", axis=1, tiled=True),
        lax.all_gather(tokens, "mp", axis=1, tiled=True),
    )
    seg_len = fresh.shape[1]
    prior_rows = old_comp.shape[1] + old_mem.shape[1]
    context_tokens = jnp.concatenate([old_comp, old_mem, fresh], axis=1).astype(jnp.float32)
    ctx_len = context_tokens.shape[1]
    standardized_full, inverse_deviation_full = apply_layer_norm(context_tokens)
    normed_rows = (standardized_full * attention_norm_gain + attention_norm_bias).astype(
        jnp.bfloat16
    )
    token_rows_normed = normed_rows[:, prior_rows:]
    queries = jnp.einsum(
        "xhp,pj->xhj", token_rows_normed, query_projection, preferred_element_type=jnp.float32
    ).astype(jnp.bfloat16)
    key_rows = jnp.einsum(
        "xhp,pj->xhj", normed_rows, key_projection, preferred_element_type=jnp.float32
    ).astype(jnp.bfloat16)
    values = jnp.einsum(
        "xhp,pj->xhj", normed_rows, value_projection, preferred_element_type=jnp.float32
    ).astype(jnp.bfloat16)
    local_heads = query_projection.shape[1] // HEAD_DIM
    score_scale = HEAD_DIM ** (-0.5)

    def by_heads(matrix):
        return matrix.reshape(matrix.shape[0], matrix.shape[1], local_heads, HEAD_DIM)

    query_pos = jnp.arange(seg_len)[:, None]
    key_pos = jnp.arange(ctx_len)[None, :] - prior_rows
    allowed = (key_pos[None] < 0) | (key_pos <= query_pos)[None] & (
        key_pos[None] < valid_counts[:, None, None]
    )

    def scores_of(query_in, key_in):
        raw = (
            jnp.einsum(
                "gqhe,gkhe->ghqk",
                by_heads(query_in),
                by_heads(key_in),
                preferred_element_type=jnp.float32,
            )
            * score_scale
        )
        return jnp.where(allowed[:, None], raw, -1e30)

    scores = scores_of(queries, key_rows)
    peak_score = jnp.max(scores, axis=-1, keepdims=True)
    exponent = jnp.exp(scores - peak_score)
    exp_total = jnp.sum(exponent, axis=-1, keepdims=True)
    log_total = peak_score + jnp.log(exp_total)
    probs_low = (exponent / exp_total).astype(jnp.bfloat16)
    mixed_heads = jnp.einsum(
        "ghqk,gkhe->gqhe", probs_low, by_heads(values), preferred_element_type=jnp.float32
    ).astype(jnp.bfloat16)
    mixed_heads = mixed_heads.reshape(batch_segs, seg_len, local_heads * HEAD_DIM)
    partial_attn = jnp.einsum(
        "gsc,cd->gsd", mixed_heads, out_weight, preferred_element_type=jnp.float32
    )
    attention = lax.psum_scatter(partial_attn, "mp", scatter_dimension=1, tiled=True)
    residual_stream = tokens.astype(jnp.float32) + attention
    standardized_feedforward, inverse_deviation_feedforward = apply_layer_norm(residual_stream)
    feedforward_input = (
        standardized_feedforward * feedforward_norm_gain + feedforward_norm_bias
    ).astype(jnp.bfloat16)
    second_all = lax.all_gather(feedforward_input, "mp", axis=1, tiled=True)
    upper_in = (
        jnp.einsum("gsd,df->gsf", second_all, up_weight, preferred_element_type=jnp.float32)
        + up_bias
    )
    active, gelu_back = jax.vjp(jax.nn.gelu, upper_in)
    active_low = active.astype(jnp.bfloat16)
    partial_ffn = jnp.einsum(
        "gsf,fd->gsd", active_low, down_weight, preferred_element_type=jnp.float32
    )
    down_out = lax.psum_scatter(
        partial_ffn.astype(jnp.bfloat16), "mp", scatter_dimension=1, tiled=True
    ).astype(jnp.float32)
    output = (residual_stream + down_out + down_bias).astype(jnp.bfloat16)

    def update_one(comp_seg, mem_seg, fresh_seg, valid_count):
        return squeeze_rows(
            comp_seg, mem_seg, fresh_seg, valid_count, offset, own_rows, squeeze_weight
        )

    new_memory, new_compressed = jax.vmap(update_one)(old_comp, old_mem, fresh, valid_counts)
    output_gradient = cotangent.astype(jnp.float32)
    down_bias_grad = jnp.sum(output_gradient, axis=(0, 1))
    grad_all = lax.all_gather(cotangent, "mp", axis=1, tiled=True)
    down_weight_grad = jnp.einsum(
        "gsf,gsd->fd", active_low, grad_all, preferred_element_type=jnp.float32
    )
    grad_active = jnp.einsum(
        "gsd,fd->gsf", grad_all, down_weight, preferred_element_type=jnp.float32
    )
    grad_upper = gelu_back(grad_active)[0].astype(jnp.bfloat16)
    up_weight_grad = jnp.einsum(
        "gsd,gsf->df", second_all, grad_upper, preferred_element_type=jnp.float32
    )
    up_bias_grad = jnp.sum(grad_upper.astype(jnp.float32), axis=(0, 1))
    partial_second = jnp.einsum(
        "gsf,df->gsd", grad_upper, up_weight, preferred_element_type=jnp.float32
    )
    feedforward_gradient = lax.psum_scatter(partial_second, "mp", scatter_dimension=1, tiled=True)
    feedforward_gain_gradient = jnp.sum(
        feedforward_gradient * standardized_feedforward, axis=(0, 1)
    )
    second_bias_grad = jnp.sum(feedforward_gradient, axis=(0, 1))
    residual_gradient = output_gradient + norm_backward_pass(
        feedforward_gradient,
        standardized_feedforward,
        inverse_deviation_feedforward,
        feedforward_norm_gain,
    )
    grad_resid_all = lax.all_gather(
        residual_gradient.astype(jnp.bfloat16), "mp", axis=1, tiled=True
    )
    out_weight_grad = jnp.einsum(
        "gsc,gsd->cd", mixed_heads, grad_resid_all, preferred_element_type=jnp.float32
    )
    grad_mixed = jnp.einsum(
        "gsd,cd->gsc", grad_resid_all, out_weight, preferred_element_type=jnp.float32
    ).astype(jnp.bfloat16)
    probs_again = jnp.exp(scores_of(queries, key_rows) - log_total)
    grad_probs = jnp.einsum(
        "gqhe,gkhe->ghqk",
        by_heads(grad_mixed),
        by_heads(values),
        preferred_element_type=jnp.float32,
    )
    row_dot = jnp.sum(probs_again * grad_probs, axis=-1, keepdims=True)
    grad_scores = (probs_again * (grad_probs - row_dot)).astype(jnp.bfloat16)
    query_gradient = (
        score_scale
        * jnp.einsum(
            "ghqk,gkhe->gqhe", grad_scores, by_heads(key_rows), preferred_element_type=jnp.float32
        )
    ).astype(jnp.bfloat16)
    key_gradient = (
        score_scale
        * jnp.einsum(
            "ghqk,gqhe->gkhe", grad_scores, by_heads(queries), preferred_element_type=jnp.float32
        )
    ).astype(jnp.bfloat16)
    value_gradient = jnp.einsum(
        "ghqk,gqhe->gkhe",
        probs_again.astype(jnp.bfloat16),
        by_heads(grad_mixed),
        preferred_element_type=jnp.float32,
    ).astype(jnp.bfloat16)
    query_gradient = query_gradient.reshape(batch_segs, seg_len, -1)
    key_gradient = key_gradient.reshape(batch_segs, ctx_len, -1)
    value_gradient = value_gradient.reshape(batch_segs, ctx_len, -1)
    query_weight_grad = jnp.einsum(
        "nja,njr->ar", token_rows_normed, query_gradient, preferred_element_type=jnp.float32
    )
    key_weight_grad = jnp.einsum(
        "nja,njr->ar", normed_rows, key_gradient, preferred_element_type=jnp.float32
    )
    value_weight_grad = jnp.einsum(
        "nja,njr->ar", normed_rows, value_gradient, preferred_element_type=jnp.float32
    )
    partial_normed = jnp.einsum(
        "xmo,qo->xmq", key_gradient, key_projection, preferred_element_type=jnp.float32
    )
    partial_normed = partial_normed + jnp.einsum(
        "xmo,qo->xmq", value_gradient, value_projection, preferred_element_type=jnp.float32
    )
    partial_normed = partial_normed.at[:, prior_rows:].add(
        jnp.einsum(
            "xmo,qo->xmq", query_gradient, query_projection, preferred_element_type=jnp.float32
        )
    )
    partial_normed = partial_normed.reshape(batch_segs, 3, seg_len, features)
    normed_gradient = lax.psum_scatter(
        partial_normed.astype(jnp.bfloat16), "mp", scatter_dimension=2, tiled=True
    ).astype(jnp.float32)
    segment_context = jnp.stack([compressed, memory, tokens], axis=1).astype(jnp.float32)
    standardized_segment, inverse_deviation_segment = apply_layer_norm(segment_context)
    attention_gain_gradient = jnp.sum(normed_gradient * standardized_segment, axis=(0, 1, 2))
    first_bias_grad = jnp.sum(normed_gradient, axis=(0, 1, 2))
    tokens_grad = residual_gradient + norm_backward_pass(
        normed_gradient[:, 2],
        standardized_segment[:, 2],
        inverse_deviation_segment[:, 2],
        attention_norm_gain,
    )
    summed = (
        lax.psum(query_weight_grad.astype(jnp.bfloat16), "dp").astype(jnp.float32),
        lax.psum(key_weight_grad.astype(jnp.bfloat16), "dp").astype(jnp.float32),
        lax.psum(value_weight_grad.astype(jnp.bfloat16), "dp").astype(jnp.float32),
        lax.psum(out_weight_grad.astype(jnp.bfloat16), "dp").astype(jnp.float32),
        lax.psum(up_weight_grad.astype(jnp.bfloat16), "dp").astype(jnp.float32),
        lax.psum(up_bias_grad.astype(jnp.bfloat16), "dp").astype(jnp.float32),
        lax.psum(down_weight_grad.astype(jnp.bfloat16), "dp").astype(jnp.float32),
    )
    norms = lax.psum(
        (
            attention_gain_gradient,
            first_bias_grad,
            feedforward_gain_gradient,
            second_bias_grad,
            down_bias_grad,
        ),
        ("dp", "mp"),
    )
    return (
        output,
        tokens_grad,
        norms[0],
        norms[1],
        summed[0],
        summed[1],
        summed[2],
        summed[3],
        norms[2],
        norms[3],
        summed[4],
        summed[5],
        summed[6],
        norms[4],
        new_memory,
        new_compressed,
    )


BF = jnp.bfloat16
F32 = jnp.float32
MESH = pl.DeviceIdType.MESH
ANY = pl.BlockSpec(memory_space=pl.ANY)
VM = pl.BlockSpec(memory_space=pltpu.VMEM)
DMA = pltpu.SemaphoreType.DMA


def sds(shape, dtype):
    return jax.ShapeDtypeStruct(shape, dtype)


def where_am_i(chips, depth):
    dp = lax.axis_index("dp")
    return dp, lax.rem(dp, 2), dp // 2, lax.axis_index("mp")


def rcopy(src, dst, send, recv, device):
    return pltpu.make_async_remote_copy(
        src_ref=src,
        dst_ref=dst,
        send_sem=send,
        recv_sem=recv,
        device_id=device,
        device_id_type=MESH,
    )


def lcopy(src, dst, sem):
    return pltpu.make_async_copy(src, dst, sem)


def enter(partners):
    barrier = pltpu.get_barrier_semaphore()
    for p in partners:
        pl.semaphore_signal(barrier, inc=1, device_id=p, device_id_type=MESH)
    pl.semaphore_wait(barrier, len(partners))


def gather_kernel(Q, Z, comp, mem, tok, cot, wq, wk, wv, wo, ub, vc, ctx, wqg, wkg, wvg, wog, ubg, vco,
                  ws, wr, ps, pr, cs, cr, fs, fr, ls, us, ur, ms):
    dp, c, q, z = where_am_i(Q, Z)
    sib = dp + 1 - 2 * c
    partners = [(sib, z)]
    for r in range(1, Z):
        for d in (dp, sib):
            partners.append((d, lax.rem(z + r, Z)))
    for k in range(1, Q):
        partners.append((2 * lax.rem(q + k, Q) + c, z))
    enter(partners)
    B, R, D = tok.shape
    H = wq.shape[1]
    QR = wq.shape[0] // Q
    OR = wo.shape[0] // Q
    HR = R // 2
    mine = c == z // B
    weights = [(wq, wqg), (wk, wkg), (wv, wvg), (wo, wog)]
    acts = [comp, mem, tok, cot]

    def piece(a):
        if a < 3:
            return weights[a][0].at[pl.ds(q * QR, QR), :]
        return wo.at[pl.ds(q * OR, OR), :]

    def place(a, j, qq):
        if a < 3:
            return weights[a][1].at[j, pl.ds(qq * QR, QR), :]
        return wog.at[j, pl.ds(qq * OR, OR), :]

    def w_z(a, r):
        zt = lax.rem(z + r, Z)
        return rcopy(piece(a), place(a, lax.rem(z, B), q), ws.at[a, r - 1], wr.at[a, lax.rem(z, B)], (dp, zt))

    def u_z(r):
        return rcopy(ub.at[dp], ubg.at[r], us.at[r - 1], ur.at[r - 1], (dp, lax.rem(z + r, Z)))

    v_s = rcopy(vc, vco, ms.at[0], ms.at[1], (sib, z))
    u_l = lcopy(ub.at[dp], ubg.at[0], ls.at[0])

    def w_l(a):
        return lcopy(weights[a][0], weights[a][1].at[lax.rem(z, B)], ls.at[1 + a])

    def c_l(t):
        return lcopy(acts[t].at[lax.rem(z, B)], ctx.at[t, pl.ds(z * R, R), :], ls.at[5 + t])

    def c_sib(t):
        return rcopy(acts[t].at[lax.rem(z, B)], ctx.at[t, pl.ds(z * R, R), :], fs.at[t, z], fr.at[t, z], (sib, z))

    def c_z(t, s, h):
        return rcopy(
            acts[t].at[s, pl.ds(HR * h, HR), :],
            ctx.at[t, pl.ds(z * R + HR * h, HR), :],
            cs.at[t, s, h],
            cr.at[t, z],
            (2 * q + h, B * c + s),
        )

    def c_arrive(t, zs):
        rows = ctx.at[t, pl.ds(zs * R + HR * c, HR), :]
        return rcopy(rows, rows, cs.at[t, 0, 0], cr.at[t, zs], (dp, z))

    def c_fwd(t, zs, half):
        rows = ctx.at[t, pl.ds(zs * R + HR * half, HR), :]
        return rcopy(rows, rows, fs.at[t, zs], fr.at[t, zs], (sib, z))

    def w_arrive(a, j):
        return rcopy(place(a, j, q), place(a, j, q), ws.at[a, 0], wr.at[a, j], (dp, z))

    def w_p(a, j, k, qq):
        return rcopy(
            place(a, j, qq), place(a, j, qq), ps.at[a, j, k - 1], pr.at[a, j, k - 1], (2 * lax.rem(q + k, Q) + c, z)
        )

    @pl.when(mine)
    def _():
        for a in range(4):
            for r in range(1, Z):
                w_z(a, r).start()
    for r in range(1, Z):
        u_z(r).start()
    v_s.start()
    u_l.start()

    @pl.when(mine)
    def _():
        for a in range(4):
            w_l(a).start()
        for t in range(4):
            c_l(t).start()
            c_sib(t).start()
    for j in range(B):
        @pl.when(B * c + j != z)
        def _():
            for a in range(4):
                w_arrive(a, j).wait_recv()
                for k in range(1, Q):
                    w_p(a, j, k, q).start()
    for s in range(B):
        @pl.when(B * c + s != z)
        def _():
            for t in range(4):
                for h in range(2):
                    c_z(t, s, h).start()
    for zs in range(Z):
        @pl.when(zs != z)
        def _():
            for t in range(4):
                c_arrive(t, zs).wait_recv()
                c_fwd(t, zs, c).start()
    for zs in range(Z):
        @pl.when(zs != z)
        def _():
            for t in range(4):
                c_fwd(t, zs, 1 - c).wait_recv()
                c_fwd(t, zs, c).wait_send()

    @pl.when(mine)
    def _():
        for a in range(4):
            w_l(a).wait()
            for r in range(1, Z):
                w_z(a, r).wait_send()
        for t in range(4):
            c_l(t).wait()
            c_sib(t).wait_send()

    @pl.when(jnp.logical_not(mine))
    def _():
        for t in range(4):
            rows = ctx.at[t, pl.ds(z * R, R), :]
            rcopy(rows, rows, fs.at[t, z], fr.at[t, z], (sib, z)).wait_recv()
    for j in range(B):
        @pl.when(B * c + j != z)
        def _():
            for a in range(4):
                for k in range(1, Q):
                    w_p(a, j, k, q).wait_send()
                    w_p(a, j, k, lax.rem(q + Q - k, Q)).wait_recv()
    for s in range(B):
        @pl.when(B * c + s != z)
        def _():
            for t in range(4):
                for h in range(2):
                    c_z(t, s, h).wait_send()
    for r in range(1, Z):
        u_z(r).wait()
    v_s.wait()
    u_l.wait()


def gather_inputs(Q, Z, comp, mem, tok, cot, wq, wk, wv, wo, ub, vc):
    B, R, D = tok.shape
    H = wq.shape[1]
    return pl.pallas_call(
        functools.partial(gather_kernel, Q, Z),
        out_shape=[
            sds((4, R * Z, D), BF),
            sds((B, D, H), BF),
            sds((B, D, H), BF),
            sds((B, D, H), BF),
            sds((B, H, D), BF),
            sds((Z,) + ub.shape[1:], F32),
            sds(vc.shape, jnp.int32),
        ],
        in_specs=[ANY] * 10,
        out_specs=[ANY] * 7,
        scratch_shapes=[
            DMA((4, Z - 1)), DMA((4, B)),
            DMA((4, B, Q - 1)), DMA((4, B, Q - 1)),
            DMA((4, B, 2)), DMA((4, Z)),
            DMA((4, Z)), DMA((4, Z)),
            DMA((9,)),
            DMA((Z - 1,)), DMA((Z - 1,)), DMA((2,)),
        ],
        compiler_params=pltpu.CompilerParams(collective_id=1, has_side_effects=True, vmem_limit_bytes=16 << 20),
        name="gather_inputs",
    )(comp, mem, tok, cot, wq, wk, wv, wo, ub, vc)


def layer_norm_rows(rows):
    center = jnp.mean(rows, axis=-1, keepdims=True)
    centered = rows - center
    spread = jnp.mean(centered * centered, axis=-1, keepdims=True)
    inv = lax.rsqrt(spread + 1e-05)
    return centered * inv, inv


def second_kernel(Q, part, tok, gain, bias, resid, sec, got, own, ss, sr, ps, pr, fs, fr, ls):
    dp, c, q, z = where_am_i(Q, 1)
    sib = dp + 1 - 2 * c
    enter([(sib, z)] + [(2 * lax.rem(q + k, Q) + c, z) for k in range(1, Q)])
    N = own.shape[0]
    parts = ss.shape[0]
    C = N // parts

    def s_x(i):
        return rcopy(part.at[pl.ds((1 - c) * N + i * C, C), :], got.at[pl.ds(i * C, C), :], ss.at[i], sr.at[i], (sib, z))

    def p_x(i, k):
        return rcopy(
            own.at[pl.ds(i * C, C), :], sec.at[k, 0, pl.ds(i * C, C), :], ps.at[i, k], pr.at[i, k], (2 * lax.rem(q + k, Q) + c, z)
        )

    def f_x(i, k):
        src = own.at[pl.ds(i * C, C), :] if k == 0 else sec.at[k, 0, pl.ds(i * C, C), :]
        return rcopy(src, sec.at[k, 1, pl.ds(i * C, C), :], fs.at[i, k], fr.at[i, k], (sib, z))

    def l_x(i):
        return lcopy(own.at[pl.ds(i * C, C), :], sec.at[0, 0, pl.ds(i * C, C), :], ls.at[i])

    for i in range(parts):
        s_x(i).start()
    for i in range(parts):
        s_x(i).wait_recv()
        at = pl.multiple_of(c * N + i * C, C)
        r = tok[pl.ds(at, C), :].astype(F32) + (part[pl.ds(at, C), :] + got[pl.ds(i * C, C), :])
        resid[pl.ds(i * C, C), :] = r
        xhat, _ = layer_norm_rows(r)
        own[pl.ds(i * C, C), :] = (xhat * gain[...] + bias[...]).astype(BF)
        for k in range(1, Q):
            p_x(i, k).start()
        f_x(i, 0).start()
        l_x(i).start()
    for i in range(parts):
        for k in range(1, Q):
            p_x(i, k).wait_recv()
            f_x(i, k).start()
    for i in range(parts):
        s_x(i).wait_send()
        l_x(i).wait()
        for k in range(1, Q):
            p_x(i, k).wait_send()
        for k in range(Q):
            f_x(i, k).wait()


def second_rows(Q, part, tok, gain, bias, parts=2):
    rows, D = part.shape
    N = rows // 2
    return pl.pallas_call(
        functools.partial(second_kernel, Q),
        out_shape=[sds((N, D), F32), sds((Q, 2, N, D), BF)],
        in_specs=[VM] * 4,
        out_specs=[VM, ANY],
        scratch_shapes=[
            pltpu.VMEM((N, D), F32), pltpu.VMEM((N, D), BF),
            DMA((parts,)), DMA((parts,)), DMA((parts, Q)), DMA((parts, Q)), DMA((parts, Q)), DMA((parts, Q)), DMA((parts,)),
        ],
        compiler_params=pltpu.CompilerParams(collective_id=2, has_side_effects=True, vmem_limit_bytes=32 << 20),
        name="second_rows",
    )(part, tok, gain, bias)


def resid_kernel(Q, part, resid, cot, gain, grad, all_low, sums, got1, send2, got2, low, ss, sr, ps, pr, fs, ls):
    dp, c, q, z = where_am_i(Q, 1)
    sib = dp + 1 - 2 * c
    enter([(sib, z)] + [(2 * lax.rem(q + k, Q) + c, z) for k in range(1, Q)])
    N, D = resid.shape

    def s_x(k):
        return rcopy(part.at[k, 1], got1.at[k], ss.at[k], sr.at[k], (sib, z))

    def p_x(k):
        return rcopy(send2.at[k - 1], got2.at[k - 1], ps.at[k - 1], pr.at[k - 1], (2 * lax.rem(q + Q - k, Q) + c, z))

    order = list(range(1, Q)) + [0]
    for k in order:
        s_x(k).start()
    for k in range(1, Q):
        s_x(k).wait_recv()
        send2[k - 1] = (part[k, 0].astype(F32) + got1[k].astype(F32)).astype(BF)
        p_x(k).start()
    s_x(0).wait_recv()
    for k in range(1, Q):
        p_x(k).wait_recv()
    g_gain = jnp.zeros((1, D), F32)
    g_bias = jnp.zeros((1, D), F32)
    C = 64
    for i in range(N // C):
        at = pl.ds(i * C, C)
        gs = part[0, 0, at, :].astype(F32) + got1[0, at, :].astype(F32)
        for k in range(1, Q):
            gs = gs + got2[k - 1, at, :].astype(F32)
        xhat, inv = layer_norm_rows(resid[at, :])
        g_gain = g_gain + jnp.sum(gs * xhat, axis=0, keepdims=True)
        g_bias = g_bias + jnp.sum(gs, axis=0, keepdims=True)
        e = gs * gain[...]
        m1 = jnp.mean(e, axis=-1, keepdims=True)
        m2 = jnp.mean(e * xhat, axis=-1, keepdims=True)
        gr = cot[at, :].astype(F32) + inv * (e - m1 - xhat * m2)
        grad[at, :] = gr
        low[at, :] = gr.astype(BF)
    sums[0:1, :] = g_gain
    sums[1:2, :] = g_bias
    far = rcopy(low, all_low.at[pl.ds(c * N, N), :], fs.at[0], fs.at[1], (sib, z))
    near = lcopy(low, all_low.at[pl.ds(c * N, N), :], ls.at[0])
    far.start()
    near.start()
    for k in range(Q):
        s_x(k).wait_send()
    for k in range(1, Q):
        p_x(k).wait_send()
    near.wait()
    far.wait()


def resid_grads(Q, part, resid, cot, gain):
    N, D = resid.shape
    return pl.pallas_call(
        functools.partial(resid_kernel, Q),
        out_shape=[sds((N, D), F32), sds((2 * N, D), BF), sds((2, D), F32)],
        in_specs=[VM] * 4,
        out_specs=[VM, ANY, VM],
        scratch_shapes=[
            pltpu.VMEM((Q, N, D), BF), pltpu.VMEM((Q - 1, N, D), BF), pltpu.VMEM((Q - 1, N, D), BF), pltpu.VMEM((N, D), BF),
            DMA((Q,)), DMA((Q,)), DMA((Q - 1,)), DMA((Q - 1,)), DMA((2,)), DMA((1,)),
        ],
        compiler_params=pltpu.CompilerParams(collective_id=3, has_side_effects=True, vmem_limit_bytes=40 << 20),
        name="resid_grads",
    )(part, resid, cot, gain)


def final_kernel(Q, Z, B, gq, gk, gv, go, fu, fd, r0, r1, r2, r3, agq, agk, agv, ago, afu, afd, o0, o1, o2, o3,
                 bq, bk, bv, bo, zq, zk, zv, zo, dq, dk, dv, do, ps, pr, zs_, zr, gs_, gr, hs, hr, us, ur, vs, vr, ls, rs, rr):
    dp, c, q, z = where_am_i(Q, Z)
    sib = dp + 1 - 2 * c
    partners = [(sib, z)]
    for r in range(1, Z):
        for d in (dp, sib):
            partners.append((d, lax.rem(z + r, Z)))
    for k in range(1, Q):
        partners.append((2 * lax.rem(q + k, Q) + c, z))
    enter(partners)
    grads = [gq, gk, gv, go]
    bufs = [bq, bk, bv, bo]
    zbufs = [zq, zk, zv, zo]
    done = [dq, dk, dv, do]
    outs = [agq, agk, agv, ago]
    rows_in = [r0, r1, r2, r3]
    rows_out = [o0, o1, o2, o3]
    M = agq.shape[0] // Q
    OM = ago.shape[0] // Q
    RR = o0.shape[1]
    mine = c == z // B
    jz = lax.rem(z, B)
    zc = z // B

    def quarter(a, qq):
        n = OM if a == 3 else M
        return grads[a].at[:, pl.ds(qq * n, n), :]

    def p_x(a, k):
        return rcopy(quarter(a, lax.rem(q + k, Q)), bufs[a].at[k - 1], ps.at[a, k - 1], pr.at[a, k - 1],
                     (2 * lax.rem(q + k, Q) + c, z))

    def z_x(a, j):
        return rcopy(done[a].at[j], zbufs[a].at[z], zs_.at[a, j], zr.at[a, z], (dp, B * c + j))

    def z_arrive(a, zz):
        return rcopy(zbufs[a].at[zz], zbufs[a].at[zz], zs_.at[a, 0], zr.at[a, zz], (dp, z))

    def where_out(a, qq):
        n = OM if a == 3 else M
        return outs[a].at[pl.ds(qq * n, n), :]

    def f_out(i, d):
        return (afu if i == 0 else afd).at[d]

    def u_x(i, k):
        src = (fu, fd)[i]
        return rcopy(src, f_out(i, dp), us.at[i, k], ur.at[i, k], (2 * lax.rem(q + k, Q) + c, z))

    def v_x(i, k, d):
        src = (fu, fd)[i] if k == 0 else f_out(i, d)
        return rcopy(src, f_out(i, d), vs.at[i, k], vr.at[i, k], (sib, z))

    def u_l(i):
        return lcopy((fu, fd)[i], f_out(i, dp), ls.at[i])

    per = r0.shape[0] // RR

    def row_x(i, p):
        zt = c * per + p
        return rcopy(rows_in[i].at[pl.ds(p * RR, RR), :], rows_out[i].at[jz], rs.at[i, p], rr.at[i, jz], (2 * q + zc, zt))

    def row_l(i, p):
        return lcopy(rows_in[i].at[pl.ds(p * RR, RR), :], rows_out[i].at[jz], ls.at[2 + i])

    for a in range(4):
        for k in range(1, Q):
            p_x(a, k).start()
    for p in range(per):
        here = (c * per + p == z) & mine
        @pl.when(here)
        def _():
            for i in range(4):
                row_l(i, p).start()

        @pl.when(jnp.logical_not(here))
        def _():
            for i in range(4):
                row_x(i, p).start()
    for i in range(2):
        for k in range(1, Q):
            u_x(i, k).start()
        v_x(i, 0, dp).start()
        u_l(i).start()
    for a in range(4):
        n = OM if a == 3 else M
        for k in range(1, Q):
            p_x(a, k).wait_recv()
        for j in range(B):
            t = grads[a][j, pl.ds(pl.multiple_of(q * n, n), n), :].astype(F32)
            for k in range(1, Q):
                t = t + bufs[a][k - 1, j].astype(F32)
            done[a][j] = t.astype(BF)

            @pl.when(B * c + j != z)
            def _():
                z_x(a, j).start()
    @pl.when(mine)
    def _():
        for a in range(4):
            for zz in range(Z):
                @pl.when(zz != z)
                def _():
                    z_arrive(a, zz).wait_recv()
    for a in range(4):
        @pl.when(mine)
        def _():
            zbufs[a][z] = done[a][jz]
            t = zbufs[a][0].astype(F32)
            for zz in range(1, Z):
                t = t + zbufs[a][zz].astype(F32)
            n = OM if a == 3 else M
            outs[a][pl.ds(pl.multiple_of(q * n, n), n), :] = t.astype(BF)

    def g_x(a, k):
        return rcopy(where_out(a, q), where_out(a, q), gs_.at[a, k], gr.at[a, k], (2 * lax.rem(q + k, Q) + c, z))

    def h_x(a, k):
        qq = lax.rem(q + Q - k, Q)
        return rcopy(where_out(a, qq), where_out(a, qq), hs.at[a, k], hr.at[a, k], (sib, z))

    @pl.when(mine)
    def _():
        for a in range(4):
            for k in range(1, Q):
                g_x(a, k).start()
            h_x(a, 0).start()
    for i in range(2):
        for k in range(1, Q):
            u_x(i, k).wait_recv()
            v_x(i, k, 2 * lax.rem(q + Q - k, Q) + c).start()

    @pl.when(mine)
    def _():
        for a in range(4):
            for k in range(1, Q):
                g_x(a, k).wait_recv()
                h_x(a, k).start()

    @pl.when(mine)
    def _():
        for a in range(4):
            for k in range(1, Q):
                g_x(a, k).wait_send()
            for k in range(Q):
                h_x(a, k).wait_send()

    @pl.when(jnp.logical_not(mine))
    def _():
        for a in range(4):
            for k in range(Q):
                h_x(a, k).wait_recv()
    for a in range(4):
        for k in range(1, Q):
            p_x(a, k).wait_send()
        for j in range(B):
            @pl.when(B * c + j != z)
            def _():
                z_x(a, j).wait_send()
    for i in range(2):
        for k in range(1, Q):
            u_x(i, k).wait_send()
        for k in range(Q):
            v_x(i, k, dp).wait_send()
            v_x(i, k, dp).wait_recv()
        u_l(i).wait()
    for p in range(per):
        here = (c * per + p == z) & mine
        @pl.when(here)
        def _():
            for i in range(4):
                row_l(i, p).wait()

        @pl.when(jnp.logical_not(here))
        def _():
            for i in range(4):
                row_x(i, p).wait_send()
    for s in range(B):
        @pl.when(jnp.logical_not((B * c + s == z) & mine))
        def _():
            for i in range(4):
                rcopy(rows_out[i].at[s], rows_out[i].at[s], rs.at[i, 0], rr.at[i, s], (dp, z)).wait_recv()


def final_exchange(Q, Z, gq, gk, gv, go, fu, fd, r0, r1, r2, r3):
    B, D, H = gq.shape
    RR = r0.shape[0] * 2 // Z
    M, OM = D // Q, H // Q
    qs, os_ = (M, H), (OM, D)
    return pl.pallas_call(
        functools.partial(final_kernel, Q, Z, B),
        out_shape=[sds((D, H), BF)] * 3 + [sds((H, D), BF)]
        + [sds((2 * Q,) + fu.shape, BF), sds((2 * Q,) + fd.shape, BF)]
        + [sds((B, RR, D), BF)] * 4,
        in_specs=[VM] * 4 + [ANY] * 6,
        out_specs=[VM] * 4 + [ANY] * 6,
        scratch_shapes=[pltpu.VMEM((Q - 1, B) + qs, BF)] * 3 + [pltpu.VMEM((Q - 1, B) + os_, BF)]
        + [pltpu.VMEM((Z,) + qs, BF)] * 3 + [pltpu.VMEM((Z,) + os_, BF)]
        + [pltpu.VMEM((B,) + qs, BF)] * 3 + [pltpu.VMEM((B,) + os_, BF)]
        + [
            DMA((4, Q - 1)), DMA((4, Q - 1)), DMA((4, B)), DMA((4, Z)),
            DMA((4, Q)), DMA((4, Q)), DMA((4, Q)), DMA((4, Q)),
            DMA((2, Q)), DMA((2, Q)), DMA((2, Q)), DMA((2, Q)), DMA((6,)), DMA((4, 2)), DMA((4, B)),
        ],
        compiler_params=pltpu.CompilerParams(collective_id=4, has_side_effects=True, vmem_limit_bytes=40 << 20),
        name="final_exchange",
    )(gq, gk, gv, go, fu, fd, r0, r1, r2, r3)


def chip_device(Q, Z, tokens, memory, compressed, valid_counts, attention_norm_gain, attention_norm_bias,
                query_projection, key_projection, value_projection, out_weight, feedforward_norm_gain,
                feedforward_norm_bias, up_weight, up_bias, down_weight, down_bias, squeeze_weight, cotangent):
    B, R, D = tokens.shape
    H = query_projection.shape[1]
    FL = up_weight.shape[1]
    dp = lax.axis_index("dp")
    z = lax.axis_index("mp")
    c = lax.rem(dp, 2)
    S = R * Z
    N = S // 2
    E = FL // (2 * Q)
    jz = lax.rem(z, B)

    def turn_z(a, r):
        return lax.ppermute(a, "mp", [(i, (i + r) % Z) for i in range(Z)])

    def turn_q(a, k):
        return lax.ppermute(a, "dp", [(2 * i + s, 2 * ((i + k) % Q) + s) for i in range(Q) for s in range(2)])

    def swap(a):
        return lax.ppermute(a, "dp", [(i, i ^ 1) for i in range(2 * Q)])

    ctx, wqg, wkg, wvg, wog, ubg, vco = gather_inputs(
        Q, Z, compressed, memory, tokens, cotangent, query_projection, key_projection, value_projection, out_weight,
        up_bias.reshape(2 * Q, 1, E), jnp.broadcast_to(valid_counts[:, None, None], (B, 8, 128)),
    )
    counts = jnp.where(c == z // B, valid_counts, vco[:, 0, 0])
    count = jnp.where(jz == 0, counts[0], counts[1])
    up_own = lax.dynamic_slice_in_dim(up_weight, dp * E, E, 1)
    down_own = lax.dynamic_slice_in_dim(down_weight, dp * E, E, 0)
    up_loc = jnp.concatenate([up_own] + [turn_z(up_own, r) for r in range(1, Z)], axis=1)
    down_loc = jnp.concatenate([down_own] + [turn_z(down_own, r) for r in range(1, Z)], axis=0)
    ub_loc = ubg.reshape(Z * E)
    cot_own = lax.dynamic_slice_in_dim(ctx[3], c * N, N, 0)
    cot_q = jnp.stack([cot_own] + [turn_q(cot_own, k) for k in range(1, Q)])
    cot_all = jnp.stack([cot_q, swap(cot_q)], axis=1).reshape(2 * Q * N, D)

    rows = ctx[:3].reshape(3 * S, D).astype(F32)
    xhat1, inv1 = layer_norm_rows(rows)
    normed = (xhat1 * attention_norm_gain + attention_norm_bias).astype(BF)
    nt = normed[2 * S:]
    q_ = jnp.einsum("sd,jdh->sjh", nt, wqg, preferred_element_type=F32).astype(BF)
    k_ = jnp.einsum("sd,jdh->sjh", normed, wkg, preferred_element_type=F32).astype(BF)
    v_ = jnp.einsum("sd,jdh->sjh", normed, wvg, preferred_element_type=F32).astype(BF)
    heads = B * H // HEAD_DIM

    def by_heads(m):
        return m.reshape(m.shape[0], heads, HEAD_DIM)

    scale = HEAD_DIM ** (-0.5)
    qpos = jnp.arange(S)[:, None]
    kpos = jnp.arange(3 * S)[None, :] - 2 * S
    allowed = (kpos < 0) | ((kpos <= qpos) & (kpos < count))

    def scores_of():
        raw = jnp.einsum("qhe,khe->hqk", by_heads(q_), by_heads(k_), preferred_element_type=F32) * scale
        return jnp.where(allowed[None], raw, -1e30)

    scores = scores_of()
    peak = jnp.max(scores, axis=-1, keepdims=True)
    expo = jnp.exp(scores - peak)
    total = jnp.sum(expo, axis=-1, keepdims=True)
    log_total = peak + jnp.log(total)
    probs_low = (expo / total).astype(BF)
    mixed = jnp.einsum("hqk,khe->qhe", probs_low, by_heads(v_), preferred_element_type=F32).astype(BF)
    mixed = mixed.reshape(S, B, H)
    part = jnp.einsum("sjh,jhd->sd", mixed, wog, preferred_element_type=F32)
    resid, sec = second_rows(Q, part, ctx[2], feedforward_norm_gain.reshape(1, D), feedforward_norm_bias.reshape(1, D))
    sec = sec.reshape(2 * Q * N, D)
    upper = jnp.dot(sec, up_loc, preferred_element_type=F32) + ub_loc
    active, gelu_back = jax.vjp(jax.nn.gelu, upper)
    active = active.astype(BF)
    g_active = lax.dot_general(cot_all, down_loc, (((1,), (1,)), ((), ())), preferred_element_type=F32)
    g_upper = gelu_back(g_active)[0].astype(BF)
    g_sec = lax.dot_general(g_upper, up_loc, (((1,), (1,)), ((), ())), preferred_element_type=F32)
    g_sec = g_sec.astype(BF).reshape(Q, 2, N, D)
    g_resid, g_low, ff_sums = resid_grads(Q, g_sec, resid, cot_own, feedforward_norm_gain.reshape(1, D))
    down = jnp.dot(active, down_loc, preferred_element_type=F32).astype(BF).reshape(Q, 2, N, D)
    down_half = down[:, 0].astype(F32) + swap(down[:, 1]).astype(F32)
    down_low = down_half.astype(BF)
    down_sum = down_half[0]
    for k in range(1, Q):
        down_sum = down_sum + turn_q(down_low[k], Q - k).astype(F32)
    output = (resid + down_sum + down_bias).astype(BF)
    up_grad = lax.dot_general(sec, g_upper, (((0,), (0,)), ((), ())), preferred_element_type=F32)
    down_grad = lax.dot_general(active, cot_all, (((0,), (0,)), ((), ())), preferred_element_type=F32)
    ub_grad = jnp.sum(g_upper.astype(F32), axis=0).reshape(Z, E)
    fu = up_grad[:, :E]
    fd = down_grad[:E]
    up_low, down_g_low = up_grad.astype(BF), down_grad.astype(BF)
    for r in range(1, Z):
        fu = fu + turn_z(up_low[:, r * E:(r + 1) * E], Z - r).astype(F32)
        fd = fd + turn_z(down_g_low[r * E:(r + 1) * E], Z - r).astype(F32)

    go = jnp.einsum("sjh,sd->jhd", mixed, g_low, preferred_element_type=F32).astype(BF)
    g_mixed = jnp.einsum("sd,jhd->sjh", g_low, wog, preferred_element_type=F32).astype(BF).reshape(S, B * H)
    probs = jnp.exp(scores_of() - log_total)
    g_probs = jnp.einsum("qhe,khe->hqk", by_heads(g_mixed), by_heads(v_), preferred_element_type=F32)
    row_dot = jnp.sum(probs * g_probs, axis=-1, keepdims=True)
    g_scores = (probs * (g_probs - row_dot)).astype(BF)
    gq_ = (scale * jnp.einsum("hqk,khe->qhe", g_scores, by_heads(k_), preferred_element_type=F32)).astype(BF)
    gk_ = (scale * jnp.einsum("hqk,qhe->khe", g_scores, by_heads(q_), preferred_element_type=F32)).astype(BF)
    gv_ = jnp.einsum("hqk,qhe->khe", probs.astype(BF), by_heads(g_mixed), preferred_element_type=F32).astype(BF)
    gq_, gk_, gv_ = (g.reshape(g.shape[0], B, H) for g in (gq_, gk_, gv_))
    gwq = jnp.einsum("sd,sjh->jdh", nt, gq_, preferred_element_type=F32).astype(BF)
    gwk = jnp.einsum("sd,sjh->jdh", normed, gk_, preferred_element_type=F32).astype(BF)
    gwv = jnp.einsum("sd,sjh->jdh", normed, gv_, preferred_element_type=F32).astype(BF)
    g_normed = jnp.einsum("sjh,jdh->sd", gk_, wkg, preferred_element_type=F32)
    g_normed = g_normed + jnp.einsum("sjh,jdh->sd", gv_, wvg, preferred_element_type=F32)
    g_normed = g_normed.at[2 * S:].add(jnp.einsum("sjh,jdh->sd", gq_, wqg, preferred_element_type=F32))
    at_gain = jnp.sum(g_normed * xhat1, axis=0)
    at_bias = jnp.sum(g_normed, axis=0)
    keep = lax.dynamic_slice_in_dim(g_normed, 2 * S + c * N, N, 0)
    give = lax.dynamic_slice_in_dim(g_normed, 2 * S + (1 - c) * N, N, 0)
    gn = keep + swap(give)
    xt = lax.dynamic_slice_in_dim(xhat1, 2 * S + c * N, N, 0)
    it = lax.dynamic_slice_in_dim(inv1, 2 * S + c * N, N, 0)
    e = gn * attention_norm_gain
    tokens_grad = g_resid + it * (
        e - jnp.mean(e, axis=-1, keepdims=True) - xt * jnp.mean(e * xt, axis=-1, keepdims=True)
    )

    new_memory = lax.dynamic_slice_in_dim(ctx[1:3].reshape(2 * S, D), count + c * N, N, 0)
    groups = S // RATE
    squeezed = jnp.zeros((groups, D), F32)
    for r in range(RATE):
        pick = (jnp.arange(groups)[:, None] * RATE + r == jnp.arange(S)[None, :]).astype(BF)
        picked = jnp.dot(pick, ctx[1], preferred_element_type=F32).astype(BF)
        squeezed = squeezed + jnp.dot(picked, squeeze_weight[r * D:(r + 1) * D], preferred_element_type=F32)
    stacked = jnp.concatenate([ctx[0], squeezed.astype(BF), jnp.zeros((8, D), BF)], axis=0)
    new_compressed = lax.dynamic_slice_in_dim(stacked, count // RATE + c * N, N, 0)

    agq, agk, agv, ago, afu, afd, o_out, o_tg, o_nm, o_nc = final_exchange(
        Q, Z, gwq, gwk, gwv, go, fu.astype(BF), fd.astype(BF), output, tokens_grad.astype(BF), new_memory, new_compressed
    )
    local_down_bias = jnp.sum(cotangent.astype(F32), axis=(0, 1))
    ub_slots = jnp.zeros((Z, 2 * Q, E), F32)
    for r in range(Z):
        ub_slots = lax.dynamic_update_slice(ub_slots, ub_grad[r].reshape(1, 1, E), (lax.rem(z + Z - r, Z), dp, 0))
    small = jnp.concatenate([
        jnp.stack([at_gain, at_bias, ff_sums[0], ff_sums[1], local_down_bias]).reshape(-1), ub_slots.reshape(-1)
    ])
    small = lax.psum(small, ("dp", "mp"))
    vecs = small[:5 * D].reshape(5, D)
    ub_out = lax.dynamic_slice_in_dim(small[5 * D:], z * FL, FL, 0)
    up_out = jnp.swapaxes(afu, 0, 1).reshape(D, FL).astype(F32)
    down_out = afd.reshape(FL, D).astype(F32)
    return (
        o_out, o_tg.astype(F32), vecs[0], vecs[1], agq.astype(F32), agk.astype(F32), agv.astype(F32), ago.astype(F32),
        vecs[2], vecs[3], up_out, ub_out, down_out, vecs[4], o_nm, o_nc,
    )


def solution(mesh):
    in_specs = (
        P("dp", "mp", None),
        P("dp", "mp", None),
        P("dp", "mp", None),
        P("dp"),
        P(),
        P(),
        P(None, "mp"),
        P(None, "mp"),
        P(None, "mp"),
        P("mp", None),
        P(),
        P(),
        P(None, "mp"),
        P("mp"),
        P("mp", None),
        P(),
        P(),
        P("dp", "mp", None),
    )
    out_specs = (
        P("dp", "mp", None),
        P("dp", "mp", None),
        P(),
        P(),
        P(None, "mp"),
        P(None, "mp"),
        P(None, "mp"),
        P("mp", None),
        P(),
        P(),
        P(None, "mp"),
        P("mp"),
        P("mp", None),
        P(),
        P("dp", "mp", None),
        P("dp", "mp", None),
    )
    Q, Z = mesh.shape["dp"] // 2, mesh.shape["mp"]

    def per_device(*args):
        B, R, D = args[0].shape
        H, FL = args[6].shape[1], args[12].shape[1]
        whole = B == 2 and 2 * B == Z and H % HEAD_DIM == 0 and D % (16 * Q) == 0 and H % (16 * Q) == 0
        if whole and R % 32 == 0 and FL % (256 * Q) == 0:
            return chip_device(Q, Z, *args)
        return general_device(*args)

    return jax.shard_map(
        per_device, mesh=mesh, in_specs=in_specs, out_specs=out_specs, check_vma=False
    )
```

```python
import functools

import jax
import jax.numpy as jnp
from jax import lax
from jax.experimental import pallas as pl
from jax.experimental.pallas import tpu as pltpu
from jax.sharding import PartitionSpec as P

HEAD_DIM = 128
RATE = 3


def apply_layer_norm(rows):
    center = jnp.mean(rows, axis=-1, keepdims=True)
    centered = rows - center
    spread = jnp.mean(centered * centered, axis=-1, keepdims=True)
    inverse_deviation = lax.rsqrt(spread + 1e-05)
    return (centered * inverse_deviation, inverse_deviation)


def norm_backward_pass(input_gradient, standardized_rows, inverse_deviation, scale_factor):
    scaled_rows = input_gradient * scale_factor
    attention_norm_mean = jnp.mean(scaled_rows, axis=-1, keepdims=True)
    feedforward_norm_mean = jnp.mean(scaled_rows * standardized_rows, axis=-1, keepdims=True)
    return inverse_deviation * (
        scaled_rows - attention_norm_mean - standardized_rows * feedforward_norm_mean
    )


def squeeze_rows(old_comp, old_mem, fresh, valid_count, offset, own_rows, squeeze_weight):
    features = old_mem.shape[1]
    joined = jnp.concatenate([old_mem, fresh], axis=0)
    new_memory = lax.dynamic_slice_in_dim(joined, valid_count + offset, own_rows, 0)
    comp_len = old_comp.shape[0]
    evicted = valid_count // RATE
    first_row = evicted + offset
    window_start = jnp.maximum(first_row - comp_len, 0)
    padded = jnp.concatenate(
        [old_mem, jnp.zeros((RATE * own_rows, features), jnp.bfloat16)], axis=0
    )
    window = lax.dynamic_slice_in_dim(padded, window_start * RATE, RATE * own_rows, 0)
    squeezed = jnp.dot(
        window.reshape(own_rows, RATE * features),
        squeeze_weight,
        preferred_element_type=jnp.float32,
    ).astype(jnp.bfloat16)
    positions = first_row + jnp.arange(own_rows)
    from_old = jnp.take(old_comp, jnp.clip(positions, 0, comp_len - 1), axis=0)
    from_new = jnp.take(
        squeezed, jnp.clip(positions - comp_len - window_start, 0, own_rows - 1), axis=0
    )
    new_compressed = jnp.where((positions < comp_len)[:, None], from_old, from_new)
    return (new_memory, new_compressed)


def general_device(
    tokens,
    memory,
    compressed,
    valid_counts,
    attention_norm_gain,
    attention_norm_bias,
    query_projection,
    key_projection,
    value_projection,
    out_weight,
    feedforward_norm_gain,
    feedforward_norm_bias,
    up_weight,
    up_bias,
    down_weight,
    down_bias,
    squeeze_weight,
    cotangent,
):
    batch_segs, own_rows, features = tokens.shape
    offset = lax.axis_index("mp") * own_rows
    old_comp, old_mem, fresh = (
        lax.all_gather(compressed, "mp", axis=1, tiled=True),
        lax.all_gather(memory, "mp", axis=1, tiled=True),
        lax.all_gather(tokens, "mp", axis=1, tiled=True),
    )
    seg_len = fresh.shape[1]
    prior_rows = old_comp.shape[1] + old_mem.shape[1]
    context_tokens = jnp.concatenate([old_comp, old_mem, fresh], axis=1).astype(jnp.float32)
    ctx_len = context_tokens.shape[1]
    standardized_full, inverse_deviation_full = apply_layer_norm(context_tokens)
    normed_rows = (standardized_full * attention_norm_gain + attention_norm_bias).astype(
        jnp.bfloat16
    )
    token_rows_normed = normed_rows[:, prior_rows:]
    queries = jnp.einsum(
        "xhp,pj->xhj", token_rows_normed, query_projection, preferred_element_type=jnp.float32
    ).astype(jnp.bfloat16)
    key_rows = jnp.einsum(
        "xhp,pj->xhj", normed_rows, key_projection, preferred_element_type=jnp.float32
    ).astype(jnp.bfloat16)
    values = jnp.einsum(
        "xhp,pj->xhj", normed_rows, value_projection, preferred_element_type=jnp.float32
    ).astype(jnp.bfloat16)
    local_heads = query_projection.shape[1] // HEAD_DIM
    score_scale = HEAD_DIM ** (-0.5)

    def by_heads(matrix):
        return matrix.reshape(matrix.shape[0], matrix.shape[1], local_heads, HEAD_DIM)

    query_pos = jnp.arange(seg_len)[:, None]
    key_pos = jnp.arange(ctx_len)[None, :] - prior_rows
    allowed = (key_pos[None] < 0) | (key_pos <= query_pos)[None] & (
        key_pos[None] < valid_counts[:, None, None]
    )

    def scores_of(query_in, key_in):
        raw = (
            jnp.einsum(
                "gqhe,gkhe->ghqk",
                by_heads(query_in),
                by_heads(key_in),
                preferred_element_type=jnp.float32,
            )
            * score_scale
        )
        return jnp.where(allowed[:, None], raw, -1e30)

    scores = scores_of(queries, key_rows)
    peak_score = jnp.max(scores, axis=-1, keepdims=True)
    exponent = jnp.exp(scores - peak_score)
    exp_total = jnp.sum(exponent, axis=-1, keepdims=True)
    log_total = peak_score + jnp.log(exp_total)
    probs_low = (exponent / exp_total).astype(jnp.bfloat16)
    mixed_heads = jnp.einsum(
        "ghqk,gkhe->gqhe", probs_low, by_heads(values), preferred_element_type=jnp.float32
    ).astype(jnp.bfloat16)
    mixed_heads = mixed_heads.reshape(batch_segs, seg_len, local_heads * HEAD_DIM)
    partial_attn = jnp.einsum(
        "gsc,cd->gsd", mixed_heads, out_weight, preferred_element_type=jnp.float32
    )
    attention = lax.psum_scatter(partial_attn, "mp", scatter_dimension=1, tiled=True)
    residual_stream = tokens.astype(jnp.float32) + attention
    standardized_feedforward, inverse_deviation_feedforward = apply_layer_norm(residual_stream)
    feedforward_input = (
        standardized_feedforward * feedforward_norm_gain + feedforward_norm_bias
    ).astype(jnp.bfloat16)
    second_all = lax.all_gather(feedforward_input, "mp", axis=1, tiled=True)
    upper_in = (
        jnp.einsum("gsd,df->gsf", second_all, up_weight, preferred_element_type=jnp.float32)
        + up_bias
    )
    active, gelu_back = jax.vjp(jax.nn.gelu, upper_in)
    active_low = active.astype(jnp.bfloat16)
    partial_ffn = jnp.einsum(
        "gsf,fd->gsd", active_low, down_weight, preferred_element_type=jnp.float32
    )
    down_out = lax.psum_scatter(
        partial_ffn.astype(jnp.bfloat16), "mp", scatter_dimension=1, tiled=True
    ).astype(jnp.float32)
    output = (residual_stream + down_out + down_bias).astype(jnp.bfloat16)

    def update_one(comp_seg, mem_seg, fresh_seg, valid_count):
        return squeeze_rows(
            comp_seg, mem_seg, fresh_seg, valid_count, offset, own_rows, squeeze_weight
        )

    new_memory, new_compressed = jax.vmap(update_one)(old_comp, old_mem, fresh, valid_counts)
    output_gradient = cotangent.astype(jnp.float32)
    down_bias_grad = jnp.sum(output_gradient, axis=(0, 1))
    grad_all = lax.all_gather(cotangent, "mp", axis=1, tiled=True)
    down_weight_grad = jnp.einsum(
        "gsf,gsd->fd", active_low, grad_all, preferred_element_type=jnp.float32
    )
    grad_active = jnp.einsum(
        "gsd,fd->gsf", grad_all, down_weight, preferred_element_type=jnp.float32
    )
    grad_upper = gelu_back(grad_active)[0].astype(jnp.bfloat16)
    up_weight_grad = jnp.einsum(
        "gsd,gsf->df", second_all, grad_upper, preferred_element_type=jnp.float32
    )
    up_bias_grad = jnp.sum(grad_upper.astype(jnp.float32), axis=(0, 1))
    partial_second = jnp.einsum(
        "gsf,df->gsd", grad_upper, up_weight, preferred_element_type=jnp.float32
    )
    feedforward_gradient = lax.psum_scatter(partial_second, "mp", scatter_dimension=1, tiled=True)
    feedforward_gain_gradient = jnp.sum(
        feedforward_gradient * standardized_feedforward, axis=(0, 1)
    )
    second_bias_grad = jnp.sum(feedforward_gradient, axis=(0, 1))
    residual_gradient = output_gradient + norm_backward_pass(
        feedforward_gradient,
        standardized_feedforward,
        inverse_deviation_feedforward,
        feedforward_norm_gain,
    )
    grad_resid_all = lax.all_gather(
        residual_gradient.astype(jnp.bfloat16), "mp", axis=1, tiled=True
    )
    out_weight_grad = jnp.einsum(
        "gsc,gsd->cd", mixed_heads, grad_resid_all, preferred_element_type=jnp.float32
    )
    grad_mixed = jnp.einsum(
        "gsd,cd->gsc", grad_resid_all, out_weight, preferred_element_type=jnp.float32
    ).astype(jnp.bfloat16)
    probs_again = jnp.exp(scores_of(queries, key_rows) - log_total)
    grad_probs = jnp.einsum(
        "gqhe,gkhe->ghqk",
        by_heads(grad_mixed),
        by_heads(values),
        preferred_element_type=jnp.float32,
    )
    row_dot = jnp.sum(probs_again * grad_probs, axis=-1, keepdims=True)
    grad_scores = (probs_again * (grad_probs - row_dot)).astype(jnp.bfloat16)
    query_gradient = (
        score_scale
        * jnp.einsum(
            "ghqk,gkhe->gqhe", grad_scores, by_heads(key_rows), preferred_element_type=jnp.float32
        )
    ).astype(jnp.bfloat16)
    key_gradient = (
        score_scale
        * jnp.einsum(
            "ghqk,gqhe->gkhe", grad_scores, by_heads(queries), preferred_element_type=jnp.float32
        )
    ).astype(jnp.bfloat16)
    value_gradient = jnp.einsum(
        "ghqk,gqhe->gkhe",
        probs_again.astype(jnp.bfloat16),
        by_heads(grad_mixed),
        preferred_element_type=jnp.float32,
    ).astype(jnp.bfloat16)
    query_gradient = query_gradient.reshape(batch_segs, seg_len, -1)
    key_gradient = key_gradient.reshape(batch_segs, ctx_len, -1)
    value_gradient = value_gradient.reshape(batch_segs, ctx_len, -1)
    query_weight_grad = jnp.einsum(
        "nja,njr->ar", token_rows_normed, query_gradient, preferred_element_type=jnp.float32
    )
    key_weight_grad = jnp.einsum(
        "nja,njr->ar", normed_rows, key_gradient, preferred_element_type=jnp.float32
    )
    value_weight_grad = jnp.einsum(
        "nja,njr->ar", normed_rows, value_gradient, preferred_element_type=jnp.float32
    )
    partial_normed = jnp.einsum(
        "xmo,qo->xmq", key_gradient, key_projection, preferred_element_type=jnp.float32
    )
    partial_normed = partial_normed + jnp.einsum(
        "xmo,qo->xmq", value_gradient, value_projection, preferred_element_type=jnp.float32
    )
    partial_normed = partial_normed.at[:, prior_rows:].add(
        jnp.einsum(
            "xmo,qo->xmq", query_gradient, query_projection, preferred_element_type=jnp.float32
        )
    )
    partial_normed = partial_normed.reshape(batch_segs, 3, seg_len, features)
    normed_gradient = lax.psum_scatter(
        partial_normed.astype(jnp.bfloat16), "mp", scatter_dimension=2, tiled=True
    ).astype(jnp.float32)
    segment_context = jnp.stack([compressed, memory, tokens], axis=1).astype(jnp.float32)
    standardized_segment, inverse_deviation_segment = apply_layer_norm(segment_context)
    attention_gain_gradient = jnp.sum(normed_gradient * standardized_segment, axis=(0, 1, 2))
    first_bias_grad = jnp.sum(normed_gradient, axis=(0, 1, 2))
    tokens_grad = residual_gradient + norm_backward_pass(
        normed_gradient[:, 2],
        standardized_segment[:, 2],
        inverse_deviation_segment[:, 2],
        attention_norm_gain,
    )
    summed = (
        lax.psum(query_weight_grad.astype(jnp.bfloat16), "dp").astype(jnp.float32),
        lax.psum(key_weight_grad.astype(jnp.bfloat16), "dp").astype(jnp.float32),
        lax.psum(value_weight_grad.astype(jnp.bfloat16), "dp").astype(jnp.float32),
        lax.psum(out_weight_grad.astype(jnp.bfloat16), "dp").astype(jnp.float32),
        lax.psum(up_weight_grad.astype(jnp.bfloat16), "dp").astype(jnp.float32),
        lax.psum(up_bias_grad.astype(jnp.bfloat16), "dp").astype(jnp.float32),
        lax.psum(down_weight_grad.astype(jnp.bfloat16), "dp").astype(jnp.float32),
    )
    norms = lax.psum(
        (
            attention_gain_gradient,
            first_bias_grad,
            feedforward_gain_gradient,
            second_bias_grad,
            down_bias_grad,
        ),
        ("dp", "mp"),
    )
    return (
        output,
        tokens_grad,
        norms[0],
        norms[1],
        summed[0],
        summed[1],
        summed[2],
        summed[3],
        norms[2],
        norms[3],
        summed[4],
        summed[5],
        summed[6],
        norms[4],
        new_memory,
        new_compressed,
    )


BF = jnp.bfloat16
F32 = jnp.float32
MESH = pl.DeviceIdType.MESH
ANY = pl.BlockSpec(memory_space=pl.ANY)
VM = pl.BlockSpec(memory_space=pltpu.VMEM)
DMA = pltpu.SemaphoreType.DMA


def sds(shape, dtype):
    return jax.ShapeDtypeStruct(shape, dtype)


def where_am_i(chips, depth):
    dp = lax.axis_index("dp")
    return dp, lax.rem(dp, 2), dp // 2, lax.axis_index("mp")


def rcopy(src, dst, send, recv, device):
    return pltpu.make_async_remote_copy(
        src_ref=src,
        dst_ref=dst,
        send_sem=send,
        recv_sem=recv,
        device_id=device,
        device_id_type=MESH,
    )


def lcopy(src, dst, sem):
    return pltpu.make_async_copy(src, dst, sem)


def enter(partners):
    barrier = pltpu.get_barrier_semaphore()
    for p in partners:
        pl.semaphore_signal(barrier, inc=1, device_id=p, device_id_type=MESH)
    pl.semaphore_wait(barrier, len(partners))


def across(q, k):
    if k == 0:
        return q
    if k == 1:
        return q + 1 - 2 * lax.rem(q, 2)
    if k == 2:
        return lax.rem(q + 2, 4)
    return 3 - q


def layer_norm_rows(rows):
    center = jnp.mean(rows, axis=-1, keepdims=True)
    centered = rows - center
    spread = jnp.mean(centered * centered, axis=-1, keepdims=True)
    inv = lax.rsqrt(spread + 1e-05)
    return centered * inv, inv


class Slots:
    def __init__(self, ref):
        self.ref = ref
        self.used = 0

    def take(self, *shape):
        base = self.used
        size = 1
        for n in shape:
            size *= n
        self.used += size

        def at(*index):
            flat = 0
            for n, i in zip(shape, index):
                flat = flat * n + i
            return self.ref.at[base + flat]

        return at


def nt_dot(a, b):
    return lax.dot_general(a, b, (((1,), (1,)), ((), ())), preferred_element_type=F32)


def tn_dot(a, b):
    return lax.dot_general(a, b, (((0,), (0,)), ((), ())), preferred_element_type=F32)


def nn_dot(a, b):
    return jnp.dot(a, b, preferred_element_type=F32)


def one_hot(shape, offset):
    row = lax.broadcasted_iota(jnp.int32, shape, 0)
    col = lax.broadcasted_iota(jnp.int32, shape, 1)
    return jnp.where(col == row + offset, 1.0, 0.0).astype(BF)


FRONT_SEMS = 400


def front_kernel(Q, Z, comp, mem, tok, cot, wq, wk, wv, wo, up, down, ub, vc, sq, g1, b1, g2, b2,
                 tok_o, normed_o, q_o, k_o, v_o, probs_o, mixed_o, wq_o, wk_o, wv_o, wo_o,
                 resid_o, gresid_o, glow_o, gu_o, gd_o, down_o, small_o, nm_o, nc_o,
                 ctx, normed, wqs, wks, wvs, wos, qs, ks, vs, probs, mixed, phalf, got, resid, sec, cots, ups, downs,
                 ubs, vco, act, gup, gbuf, got1, send2, got2, low, nms, ncs, gus, gds, dns, sems):
    dp, c, q, z = where_am_i(Q, Z)
    sib = dp + 1 - 2 * c
    partners = [(sib, z)]
    for r in range(1, Z):
        for d in (dp, sib):
            partners.append((d, lax.rem(z + r, Z)))
    for k in range(1, Q):
        partners.append((2 * across(q, k) + c, z))
    enter(partners)
    B, R, D = tok.shape
    H = wq.shape[1]
    QR = D // Q
    OR = H // Q
    HR = R // 2
    S = R * Z
    N = S // 2
    E = up.shape[1] // (2 * Q)
    heads = B * H // HEAD_DIM
    mine = c == z // B
    jz = lax.rem(z, B)
    al = Slots(sems)

    def peer(k):
        return (2 * across(q, k) + c, z)

    wins = [wq, wk, wv, wo]
    wss = [wqs, wks, wvs, wos]

    def piece(a):
        if a < 3:
            return wins[a].at[pl.ds(q * QR, QR), :]
        return wo.at[pl.ds(q * OR, OR), :]

    def place(a, j, qq):
        if a < 3:
            return wss[a].at[pl.ds(pl.multiple_of(qq * QR, QR), QR), pl.ds(pl.multiple_of(j * H, H), H)]
        return wos.at[pl.ds(pl.multiple_of(j * H + qq * OR, OR), OR), :]

    def place_whole(a, j):
        if a < 3:
            return wss[a].at[:, pl.ds(pl.multiple_of(j * H, H), H)]
        return wos.at[pl.ds(pl.multiple_of(j * H, H), H), :]

    ws, wr = al.take(4, Z - 1), al.take(4, B)
    ps, pr = al.take(4, B, Q - 1), al.take(4, B, Q - 1)
    wl = al.take(4)

    def w_z(a, r):
        return rcopy(piece(a), place(a, jz, q), ws(a, r - 1), wr(a, jz), (dp, lax.rem(z + r, Z)))

    def w_arrive(a, j):
        return rcopy(place(a, j, q), place(a, j, q), ws(a, 0), wr(a, j), (dp, z))

    def w_p(a, j, k, qq):
        return rcopy(place(a, j, qq), place(a, j, qq), ps(a, j, k - 1), pr(a, j, k - 1), peer(k))

    def w_l(a):
        return lcopy(wins[a], place_whole(a, jz), wl(a))

    acts = [comp, mem, tok]
    cs, cr = al.take(3, B, 2), al.take(3, Z)
    fs, fr = al.take(3, Z), al.take(3, Z)
    cl = al.take(3)

    def c_rows(t, zs):
        return ctx.at[t, pl.ds(pl.multiple_of(zs * R, R), R), :]

    def c_half(t, zs, h):
        return ctx.at[t, pl.ds(pl.multiple_of(zs * R + HR * h, HR), HR), :]

    def c_l(t):
        return lcopy(acts[t].at[jz], c_rows(t, z), cl(t))

    def c_sib(t):
        return rcopy(acts[t].at[jz], c_rows(t, z), fs(t, z), fr(t, z), (sib, z))

    def c_z(t, s, h):
        return rcopy(acts[t].at[s, pl.ds(HR * h, HR), :], c_half(t, z, h), cs(t, s, h), cr(t, z), (2 * q + h, B * c + s))

    def c_arrive(t, zs):
        return rcopy(c_half(t, zs, c), c_half(t, zs, c), cs(t, 0, 0), cr(t, zs), (dp, z))

    def c_fwd(t, zs, half):
        return rcopy(c_half(t, zs, half), c_half(t, zs, half), fs(t, zs), fr(t, zs), (sib, z))

    us, ur, ul = al.take(Z - 1), al.take(Z - 1), al.take(1)
    vs_, vr_ = al.take(1), al.take(1)

    def u_z(r):
        return rcopy(ub.at[dp], ubs.at[r], us(r - 1), ur(r - 1), (dp, lax.rem(z + r, Z)))

    u_l = lcopy(ub.at[dp], ubs.at[0], ul(0))
    v_s = rcopy(vc, vco, vs_(0), vr_(0), (sib, z))

    ts, tr, tl = al.take(B), al.take(B), al.take(1)
    tps, tpr, tfs, tfr = al.take(Q), al.take(Q), al.take(Q), al.take(Q)

    def slot(ref, k, cc):
        return ref.at[pl.ds((2 * k + cc) * N, N), :]

    def t_z(s):
        return rcopy(cot.at[s], cots.at[pl.ds(pl.multiple_of(jz * R, R), R), :], ts(s), tr(jz), (2 * q + z // B, B * c + s))

    def t_l():
        return lcopy(cot.at[jz], cots.at[pl.ds(pl.multiple_of(jz * R, R), R), :], tl(0))

    def t_arrive(i):
        return rcopy(cots.at[pl.ds(i * R, R), :], cots.at[pl.ds(i * R, R), :], ts(0), tr(i), (dp, z))

    def t_p(k):
        return rcopy(slot(cots, 0, 0), slot(cots, k, 0), tps(k), tpr(k), peer(k))

    def t_f(k):
        return rcopy(slot(cots, k, 0), slot(cots, k, 1), tfs(k), tfr(k), (sib, z))

    xs, xr_, xl = al.take(2, Z), al.take(2, Z), al.take(2)

    def x_z(i, r):
        if i == 0:
            return rcopy(up.at[:, pl.ds(pl.multiple_of(dp * E, E), E)], ups.at[:, pl.ds(r * E, E)], xs(0, r), xr_(0, r),
                         (dp, lax.rem(z + r, Z)))
        return rcopy(down.at[pl.ds(pl.multiple_of(dp * E, E), E), :], downs.at[pl.ds(r * E, E), :], xs(1, r), xr_(1, r),
                     (dp, lax.rem(z + r, Z)))

    x_l = [lcopy(up.at[:, pl.ds(pl.multiple_of(dp * E, E), E)], ups.at[:, pl.ds(0, E)], xl(0)),
           lcopy(down.at[pl.ds(pl.multiple_of(dp * E, E), E), :], downs.at[pl.ds(0, E), :], xl(1))]

    @pl.when(mine)
    def _():
        for a in range(4):
            for r in range(1, Z):
                w_z(a, r).start()
        for a in range(4):
            w_l(a).start()
        for t in range(3):
            c_l(t).start()
            c_sib(t).start()
    for r in range(1, Z):
        u_z(r).start()
    v_s.start()
    u_l.start()
    for x in x_l:
        x.start()
    for j in range(B):
        @pl.when(B * c + j != z)
        def _():
            for a in range(4):
                w_arrive(a, j).wait_recv()
                for k in range(1, Q):
                    w_p(a, j, k, q).start()
    for s in range(B):
        @pl.when(B * c + s != z)
        def _():
            for t in range(3):
                for h in range(2):
                    c_z(t, s, h).start()

    def norm_block(t, zs):
        at = pl.ds(pl.multiple_of(zs * R, R), R)
        to = pl.ds(pl.multiple_of(t * S + zs * R, R), R)
        xhat, _ = layer_norm_rows(ctx[t, at, :].astype(F32))
        normed[to, :] = (xhat * g1[...] + b1[...]).astype(BF)

    @pl.when(mine)
    def _():
        for t in range(3):
            c_l(t).wait()

    @pl.when(jnp.logical_not(mine))
    def _():
        for t in range(3):
            rcopy(c_rows(t, z), c_rows(t, z), fs(t, z), fr(t, z), (sib, z)).wait_recv()

    def norm_own(t, carry):
        norm_block(t, z)
        return carry

    lax.fori_loop(0, 3, norm_own, 0)
    for r in range(1, Z):
        zs = lax.rem(z + r, Z)
        for t in range(3):
            c_arrive(t, zs).wait_recv()
            c_fwd(t, zs, c).start()
    for s in range(B):
        @pl.when(B * c + s != z)
        def _():
            for t in range(3):
                for h in range(2):
                    c_z(t, s, h).wait_send()
    for s in range(B):
        here = (B * c + s == z) & mine

        @pl.when(here)
        def _():
            t_l().start()

        @pl.when(jnp.logical_not(here))
        def _():
            t_z(s).start()
    for i in range(2):
        for r in range(1, Z):
            x_z(i, r).start()
    for r in range(1, Z):
        zs = lax.rem(z + r, Z)
        for t in range(3):
            c_fwd(t, zs, 1 - c).wait_recv()

        def norm_one(t, carry, zs=zs):
            norm_block(t, zs)
            return carry

        lax.fori_loop(0, 3, norm_one, 0)
    outs = al.take(16)
    copies = []

    def leave(src, dst):
        cp = lcopy(src, dst, outs(len(copies)))
        cp.start()
        copies.append(cp)

    leave(normed, normed_o)
    leave(ctx.at[2], tok_o)
    for j in range(B):
        @pl.when(B * c + j != z)
        def _():
            for a in range(4):
                for k in range(1, Q):
                    w_p(a, j, k, across(q, k)).wait_recv()

    @pl.when(mine)
    def _():
        for a in range(4):
            w_l(a).wait()
    for a in range(4):
        leave(wss[a], (wq_o, wk_o, wv_o, wo_o)[a])

    T = 256

    def project(i, carry):
        at = pl.ds(pl.multiple_of(i * T, T), T)
        ks[at, :] = nn_dot(normed[at, :], wks[...]).astype(BF)
        vs[at, :] = nn_dot(normed[at, :], wvs[...]).astype(BF)
        return carry

    lax.fori_loop(0, 3 * S // T, project, 0)

    def project_q(i, carry):
        at = pl.ds(pl.multiple_of(i * T, T), T)
        qs[at, :] = nn_dot(normed[pl.ds(pl.multiple_of(2 * S + i * T, T), T), :], wqs[...]).astype(BF)
        return carry

    lax.fori_loop(0, S // T, project_q, 0)
    leave(qs, q_o)
    leave(ks, k_o)
    leave(vs, v_o)

    v_s.wait()
    counts = jnp.where(mine, vc[jz], vco[jz])
    count = counts[0:1, 0:1]
    scale = HEAD_DIM ** (-0.5)
    P2 = 2 * S
    pouts = al.take(2, heads)

    def attend(half, tag):
        r0 = pl.multiple_of(half * N, N)

        def head(h, carry):
            hd = pl.ds(pl.multiple_of(h * HEAD_DIM, HEAD_DIM), HEAD_DIM)
            qh = qs[pl.ds(r0, N), hd]
            s1 = nt_dot(qh, ks[pl.ds(0, P2), hd])
            s2 = nt_dot(qh, ks[pl.ds(P2, S), hd])
            row = lax.broadcasted_iota(jnp.int32, (N, S), 0) + half * N
            col = lax.broadcasted_iota(jnp.int32, (N, S), 1)
            s2 = jnp.where((col <= row) & (col < count), s2, -1e30)
            top = jnp.maximum(jnp.max(s1, axis=-1, keepdims=True), jnp.max(s2, axis=-1, keepdims=True))
            p1 = jnp.exp((s1 - top) * scale)
            p2 = jnp.exp((s2 - top) * scale)
            inv = 1.0 / (jnp.sum(p1, axis=-1, keepdims=True) + jnp.sum(p2, axis=-1, keepdims=True))
            p1 = (p1 * inv).astype(BF)
            p2 = (p2 * inv).astype(BF)
            probs[h, pl.ds(r0, N), pl.ds(0, P2)] = p1
            probs[h, pl.ds(r0, N), pl.ds(P2, S)] = p2
            lcopy(probs.at[h, pl.ds(r0, N), :], probs_o.at[h, pl.ds(r0, N), :], pouts(tag, h)).start()
            mix = nn_dot(p1, vs[pl.ds(0, P2), hd]) + nn_dot(p2, vs[pl.ds(P2, S), hd])
            mixed[pl.ds(r0, N), hd] = mix.astype(BF)
            return carry

        lax.fori_loop(0, heads, head, 0)

    hs, hr = al.take(1), al.take(1)
    h_x = rcopy(phalf, got, hs(0), hr(0), (sib, z))
    attend(1 - c, 0)
    phalf[...] = nn_dot(mixed[pl.ds(pl.multiple_of((1 - c) * N, N), N), :], wos[...])
    h_x.start()
    for i in range(B):
        @pl.when(jnp.logical_not((B * c + i == z) & mine))
        def _():
            t_arrive(i).wait_recv()

        @pl.when((B * c + i == z) & mine)
        def _():
            t_l().wait()
    for k in range(1, Q):
        t_p(k).start()
    t_f(0).start()
    attend(c, 1)
    leave(mixed, mixed_o)
    own_part = nn_dot(mixed[pl.ds(pl.multiple_of(c * N, N), N), :], wos[...])
    h_x.wait_recv()
    resid[...] = ctx[2, pl.ds(pl.multiple_of(c * N, N), N), :].astype(F32) + (own_part + got[...])
    leave(resid, resid_o)
    xhat2, _ = layer_norm_rows(resid[...])
    sec[pl.ds(0, N), :] = (xhat2 * g2[...] + b2[...]).astype(BF)

    as_, ar, afs, afr = al.take(Q), al.take(Q), al.take(Q), al.take(Q)

    def a_p(k):
        return rcopy(slot(sec, 0, 0), slot(sec, k, 0), as_(k), ar(k), peer(k))

    def a_f(k):
        return rcopy(slot(sec, k, 0), slot(sec, k, 1), afs(k), afr(k), (sib, z))

    for k in range(1, Q):
        t_p(k).wait_recv()
        t_f(k).start()
    for k in range(1, Q - 1):
        a_p(k).start()
    a_f(0).start()
    sqc = al.take(RATE)
    sqs = [dns.at[pl.ds(0, D), :], dns.at[pl.ds(D, D), :], gbuf.at[pl.ds(D, D), :]]
    sq_x = [lcopy(sq.at[pl.ds(r * D, D), :], sqs[r], sqc(r)) for r in range(RATE)]
    for x in sq_x:
        x.start()
    for r in range(1, Z):
        u_z(r).wait()
        for i in range(2):
            x_z(i, r).wait_recv()
    u_l.wait()
    for x in x_l:
        x.wait()
    ss, sr = al.take(Q), al.take(Q)
    gps, gpr = al.take(Q), al.take(Q)

    def s_x(k):
        return rcopy(slot(gbuf, k, 1), got1.at[k], ss(k), sr(k), (sib, z))

    def p_x(k):
        return rcopy(send2.at[k - 1], got2.at[k - 1], gps(k), gpr(k), peer(k))

    bias_row = jnp.concatenate([ubs[r] for r in range(Z)], axis=1)
    small_o[...] = jnp.zeros_like(small_o)

    def forward_block(b, carry):
        at = pl.ds(pl.multiple_of(b * N, N), N)
        x = nn_dot(sec[at, :], ups[...]) + bias_row
        ga = nt_dot(cots[at, :], downs[...])
        x2 = x * x
        root = 0.7978845608028654
        th = jnp.tanh(root * (x + 0.044715 * (x2 * x)))
        act[at, :] = (0.5 * x * (1.0 + th)).astype(BF)
        slope = 0.5 * (1.0 + th) + 0.5 * x * (1.0 - th * th) * (root * (1.0 + 0.134145 * x2))
        gu = (ga * slope).astype(BF)
        gup[at, :] = gu
        small_o[2:3, pl.ds(0, Z * E)] = small_o[2:3, pl.ds(0, Z * E)] + jnp.sum(gu.astype(F32), axis=0, keepdims=True)
        gbuf[at, :] = nt_dot(gu, ups[...]).astype(BF)
        return carry

    def feed(k):
        lax.fori_loop(2 * k, 2 * k + 2, forward_block, 0)
        s_x(k).start()

    def combine(k):
        s_x(k).wait_recv()
        send2[k - 1] = (gbuf[pl.ds(2 * k * N, N), :].astype(F32) + got1[k].astype(F32)).astype(BF)
        p_x(k).start()

    t_f(0).wait_recv()
    a_f(0).wait_recv()
    feed(0)

    groups = S // RATE
    squeezed = None
    for r in range(RATE):
        sq_x[r].wait()
        row = lax.broadcasted_iota(jnp.int32, (ncs.shape[0], S), 0)
        col = lax.broadcasted_iota(jnp.int32, (ncs.shape[0], S), 1)
        pick = jnp.where((col == row * RATE + r) & (row < groups), 1.0, 0.0).astype(BF)
        picked = nn_dot(pick, ctx[1]).astype(BF)
        term = nn_dot(picked, sqs[r][...])
        squeezed = term if squeezed is None else squeezed + term
    ncs[...] = squeezed.astype(BF)
    shift = count + c * N
    new_mem = nn_dot(one_hot((N, S), shift), ctx[1]) + nn_dot(one_hot((N, S), shift - S), ctx[2])
    nms[...] = new_mem.astype(BF)
    third = lax.shift_right_logical(count * 21846, 16)
    shift = third + c * N
    new_comp = nn_dot(one_hot((N, S), shift), ctx[0]) + nn_dot(one_hot((N, ncs.shape[0]), shift - S), ncs[...])
    ncs[pl.ds(0, N), :] = new_comp.astype(BF)
    per = N // R
    ms, mr, ml = al.take(2, 2), al.take(2, B), al.take(2)
    rows_in = [nms, ncs]
    rows_out = [nm_o, nc_o]

    def row_x(i, p):
        return rcopy(rows_in[i].at[pl.ds(p * R, R), :], rows_out[i].at[jz], ms(i, p), mr(i, jz), (2 * q + z // B, c * per + p))

    def row_l(i, p):
        return lcopy(rows_in[i].at[pl.ds(p * R, R), :], rows_out[i].at[jz], ml(i))

    for p in range(per):
        here = (c * per + p == z) & mine

        @pl.when(here)
        def _():
            for i in range(2):
                row_l(i, p).start()

        @pl.when(jnp.logical_not(here))
        def _():
            for i in range(2):
                row_x(i, p).start()

    for k in range(1, Q):
        a_p(k).wait_recv()
        if k == Q - 2:
            a_p(Q - 1).start()
        a_f(k).start()
        t_f(k).wait_recv()
        a_f(k).wait_recv()
        feed(k)
        if k > 1:
            combine(k - 1)
    combine(Q - 1)

    def up_grad(i, carry):
        at = pl.ds(pl.multiple_of(i * T, T), T)
        gus[at, :] = tn_dot(sec[:, at], gup[...]).astype(BF)
        return carry

    lax.fori_loop(0, D // T, up_grad, 0)
    leave(gus, gu_o)

    def down_grad(i, carry):
        at = pl.ds(pl.multiple_of(i * T, T), T)
        gds[at, :] = tn_dot(act[:, at], cots[...]).astype(BF)
        return carry

    lax.fori_loop(0, Z * E // T, down_grad, 0)
    leave(gds, gd_o)

    def down_rows(b, carry):
        at = pl.ds(pl.multiple_of(b * N, N), N)
        dns[at, :] = nn_dot(act[at, :], downs[...]).astype(BF)
        return carry

    lax.fori_loop(0, 2 * Q, down_rows, 0)
    leave(dns, down_o)

    s_x(0).wait_recv()
    for k in range(1, Q):
        p_x(k).wait_recv()
    C = 64

    def back_rows(i, carry):
        at = pl.ds(pl.multiple_of(i * C, C), C)
        gs = gbuf[at, :].astype(F32) + got1[0, at, :].astype(F32)
        for k in range(1, Q):
            gs = gs + got2[k - 1, at, :].astype(F32)
        xhat, inv = layer_norm_rows(resid[at, :])
        small_o[0:1, :] = small_o[0:1, :] + jnp.sum(gs * xhat, axis=0, keepdims=True)
        small_o[1:2, :] = small_o[1:2, :] + jnp.sum(gs, axis=0, keepdims=True)
        e = gs * g2[...]
        m1 = jnp.mean(e, axis=-1, keepdims=True)
        m2 = jnp.mean(e * xhat, axis=-1, keepdims=True)
        gr = cots[at, :].astype(F32) + inv * (e - m1 - xhat * m2)
        got[at, :] = gr
        low[at, :] = gr.astype(BF)
        return carry

    lax.fori_loop(0, N // C, back_rows, 0)
    leave(got, gresid_o)
    ls_, lr_, ll_ = al.take(1), al.take(1), al.take(1)
    mine_rows = glow_o.at[pl.ds(pl.multiple_of(c * N, N), N), :]
    far = rcopy(low, mine_rows, ls_(0), lr_(0), (sib, z))
    near = lcopy(low, mine_rows, ll_(0))
    far.start()
    near.start()

    for cp in copies:
        cp.wait()
    for h in range(heads):
        for half, tag in ((1 - c, 0), (c, 1)):
            rows = pl.ds(pl.multiple_of(half * N, N), N)
            lcopy(probs.at[h, rows, :], probs_o.at[h, rows, :], pouts(tag, h)).wait()

    @pl.when(mine)
    def _():
        for a in range(4):
            for r in range(1, Z):
                w_z(a, r).wait_send()
        for t in range(3):
            c_sib(t).wait_send()
    for j in range(B):
        @pl.when(B * c + j != z)
        def _():
            for a in range(4):
                for k in range(1, Q):
                    w_p(a, j, k, q).wait_send()
    for r in range(1, Z):
        for t in range(3):
            c_fwd(t, lax.rem(z + r, Z), c).wait_send()
        for i in range(2):
            x_z(i, r).wait_send()
    for s in range(B):
        @pl.when(jnp.logical_not((B * c + s == z) & mine))
        def _():
            t_z(s).wait_send()
    for k in range(1, Q):
        t_p(k).wait_send()
        a_p(k).wait_send()
        p_x(k).wait_send()
    for k in range(Q):
        t_f(k).wait_send()
        a_f(k).wait_send()
        s_x(k).wait_send()
    h_x.wait_send()
    for p in range(per):
        here = (c * per + p == z) & mine

        @pl.when(here)
        def _():
            for i in range(2):
                row_l(i, p).wait()

        @pl.when(jnp.logical_not(here))
        def _():
            for i in range(2):
                row_x(i, p).wait_send()
    for s in range(B):
        @pl.when(jnp.logical_not((B * c + s == z) & mine))
        def _():
            for i in range(2):
                rcopy(rows_out[i].at[s], rows_out[i].at[s], ms(i, 0), mr(i, s), (dp, z)).wait_recv()
    near.wait()
    far.wait()
    assert al.used <= FRONT_SEMS


def front(Q, Z, comp, mem, tok, cot, wq, wk, wv, wo, up, down, ub, vc, sq, g1, b1, g2, b2):
    B, R, D = tok.shape
    H = wq.shape[1]
    S = R * Z
    N = S // 2
    W = B * H
    heads = W // HEAD_DIM
    F = up.shape[1] // 2 // Q * Z
    rows = 2 * Q * N
    vm = pltpu.VMEM
    return pl.pallas_call(
        functools.partial(front_kernel, Q, Z),
        out_shape=[
            sds((S, D), BF), sds((3 * S, D), BF), sds((S, W), BF), sds((3 * S, W), BF), sds((3 * S, W), BF),
            sds((heads, S, 3 * S), BF), sds((S, W), BF), sds((D, W), BF), sds((D, W), BF), sds((D, W), BF), sds((W, D), BF),
            sds((N, D), F32), sds((N, D), F32), sds((S, D), BF), sds((D, F), BF), sds((F, D), BF), sds((rows, D), BF),
            sds((8, D), F32), sds((B, R, D), BF), sds((B, R, D), BF),
        ],
        in_specs=[ANY] * 11 + [VM] + [ANY] + [VM] * 4,
        out_specs=[ANY] * 17 + [VM] + [ANY] * 2,
        scratch_shapes=[
            vm((3, S, D), BF), vm((3 * S, D), BF), vm((D, W), BF), vm((D, W), BF), vm((D, W), BF), vm((W, D), BF),
            vm((S, W), BF), vm((3 * S, W), BF), vm((3 * S, W), BF), vm((heads, S, 3 * S), BF), vm((S, W), BF),
            vm((N, D), F32), vm((N, D), F32), vm((N, D), F32), vm((rows, D), BF), vm((rows, D), BF), vm((D, F), BF), vm((F, D), BF),
            vm((Z, 1, F // Z), F32), vm(vc.shape, jnp.int32), vm((rows, F), BF), vm((rows, F), BF), vm((rows, D), BF),
            vm((Q, N, D), BF), vm((Q - 1, N, D), BF), vm((Q - 1, N, D), BF), vm((N, D), BF),
            vm((N, D), BF), vm((N, D), BF), vm((D, F), BF), vm((F, D), BF), vm((rows, D), BF),
            DMA((FRONT_SEMS,)),
        ],
        compiler_params=pltpu.CompilerParams(collective_id=1, has_side_effects=True, vmem_limit_bytes=63 << 20),
        name="front",
    )(comp, mem, tok, cot, wq, wk, wv, wo, up, down, ub, vc, sq, g1, b1, g2, b2)


def final_kernel(Q, Z, B, gq, gk, gv, go, fu, fd, r0, r1, agq, agk, agv, ago, afu, afd, o0, o1,
                 bq, bk, bv, bo, zq, zk, zv, zo, dq, dk, dv, do, ps, pr, zs_, zr, gs_, gr, hs, hr, us, ur, vs, vr, ls, rs, rr):
    dp, c, q, z = where_am_i(Q, Z)
    sib = dp + 1 - 2 * c
    partners = [(sib, z)]
    for r in range(1, Z):
        for d in (dp, sib):
            partners.append((d, lax.rem(z + r, Z)))
    for k in range(1, Q):
        partners.append((2 * lax.rem(q + k, Q) + c, z))
    enter(partners)
    grads = [gq, gk, gv, go]
    bufs = [bq, bk, bv, bo]
    zbufs = [zq, zk, zv, zo]
    done = [dq, dk, dv, do]
    outs = [agq, agk, agv, ago]
    rows_in = [r0, r1]
    rows_out = [o0, o1]
    M = agq.shape[0] // Q
    OM = ago.shape[0] // Q
    RR = o0.shape[1]
    mine = c == z // B
    jz = lax.rem(z, B)
    zc = z // B

    def quarter(a, qq):
        n = OM if a == 3 else M
        return grads[a].at[:, pl.ds(qq * n, n), :]

    def p_x(a, k):
        return rcopy(quarter(a, lax.rem(q + k, Q)), bufs[a].at[k - 1], ps.at[a, k - 1], pr.at[a, k - 1],
                     (2 * lax.rem(q + k, Q) + c, z))

    def z_x(a, j):
        return rcopy(done[a].at[j], zbufs[a].at[z], zs_.at[a, j], zr.at[a, z], (dp, B * c + j))

    def z_arrive(a, zz):
        return rcopy(zbufs[a].at[zz], zbufs[a].at[zz], zs_.at[a, 0], zr.at[a, zz], (dp, z))

    def where_out(a, qq):
        n = OM if a == 3 else M
        return outs[a].at[pl.ds(qq * n, n), :]

    def f_out(i, d):
        return (afu if i == 0 else afd).at[d]

    def u_x(i, k):
        src = (fu, fd)[i]
        return rcopy(src, f_out(i, dp), us.at[i, k], ur.at[i, k], (2 * lax.rem(q + k, Q) + c, z))

    def v_x(i, k, d):
        src = (fu, fd)[i] if k == 0 else f_out(i, d)
        return rcopy(src, f_out(i, d), vs.at[i, k], vr.at[i, k], (sib, z))

    def u_l(i):
        return lcopy((fu, fd)[i], f_out(i, dp), ls.at[i])

    per = r0.shape[0] // RR

    def row_x(i, p):
        zt = c * per + p
        return rcopy(rows_in[i].at[pl.ds(p * RR, RR), :], rows_out[i].at[jz], rs.at[i, p], rr.at[i, jz], (2 * q + zc, zt))

    def row_l(i, p):
        return lcopy(rows_in[i].at[pl.ds(p * RR, RR), :], rows_out[i].at[jz], ls.at[2 + i])

    for a in range(4):
        for k in range(1, Q):
            p_x(a, k).start()
    for p in range(per):
        here = (c * per + p == z) & mine
        @pl.when(here)
        def _():
            for i in range(2):
                row_l(i, p).start()

        @pl.when(jnp.logical_not(here))
        def _():
            for i in range(2):
                row_x(i, p).start()
    for i in range(2):
        for k in range(1, Q):
            u_x(i, k).start()
        v_x(i, 0, dp).start()
        u_l(i).start()
    for a in range(4):
        n = OM if a == 3 else M
        for k in range(1, Q):
            p_x(a, k).wait_recv()
        for j in range(B):
            t = grads[a][j, pl.ds(pl.multiple_of(q * n, n), n), :].astype(F32)
            for k in range(1, Q):
                t = t + bufs[a][k - 1, j].astype(F32)
            done[a][j] = t.astype(BF)

            @pl.when(B * c + j != z)
            def _():
                z_x(a, j).start()
    @pl.when(mine)
    def _():
        for a in range(4):
            for zz in range(Z):
                @pl.when(zz != z)
                def _():
                    z_arrive(a, zz).wait_recv()
    for a in range(4):
        @pl.when(mine)
        def _():
            zbufs[a][z] = done[a][jz]
            t = zbufs[a][0].astype(F32)
            for zz in range(1, Z):
                t = t + zbufs[a][zz].astype(F32)
            n = OM if a == 3 else M
            outs[a][pl.ds(pl.multiple_of(q * n, n), n), :] = t.astype(BF)

    def g_x(a, k):
        return rcopy(where_out(a, q), where_out(a, q), gs_.at[a, k], gr.at[a, k], (2 * lax.rem(q + k, Q) + c, z))

    def h_x(a, k):
        qq = lax.rem(q + Q - k, Q)
        return rcopy(where_out(a, qq), where_out(a, qq), hs.at[a, k], hr.at[a, k], (sib, z))

    @pl.when(mine)
    def _():
        for a in range(4):
            for k in range(1, Q):
                g_x(a, k).start()
            h_x(a, 0).start()
    for i in range(2):
        for k in range(1, Q):
            u_x(i, k).wait_recv()
            v_x(i, k, 2 * lax.rem(q + Q - k, Q) + c).start()

    @pl.when(mine)
    def _():
        for a in range(4):
            for k in range(1, Q):
                g_x(a, k).wait_recv()
                h_x(a, k).start()

    @pl.when(mine)
    def _():
        for a in range(4):
            for k in range(1, Q):
                g_x(a, k).wait_send()
            for k in range(Q):
                h_x(a, k).wait_send()

    @pl.when(jnp.logical_not(mine))
    def _():
        for a in range(4):
            for k in range(Q):
                h_x(a, k).wait_recv()
    for a in range(4):
        for k in range(1, Q):
            p_x(a, k).wait_send()
        for j in range(B):
            @pl.when(B * c + j != z)
            def _():
                z_x(a, j).wait_send()
    for i in range(2):
        for k in range(1, Q):
            u_x(i, k).wait_send()
        for k in range(Q):
            v_x(i, k, dp).wait_send()
            v_x(i, k, dp).wait_recv()
        u_l(i).wait()
    for p in range(per):
        here = (c * per + p == z) & mine
        @pl.when(here)
        def _():
            for i in range(2):
                row_l(i, p).wait()

        @pl.when(jnp.logical_not(here))
        def _():
            for i in range(2):
                row_x(i, p).wait_send()
    for s in range(B):
        @pl.when(jnp.logical_not((B * c + s == z) & mine))
        def _():
            for i in range(2):
                rcopy(rows_out[i].at[s], rows_out[i].at[s], rs.at[i, 0], rr.at[i, s], (dp, z)).wait_recv()


def final_exchange(Q, Z, gq, gk, gv, go, fu, fd, r0, r1):
    B, D, H = gq.shape
    RR = r0.shape[0] * 2 // Z
    M, OM = D // Q, H // Q
    qs, os_ = (M, H), (OM, D)
    return pl.pallas_call(
        functools.partial(final_kernel, Q, Z, B),
        out_shape=[sds((D, H), BF)] * 3 + [sds((H, D), BF)]
        + [sds((2 * Q,) + fu.shape, BF), sds((2 * Q,) + fd.shape, BF)]
        + [sds((B, RR, D), BF)] * 2,
        in_specs=[VM] * 4 + [ANY] * 4,
        out_specs=[VM] * 4 + [ANY] * 4,
        scratch_shapes=[pltpu.VMEM((Q - 1, B) + qs, BF)] * 3 + [pltpu.VMEM((Q - 1, B) + os_, BF)]
        + [pltpu.VMEM((Z,) + qs, BF)] * 3 + [pltpu.VMEM((Z,) + os_, BF)]
        + [pltpu.VMEM((B,) + qs, BF)] * 3 + [pltpu.VMEM((B,) + os_, BF)]
        + [
            DMA((4, Q - 1)), DMA((4, Q - 1)), DMA((4, B)), DMA((4, Z)),
            DMA((4, Q)), DMA((4, Q)), DMA((4, Q)), DMA((4, Q)),
            DMA((2, Q)), DMA((2, Q)), DMA((2, Q)), DMA((2, Q)), DMA((6,)), DMA((4, 2)), DMA((4, B)),
        ],
        compiler_params=pltpu.CompilerParams(collective_id=4, has_side_effects=True, vmem_limit_bytes=40 << 20),
        name="final_exchange",
    )(gq, gk, gv, go, fu, fd, r0, r1)


def chip_device(Q, Z, tokens, memory, compressed, valid_counts, attention_norm_gain, attention_norm_bias,
                query_projection, key_projection, value_projection, out_weight, feedforward_norm_gain,
                feedforward_norm_bias, up_weight, up_bias, down_weight, down_bias, squeeze_weight, cotangent):
    B, R, D = tokens.shape
    H = query_projection.shape[1]
    FL = up_weight.shape[1]
    dp = lax.axis_index("dp")
    z = lax.axis_index("mp")
    c = lax.rem(dp, 2)
    S = R * Z
    N = S // 2
    E = FL // (2 * Q)
    jz = lax.rem(z, B)

    def turn_z(a, r):
        return lax.ppermute(a, "mp", [(i, (i + r) % Z) for i in range(Z)])

    def turn_q(a, k):
        return lax.ppermute(a, "dp", [(2 * i + s, 2 * (i ^ k) + s) for i in range(Q) for s in range(2)])

    def swap(a):
        return lax.ppermute(a, "dp", [(i, i ^ 1) for i in range(2 * Q)])

    (tok_all, normed, q_, k_, v_, probs, mixed, wqg, wkg, wvg, wog, resid, g_resid, g_low, up_low, down_g_low, down,
     ff_small, o_nm, o_nc) = front(
        Q, Z, compressed, memory, tokens, cotangent, query_projection, key_projection, value_projection, out_weight,
        up_weight, down_weight, up_bias.reshape(2 * Q, 1, E), jnp.broadcast_to(valid_counts[:, None, None], (B, 8, 128)),
        squeeze_weight, attention_norm_gain.reshape(1, D), attention_norm_bias.reshape(1, D),
        feedforward_norm_gain.reshape(1, D), feedforward_norm_bias.reshape(1, D),
    )
    heads = B * H // HEAD_DIM
    scale = HEAD_DIM ** (-0.5)
    nt = normed[2 * S:]

    def by_heads(m):
        return m.reshape(m.shape[0], heads, HEAD_DIM)

    down = down.reshape(Q, 2, N, D)
    down_half = down[:, 0].astype(F32) + swap(down[:, 1]).astype(F32)
    down_low = down_half.astype(BF)
    down_sum = down_half[0]
    for k in range(1, Q):
        down_sum = down_sum + turn_q(down_low[k], k).astype(F32)
    output = (resid + down_sum + down_bias).astype(BF)
    ub_grad = ff_small[2, :Z * E].reshape(Z, E)
    fu = up_low[:, :E].astype(F32)
    fd = down_g_low[:E].astype(F32)
    for r in range(1, Z):
        fu = fu + turn_z(up_low[:, r * E:(r + 1) * E], Z - r).astype(F32)
        fd = fd + turn_z(down_g_low[r * E:(r + 1) * E], Z - r).astype(F32)

    go = tn_dot(mixed, g_low).astype(BF)
    g_mixed = nt_dot(g_low, wog).astype(BF)
    g_probs = jnp.einsum("qhe,khe->hqk", by_heads(g_mixed), by_heads(v_), preferred_element_type=F32)
    delta = jnp.einsum("qhe,qhe->hq", by_heads(g_mixed).astype(F32), by_heads(mixed).astype(F32))[..., None]
    g_scores = (probs.astype(F32) * (g_probs - delta)).astype(BF)
    gq_ = (scale * jnp.einsum("hqk,khe->qhe", g_scores, by_heads(k_), preferred_element_type=F32)).astype(BF)
    gk_ = (scale * jnp.einsum("hqk,qhe->khe", g_scores, by_heads(q_), preferred_element_type=F32)).astype(BF)
    gv_ = jnp.einsum("hqk,qhe->khe", probs, by_heads(g_mixed), preferred_element_type=F32).astype(BF)
    gq_, gk_, gv_ = (g.reshape(g.shape[0], B * H) for g in (gq_, gk_, gv_))
    gwq, gwk, gwv = tn_dot(nt, gq_), tn_dot(normed, gk_), tn_dot(normed, gv_)
    g_normed = nt_dot(gk_[2 * S:], wkg) + nt_dot(gv_[2 * S:], wvg) + nt_dot(gq_, wqg)
    at_gain = jnp.zeros((D,), F32)
    at_bias = jnp.zeros((D,), F32)
    for g, gw, w in ((gq_, gwq, wqg), (gk_, gwk, wkg), (gv_, gwv, wvg)):
        col = jnp.sum(g.astype(F32), axis=0)
        wf = w.astype(F32)
        at_bias = at_bias + jnp.sum(wf * col, axis=1)
        at_gain = at_gain + jnp.sum(wf * (gw - attention_norm_bias[:, None] * col), axis=1)
    at_gain = at_gain / attention_norm_gain
    keep = lax.dynamic_slice_in_dim(g_normed, c * N, N, 0)
    give = lax.dynamic_slice_in_dim(g_normed, (1 - c) * N, N, 0)
    gn = keep + swap(give)
    xt, it = layer_norm_rows(lax.dynamic_slice_in_dim(tok_all, c * N, N, 0).astype(F32))
    e = gn * attention_norm_gain
    tokens_grad = g_resid + it * (
        e - jnp.mean(e, axis=-1, keepdims=True) - xt * jnp.mean(e * xt, axis=-1, keepdims=True)
    )

    def halves(w):
        return jnp.swapaxes(w.reshape(D, B, H), 0, 1).astype(BF)

    gwq, gwk, gwv = halves(gwq), halves(gwk), halves(gwv)
    go = go.reshape(B, H, D)
    agq, agk, agv, ago, afu, afd, o_out, o_tg = final_exchange(
        Q, Z, gwq, gwk, gwv, go, fu.astype(BF), fd.astype(BF), output, tokens_grad.astype(BF)
    )
    local_down_bias = jnp.sum(cotangent.astype(F32), axis=(0, 1))
    ub_slots = jnp.zeros((Z, 2 * Q, E), F32)
    for r in range(Z):
        ub_slots = lax.dynamic_update_slice(ub_slots, ub_grad[r].reshape(1, 1, E), (lax.rem(z + Z - r, Z), dp, 0))
    small = jnp.concatenate([
        jnp.stack([at_gain, at_bias, ff_small[0], ff_small[1], local_down_bias]).reshape(-1), ub_slots.reshape(-1)
    ])
    small = lax.psum(small, ("dp", "mp"))
    vecs = small[:5 * D].reshape(5, D)
    ub_out = lax.dynamic_slice_in_dim(small[5 * D:], z * FL, FL, 0)
    up_out = jnp.swapaxes(afu, 0, 1).reshape(D, FL).astype(F32)
    down_out = afd.reshape(FL, D).astype(F32)
    return (
        o_out, o_tg.astype(F32), vecs[0], vecs[1], agq.astype(F32), agk.astype(F32), agv.astype(F32), ago.astype(F32),
        vecs[2], vecs[3], up_out, ub_out, down_out, vecs[4], o_nm, o_nc,
    )


def solution(mesh):
    in_specs = (
        P("dp", "mp", None),
        P("dp", "mp", None),
        P("dp", "mp", None),
        P("dp"),
        P(),
        P(),
        P(None, "mp"),
        P(None, "mp"),
        P(None, "mp"),
        P("mp", None),
        P(),
        P(),
        P(None, "mp"),
        P("mp"),
        P("mp", None),
        P(),
        P(),
        P("dp", "mp", None),
    )
    out_specs = (
        P("dp", "mp", None),
        P("dp", "mp", None),
        P(),
        P(),
        P(None, "mp"),
        P(None, "mp"),
        P(None, "mp"),
        P("mp", None),
        P(),
        P(),
        P(None, "mp"),
        P("mp"),
        P("mp", None),
        P(),
        P("dp", "mp", None),
        P("dp", "mp", None),
    )
    Q, Z = mesh.shape["dp"] // 2, mesh.shape["mp"]

    def per_device(*args):
        B, R, D = args[0].shape
        H, FL = args[6].shape[1], args[12].shape[1]
        whole = Q == 4 and B == 2 and 2 * B == Z and H % HEAD_DIM == 0 and D % (16 * Q) == 0 and H % (16 * Q) == 0
        if whole and R % 32 == 0 and FL % (256 * Q) == 0:
            return chip_device(Q, Z, *args)
        return general_device(*args)

    return jax.shard_map(
        per_device, mesh=mesh, in_specs=in_specs, out_specs=out_specs, check_vma=False
    )
```

```python
import functools

import jax
import jax.numpy as jnp
from jax import lax
from jax.experimental import pallas as pl
from jax.experimental.pallas import tpu as pltpu
from jax.sharding import PartitionSpec as P

HEAD_DIM = 128
RATE = 3


def apply_layer_norm(rows):
    center = jnp.mean(rows, axis=-1, keepdims=True)
    centered = rows - center
    spread = jnp.mean(centered * centered, axis=-1, keepdims=True)
    inverse_deviation = lax.rsqrt(spread + 1e-05)
    return (centered * inverse_deviation, inverse_deviation)


def norm_backward_pass(input_gradient, standardized_rows, inverse_deviation, scale_factor):
    scaled_rows = input_gradient * scale_factor
    attention_norm_mean = jnp.mean(scaled_rows, axis=-1, keepdims=True)
    feedforward_norm_mean = jnp.mean(scaled_rows * standardized_rows, axis=-1, keepdims=True)
    return inverse_deviation * (
        scaled_rows - attention_norm_mean - standardized_rows * feedforward_norm_mean
    )


def squeeze_rows(old_comp, old_mem, fresh, valid_count, offset, own_rows, squeeze_weight):
    features = old_mem.shape[1]
    joined = jnp.concatenate([old_mem, fresh], axis=0)
    new_memory = lax.dynamic_slice_in_dim(joined, valid_count + offset, own_rows, 0)
    comp_len = old_comp.shape[0]
    evicted = valid_count // RATE
    first_row = evicted + offset
    window_start = jnp.maximum(first_row - comp_len, 0)
    padded = jnp.concatenate(
        [old_mem, jnp.zeros((RATE * own_rows, features), jnp.bfloat16)], axis=0
    )
    window = lax.dynamic_slice_in_dim(padded, window_start * RATE, RATE * own_rows, 0)
    squeezed = jnp.dot(
        window.reshape(own_rows, RATE * features),
        squeeze_weight,
        preferred_element_type=jnp.float32,
    ).astype(jnp.bfloat16)
    positions = first_row + jnp.arange(own_rows)
    from_old = jnp.take(old_comp, jnp.clip(positions, 0, comp_len - 1), axis=0)
    from_new = jnp.take(
        squeezed, jnp.clip(positions - comp_len - window_start, 0, own_rows - 1), axis=0
    )
    new_compressed = jnp.where((positions < comp_len)[:, None], from_old, from_new)
    return (new_memory, new_compressed)


def general_device(
    tokens,
    memory,
    compressed,
    valid_counts,
    attention_norm_gain,
    attention_norm_bias,
    query_projection,
    key_projection,
    value_projection,
    out_weight,
    feedforward_norm_gain,
    feedforward_norm_bias,
    up_weight,
    up_bias,
    down_weight,
    down_bias,
    squeeze_weight,
    cotangent,
):
    batch_segs, own_rows, features = tokens.shape
    offset = lax.axis_index("mp") * own_rows
    old_comp, old_mem, fresh = (
        lax.all_gather(compressed, "mp", axis=1, tiled=True),
        lax.all_gather(memory, "mp", axis=1, tiled=True),
        lax.all_gather(tokens, "mp", axis=1, tiled=True),
    )
    seg_len = fresh.shape[1]
    prior_rows = old_comp.shape[1] + old_mem.shape[1]
    context_tokens = jnp.concatenate([old_comp, old_mem, fresh], axis=1).astype(jnp.float32)
    ctx_len = context_tokens.shape[1]
    standardized_full, inverse_deviation_full = apply_layer_norm(context_tokens)
    normed_rows = (standardized_full * attention_norm_gain + attention_norm_bias).astype(
        jnp.bfloat16
    )
    token_rows_normed = normed_rows[:, prior_rows:]
    queries = jnp.einsum(
        "xhp,pj->xhj", token_rows_normed, query_projection, preferred_element_type=jnp.float32
    ).astype(jnp.bfloat16)
    key_rows = jnp.einsum(
        "xhp,pj->xhj", normed_rows, key_projection, preferred_element_type=jnp.float32
    ).astype(jnp.bfloat16)
    values = jnp.einsum(
        "xhp,pj->xhj", normed_rows, value_projection, preferred_element_type=jnp.float32
    ).astype(jnp.bfloat16)
    local_heads = query_projection.shape[1] // HEAD_DIM
    score_scale = HEAD_DIM ** (-0.5)

    def by_heads(matrix):
        return matrix.reshape(matrix.shape[0], matrix.shape[1], local_heads, HEAD_DIM)

    query_pos = jnp.arange(seg_len)[:, None]
    key_pos = jnp.arange(ctx_len)[None, :] - prior_rows
    allowed = (key_pos[None] < 0) | (key_pos <= query_pos)[None] & (
        key_pos[None] < valid_counts[:, None, None]
    )

    def scores_of(query_in, key_in):
        raw = (
            jnp.einsum(
                "gqhe,gkhe->ghqk",
                by_heads(query_in),
                by_heads(key_in),
                preferred_element_type=jnp.float32,
            )
            * score_scale
        )
        return jnp.where(allowed[:, None], raw, -1e30)

    scores = scores_of(queries, key_rows)
    peak_score = jnp.max(scores, axis=-1, keepdims=True)
    exponent = jnp.exp(scores - peak_score)
    exp_total = jnp.sum(exponent, axis=-1, keepdims=True)
    log_total = peak_score + jnp.log(exp_total)
    probs_low = (exponent / exp_total).astype(jnp.bfloat16)
    mixed_heads = jnp.einsum(
        "ghqk,gkhe->gqhe", probs_low, by_heads(values), preferred_element_type=jnp.float32
    ).astype(jnp.bfloat16)
    mixed_heads = mixed_heads.reshape(batch_segs, seg_len, local_heads * HEAD_DIM)
    partial_attn = jnp.einsum(
        "gsc,cd->gsd", mixed_heads, out_weight, preferred_element_type=jnp.float32
    )
    attention = lax.psum_scatter(partial_attn, "mp", scatter_dimension=1, tiled=True)
    residual_stream = tokens.astype(jnp.float32) + attention
    standardized_feedforward, inverse_deviation_feedforward = apply_layer_norm(residual_stream)
    feedforward_input = (
        standardized_feedforward * feedforward_norm_gain + feedforward_norm_bias
    ).astype(jnp.bfloat16)
    second_all = lax.all_gather(feedforward_input, "mp", axis=1, tiled=True)
    upper_in = (
        jnp.einsum("gsd,df->gsf", second_all, up_weight, preferred_element_type=jnp.float32)
        + up_bias
    )
    active, gelu_back = jax.vjp(jax.nn.gelu, upper_in)
    active_low = active.astype(jnp.bfloat16)
    partial_ffn = jnp.einsum(
        "gsf,fd->gsd", active_low, down_weight, preferred_element_type=jnp.float32
    )
    down_out = lax.psum_scatter(
        partial_ffn.astype(jnp.bfloat16), "mp", scatter_dimension=1, tiled=True
    ).astype(jnp.float32)
    output = (residual_stream + down_out + down_bias).astype(jnp.bfloat16)

    def update_one(comp_seg, mem_seg, fresh_seg, valid_count):
        return squeeze_rows(
            comp_seg, mem_seg, fresh_seg, valid_count, offset, own_rows, squeeze_weight
        )

    new_memory, new_compressed = jax.vmap(update_one)(old_comp, old_mem, fresh, valid_counts)
    output_gradient = cotangent.astype(jnp.float32)
    down_bias_grad = jnp.sum(output_gradient, axis=(0, 1))
    grad_all = lax.all_gather(cotangent, "mp", axis=1, tiled=True)
    down_weight_grad = jnp.einsum(
        "gsf,gsd->fd", active_low, grad_all, preferred_element_type=jnp.float32
    )
    grad_active = jnp.einsum(
        "gsd,fd->gsf", grad_all, down_weight, preferred_element_type=jnp.float32
    )
    grad_upper = gelu_back(grad_active)[0].astype(jnp.bfloat16)
    up_weight_grad = jnp.einsum(
        "gsd,gsf->df", second_all, grad_upper, preferred_element_type=jnp.float32
    )
    up_bias_grad = jnp.sum(grad_upper.astype(jnp.float32), axis=(0, 1))
    partial_second = jnp.einsum(
        "gsf,df->gsd", grad_upper, up_weight, preferred_element_type=jnp.float32
    )
    feedforward_gradient = lax.psum_scatter(partial_second, "mp", scatter_dimension=1, tiled=True)
    feedforward_gain_gradient = jnp.sum(
        feedforward_gradient * standardized_feedforward, axis=(0, 1)
    )
    second_bias_grad = jnp.sum(feedforward_gradient, axis=(0, 1))
    residual_gradient = output_gradient + norm_backward_pass(
        feedforward_gradient,
        standardized_feedforward,
        inverse_deviation_feedforward,
        feedforward_norm_gain,
    )
    grad_resid_all = lax.all_gather(
        residual_gradient.astype(jnp.bfloat16), "mp", axis=1, tiled=True
    )
    out_weight_grad = jnp.einsum(
        "gsc,gsd->cd", mixed_heads, grad_resid_all, preferred_element_type=jnp.float32
    )
    grad_mixed = jnp.einsum(
        "gsd,cd->gsc", grad_resid_all, out_weight, preferred_element_type=jnp.float32
    ).astype(jnp.bfloat16)
    probs_again = jnp.exp(scores_of(queries, key_rows) - log_total)
    grad_probs = jnp.einsum(
        "gqhe,gkhe->ghqk",
        by_heads(grad_mixed),
        by_heads(values),
        preferred_element_type=jnp.float32,
    )
    row_dot = jnp.sum(probs_again * grad_probs, axis=-1, keepdims=True)
    grad_scores = (probs_again * (grad_probs - row_dot)).astype(jnp.bfloat16)
    query_gradient = (
        score_scale
        * jnp.einsum(
            "ghqk,gkhe->gqhe", grad_scores, by_heads(key_rows), preferred_element_type=jnp.float32
        )
    ).astype(jnp.bfloat16)
    key_gradient = (
        score_scale
        * jnp.einsum(
            "ghqk,gqhe->gkhe", grad_scores, by_heads(queries), preferred_element_type=jnp.float32
        )
    ).astype(jnp.bfloat16)
    value_gradient = jnp.einsum(
        "ghqk,gqhe->gkhe",
        probs_again.astype(jnp.bfloat16),
        by_heads(grad_mixed),
        preferred_element_type=jnp.float32,
    ).astype(jnp.bfloat16)
    query_gradient = query_gradient.reshape(batch_segs, seg_len, -1)
    key_gradient = key_gradient.reshape(batch_segs, ctx_len, -1)
    value_gradient = value_gradient.reshape(batch_segs, ctx_len, -1)
    query_weight_grad = jnp.einsum(
        "nja,njr->ar", token_rows_normed, query_gradient, preferred_element_type=jnp.float32
    )
    key_weight_grad = jnp.einsum(
        "nja,njr->ar", normed_rows, key_gradient, preferred_element_type=jnp.float32
    )
    value_weight_grad = jnp.einsum(
        "nja,njr->ar", normed_rows, value_gradient, preferred_element_type=jnp.float32
    )
    partial_normed = jnp.einsum(
        "xmo,qo->xmq", key_gradient, key_projection, preferred_element_type=jnp.float32
    )
    partial_normed = partial_normed + jnp.einsum(
        "xmo,qo->xmq", value_gradient, value_projection, preferred_element_type=jnp.float32
    )
    partial_normed = partial_normed.at[:, prior_rows:].add(
        jnp.einsum(
            "xmo,qo->xmq", query_gradient, query_projection, preferred_element_type=jnp.float32
        )
    )
    partial_normed = partial_normed.reshape(batch_segs, 3, seg_len, features)
    normed_gradient = lax.psum_scatter(
        partial_normed.astype(jnp.bfloat16), "mp", scatter_dimension=2, tiled=True
    ).astype(jnp.float32)
    segment_context = jnp.stack([compressed, memory, tokens], axis=1).astype(jnp.float32)
    standardized_segment, inverse_deviation_segment = apply_layer_norm(segment_context)
    attention_gain_gradient = jnp.sum(normed_gradient * standardized_segment, axis=(0, 1, 2))
    first_bias_grad = jnp.sum(normed_gradient, axis=(0, 1, 2))
    tokens_grad = residual_gradient + norm_backward_pass(
        normed_gradient[:, 2],
        standardized_segment[:, 2],
        inverse_deviation_segment[:, 2],
        attention_norm_gain,
    )
    summed = (
        lax.psum(query_weight_grad.astype(jnp.bfloat16), "dp").astype(jnp.float32),
        lax.psum(key_weight_grad.astype(jnp.bfloat16), "dp").astype(jnp.float32),
        lax.psum(value_weight_grad.astype(jnp.bfloat16), "dp").astype(jnp.float32),
        lax.psum(out_weight_grad.astype(jnp.bfloat16), "dp").astype(jnp.float32),
        lax.psum(up_weight_grad.astype(jnp.bfloat16), "dp").astype(jnp.float32),
        lax.psum(up_bias_grad.astype(jnp.bfloat16), "dp").astype(jnp.float32),
        lax.psum(down_weight_grad.astype(jnp.bfloat16), "dp").astype(jnp.float32),
    )
    norms = lax.psum(
        (
            attention_gain_gradient,
            first_bias_grad,
            feedforward_gain_gradient,
            second_bias_grad,
            down_bias_grad,
        ),
        ("dp", "mp"),
    )
    return (
        output,
        tokens_grad,
        norms[0],
        norms[1],
        summed[0],
        summed[1],
        summed[2],
        summed[3],
        norms[2],
        norms[3],
        summed[4],
        summed[5],
        summed[6],
        norms[4],
        new_memory,
        new_compressed,
    )


BF = jnp.bfloat16
F32 = jnp.float32
MESH = pl.DeviceIdType.MESH
ANY = pl.BlockSpec(memory_space=pl.ANY)
VM = pl.BlockSpec(memory_space=pltpu.VMEM)
DMA = pltpu.SemaphoreType.DMA


def sds(shape, dtype):
    return jax.ShapeDtypeStruct(shape, dtype)


def where_am_i(chips, depth):
    dp = lax.axis_index("dp")
    return dp, lax.rem(dp, 2), dp // 2, lax.axis_index("mp")


def rcopy(src, dst, send, recv, device):
    return pltpu.make_async_remote_copy(
        src_ref=src,
        dst_ref=dst,
        send_sem=send,
        recv_sem=recv,
        device_id=device,
        device_id_type=MESH,
    )


def lcopy(src, dst, sem):
    return pltpu.make_async_copy(src, dst, sem)


def enter(partners):
    barrier = pltpu.get_barrier_semaphore()
    for p in partners:
        pl.semaphore_signal(barrier, inc=1, device_id=p, device_id_type=MESH)
    pl.semaphore_wait(barrier, len(partners))


def across(q, k):
    if k == 0:
        return q
    if k == 1:
        return q + 1 - 2 * lax.rem(q, 2)
    if k == 2:
        return lax.rem(q + 2, 4)
    return 3 - q


def layer_norm_rows(rows):
    center = jnp.mean(rows, axis=-1, keepdims=True)
    centered = rows - center
    spread = jnp.mean(centered * centered, axis=-1, keepdims=True)
    inv = lax.rsqrt(spread + 1e-05)
    return centered * inv, inv


class Slots:
    def __init__(self, ref):
        self.ref = ref
        self.used = 0

    def take(self, *shape):
        base = self.used
        size = 1
        for n in shape:
            size *= n
        self.used += size

        def at(*index):
            flat = 0
            for n, i in zip(shape, index):
                flat = flat * n + i
            return self.ref.at[base + flat]

        return at


def nt_dot(a, b):
    return lax.dot_general(a, b, (((1,), (1,)), ((), ())), preferred_element_type=F32)


def tn_dot(a, b):
    return lax.dot_general(a, b, (((0,), (0,)), ((), ())), preferred_element_type=F32)


def nn_dot(a, b):
    return jnp.dot(a, b, preferred_element_type=F32)


def one_hot(shape, offset):
    row = lax.broadcasted_iota(jnp.int32, shape, 0)
    col = lax.broadcasted_iota(jnp.int32, shape, 1)
    return jnp.where(col == row + offset, 1.0, 0.0).astype(BF)


FRONT_SEMS = 400


def front_kernel(Q, Z, comp, mem, tok, cot, wq, wk, wv, wo, up, down, ub, vc, sq, g1, b1, g2, b2,
                 tok_o, normed_o, q_o, k_o, v_o, probs_o, mixed_o, wq_o, wk_o, wv_o, wo_o,
                 resid_o, gresid_o, glow_o, gu_o, gd_o, down_o, small_o, nm_o, nc_o,
                 ctx, normed, wqs, wks, wvs, wos, qs, ks, vs, probs, mixed, phalf, got, resid, sec, cots, ups, downs,
                 ubs, vco, act, gup, gbuf, got1, send2, got2, low, nms, ncs, gus, gds, dns, sems):
    dp, c, q, z = where_am_i(Q, Z)
    sib = dp + 1 - 2 * c
    partners = [(sib, z)]
    for r in range(1, Z):
        for d in (dp, sib):
            partners.append((d, lax.rem(z + r, Z)))
    for k in range(1, Q):
        partners.append((2 * across(q, k) + c, z))
    enter(partners)
    B, R, D = tok.shape
    H = wq.shape[1]
    QR = D // Q
    OR = H // Q
    HR = R // 2
    S = R * Z
    N = S // 2
    E = up.shape[1] // (2 * Q)
    heads = B * H // HEAD_DIM
    mine = c == z // B
    jz = lax.rem(z, B)
    al = Slots(sems)

    def peer(k):
        return (2 * across(q, k) + c, z)

    wins = [wq, wk, wv, wo]
    wss = [wqs, wks, wvs, wos]

    def piece(a):
        if a < 3:
            return wins[a].at[pl.ds(q * QR, QR), :]
        return wo.at[pl.ds(q * OR, OR), :]

    def place(a, j, qq):
        if a < 3:
            return wss[a].at[pl.ds(pl.multiple_of(qq * QR, QR), QR), pl.ds(pl.multiple_of(j * H, H), H)]
        return wos.at[pl.ds(pl.multiple_of(j * H + qq * OR, OR), OR), :]

    def place_whole(a, j):
        if a < 3:
            return wss[a].at[:, pl.ds(pl.multiple_of(j * H, H), H)]
        return wos.at[pl.ds(pl.multiple_of(j * H, H), H), :]

    ws, wr = al.take(4, Z - 1), al.take(4, B)
    ps, pr = al.take(4, B, Q - 1), al.take(4, B, Q - 1)
    wl = al.take(4)

    def w_z(a, r):
        return rcopy(piece(a), place(a, jz, q), ws(a, r - 1), wr(a, jz), (dp, lax.rem(z + r, Z)))

    def w_arrive(a, j):
        return rcopy(place(a, j, q), place(a, j, q), ws(a, 0), wr(a, j), (dp, z))

    def w_p(a, j, k, qq):
        return rcopy(place(a, j, qq), place(a, j, qq), ps(a, j, k - 1), pr(a, j, k - 1), peer(k))

    def w_l(a):
        return lcopy(wins[a], place_whole(a, jz), wl(a))

    acts = [comp, mem, tok]
    cs, cr = al.take(3, B, 2), al.take(3, Z)
    fs, fr = al.take(3, Z), al.take(3, Z)
    cl = al.take(3)

    def c_rows(t, zs):
        return ctx.at[t, pl.ds(pl.multiple_of(zs * R, R), R), :]

    def c_half(t, zs, h):
        return ctx.at[t, pl.ds(pl.multiple_of(zs * R + HR * h, HR), HR), :]

    def c_l(t):
        return lcopy(acts[t].at[jz], c_rows(t, z), cl(t))

    def c_sib(t):
        return rcopy(acts[t].at[jz], c_rows(t, z), fs(t, z), fr(t, z), (sib, z))

    def c_z(t, s, h):
        return rcopy(acts[t].at[s, pl.ds(HR * h, HR), :], c_half(t, z, h), cs(t, s, h), cr(t, z), (2 * q + h, B * c + s))

    def c_arrive(t, zs):
        return rcopy(c_half(t, zs, c), c_half(t, zs, c), cs(t, 0, 0), cr(t, zs), (dp, z))

    def c_fwd(t, zs, half):
        return rcopy(c_half(t, zs, half), c_half(t, zs, half), fs(t, zs), fr(t, zs), (sib, z))

    us, ur, ul = al.take(Z - 1), al.take(Z - 1), al.take(1)
    vs_, vr_ = al.take(1), al.take(1)

    def u_z(r):
        return rcopy(ub.at[dp], ubs.at[r], us(r - 1), ur(r - 1), (dp, lax.rem(z + r, Z)))

    u_l = lcopy(ub.at[dp], ubs.at[0], ul(0))
    v_s = rcopy(vc, vco, vs_(0), vr_(0), (sib, z))

    ts, tr, tl = al.take(B), al.take(B), al.take(1)
    tps, tpr, tfs, tfr = al.take(Q), al.take(Q), al.take(Q), al.take(Q)

    def slot(ref, k, cc):
        return ref.at[pl.ds((2 * k + cc) * N, N), :]

    def t_z(s):
        return rcopy(cot.at[s], cots.at[pl.ds(pl.multiple_of(jz * R, R), R), :], ts(s), tr(jz), (2 * q + z // B, B * c + s))

    def t_l():
        return lcopy(cot.at[jz], cots.at[pl.ds(pl.multiple_of(jz * R, R), R), :], tl(0))

    def t_arrive(i):
        return rcopy(cots.at[pl.ds(i * R, R), :], cots.at[pl.ds(i * R, R), :], ts(0), tr(i), (dp, z))

    def t_p(k):
        return rcopy(slot(cots, 0, 0), slot(cots, k, 0), tps(k), tpr(k), peer(k))

    def t_f(k):
        return rcopy(slot(cots, k, 0), slot(cots, k, 1), tfs(k), tfr(k), (sib, z))

    xs, xr_, xl = al.take(2, Z), al.take(2, Z), al.take(2)

    def x_z(i, r):
        if i == 0:
            return rcopy(up.at[:, pl.ds(pl.multiple_of(dp * E, E), E)], ups.at[:, pl.ds(r * E, E)], xs(0, r), xr_(0, r),
                         (dp, lax.rem(z + r, Z)))
        return rcopy(down.at[pl.ds(pl.multiple_of(dp * E, E), E), :], downs.at[pl.ds(r * E, E), :], xs(1, r), xr_(1, r),
                     (dp, lax.rem(z + r, Z)))

    x_l = [lcopy(up.at[:, pl.ds(pl.multiple_of(dp * E, E), E)], ups.at[:, pl.ds(0, E)], xl(0)),
           lcopy(down.at[pl.ds(pl.multiple_of(dp * E, E), E), :], downs.at[pl.ds(0, E), :], xl(1))]

    @pl.when(mine)
    def _():
        for a in range(4):
            for r in range(1, Z):
                w_z(a, r).start()
        for a in range(4):
            w_l(a).start()
        for t in range(3):
            c_l(t).start()
            c_sib(t).start()
    for r in range(1, Z):
        u_z(r).start()
    v_s.start()
    u_l.start()
    for x in x_l:
        x.start()
    for j in range(B):
        @pl.when(B * c + j != z)
        def _():
            for a in range(4):
                w_arrive(a, j).wait_recv()
                for k in range(1, Q):
                    w_p(a, j, k, q).start()
    for s in range(B):
        @pl.when(B * c + s != z)
        def _():
            for t in range(3):
                for h in range(2):
                    c_z(t, s, h).start()

    def norm_block(t, zs):
        at = pl.ds(pl.multiple_of(zs * R, R), R)
        to = pl.ds(pl.multiple_of(t * S + zs * R, R), R)
        xhat, _ = layer_norm_rows(ctx[t, at, :].astype(F32))
        normed[to, :] = (xhat * g1[...] + b1[...]).astype(BF)

    @pl.when(mine)
    def _():
        for t in range(3):
            c_l(t).wait()

    @pl.when(jnp.logical_not(mine))
    def _():
        for t in range(3):
            rcopy(c_rows(t, z), c_rows(t, z), fs(t, z), fr(t, z), (sib, z)).wait_recv()

    def norm_own(t, carry):
        norm_block(t, z)
        return carry

    lax.fori_loop(0, 3, norm_own, 0)
    for r in range(1, Z):
        zs = lax.rem(z + r, Z)
        for t in range(3):
            c_arrive(t, zs).wait_recv()
            c_fwd(t, zs, c).start()
    for s in range(B):
        @pl.when(B * c + s != z)
        def _():
            for t in range(3):
                for h in range(2):
                    c_z(t, s, h).wait_send()
    for s in range(B):
        here = (B * c + s == z) & mine

        @pl.when(here)
        def _():
            t_l().start()

        @pl.when(jnp.logical_not(here))
        def _():
            t_z(s).start()
    for i in range(2):
        for r in range(1, Z):
            x_z(i, r).start()
    for r in range(1, Z):
        zs = lax.rem(z + r, Z)
        for t in range(3):
            c_fwd(t, zs, 1 - c).wait_recv()

        def norm_one(t, carry, zs=zs):
            norm_block(t, zs)
            return carry

        lax.fori_loop(0, 3, norm_one, 0)
    outs = al.take(16)
    copies = []

    def leave(src, dst):
        cp = lcopy(src, dst, outs(len(copies)))
        cp.start()
        copies.append(cp)

    leave(normed, normed_o)
    leave(ctx.at[2], tok_o)
    for j in range(B):
        @pl.when(B * c + j != z)
        def _():
            for a in range(4):
                for k in range(1, Q):
                    w_p(a, j, k, across(q, k)).wait_recv()

    @pl.when(mine)
    def _():
        for a in range(4):
            w_l(a).wait()
    for a in range(4):
        leave(wss[a], (wq_o, wk_o, wv_o, wo_o)[a])

    T = 256

    def project(i, carry):
        at = pl.ds(pl.multiple_of(i * T, T), T)
        ks[at, :] = nn_dot(normed[at, :], wks[...]).astype(BF)
        vs[at, :] = nn_dot(normed[at, :], wvs[...]).astype(BF)
        return carry

    lax.fori_loop(0, 3 * S // T, project, 0)

    def project_q(i, carry):
        at = pl.ds(pl.multiple_of(i * T, T), T)
        qs[at, :] = nn_dot(normed[pl.ds(pl.multiple_of(2 * S + i * T, T), T), :], wqs[...]).astype(BF)
        return carry

    lax.fori_loop(0, S // T, project_q, 0)
    leave(qs, q_o)
    leave(ks, k_o)
    leave(vs, v_o)

    v_s.wait()
    counts = jnp.where(mine, vc[jz], vco[jz])
    count = counts[0:1, 0:1]
    scale = HEAD_DIM ** (-0.5)
    P2 = 2 * S
    pouts = al.take(2, heads)

    def attend(half, tag):
        r0 = pl.multiple_of(half * N, N)

        def head(h, carry):
            hd = pl.ds(pl.multiple_of(h * HEAD_DIM, HEAD_DIM), HEAD_DIM)
            qh = qs[pl.ds(r0, N), hd]
            s1 = nt_dot(qh, ks[pl.ds(0, P2), hd])
            s2 = nt_dot(qh, ks[pl.ds(P2, S), hd])
            row = lax.broadcasted_iota(jnp.int32, (N, S), 0) + half * N
            col = lax.broadcasted_iota(jnp.int32, (N, S), 1)
            s2 = jnp.where((col <= row) & (col < count), s2, -1e30)
            top = jnp.maximum(jnp.max(s1, axis=-1, keepdims=True), jnp.max(s2, axis=-1, keepdims=True))
            p1 = jnp.exp((s1 - top) * scale)
            p2 = jnp.exp((s2 - top) * scale)
            inv = 1.0 / (jnp.sum(p1, axis=-1, keepdims=True) + jnp.sum(p2, axis=-1, keepdims=True))
            p1 = (p1 * inv).astype(BF)
            p2 = (p2 * inv).astype(BF)
            probs[h, pl.ds(r0, N), pl.ds(0, P2)] = p1
            probs[h, pl.ds(r0, N), pl.ds(P2, S)] = p2
            lcopy(probs.at[h, pl.ds(r0, N), :], probs_o.at[h, pl.ds(r0, N), :], pouts(tag, h)).start()
            mix = nn_dot(p1, vs[pl.ds(0, P2), hd]) + nn_dot(p2, vs[pl.ds(P2, S), hd])
            mixed[pl.ds(r0, N), hd] = mix.astype(BF)
            return carry

        lax.fori_loop(0, heads, head, 0)

    hs, hr = al.take(1), al.take(1)
    h_x = rcopy(phalf, got, hs(0), hr(0), (sib, z))
    attend(1 - c, 0)
    phalf[...] = nn_dot(mixed[pl.ds(pl.multiple_of((1 - c) * N, N), N), :], wos[...])
    h_x.start()
    for i in range(B):
        @pl.when(jnp.logical_not((B * c + i == z) & mine))
        def _():
            t_arrive(i).wait_recv()

        @pl.when((B * c + i == z) & mine)
        def _():
            t_l().wait()
    for k in range(1, Q):
        t_p(k).start()
    t_f(0).start()
    attend(c, 1)
    leave(mixed, mixed_o)
    own_part = nn_dot(mixed[pl.ds(pl.multiple_of(c * N, N), N), :], wos[...])
    h_x.wait_recv()
    resid[...] = ctx[2, pl.ds(pl.multiple_of(c * N, N), N), :].astype(F32) + (own_part + got[...])
    leave(resid, resid_o)
    xhat2, _ = layer_norm_rows(resid[...])
    sec[pl.ds(0, N), :] = (xhat2 * g2[...] + b2[...]).astype(BF)

    as_, ar, afs, afr = al.take(Q), al.take(Q), al.take(Q), al.take(Q)

    def a_p(k):
        return rcopy(slot(sec, 0, 0), slot(sec, k, 0), as_(k), ar(k), peer(k))

    def a_f(k):
        return rcopy(slot(sec, k, 0), slot(sec, k, 1), afs(k), afr(k), (sib, z))

    for k in range(1, Q):
        t_p(k).wait_recv()
        t_f(k).start()
    for k in range(1, Q - 1):
        a_p(k).start()
    a_f(0).start()
    sqc = al.take(RATE)
    sqs = [dns.at[pl.ds(0, D), :], dns.at[pl.ds(D, D), :], gbuf.at[pl.ds(D, D), :]]
    sq_x = [lcopy(sq.at[pl.ds(r * D, D), :], sqs[r], sqc(r)) for r in range(RATE)]
    for x in sq_x:
        x.start()
    for r in range(1, Z):
        u_z(r).wait()
        for i in range(2):
            x_z(i, r).wait_recv()
    u_l.wait()
    for x in x_l:
        x.wait()
    ss, sr = al.take(Q), al.take(Q)
    gps, gpr = al.take(Q), al.take(Q)

    def s_x(k):
        return rcopy(slot(gbuf, k, 1), got1.at[k], ss(k), sr(k), (sib, z))

    def p_x(k):
        return rcopy(send2.at[k - 1], got2.at[k - 1], gps(k), gpr(k), peer(k))

    bias_row = jnp.concatenate([ubs[r] for r in range(Z)], axis=1)
    small_o[...] = jnp.zeros_like(small_o)

    def forward_block(b, carry):
        at = pl.ds(pl.multiple_of(b * N, N), N)
        x = nn_dot(sec[at, :], ups[...]) + bias_row
        ga = nt_dot(cots[at, :], downs[...])
        x2 = x * x
        root = 0.7978845608028654
        th = jnp.tanh(root * (x + 0.044715 * (x2 * x)))
        act[at, :] = (0.5 * x * (1.0 + th)).astype(BF)
        slope = 0.5 * (1.0 + th) + 0.5 * x * (1.0 - th * th) * (root * (1.0 + 0.134145 * x2))
        gu = (ga * slope).astype(BF)
        gup[at, :] = gu
        small_o[2:3, pl.ds(0, Z * E)] = small_o[2:3, pl.ds(0, Z * E)] + jnp.sum(gu.astype(F32), axis=0, keepdims=True)
        gbuf[at, :] = nt_dot(gu, ups[...]).astype(BF)
        return carry

    def feed(k):
        lax.fori_loop(2 * k, 2 * k + 2, forward_block, 0)
        s_x(k).start()

    def combine(k):
        s_x(k).wait_recv()
        send2[k - 1] = (gbuf[pl.ds(2 * k * N, N), :].astype(F32) + got1[k].astype(F32)).astype(BF)
        p_x(k).start()

    t_f(0).wait_recv()
    a_f(0).wait_recv()
    feed(0)

    groups = S // RATE
    squeezed = None
    for r in range(RATE):
        sq_x[r].wait()
        row = lax.broadcasted_iota(jnp.int32, (ncs.shape[0], S), 0)
        col = lax.broadcasted_iota(jnp.int32, (ncs.shape[0], S), 1)
        pick = jnp.where((col == row * RATE + r) & (row < groups), 1.0, 0.0).astype(BF)
        picked = nn_dot(pick, ctx[1]).astype(BF)
        term = nn_dot(picked, sqs[r][...])
        squeezed = term if squeezed is None else squeezed + term
    ncs[...] = squeezed.astype(BF)
    shift = count + c * N
    new_mem = nn_dot(one_hot((N, S), shift), ctx[1]) + nn_dot(one_hot((N, S), shift - S), ctx[2])
    nms[...] = new_mem.astype(BF)
    third = lax.shift_right_logical(count * 21846, 16)
    shift = third + c * N
    new_comp = nn_dot(one_hot((N, S), shift), ctx[0]) + nn_dot(one_hot((N, ncs.shape[0]), shift - S), ncs[...])
    ncs[pl.ds(0, N), :] = new_comp.astype(BF)
    per = N // R
    ms, mr, ml = al.take(2, 2), al.take(2, B), al.take(2)
    rows_in = [nms, ncs]
    rows_out = [nm_o, nc_o]

    def row_x(i, p):
        return rcopy(rows_in[i].at[pl.ds(p * R, R), :], rows_out[i].at[jz], ms(i, p), mr(i, jz), (2 * q + z // B, c * per + p))

    def row_l(i, p):
        return lcopy(rows_in[i].at[pl.ds(p * R, R), :], rows_out[i].at[jz], ml(i))

    for p in range(per):
        here = (c * per + p == z) & mine

        @pl.when(here)
        def _():
            for i in range(2):
                row_l(i, p).start()

        @pl.when(jnp.logical_not(here))
        def _():
            for i in range(2):
                row_x(i, p).start()

    for k in range(1, Q):
        a_p(k).wait_recv()
        if k == Q - 2:
            a_p(Q - 1).start()
        a_f(k).start()
        t_f(k).wait_recv()
        a_f(k).wait_recv()
        feed(k)
        if k > 1:
            combine(k - 1)
    combine(Q - 1)

    def up_grad(i, carry):
        at = pl.ds(pl.multiple_of(i * T, T), T)
        gus[at, :] = tn_dot(sec[:, at], gup[...]).astype(BF)
        return carry

    lax.fori_loop(0, D // T, up_grad, 0)
    leave(gus, gu_o)

    def down_grad(i, carry):
        at = pl.ds(pl.multiple_of(i * T, T), T)
        gds[at, :] = tn_dot(act[:, at], cots[...]).astype(BF)
        return carry

    lax.fori_loop(0, Z * E // T, down_grad, 0)
    leave(gds, gd_o)

    def down_rows(b, carry):
        at = pl.ds(pl.multiple_of(b * N, N), N)
        dns[at, :] = nn_dot(act[at, :], downs[...]).astype(BF)
        return carry

    lax.fori_loop(0, 2 * Q, down_rows, 0)
    leave(dns, down_o)

    s_x(0).wait_recv()
    for k in range(1, Q):
        p_x(k).wait_recv()
    C = 64

    def back_rows(i, carry):
        at = pl.ds(pl.multiple_of(i * C, C), C)
        gs = gbuf[at, :].astype(F32) + got1[0, at, :].astype(F32)
        for k in range(1, Q):
            gs = gs + got2[k - 1, at, :].astype(F32)
        xhat, inv = layer_norm_rows(resid[at, :])
        small_o[0:1, :] = small_o[0:1, :] + jnp.sum(gs * xhat, axis=0, keepdims=True)
        small_o[1:2, :] = small_o[1:2, :] + jnp.sum(gs, axis=0, keepdims=True)
        e = gs * g2[...]
        m1 = jnp.mean(e, axis=-1, keepdims=True)
        m2 = jnp.mean(e * xhat, axis=-1, keepdims=True)
        gr = cots[at, :].astype(F32) + inv * (e - m1 - xhat * m2)
        got[at, :] = gr
        low[at, :] = gr.astype(BF)
        return carry

    lax.fori_loop(0, N // C, back_rows, 0)
    leave(got, gresid_o)
    ls_, lr_, ll_ = al.take(1), al.take(1), al.take(1)
    mine_rows = glow_o.at[pl.ds(pl.multiple_of(c * N, N), N), :]
    far = rcopy(low, mine_rows, ls_(0), lr_(0), (sib, z))
    near = lcopy(low, mine_rows, ll_(0))
    far.start()
    near.start()

    for cp in copies:
        cp.wait()
    for h in range(heads):
        for half, tag in ((1 - c, 0), (c, 1)):
            rows = pl.ds(pl.multiple_of(half * N, N), N)
            lcopy(probs.at[h, rows, :], probs_o.at[h, rows, :], pouts(tag, h)).wait()

    @pl.when(mine)
    def _():
        for a in range(4):
            for r in range(1, Z):
                w_z(a, r).wait_send()
        for t in range(3):
            c_sib(t).wait_send()
    for j in range(B):
        @pl.when(B * c + j != z)
        def _():
            for a in range(4):
                for k in range(1, Q):
                    w_p(a, j, k, q).wait_send()
    for r in range(1, Z):
        for t in range(3):
            c_fwd(t, lax.rem(z + r, Z), c).wait_send()
        for i in range(2):
            x_z(i, r).wait_send()
    for s in range(B):
        @pl.when(jnp.logical_not((B * c + s == z) & mine))
        def _():
            t_z(s).wait_send()
    for k in range(1, Q):
        t_p(k).wait_send()
        a_p(k).wait_send()
        p_x(k).wait_send()
    for k in range(Q):
        t_f(k).wait_send()
        a_f(k).wait_send()
        s_x(k).wait_send()
    h_x.wait_send()
    for p in range(per):
        here = (c * per + p == z) & mine

        @pl.when(here)
        def _():
            for i in range(2):
                row_l(i, p).wait()

        @pl.when(jnp.logical_not(here))
        def _():
            for i in range(2):
                row_x(i, p).wait_send()
    for s in range(B):
        @pl.when(jnp.logical_not((B * c + s == z) & mine))
        def _():
            for i in range(2):
                rcopy(rows_out[i].at[s], rows_out[i].at[s], ms(i, 0), mr(i, s), (dp, z)).wait_recv()
    near.wait()
    far.wait()
    assert al.used <= FRONT_SEMS


def front(Q, Z, comp, mem, tok, cot, wq, wk, wv, wo, up, down, ub, vc, sq, g1, b1, g2, b2):
    B, R, D = tok.shape
    H = wq.shape[1]
    S = R * Z
    N = S // 2
    W = B * H
    heads = W // HEAD_DIM
    F = up.shape[1] // 2 // Q * Z
    rows = 2 * Q * N
    vm = pltpu.VMEM
    return pl.pallas_call(
        functools.partial(front_kernel, Q, Z),
        out_shape=[
            sds((S, D), BF), sds((3 * S, D), BF), sds((S, W), BF), sds((3 * S, W), BF), sds((3 * S, W), BF),
            sds((heads, S, 3 * S), BF), sds((S, W), BF), sds((D, W), BF), sds((D, W), BF), sds((D, W), BF), sds((W, D), BF),
            sds((N, D), F32), sds((N, D), F32), sds((S, D), BF), sds((D, F), BF), sds((F, D), BF), sds((rows, D), BF),
            sds((8, D), F32), sds((B, R, D), BF), sds((B, R, D), BF),
        ],
        in_specs=[ANY] * 11 + [VM] + [ANY] + [VM] * 4,
        out_specs=[ANY] * 17 + [VM] + [ANY] * 2,
        scratch_shapes=[
            vm((3, S, D), BF), vm((3 * S, D), BF), vm((D, W), BF), vm((D, W), BF), vm((D, W), BF), vm((W, D), BF),
            vm((S, W), BF), vm((3 * S, W), BF), vm((3 * S, W), BF), vm((heads, S, 3 * S), BF), vm((S, W), BF),
            vm((N, D), F32), vm((N, D), F32), vm((N, D), F32), vm((rows, D), BF), vm((rows, D), BF), vm((D, F), BF), vm((F, D), BF),
            vm((Z, 1, F // Z), F32), vm(vc.shape, jnp.int32), vm((rows, F), BF), vm((rows, F), BF), vm((rows, D), BF),
            vm((Q, N, D), BF), vm((Q - 1, N, D), BF), vm((Q - 1, N, D), BF), vm((N, D), BF),
            vm((N, D), BF), vm((N, D), BF), vm((D, F), BF), vm((F, D), BF), vm((rows, D), BF),
            DMA((FRONT_SEMS,)),
        ],
        compiler_params=pltpu.CompilerParams(collective_id=1, has_side_effects=True, vmem_limit_bytes=63 << 20),
        name="front",
    )(comp, mem, tok, cot, wq, wk, wv, wo, up, down, ub, vc, sq, g1, b1, g2, b2)


class PlaneSum:
    def __init__(self, al, peer, blk, rows, h, g):
        self.peer, self.blk, self.half, self.rows, self.h, self.g = peer, blk, rows // 2, rows, h, g
        self.hs, self.hr, self.gs, self.gr = al.take(2), al.take(2), al.take(2), al.take(2)

    def h_x(self, i):
        return rcopy(self.blk(3, i * self.half, self.half), self.h.at[i], self.hs(i), self.hr(i), self.peer(i + 1))

    def g_x(self, i):
        return rcopy(self.blk(i + 1, 0, self.rows), self.g.at[i], self.gs(i), self.gr(i), self.peer(i + 1))

    def start(self):
        for i in range(2):
            self.h_x(i).start()

    def middle(self):
        for i in range(2):
            self.h_x(i).wait_recv()
            mine = self.blk(2 - i, i * self.half, self.half)
            mine[...] = (mine[...].astype(F32) + self.h[i].astype(F32)).astype(BF)
            self.g_x(1 - i).start()

    def total(self):
        for i in range(2):
            self.g_x(i).wait_recv()
        own = self.blk(0, 0, self.rows)
        return own[...].astype(F32) + (self.g[0].astype(F32) + self.g[1].astype(F32))

    def drain(self):
        for i in range(2):
            self.h_x(i).wait_send()
            self.g_x(i).wait_send()


class PlaneGather:
    def __init__(self, al, peer, sib, loc, rows, own=None):
        self.peer, self.sib, self.loc, self.half, self.rows = peer, sib, loc, rows // 2, rows
        self.own = own
        self.as_, self.ar, self.hs, self.hr = al.take(2), al.take(2), al.take(2), al.take(2)
        self.fs, self.fr = al.take(4), al.take(4)

    def a_x(self, i, k=0):
        src = self.loc(0, 0, self.rows) if self.own is None else self.own
        return rcopy(src, self.loc(k, 0, self.rows), self.as_(i), self.ar(i), self.peer(i + 1))

    def h_x(self, i, k=None):
        k = 2 - (1 - i) if k is None else k
        rows = self.loc(k, i * self.half, self.half)
        return rcopy(rows, rows, self.hs(i), self.hr(i), self.peer(2 - i))

    def f_x(self, k, other=None):
        src = self.loc(k, 0, self.rows)
        if k == 0 and self.own is not None:
            src = self.own
        dst = self.loc(k, 0, self.rows) if other is None else other(k, 0, self.rows)
        return rcopy(src, dst, self.fs(k), self.fr(k), self.sib)

    def start(self):
        for i in range(2):
            self.a_x(i).start()
        self.f_x(0).start()

    def middle(self):
        for i in range(2):
            rcopy(self.loc(i + 1, 0, self.rows), self.loc(i + 1, 0, self.rows), self.as_(i), self.ar(i), self.peer(1)).wait_recv()
            self.h_x(i).start()
            self.f_x(i + 1).start()

    def last(self):
        for i in range(2):
            self.h_x(i, 3).wait_recv()
        self.f_x(3).start()

    def drain(self):
        for i in range(2):
            self.a_x(i).wait_send()
            self.h_x(i).wait_send()
        for k in range(4):
            self.f_x(k).wait_send()

    def arrivals(self, other):
        for k in range(4):
            rcopy(other(k, 0, self.rows), other(k, 0, self.rows), self.fs(k), self.fr(k), self.sib).wait_recv()


BACK_SEMS = 300


def back_kernel(Q, Z, B, tok, normed_i, q_i, k_i, v_i, probs_i, mixed_i, wq_i, wk_i, wv_i, wo_i, resid_i, gresid_i, glow_i,
                gu, gd, down_i, ffs, cot, g1, b1, db,
                aw, ago, afu, afd, aub, small_o, out_o, tg_o,
                normed, qs, ks, vs, probs, mixed, wqs, wks, wvs, wos, toks, resid, gresid, glow, gms,
                xu, xd, xb, fus, fds, fbs, dgot, dnb, dh, dg, gkv, gqs, gos, gwb, gh, gg, oh, og,
                wdone, odone, zb, zo, wfin, ofin, ghalf, ggot, cots, arow, sums, sgot, srow, pgot, zgot, outs, tgs, sems):
    dp, c, q, z = where_am_i(Q, Z)
    sib = (dp + 1 - 2 * c, z)
    partners = [sib]
    for r in range(1, Z):
        for d in (dp, dp + 1 - 2 * c):
            partners.append((d, lax.rem(z + r, Z)))

    def peer(k):
        return (2 * across(q, k) + c, z)

    for k in range(1, Q):
        partners.append(peer(k))
    enter(partners)
    S, D = glow.shape
    N = S // 2
    W = qs.shape[1]
    H = W // B
    F = gd.shape[0]
    E = F // Z
    R = S // Z
    heads = W // HEAD_DIM
    hj = H // HEAD_DIM
    mine = c == z // B
    jz = lax.rem(z, B)
    al = Slots(sems)

    def up_to_z(r):
        return (dp, lax.rem(z + Z - r, Z))

    xs, xr = al.take(3, Z), al.take(3, Z)

    def x_z(i, r):
        if i == 0:
            return rcopy(gu.at[:, pl.ds(r * E, E)], xu.at[r], xs(0, r), xr(0, r), up_to_z(r))
        if i == 1:
            return rcopy(gd.at[pl.ds(r * E, E), :], xd.at[r], xs(1, r), xr(1, r), up_to_z(r))
        return rcopy(ffs.at[pl.ds(2, 1), pl.ds(r * E, E)], xb.at[r], xs(2, r), xr(2, r), up_to_z(r))

    ss, sr = al.take(Q), al.take(Q)

    def d_x(k):
        return rcopy(down_i.at[pl.ds((2 * k + 1) * N, N), :], dgot.at[k], ss(k), sr(k), sib)

    ld = al.take(30)
    pairs = [(wo_i, wos), (glow_i, glow), (mixed_i, mixed), (probs_i, probs), (v_i, vs), (k_i, ks), (q_i, qs),
             (normed_i, normed), (wq_i, wqs), (wk_i, wks), (wv_i, wvs), (gresid_i, gresid), (resid_i, resid),
             (tok.at[pl.ds(pl.multiple_of(c * N, N), N), :], toks), (cot, cots),
             (gu.at[:, pl.ds(0, E)], xu.at[0]), (gd.at[pl.ds(0, E), :], xd.at[0])]
    pairs += [(down_i.at[pl.ds(2 * k * N, N), :], dnb.at[k]) for k in range(Q)]
    loads = [lcopy(src, dst, ld(i)) for i, (src, dst) in enumerate(pairs)]
    for x in loads[:3]:
        x.start()
    for k in (3, 1, 2, 0):
        d_x(k).start()
    for x in loads[3:]:
        x.start()
    for r in range(1, Z):
        for i in range(3):
            x_z(i, r).start()

    for x in loads[:3]:
        x.wait()
    T = 256

    def mix_rows(i, carry):
        at = pl.ds(pl.multiple_of(i * T, T), T)
        gms[at, :] = nt_dot(glow[at, :], wos[...]).astype(BF)
        gos[at, :] = tn_dot(mixed[:, at], glow[...]).astype(BF)
        return carry

    lax.fori_loop(0, S // T, mix_rows, 0)
    OR = H // Q
    M = D // Q

    def o_blk(j):
        def blk(k, lo, n):
            return gos.at[pl.ds(pl.multiple_of(j * H + across(q, k) * OR + lo, n), n), :]
        return blk

    def w_blk(j):
        def blk(k, lo, n):
            return gwb.at[j, pl.ds(pl.multiple_of(across(q, k) * M + lo, n), n), :]
        return blk

    osum = [PlaneSum(al, peer, o_blk(j), OR, oh.at[j], og.at[j]) for j in range(B)]
    wsum = [PlaneSum(al, peer, w_blk(j), M, gh.at[j], gg.at[j]) for j in range(B)]
    dsum = PlaneSum(al, peer, lambda k, lo, n: dnb.at[k, pl.ds(lo, n), :], N, dh, dg)
    for x in osum:
        x.start()
    sums[...] = jnp.zeros_like(sums)
    arow[...] = jnp.zeros_like(arow)
    scale = HEAD_DIM ** (-0.5)

    def head(h, hh):
        hd = pl.ds(h * HEAD_DIM, HEAD_DIM)
        ko = pl.ds(hh * HEAD_DIM, HEAD_DIM)
        vo = pl.ds(H + hh * HEAD_DIM, HEAD_DIM)
        p = probs[h]
        gm = gms[:, hd]
        gp = nt_dot(gm, vs[:, hd])
        delta = jnp.sum(gm.astype(F32) * mixed[:, hd].astype(F32), axis=-1, keepdims=True)
        gs = (p.astype(F32) * (gp - delta)).astype(BF)
        gqs[:, hd] = (scale * nn_dot(gs, ks[:, hd])).astype(BF)
        gkv[:, ko] = (scale * tn_dot(gs, qs[:, hd])).astype(BF)
        gkv[:, vo] = tn_dot(p, gm).astype(BF)

    def split_rows(v):
        hi = v.astype(BF)
        rest = v - hi.astype(F32)
        mid = rest.astype(BF)
        low = (rest - mid.astype(F32)).astype(BF)
        return jnp.concatenate([hi, mid, low, jnp.zeros((5, v.shape[1]), BF)], axis=0)

    def weights(j):
        js = pl.ds(j * H, H)

        def rows(i, carry):
            at = pl.ds(pl.multiple_of(i * T, T), T)
            kv = tn_dot(normed[:, at], gkv[...])
            gq = tn_dot(normed[pl.ds(2 * S, S), at], gqs[:, js])
            gwb[j, at, pl.ds(0, 2 * H)] = kv.astype(BF)
            gwb[j, at, pl.ds(2 * H, H)] = gq.astype(BF)
            t = (kv[:, :H] * wks[at, js].astype(F32) + kv[:, H:] * wvs[at, js].astype(F32) + gq * wqs[at, js].astype(F32))
            arow[at, :] = arow[at, :] + jnp.broadcast_to(jnp.sum(t, axis=-1, keepdims=True), (T, 128))
            return carry

        lax.fori_loop(0, D // T, rows, 0)
        wsum[j].start()
        skv = split_rows(jnp.sum(gkv[...].astype(F32), axis=0, keepdims=True))
        sq_ = split_rows(jnp.sum(gqs[:, js].astype(F32), axis=0, keepdims=True))
        b = nt_dot(skv[:, :H], wks[:, js]) + nt_dot(skv[:, H:], wvs[:, js]) + nt_dot(sq_, wqs[:, js])
        sums[1:2, :] = sums[1:2, :] + jnp.sum(b, axis=0, keepdims=True)

    for x in loads[3:7]:
        x.wait()
    for h in range(hj):
        head(h, h)
    for x in osum:
        x.middle()
    for x in loads[17:]:
        x.wait()
    for k in (3, 1, 2, 0):
        d_x(k).wait_recv()
        dnb[k] = (dnb[k].astype(F32) + dgot[k].astype(F32)).astype(BF)
    for x in loads[7:11]:
        x.wait()
    H2 = pl.ds(2 * S, S)

    def token_rows(j, half):
        js = pl.ds(j * H, H)
        rows = pl.ds(pl.multiple_of(half * N, N), N)
        krows = pl.ds(pl.multiple_of(2 * S + half * N, N), N)
        return (nt_dot(gkv[krows, pl.ds(0, H)], wks[:, js]) + nt_dot(gkv[krows, pl.ds(H, H)], wvs[:, js])
                + nt_dot(gqs[rows, js], wqs[:, js]))

    weights(0)
    ghalf[...] = token_rows(0, 1 - c)
    srow[...] = token_rows(0, c)
    dsum.start()
    for h in range(hj, 2 * hj):
        head(h, h - hj)
    wsum[0].middle()
    weights(1)
    dsum.middle()
    ghalf[...] = ghalf[...] + token_rows(1, 1 - c)
    ts_, tr_ = al.take(1), al.take(1)
    t_x = rcopy(ghalf, ggot, ts_(0), tr_(0), sib)
    t_x.start()
    srow[...] = srow[...] + token_rows(1, c)

    for x in loads[11:17]:
        x.wait()
    acol = jnp.swapaxes(arow[...], 0, 1)[0:1, :]
    bsum = sums[1:2, :]
    sums[0:1, :] = (acol - b1[...] * bsum) / g1[...]
    sums[2:3, :] = ffs[0:1, :]
    sums[3:4, :] = ffs[1:2, :]
    sums[4:5, :] = jnp.sum(cots[...].astype(F32), axis=(0, 1)).reshape(1, D)
    n1, n2 = al.take(1), al.take(1)
    v_x = rcopy(sums, sgot, n1(0), n2(0), sib)
    v_x.start()
    osums = []
    ozs, ozr = al.take(2, B), al.take(2, Z)

    def z_x(i, j):
        src, dst = ((wdone, zb), (odone, zo))[i]
        return rcopy(src.at[j], dst.at[z], ozs(i, j), ozr(i, z), (dp, B * c + j))

    def z_arrive(i, zz):
        dst = (zb, zo)[i]
        return rcopy(dst.at[zz], dst.at[zz], ozs(i, 0), ozr(i, zz), (dp, z))

    def to_plane(i, j):
        ((wdone, odone)[i])[j] = ((wsum, osum)[i])[j].total().astype(BF)

        @pl.when(B * c + j != z)
        def _():
            z_x(i, j).start()

    wsum[1].middle()
    for j in range(B):
        to_plane(1, j)
    t_x.wait_recv()
    C = 64

    def norm_rows(i, carry):
        at = pl.ds(pl.multiple_of(i * C, C), C)
        gn = srow[at, :] + ggot[at, :]
        xhat, inv = layer_norm_rows(toks[at, :].astype(F32))
        e = gn * g1[...]
        m1 = jnp.mean(e, axis=-1, keepdims=True)
        m2 = jnp.mean(e * xhat, axis=-1, keepdims=True)
        tgs[at, :] = (gresid[at, :] + inv * (e - m1 - xhat * m2)).astype(BF)
        return carry

    lax.fori_loop(0, N // C, norm_rows, 0)
    per = N // R
    rs, rr, rl = al.take(2, 2), al.take(2, B), al.take(2)
    rows_in = [tgs, outs]
    rows_out = [tg_o, out_o]

    def row_x(i, p):
        return rcopy(rows_in[i].at[pl.ds(p * R, R), :], rows_out[i].at[jz], rs(i, p), rr(i, jz), (2 * q + z // B, c * per + p))

    def row_l(i, p):
        return lcopy(rows_in[i].at[pl.ds(p * R, R), :], rows_out[i].at[jz], rl(i))

    def send_rows(i):
        for p in range(per):
            here = (c * per + p == z) & mine

            @pl.when(here)
            def _():
                row_l(i, p).start()

            @pl.when(jnp.logical_not(here))
            def _():
                row_x(i, p).start()

    send_rows(0)
    for r in range(1, Z):
        for i in range(3):
            x_z(i, r).wait_recv()
    fu, fd, fb = xu[0].astype(F32), xd[0].astype(F32), ffs[2:3, 0:E]
    for r in range(1, Z):
        fu = fu + xu[r].astype(F32)
        fd = fd + xd[r].astype(F32)
        fb = fb + xb[r]
    fus[...] = fu.astype(BF)
    fds[...] = fd.astype(BF)
    fbs[...] = fb

    def dev(k, core):
        return 2 * across(q, k) + core

    def u_loc(core):
        def loc(k, lo, n):
            return afu.at[pl.ds(lo, n), pl.ds(pl.multiple_of(dev(k, core) * E, E), E)]
        return loc

    def d_loc(core):
        def loc(k, lo, n):
            return afd.at[pl.ds(pl.multiple_of(dev(k, core) * E + lo, n), n), :]
        return loc

    ugat = PlaneGather(al, peer, sib, u_loc(c), D, own=fus)
    dgat = PlaneGather(al, peer, sib, d_loc(c), E, own=fds)
    fl = al.take(3)
    f_l = [lcopy(fus, u_loc(c)(0, 0, D), fl(0)), lcopy(fds, d_loc(c)(0, 0, E), fl(1))]
    bs, br, bfs, bfr = al.take(Q), al.take(Q), al.take(Q), al.take(Q)

    def b_x(k):
        return rcopy(fbs, aub.at[dp], bs(k), br(k), peer(k))

    def b_arrive(k):
        return rcopy(aub.at[dev(k, c)], aub.at[dev(k, c)], bs(k), br(k), peer(k))

    def b_f(k):
        src = fbs if k == 0 else aub.at[dev(k, c)]
        return rcopy(src, aub.at[dev(k, c)], bfs(k), bfr(k), sib)

    b_l = lcopy(fbs, aub.at[dp], fl(2))
    ugat.start()
    dgat.start()
    for x in f_l:
        x.start()
    b_l.start()
    for k in range(1, Q):
        b_x(k).start()
    b_f(0).start()
    v_x.wait()
    srow[0:8, :] = sums[...] + sgot[...]
    pgot[q] = srow[0:8, :]
    vps, vpr, vzs, vzr = al.take(Q), al.take(Q), al.take(Z), al.take(Z)

    def vp_x(k):
        return rcopy(srow.at[pl.ds(0, 8), :], pgot.at[q], vps(k), vpr(k), peer(k))

    def vp_arrive(k):
        return rcopy(pgot.at[across(q, k)], pgot.at[across(q, k)], vps(k), vpr(k), peer(k))

    def vz_x(r):
        return rcopy(srow.at[pl.ds(8, 8), :], zgot.at[z], vzs(r), vzr(r), (dp, lax.rem(z + r, Z)))

    def vz_arrive(r):
        zz = lax.rem(z + Z - r, Z)
        return rcopy(zgot.at[zz], zgot.at[zz], vzs(r), vzr(r), (dp, z))

    for k in range(1, Q):
        vp_x(k).start()
    for i in range(2):
        pass
    outs[...] = (resid[...] + dsum.total() + db[...]).astype(BF)
    send_rows(1)
    to_plane(0, 0)
    for k in range(1, Q):
        vp_arrive(k).wait_recv()
    psum = pgot[0]
    for k in range(1, Q):
        psum = psum + pgot[k]
    srow[8:16, :] = psum
    zgot[z] = psum
    for r in range(1, Z):
        vz_x(r).start()
    to_plane(0, 1)

    def a_loc(ref, n_rows):
        def loc(k, lo, n):
            return ref.at[pl.ds(pl.multiple_of(across(q, k) * n_rows + lo, n), n), :]
        return loc

    wgat = PlaneGather(al, peer, sib, a_loc(aw, M), M, own=wfin)
    ogat = PlaneGather(al, peer, sib, a_loc(ago, OR), OR, own=ofin)
    gl = al.take(2)
    g_l = [lcopy(wfin, a_loc(aw, M)(0, 0, M), gl(0)), lcopy(ofin, a_loc(ago, OR)(0, 0, OR), gl(1))]

    @pl.when(mine)
    def _():
        for i, (fin, done, buf, gat) in ((1, (ofin, odone, zo, ogat)), (0, (wfin, wdone, zb, wgat))):
            for zz in range(Z):
                @pl.when(zz != z)
                def _():
                    z_arrive(i, zz).wait_recv()
            buf[z] = done[jz]
            t = buf[0].astype(F32)
            for zz in range(1, Z):
                t = t + buf[zz].astype(F32)
            fin[...] = t.astype(BF)
            gat.start()
            g_l[1 if i == 1 else 0].start()
    for gat in (ugat, dgat):
        gat.middle()
    for k in range(1, Q):
        b_arrive(k).wait_recv()
        b_f(k).start()
    for r in range(1, Z):
        vz_arrive(r).wait_recv()
    zsum = zgot[0]
    for zz in range(1, Z):
        zsum = zsum + zgot[zz]
    small_o[...] = zsum

    @pl.when(mine)
    def _():
        for gat in (ogat, wgat):
            gat.middle()
    for gat in (ugat, dgat):
        gat.last()

    @pl.when(mine)
    def _():
        for gat in (ogat, wgat):
            gat.last()
    ugat.arrivals(u_loc(1 - c))
    dgat.arrivals(d_loc(1 - c))

    @pl.when(jnp.logical_not(mine))
    def _():
        ogat.arrivals(a_loc(ago, OR))
        wgat.arrivals(a_loc(aw, M))

    for k in range(Q):
        rcopy(aub.at[dev(k, 1 - c)], aub.at[dev(k, 1 - c)], bfs(k), bfr(k), sib).wait_recv()
        b_f(k).wait_send()
        d_x(k).wait_send()
    for k in range(1, Q):
        b_x(k).wait_send()
        vp_x(k).wait_send()
    b_l.wait()
    for x in f_l:
        x.wait()
    for r in range(1, Z):
        vz_x(r).wait_send()
        for i in range(3):
            x_z(i, r).wait_send()
    for x in osum + wsum + [dsum, ugat, dgat]:
        x.drain()

    @pl.when(mine)
    def _():
        for x in (ogat, wgat):
            x.drain()
        for x in g_l:
            x.wait()
    t_x.wait_send()
    for j in range(B):
        @pl.when(B * c + j != z)
        def _():
            for i in range(2):
                z_x(i, j).wait_send()
    for p in range(per):
        here = (c * per + p == z) & mine

        @pl.when(here)
        def _():
            for i in range(2):
                row_l(i, p).wait()

        @pl.when(jnp.logical_not(here))
        def _():
            for i in range(2):
                row_x(i, p).wait_send()
    for s in range(B):
        @pl.when(jnp.logical_not((B * c + s == z) & mine))
        def _():
            for i in range(2):
                rcopy(rows_out[i].at[s], rows_out[i].at[s], rs(i, 0), rr(i, s), (dp, z)).wait_recv()
    assert al.used <= BACK_SEMS


def back(Q, Z, B, tok, normed, q_, k_, v_, probs, mixed, wq, wk, wv, wo, resid, gresid, glow, gu, gd, down, ffs, cot, g1, b1, db):
    S, D = glow.shape
    N, R = S // 2, S // Z
    W = q_.shape[1]
    H = W // B
    F = gd.shape[0]
    E = F // Z
    heads = W // HEAD_DIM
    M, OR = D // Q, H // Q
    vm = pltpu.VMEM
    return pl.pallas_call(
        functools.partial(back_kernel, Q, Z, B),
        out_shape=[
            sds((D, 3 * H), BF), sds((H, D), BF), sds((D, 2 * Q * E), BF), sds((2 * Q * E, D), BF), sds((2 * Q, 1, E), F32),
            sds((8, D), F32), sds((B, R, D), BF), sds((B, R, D), BF),
        ],
        in_specs=[ANY] * 17 + [VM] + [ANY] + [VM] * 3,
        out_specs=[ANY] * 5 + [VM] + [ANY] * 2,
        scratch_shapes=[
            vm((3 * S, D), BF), vm((S, W), BF), vm((3 * S, W), BF), vm((3 * S, W), BF), vm((heads, S, 3 * S), BF), vm((S, W), BF),
            vm((D, W), BF), vm((D, W), BF), vm((D, W), BF), vm((W, D), BF),
            vm((N, D), BF), vm((N, D), F32), vm((N, D), F32), vm((S, D), BF), vm((S, W), BF),
            vm((Z, D, E), BF), vm((Z, E, D), BF), vm((Z, 1, E), F32), vm((D, E), BF), vm((E, D), BF), vm((1, E), F32),
            vm((Q, N, D), BF), vm((Q, N, D), BF), vm((2, N // 2, D), BF), vm((2, N, D), BF),
            vm((3 * S, 2 * H), BF), vm((S, W), BF), vm((W, D), BF), vm((B, D, 3 * H), BF),
            vm((B, 2, M // 2, 3 * H), BF), vm((B, 2, M, 3 * H), BF), vm((B, 2, OR // 2, D), BF), vm((B, 2, OR, D), BF),
            vm((B, M, 3 * H), BF), vm((B, OR, D), BF), vm((Z, M, 3 * H), BF), vm((Z, OR, D), BF), vm((M, 3 * H), BF), vm((OR, D), BF),
            vm((N, D), F32), vm((N, D), F32), vm(cot.shape, BF), vm((D, 128), F32),
            vm((8, D), F32), vm((8, D), F32), vm((N, D), F32), vm((Q, 8, D), F32), vm((Z, 8, D), F32), vm((N, D), BF), vm((N, D), BF),
            DMA((BACK_SEMS,)),
        ],
        compiler_params=pltpu.CompilerParams(collective_id=2, has_side_effects=True, vmem_limit_bytes=63 << 20),
        name="back",
    )(tok, normed, q_, k_, v_, probs, mixed, wq, wk, wv, wo, resid, gresid, glow, gu, gd, down, ffs, cot, g1, b1, db)


def chip_device(Q, Z, tokens, memory, compressed, valid_counts, attention_norm_gain, attention_norm_bias,
                query_projection, key_projection, value_projection, out_weight, feedforward_norm_gain,
                feedforward_norm_bias, up_weight, up_bias, down_weight, down_bias, squeeze_weight, cotangent):
    B, R, D = tokens.shape
    H = query_projection.shape[1]
    FL = up_weight.shape[1]
    E = FL // (2 * Q)
    (tok_all, normed, q_, k_, v_, probs, mixed, wqg, wkg, wvg, wog, resid, g_resid, g_low, up_low, down_g_low, down,
     ff_small, o_nm, o_nc) = front(
        Q, Z, compressed, memory, tokens, cotangent, query_projection, key_projection, value_projection, out_weight,
        up_weight, down_weight, up_bias.reshape(2 * Q, 1, E), jnp.broadcast_to(valid_counts[:, None, None], (B, 8, 128)),
        squeeze_weight, attention_norm_gain.reshape(1, D), attention_norm_bias.reshape(1, D),
        feedforward_norm_gain.reshape(1, D), feedforward_norm_bias.reshape(1, D),
    )
    aw, ago, afu, afd, aub, small, o_out, o_tg = back(
        Q, Z, B, tok_all, normed, q_, k_, v_, probs, mixed, wqg, wkg, wvg, wog, resid, g_resid, g_low, up_low, down_g_low, down,
        ff_small, cotangent, attention_norm_gain.reshape(1, D), attention_norm_bias.reshape(1, D), down_bias.reshape(1, D),
    )
    aw = aw.astype(F32)
    return (
        o_out, o_tg.astype(F32), small[0], small[1], aw[:, 2 * H:], aw[:, :H], aw[:, H:2 * H], ago.astype(F32),
        small[2], small[3], afu.astype(F32), aub.reshape(FL), afd.astype(F32), small[4], o_nm, o_nc,
    )


def solution(mesh):
    in_specs = (
        P("dp", "mp", None),
        P("dp", "mp", None),
        P("dp", "mp", None),
        P("dp"),
        P(),
        P(),
        P(None, "mp"),
        P(None, "mp"),
        P(None, "mp"),
        P("mp", None),
        P(),
        P(),
        P(None, "mp"),
        P("mp"),
        P("mp", None),
        P(),
        P(),
        P("dp", "mp", None),
    )
    out_specs = (
        P("dp", "mp", None),
        P("dp", "mp", None),
        P(),
        P(),
        P(None, "mp"),
        P(None, "mp"),
        P(None, "mp"),
        P("mp", None),
        P(),
        P(),
        P(None, "mp"),
        P("mp"),
        P("mp", None),
        P(),
        P("dp", "mp", None),
        P("dp", "mp", None),
    )
    Q, Z = mesh.shape["dp"] // 2, mesh.shape["mp"]

    def per_device(*args):
        B, R, D = args[0].shape
        H, FL = args[6].shape[1], args[12].shape[1]
        whole = Q == 4 and B == 2 and 2 * B == Z and H % HEAD_DIM == 0 and D % (16 * Q) == 0 and H % (16 * Q) == 0
        if whole and R % 32 == 0 and FL % (256 * Q) == 0:
            return chip_device(Q, Z, *args)
        return general_device(*args)

    return jax.shard_map(
        per_device, mesh=mesh, in_specs=in_specs, out_specs=out_specs, check_vma=False
    )
```

```python
import functools

import jax
import jax.numpy as jnp
from jax import lax
from jax.experimental import pallas as pl
from jax.experimental.pallas import tpu as pltpu
from jax.sharding import PartitionSpec as P

HEAD_DIM = 128
RATE = 3


def apply_layer_norm(rows):
    center = jnp.mean(rows, axis=-1, keepdims=True)
    centered = rows - center
    spread = jnp.mean(centered * centered, axis=-1, keepdims=True)
    inverse_deviation = lax.rsqrt(spread + 1e-05)
    return (centered * inverse_deviation, inverse_deviation)


def norm_backward_pass(input_gradient, standardized_rows, inverse_deviation, scale_factor):
    scaled_rows = input_gradient * scale_factor
    attention_norm_mean = jnp.mean(scaled_rows, axis=-1, keepdims=True)
    feedforward_norm_mean = jnp.mean(scaled_rows * standardized_rows, axis=-1, keepdims=True)
    return inverse_deviation * (
        scaled_rows - attention_norm_mean - standardized_rows * feedforward_norm_mean
    )


def squeeze_rows(old_comp, old_mem, fresh, valid_count, offset, own_rows, squeeze_weight):
    features = old_mem.shape[1]
    joined = jnp.concatenate([old_mem, fresh], axis=0)
    new_memory = lax.dynamic_slice_in_dim(joined, valid_count + offset, own_rows, 0)
    comp_len = old_comp.shape[0]
    evicted = valid_count // RATE
    first_row = evicted + offset
    window_start = jnp.maximum(first_row - comp_len, 0)
    padded = jnp.concatenate(
        [old_mem, jnp.zeros((RATE * own_rows, features), jnp.bfloat16)], axis=0
    )
    window = lax.dynamic_slice_in_dim(padded, window_start * RATE, RATE * own_rows, 0)
    squeezed = jnp.dot(
        window.reshape(own_rows, RATE * features),
        squeeze_weight,
        preferred_element_type=jnp.float32,
    ).astype(jnp.bfloat16)
    positions = first_row + jnp.arange(own_rows)
    from_old = jnp.take(old_comp, jnp.clip(positions, 0, comp_len - 1), axis=0)
    from_new = jnp.take(
        squeezed, jnp.clip(positions - comp_len - window_start, 0, own_rows - 1), axis=0
    )
    new_compressed = jnp.where((positions < comp_len)[:, None], from_old, from_new)
    return (new_memory, new_compressed)


def general_device(
    tokens,
    memory,
    compressed,
    valid_counts,
    attention_norm_gain,
    attention_norm_bias,
    query_projection,
    key_projection,
    value_projection,
    out_weight,
    feedforward_norm_gain,
    feedforward_norm_bias,
    up_weight,
    up_bias,
    down_weight,
    down_bias,
    squeeze_weight,
    cotangent,
):
    batch_segs, own_rows, features = tokens.shape
    offset = lax.axis_index("mp") * own_rows
    old_comp, old_mem, fresh = (
        lax.all_gather(compressed, "mp", axis=1, tiled=True),
        lax.all_gather(memory, "mp", axis=1, tiled=True),
        lax.all_gather(tokens, "mp", axis=1, tiled=True),
    )
    seg_len = fresh.shape[1]
    prior_rows = old_comp.shape[1] + old_mem.shape[1]
    context_tokens = jnp.concatenate([old_comp, old_mem, fresh], axis=1).astype(jnp.float32)
    ctx_len = context_tokens.shape[1]
    standardized_full, inverse_deviation_full = apply_layer_norm(context_tokens)
    normed_rows = (standardized_full * attention_norm_gain + attention_norm_bias).astype(
        jnp.bfloat16
    )
    token_rows_normed = normed_rows[:, prior_rows:]
    queries = jnp.einsum(
        "xhp,pj->xhj", token_rows_normed, query_projection, preferred_element_type=jnp.float32
    ).astype(jnp.bfloat16)
    key_rows = jnp.einsum(
        "xhp,pj->xhj", normed_rows, key_projection, preferred_element_type=jnp.float32
    ).astype(jnp.bfloat16)
    values = jnp.einsum(
        "xhp,pj->xhj", normed_rows, value_projection, preferred_element_type=jnp.float32
    ).astype(jnp.bfloat16)
    local_heads = query_projection.shape[1] // HEAD_DIM
    score_scale = HEAD_DIM ** (-0.5)

    def by_heads(matrix):
        return matrix.reshape(matrix.shape[0], matrix.shape[1], local_heads, HEAD_DIM)

    query_pos = jnp.arange(seg_len)[:, None]
    key_pos = jnp.arange(ctx_len)[None, :] - prior_rows
    allowed = (key_pos[None] < 0) | (key_pos <= query_pos)[None] & (
        key_pos[None] < valid_counts[:, None, None]
    )

    def scores_of(query_in, key_in):
        raw = (
            jnp.einsum(
                "gqhe,gkhe->ghqk",
                by_heads(query_in),
                by_heads(key_in),
                preferred_element_type=jnp.float32,
            )
            * score_scale
        )
        return jnp.where(allowed[:, None], raw, -1e30)

    scores = scores_of(queries, key_rows)
    peak_score = jnp.max(scores, axis=-1, keepdims=True)
    exponent = jnp.exp(scores - peak_score)
    exp_total = jnp.sum(exponent, axis=-1, keepdims=True)
    log_total = peak_score + jnp.log(exp_total)
    probs_low = (exponent / exp_total).astype(jnp.bfloat16)
    mixed_heads = jnp.einsum(
        "ghqk,gkhe->gqhe", probs_low, by_heads(values), preferred_element_type=jnp.float32
    ).astype(jnp.bfloat16)
    mixed_heads = mixed_heads.reshape(batch_segs, seg_len, local_heads * HEAD_DIM)
    partial_attn = jnp.einsum(
        "gsc,cd->gsd", mixed_heads, out_weight, preferred_element_type=jnp.float32
    )
    attention = lax.psum_scatter(partial_attn, "mp", scatter_dimension=1, tiled=True)
    residual_stream = tokens.astype(jnp.float32) + attention
    standardized_feedforward, inverse_deviation_feedforward = apply_layer_norm(residual_stream)
    feedforward_input = (
        standardized_feedforward * feedforward_norm_gain + feedforward_norm_bias
    ).astype(jnp.bfloat16)
    second_all = lax.all_gather(feedforward_input, "mp", axis=1, tiled=True)
    upper_in = (
        jnp.einsum("gsd,df->gsf", second_all, up_weight, preferred_element_type=jnp.float32)
        + up_bias
    )
    active, gelu_back = jax.vjp(jax.nn.gelu, upper_in)
    active_low = active.astype(jnp.bfloat16)
    partial_ffn = jnp.einsum(
        "gsf,fd->gsd", active_low, down_weight, preferred_element_type=jnp.float32
    )
    down_out = lax.psum_scatter(
        partial_ffn.astype(jnp.bfloat16), "mp", scatter_dimension=1, tiled=True
    ).astype(jnp.float32)
    output = (residual_stream + down_out + down_bias).astype(jnp.bfloat16)

    def update_one(comp_seg, mem_seg, fresh_seg, valid_count):
        return squeeze_rows(
            comp_seg, mem_seg, fresh_seg, valid_count, offset, own_rows, squeeze_weight
        )

    new_memory, new_compressed = jax.vmap(update_one)(old_comp, old_mem, fresh, valid_counts)
    output_gradient = cotangent.astype(jnp.float32)
    down_bias_grad = jnp.sum(output_gradient, axis=(0, 1))
    grad_all = lax.all_gather(cotangent, "mp", axis=1, tiled=True)
    down_weight_grad = jnp.einsum(
        "gsf,gsd->fd", active_low, grad_all, preferred_element_type=jnp.float32
    )
    grad_active = jnp.einsum(
        "gsd,fd->gsf", grad_all, down_weight, preferred_element_type=jnp.float32
    )
    grad_upper = gelu_back(grad_active)[0].astype(jnp.bfloat16)
    up_weight_grad = jnp.einsum(
        "gsd,gsf->df", second_all, grad_upper, preferred_element_type=jnp.float32
    )
    up_bias_grad = jnp.sum(grad_upper.astype(jnp.float32), axis=(0, 1))
    partial_second = jnp.einsum(
        "gsf,df->gsd", grad_upper, up_weight, preferred_element_type=jnp.float32
    )
    feedforward_gradient = lax.psum_scatter(partial_second, "mp", scatter_dimension=1, tiled=True)
    feedforward_gain_gradient = jnp.sum(
        feedforward_gradient * standardized_feedforward, axis=(0, 1)
    )
    second_bias_grad = jnp.sum(feedforward_gradient, axis=(0, 1))
    residual_gradient = output_gradient + norm_backward_pass(
        feedforward_gradient,
        standardized_feedforward,
        inverse_deviation_feedforward,
        feedforward_norm_gain,
    )
    grad_resid_all = lax.all_gather(
        residual_gradient.astype(jnp.bfloat16), "mp", axis=1, tiled=True
    )
    out_weight_grad = jnp.einsum(
        "gsc,gsd->cd", mixed_heads, grad_resid_all, preferred_element_type=jnp.float32
    )
    grad_mixed = jnp.einsum(
        "gsd,cd->gsc", grad_resid_all, out_weight, preferred_element_type=jnp.float32
    ).astype(jnp.bfloat16)
    probs_again = jnp.exp(scores_of(queries, key_rows) - log_total)
    grad_probs = jnp.einsum(
        "gqhe,gkhe->ghqk",
        by_heads(grad_mixed),
        by_heads(values),
        preferred_element_type=jnp.float32,
    )
    row_dot = jnp.sum(probs_again * grad_probs, axis=-1, keepdims=True)
    grad_scores = (probs_again * (grad_probs - row_dot)).astype(jnp.bfloat16)
    query_gradient = (
        score_scale
        * jnp.einsum(
            "ghqk,gkhe->gqhe", grad_scores, by_heads(key_rows), preferred_element_type=jnp.float32
        )
    ).astype(jnp.bfloat16)
    key_gradient = (
        score_scale
        * jnp.einsum(
            "ghqk,gqhe->gkhe", grad_scores, by_heads(queries), preferred_element_type=jnp.float32
        )
    ).astype(jnp.bfloat16)
    value_gradient = jnp.einsum(
        "ghqk,gqhe->gkhe",
        probs_again.astype(jnp.bfloat16),
        by_heads(grad_mixed),
        preferred_element_type=jnp.float32,
    ).astype(jnp.bfloat16)
    query_gradient = query_gradient.reshape(batch_segs, seg_len, -1)
    key_gradient = key_gradient.reshape(batch_segs, ctx_len, -1)
    value_gradient = value_gradient.reshape(batch_segs, ctx_len, -1)
    query_weight_grad = jnp.einsum(
        "nja,njr->ar", token_rows_normed, query_gradient, preferred_element_type=jnp.float32
    )
    key_weight_grad = jnp.einsum(
        "nja,njr->ar", normed_rows, key_gradient, preferred_element_type=jnp.float32
    )
    value_weight_grad = jnp.einsum(
        "nja,njr->ar", normed_rows, value_gradient, preferred_element_type=jnp.float32
    )
    partial_normed = jnp.einsum(
        "xmo,qo->xmq", key_gradient, key_projection, preferred_element_type=jnp.float32
    )
    partial_normed = partial_normed + jnp.einsum(
        "xmo,qo->xmq", value_gradient, value_projection, preferred_element_type=jnp.float32
    )
    partial_normed = partial_normed.at[:, prior_rows:].add(
        jnp.einsum(
            "xmo,qo->xmq", query_gradient, query_projection, preferred_element_type=jnp.float32
        )
    )
    partial_normed = partial_normed.reshape(batch_segs, 3, seg_len, features)
    normed_gradient = lax.psum_scatter(
        partial_normed.astype(jnp.bfloat16), "mp", scatter_dimension=2, tiled=True
    ).astype(jnp.float32)
    segment_context = jnp.stack([compressed, memory, tokens], axis=1).astype(jnp.float32)
    standardized_segment, inverse_deviation_segment = apply_layer_norm(segment_context)
    attention_gain_gradient = jnp.sum(normed_gradient * standardized_segment, axis=(0, 1, 2))
    first_bias_grad = jnp.sum(normed_gradient, axis=(0, 1, 2))
    tokens_grad = residual_gradient + norm_backward_pass(
        normed_gradient[:, 2],
        standardized_segment[:, 2],
        inverse_deviation_segment[:, 2],
        attention_norm_gain,
    )
    summed = (
        lax.psum(query_weight_grad.astype(jnp.bfloat16), "dp").astype(jnp.float32),
        lax.psum(key_weight_grad.astype(jnp.bfloat16), "dp").astype(jnp.float32),
        lax.psum(value_weight_grad.astype(jnp.bfloat16), "dp").astype(jnp.float32),
        lax.psum(out_weight_grad.astype(jnp.bfloat16), "dp").astype(jnp.float32),
        lax.psum(up_weight_grad.astype(jnp.bfloat16), "dp").astype(jnp.float32),
        lax.psum(up_bias_grad.astype(jnp.bfloat16), "dp").astype(jnp.float32),
        lax.psum(down_weight_grad.astype(jnp.bfloat16), "dp").astype(jnp.float32),
    )
    norms = lax.psum(
        (
            attention_gain_gradient,
            first_bias_grad,
            feedforward_gain_gradient,
            second_bias_grad,
            down_bias_grad,
        ),
        ("dp", "mp"),
    )
    return (
        output,
        tokens_grad,
        norms[0],
        norms[1],
        summed[0],
        summed[1],
        summed[2],
        summed[3],
        norms[2],
        norms[3],
        summed[4],
        summed[5],
        summed[6],
        norms[4],
        new_memory,
        new_compressed,
    )


BF = jnp.bfloat16
F32 = jnp.float32
MESH = pl.DeviceIdType.MESH
ANY = pl.BlockSpec(memory_space=pl.ANY)
VM = pl.BlockSpec(memory_space=pltpu.VMEM)
DMA = pltpu.SemaphoreType.DMA


def sds(shape, dtype):
    return jax.ShapeDtypeStruct(shape, dtype)


def where_am_i(chips, depth):
    dp = lax.axis_index("dp")
    return dp, lax.rem(dp, 2), dp // 2, lax.axis_index("mp")


def rcopy(src, dst, send, recv, device):
    return pltpu.make_async_remote_copy(
        src_ref=src,
        dst_ref=dst,
        send_sem=send,
        recv_sem=recv,
        device_id=device,
        device_id_type=MESH,
    )


def lcopy(src, dst, sem):
    return pltpu.make_async_copy(src, dst, sem)


def enter(partners):
    barrier = pltpu.get_barrier_semaphore()
    for p in partners:
        pl.semaphore_signal(barrier, inc=1, device_id=p, device_id_type=MESH)
    pl.semaphore_wait(barrier, len(partners))


def across(q, k):
    if k == 0:
        return q
    if k == 1:
        return q + 1 - 2 * lax.rem(q, 2)
    if k == 2:
        return lax.rem(q + 2, 4)
    return 3 - q


def layer_norm_rows(rows):
    center = jnp.mean(rows, axis=-1, keepdims=True)
    centered = rows - center
    spread = jnp.mean(centered * centered, axis=-1, keepdims=True)
    inv = lax.rsqrt(spread + 1e-05)
    return centered * inv, inv


class Slots:
    def __init__(self, ref):
        self.ref = ref
        self.used = 0

    def take(self, *shape):
        base = self.used
        size = 1
        for n in shape:
            size *= n
        self.used += size

        def at(*index):
            flat = 0
            for n, i in zip(shape, index):
                flat = flat * n + i
            return self.ref.at[base + flat]

        return at


def nt_dot(a, b):
    return lax.dot_general(a, b, (((1,), (1,)), ((), ())), preferred_element_type=F32)


def tn_dot(a, b):
    return lax.dot_general(a, b, (((0,), (0,)), ((), ())), preferred_element_type=F32)


def nn_dot(a, b):
    return jnp.dot(a, b, preferred_element_type=F32)


def one_hot(shape, offset):
    row = lax.broadcasted_iota(jnp.int32, shape, 0)
    col = lax.broadcasted_iota(jnp.int32, shape, 1)
    return jnp.where(col == row + offset, 1.0, 0.0).astype(BF)


class PlaneSum:
    def __init__(self, al, peer, blk, rows, h, g):
        self.peer, self.blk, self.half, self.rows, self.h, self.g = peer, blk, rows // 2, rows, h, g
        self.hs, self.hr, self.gs, self.gr = al.take(2), al.take(2), al.take(2), al.take(2)

    def h_x(self, i):
        return rcopy(self.blk(3, i * self.half, self.half), self.h.at[i], self.hs(i), self.hr(i), self.peer(i + 1))

    def g_x(self, i):
        return rcopy(self.blk(i + 1, 0, self.rows), self.g.at[i], self.gs(i), self.gr(i), self.peer(i + 1))

    def start(self):
        for i in range(2):
            self.h_x(i).start()

    def middle(self):
        for i in range(2):
            self.h_x(i).wait_recv()
            mine = self.blk(2 - i, i * self.half, self.half)
            mine[...] = (mine[...].astype(F32) + self.h[i].astype(F32)).astype(BF)
            self.g_x(1 - i).start()

    def arrive(self):
        for i in range(2):
            self.g_x(i).wait_recv()

    def total(self):
        self.arrive()
        own = self.blk(0, 0, self.rows)
        return own[...].astype(F32) + (self.g[0].astype(F32) + self.g[1].astype(F32))

    def drain(self):
        for i in range(2):
            self.h_x(i).wait_send()
            self.g_x(i).wait_send()


class PlaneGather:
    def __init__(self, al, peer, sib, loc, rows, own=None):
        self.peer, self.sib, self.loc, self.half, self.rows = peer, sib, loc, rows // 2, rows
        self.own = own
        self.as_, self.ar, self.hs, self.hr = al.take(2), al.take(2), al.take(2), al.take(2)
        self.fs, self.fr = al.take(4), al.take(4)

    def a_x(self, i, k=0):
        src = self.loc(0, 0, self.rows) if self.own is None else self.own
        return rcopy(src, self.loc(k, 0, self.rows), self.as_(i), self.ar(i), self.peer(i + 1))

    def h_x(self, i, k=None):
        k = 2 - (1 - i) if k is None else k
        rows = self.loc(k, i * self.half, self.half)
        return rcopy(rows, rows, self.hs(i), self.hr(i), self.peer(2 - i))

    def f_x(self, k, other=None):
        src = self.loc(k, 0, self.rows)
        if k == 0 and self.own is not None:
            src = self.own
        dst = self.loc(k, 0, self.rows) if other is None else other(k, 0, self.rows)
        return rcopy(src, dst, self.fs(k), self.fr(k), self.sib)

    def start(self):
        for i in range(2):
            self.a_x(i).start()
        self.f_x(0).start()

    def middle(self):
        for i in range(2):
            rcopy(self.loc(i + 1, 0, self.rows), self.loc(i + 1, 0, self.rows), self.as_(i), self.ar(i), self.peer(1)).wait_recv()
            self.h_x(i).start()
            self.f_x(i + 1).start()

    def last(self):
        for i in range(2):
            self.h_x(i, 3).wait_recv()
        self.f_x(3).start()

    def drain(self):
        for i in range(2):
            self.a_x(i).wait_send()
            self.h_x(i).wait_send()
        for k in range(4):
            self.f_x(k).wait_send()

    def arrivals(self, other):
        for k in range(4):
            rcopy(other(k, 0, self.rows), other(k, 0, self.rows), self.fs(k), self.fr(k), self.sib).wait_recv()


FRONT_SEMS = 400


def front_kernel(Q, Z, comp, mem, tok, cot, wq, wk, wv, wo, up, down, ub, vc, sq, g1, b1, g2, b2,
                 tok_o, normed_o, q_o, k_o, v_o, probs_o, mixed_o, wq_o, wk_o, wv_o, wo_o,
                 resid_o, gresid_o, glow_o, gu_o, gd_o, down_o, small_o, nm_o, nc_o,
                 ctx, normed, wqs, wks, wvs, wos, qs, ks, vs, probs, mixed, phalf, got, resid, sec, cots, ups, downs,
                 ubs, vco, act, gup, gbuf, got1, gh, gg, low, nms, ncs, gus, gds, dns, sems):
    dp, c, q, z = where_am_i(Q, Z)
    sib = dp + 1 - 2 * c
    partners = [(sib, z)]
    for r in range(1, Z):
        for d in (dp, sib):
            partners.append((d, lax.rem(z + r, Z)))
    for k in range(1, Q):
        partners.append((2 * across(q, k) + c, z))
    enter(partners)
    B, R, D = tok.shape
    H = wq.shape[1]
    QR = D // Q
    OR = H // Q
    HR = R // 2
    S = R * Z
    N = S // 2
    E = up.shape[1] // (2 * Q)
    heads = B * H // HEAD_DIM
    mine = c == z // B
    jz = lax.rem(z, B)
    al = Slots(sems)

    def peer(k):
        return (2 * across(q, k) + c, z)

    wins = [wq, wk, wv, wo]
    wss = [wqs, wks, wvs, wos]

    def piece(a):
        if a < 3:
            return wins[a].at[pl.ds(q * QR, QR), :]
        return wo.at[pl.ds(q * OR, OR), :]

    def place(a, j, qq):
        if a < 3:
            return wss[a].at[pl.ds(pl.multiple_of(qq * QR, QR), QR), pl.ds(pl.multiple_of(j * H, H), H)]
        return wos.at[pl.ds(pl.multiple_of(j * H + qq * OR, OR), OR), :]

    def place_whole(a, j):
        if a < 3:
            return wss[a].at[:, pl.ds(pl.multiple_of(j * H, H), H)]
        return wos.at[pl.ds(pl.multiple_of(j * H, H), H), :]

    ws, wr = al.take(4, Z - 1), al.take(4, B)
    ps, pr = al.take(4, B, Q - 1), al.take(4, B, Q - 1)
    wl = al.take(4)

    def w_z(a, r):
        return rcopy(piece(a), place(a, jz, q), ws(a, r - 1), wr(a, jz), (dp, lax.rem(z + r, Z)))

    def w_arrive(a, j):
        return rcopy(place(a, j, q), place(a, j, q), ws(a, 0), wr(a, j), (dp, z))

    def w_p(a, j, k, qq):
        return rcopy(place(a, j, qq), place(a, j, qq), ps(a, j, k - 1), pr(a, j, k - 1), peer(k))

    def w_l(a):
        return lcopy(wins[a], place_whole(a, jz), wl(a))

    acts = [comp, mem, tok]
    cs, cr = al.take(3, B, 2), al.take(3, Z)
    fs, fr = al.take(3, Z), al.take(3, Z)
    cl = al.take(3)

    def c_rows(t, zs):
        return ctx.at[t, pl.ds(pl.multiple_of(zs * R, R), R), :]

    def c_half(t, zs, h):
        return ctx.at[t, pl.ds(pl.multiple_of(zs * R + HR * h, HR), HR), :]

    def c_l(t):
        return lcopy(acts[t].at[jz], c_rows(t, z), cl(t))

    def c_sib(t):
        return rcopy(acts[t].at[jz], c_rows(t, z), fs(t, z), fr(t, z), (sib, z))

    def c_z(t, s, h):
        return rcopy(acts[t].at[s, pl.ds(HR * h, HR), :], c_half(t, z, h), cs(t, s, h), cr(t, z), (2 * q + h, B * c + s))

    def c_arrive(t, zs):
        return rcopy(c_half(t, zs, c), c_half(t, zs, c), cs(t, 0, 0), cr(t, zs), (dp, z))

    def c_fwd(t, zs, half):
        return rcopy(c_half(t, zs, half), c_half(t, zs, half), fs(t, zs), fr(t, zs), (sib, z))

    us, ur, ul = al.take(Z - 1), al.take(Z - 1), al.take(1)
    vs_, vr_ = al.take(1), al.take(1)

    def u_z(r):
        return rcopy(ub.at[dp], ubs.at[r], us(r - 1), ur(r - 1), (dp, lax.rem(z + r, Z)))

    u_l = lcopy(ub.at[dp], ubs.at[0], ul(0))
    v_s = rcopy(vc, vco, vs_(0), vr_(0), (sib, z))

    ts, tr, tl = al.take(B), al.take(B), al.take(1)

    def dev(k, core):
        return 2 * across(q, k) + core

    def t_rows(d, i):
        return cots.at[pl.ds(pl.multiple_of(d * N + i * R, R), R), :]

    def t_z(s):
        to = 2 * q + z // B
        return rcopy(cot.at[s], t_rows(to, jz), ts(s), tr(jz), (to, B * c + s))

    def t_l():
        return lcopy(cot.at[jz], t_rows(dp, jz), tl(0))

    def t_arrive(i):
        return rcopy(t_rows(dp, i), t_rows(dp, i), ts(0), tr(i), (dp, z))

    def rows_at(ref, core):
        def loc(k, lo, n):
            return ref.at[pl.ds(pl.multiple_of(dev(k, core) * N + lo, n), n), :]
        return loc

    tgat = PlaneGather(al, peer, (sib, z), rows_at(cots, c), N)
    agat = PlaneGather(al, peer, (sib, z), rows_at(sec, c), N)

    xs, xr_, xl = al.take(2, Z), al.take(2, Z), al.take(2)

    def x_z(i, r):
        if i == 0:
            return rcopy(up.at[:, pl.ds(pl.multiple_of(dp * E, E), E)], ups.at[:, pl.ds(r * E, E)], xs(0, r), xr_(0, r),
                         (dp, lax.rem(z + r, Z)))
        return rcopy(down.at[pl.ds(pl.multiple_of(dp * E, E), E), :], downs.at[pl.ds(r * E, E), :], xs(1, r), xr_(1, r),
                     (dp, lax.rem(z + r, Z)))

    x_l = [lcopy(up.at[:, pl.ds(pl.multiple_of(dp * E, E), E)], ups.at[:, pl.ds(0, E)], xl(0)),
           lcopy(down.at[pl.ds(pl.multiple_of(dp * E, E), E), :], downs.at[pl.ds(0, E), :], xl(1))]

    @pl.when(mine)
    def _():
        for a in range(4):
            for r in range(1, Z):
                w_z(a, r).start()
        for a in range(4):
            w_l(a).start()
        for t in range(3):
            c_l(t).start()
            c_sib(t).start()
    for r in range(1, Z):
        u_z(r).start()
    v_s.start()
    u_l.start()
    for x in x_l:
        x.start()
    for j in range(B):
        @pl.when(B * c + j != z)
        def _():
            for a in range(4):
                w_arrive(a, j).wait_recv()
                for k in range(1, Q):
                    w_p(a, j, k, q).start()
    for s in range(B):
        @pl.when(B * c + s != z)
        def _():
            for t in range(3):
                for h in range(2):
                    c_z(t, s, h).start()

    def norm_block(t, zs):
        at = pl.ds(pl.multiple_of(zs * R, R), R)
        to = pl.ds(pl.multiple_of(t * S + zs * R, R), R)
        xhat, _ = layer_norm_rows(ctx[t, at, :].astype(F32))
        normed[to, :] = (xhat * g1[...] + b1[...]).astype(BF)

    @pl.when(mine)
    def _():
        for t in range(3):
            c_l(t).wait()

    @pl.when(jnp.logical_not(mine))
    def _():
        for t in range(3):
            rcopy(c_rows(t, z), c_rows(t, z), fs(t, z), fr(t, z), (sib, z)).wait_recv()

    def norm_own(t, carry):
        norm_block(t, z)
        return carry

    lax.fori_loop(0, 3, norm_own, 0)
    for r in range(1, Z):
        zs = lax.rem(z + r, Z)
        for t in range(3):
            c_arrive(t, zs).wait_recv()
            c_fwd(t, zs, c).start()
    for s in range(B):
        @pl.when(B * c + s != z)
        def _():
            for t in range(3):
                for h in range(2):
                    c_z(t, s, h).wait_send()
    for s in range(B):
        here = (B * c + s == z) & mine

        @pl.when(here)
        def _():
            t_l().start()

        @pl.when(jnp.logical_not(here))
        def _():
            t_z(s).start()
    for r in range(1, Z):
        zs = lax.rem(z + r, Z)
        for t in range(3):
            c_fwd(t, zs, 1 - c).wait_recv()

        def norm_one(t, carry, zs=zs):
            norm_block(t, zs)
            return carry

        lax.fori_loop(0, 3, norm_one, 0)
    outs = al.take(16)
    copies = []

    def leave(src, dst):
        cp = lcopy(src, dst, outs(len(copies)))
        cp.start()
        copies.append(cp)

    leave(normed, normed_o)
    leave(ctx.at[2], tok_o)
    for j in range(B):
        @pl.when(B * c + j != z)
        def _():
            for a in range(4):
                for k in range(1, Q):
                    w_p(a, j, k, across(q, k)).wait_recv()

    @pl.when(mine)
    def _():
        for a in range(4):
            w_l(a).wait()
    for a in range(4):
        leave(wss[a], (wq_o, wk_o, wv_o, wo_o)[a])

    T = 256

    def project(i, carry):
        at = pl.ds(pl.multiple_of(i * T, T), T)
        ks[at, :] = nn_dot(normed[at, :], wks[...]).astype(BF)
        vs[at, :] = nn_dot(normed[at, :], wvs[...]).astype(BF)
        return carry

    lax.fori_loop(0, 3 * S // T, project, 0)

    def project_q(i, carry):
        at = pl.ds(pl.multiple_of(i * T, T), T)
        qs[at, :] = nn_dot(normed[pl.ds(pl.multiple_of(2 * S + i * T, T), T), :], wqs[...]).astype(BF)
        return carry

    lax.fori_loop(0, S // T, project_q, 0)
    for r in range(1, Z):
        x_z(0, r).start()
    leave(qs, q_o)
    leave(ks, k_o)
    leave(vs, v_o)

    v_s.wait()
    counts = jnp.where(mine, vc[jz], vco[jz])
    count = counts[0:1, 0:1]
    scale = HEAD_DIM ** (-0.5)
    P2 = 2 * S
    pouts = al.take(2, heads)

    def attend(half, tag):
        r0 = pl.multiple_of(half * N, N)

        def head(h, carry):
            hd = pl.ds(pl.multiple_of(h * HEAD_DIM, HEAD_DIM), HEAD_DIM)
            qh = qs[pl.ds(r0, N), hd]
            s1 = nt_dot(qh, ks[pl.ds(0, P2), hd])
            s2 = nt_dot(qh, ks[pl.ds(P2, S), hd])
            row = lax.broadcasted_iota(jnp.int32, (N, S), 0) + half * N
            col = lax.broadcasted_iota(jnp.int32, (N, S), 1)
            s2 = jnp.where((col <= row) & (col < count), s2, -1e30)
            top = jnp.maximum(jnp.max(s1, axis=-1, keepdims=True), jnp.max(s2, axis=-1, keepdims=True))
            p1 = jnp.exp((s1 - top) * scale)
            p2 = jnp.exp((s2 - top) * scale)
            inv = 1.0 / (jnp.sum(p1, axis=-1, keepdims=True) + jnp.sum(p2, axis=-1, keepdims=True))
            p1 = (p1 * inv).astype(BF)
            p2 = (p2 * inv).astype(BF)
            probs[h, pl.ds(r0, N), pl.ds(0, P2)] = p1
            probs[h, pl.ds(r0, N), pl.ds(P2, S)] = p2
            lcopy(probs.at[h, pl.ds(r0, N), :], probs_o.at[h, pl.ds(r0, N), :], pouts(tag, h)).start()
            mix = nn_dot(p1, vs[pl.ds(0, P2), hd]) + nn_dot(p2, vs[pl.ds(P2, S), hd])
            mixed[pl.ds(r0, N), hd] = mix.astype(BF)
            return carry

        lax.fori_loop(0, heads, head, 0)

    hs, hr = al.take(1), al.take(1)
    h_x = rcopy(phalf, got, hs(0), hr(0), (sib, z))
    attend(1 - c, 0)
    phalf[...] = nn_dot(mixed[pl.ds(pl.multiple_of((1 - c) * N, N), N), :], wos[...])
    h_x.start()
    for r in range(1, Z):
        x_z(1, r).start()
    for i in range(B):
        @pl.when(jnp.logical_not((B * c + i == z) & mine))
        def _():
            t_arrive(i).wait_recv()

        @pl.when((B * c + i == z) & mine)
        def _():
            t_l().wait()
    tgat.start()
    attend(c, 1)
    leave(mixed, mixed_o)
    own_part = nn_dot(mixed[pl.ds(pl.multiple_of(c * N, N), N), :], wos[...])
    h_x.wait_recv()
    resid[...] = ctx[2, pl.ds(pl.multiple_of(c * N, N), N), :].astype(F32) + (own_part + got[...])
    leave(resid, resid_o)
    xhat2, _ = layer_norm_rows(resid[...])
    sec[pl.ds(pl.multiple_of(dp * N, N), N), :] = (xhat2 * g2[...] + b2[...]).astype(BF)

    agat.start()
    sqc = al.take(RATE)
    sqs = [dns.at[pl.ds(0, D), :], dns.at[pl.ds(D, D), :], gbuf.at[pl.ds(D, D), :]]
    sq_x = [lcopy(sq.at[pl.ds(r * D, D), :], sqs[r], sqc(r)) for r in range(RATE)]
    for x in sq_x:
        x.start()
    ss, sr = al.take(Q), al.take(Q)

    def s_x(k):
        return rcopy(rows_at(gbuf, 1 - c)(k, 0, N), got1.at[k], ss(k), sr(k), (sib, z))

    gsum = PlaneSum(al, peer, rows_at(gbuf, c), N, gh, gg)
    small_o[...] = jnp.zeros_like(small_o)

    def forward_block(b, bias_row):
        at = pl.ds(pl.multiple_of(b * N, N), N)
        x = nn_dot(sec[at, :], ups[...]) + bias_row
        ga = nt_dot(cots[at, :], downs[...])
        x2 = x * x
        root = 0.7978845608028654
        th = jnp.tanh(root * (x + 0.044715 * (x2 * x)))
        act[at, :] = (0.5 * x * (1.0 + th)).astype(BF)
        slope = 0.5 * (1.0 + th) + 0.5 * x * (1.0 - th * th) * (root * (1.0 + 0.134145 * x2))
        gu = (ga * slope).astype(BF)
        gup[at, :] = gu
        small_o[2:3, pl.ds(0, Z * E)] = small_o[2:3, pl.ds(0, Z * E)] + jnp.sum(gu.astype(F32), axis=0, keepdims=True)
        gbuf[at, :] = nt_dot(gu, ups[...]).astype(BF)
        return bias_row

    def feed(k, bias_row):
        lax.fori_loop(dev(k, 0), dev(k, 0) + 2, forward_block, bias_row)
        s_x(k).start()

    def combine(k):
        s_x(k).wait_recv()
        rows = rows_at(gbuf, c)(k, 0, N)
        rows[...] = (rows[...].astype(F32) + got1[k].astype(F32)).astype(BF)

    groups = S // RATE
    squeezed = None
    for r in range(RATE):
        sq_x[r].wait()
        row = lax.broadcasted_iota(jnp.int32, (ncs.shape[0], S), 0)
        col = lax.broadcasted_iota(jnp.int32, (ncs.shape[0], S), 1)
        pick = jnp.where((col == row * RATE + r) & (row < groups), 1.0, 0.0).astype(BF)
        picked = nn_dot(pick, ctx[1]).astype(BF)
        term = nn_dot(picked, sqs[r][...])
        squeezed = term if squeezed is None else squeezed + term
    ncs[...] = squeezed.astype(BF)
    shift = count + c * N
    new_mem = nn_dot(one_hot((N, S), shift), ctx[1]) + nn_dot(one_hot((N, S), shift - S), ctx[2])
    nms[...] = new_mem.astype(BF)
    third = lax.shift_right_logical(count * 21846, 16)
    shift = third + c * N
    new_comp = nn_dot(one_hot((N, S), shift), ctx[0]) + nn_dot(one_hot((N, ncs.shape[0]), shift - S), ncs[...])
    ncs[pl.ds(0, N), :] = new_comp.astype(BF)
    per = N // R
    ms, mr, ml = al.take(2, 2), al.take(2, B), al.take(2)
    rows_in = [nms, ncs]
    rows_out = [nm_o, nc_o]

    def row_x(i, p):
        return rcopy(rows_in[i].at[pl.ds(p * R, R), :], rows_out[i].at[jz], ms(i, p), mr(i, jz), (2 * q + z // B, c * per + p))

    def row_l(i, p):
        return lcopy(rows_in[i].at[pl.ds(p * R, R), :], rows_out[i].at[jz], ml(i))

    tgat.middle()
    agat.middle()
    tgat.last()
    agat.last()
    for r in range(1, Z):
        u_z(r).wait()
        for i in range(2):
            x_z(i, r).wait_recv()
    u_l.wait()
    for x in x_l:
        x.wait()
    tgat.arrivals(rows_at(cots, 1 - c))
    agat.arrivals(rows_at(sec, 1 - c))
    for p in range(per):
        here = (c * per + p == z) & mine

        @pl.when(here)
        def _():
            for i in range(2):
                row_l(i, p).start()

        @pl.when(jnp.logical_not(here))
        def _():
            for i in range(2):
                row_x(i, p).start()

    bias = jnp.concatenate([ubs[r] for r in range(Z)], axis=1)
    feed(3, bias)
    feed(1, bias)
    combine(3)
    gsum.start()
    feed(2, bias)
    combine(1)
    feed(0, bias)
    combine(2)
    gsum.middle()

    def up_grad(i, carry):
        at = pl.ds(pl.multiple_of(i * T, T), T)
        gus[at, :] = tn_dot(sec[:, at], gup[...]).astype(BF)
        return carry

    lax.fori_loop(0, D // T, up_grad, 0)
    leave(gus, gu_o)

    def down_grad(i, carry):
        at = pl.ds(pl.multiple_of(i * T, T), T)
        gds[at, :] = tn_dot(act[:, at], cots[...]).astype(BF)
        return carry

    lax.fori_loop(0, Z * E // T, down_grad, 0)
    leave(gds, gd_o)

    def down_rows(b, carry):
        at = pl.ds(pl.multiple_of(b * N, N), N)
        dns[at, :] = nn_dot(act[at, :], downs[...]).astype(BF)
        return carry

    lax.fori_loop(0, 2 * Q, down_rows, 0)
    leave(dns, down_o)

    combine(0)
    gsum.arrive()
    C = 64

    def back_rows(i, carry):
        at = pl.ds(pl.multiple_of(i * C, C), C)
        own = pl.ds(pl.multiple_of(dp * N + i * C, C), C)
        gs = gbuf[own, :].astype(F32) + (gg[0, at, :].astype(F32) + gg[1, at, :].astype(F32))
        xhat, inv = layer_norm_rows(resid[at, :])
        small_o[0:1, :] = small_o[0:1, :] + jnp.sum(gs * xhat, axis=0, keepdims=True)
        small_o[1:2, :] = small_o[1:2, :] + jnp.sum(gs, axis=0, keepdims=True)
        e = gs * g2[...]
        m1 = jnp.mean(e, axis=-1, keepdims=True)
        m2 = jnp.mean(e * xhat, axis=-1, keepdims=True)
        gr = cots[own, :].astype(F32) + inv * (e - m1 - xhat * m2)
        got[at, :] = gr
        low[at, :] = gr.astype(BF)
        return carry

    lax.fori_loop(0, N // C, back_rows, 0)
    leave(got, gresid_o)
    ls_, lr_, ll_ = al.take(1), al.take(1), al.take(1)
    mine_rows = glow_o.at[pl.ds(pl.multiple_of(c * N, N), N), :]
    far = rcopy(low, mine_rows, ls_(0), lr_(0), (sib, z))
    near = lcopy(low, mine_rows, ll_(0))
    far.start()
    near.start()

    for cp in copies:
        cp.wait()
    for h in range(heads):
        for half, tag in ((1 - c, 0), (c, 1)):
            rows = pl.ds(pl.multiple_of(half * N, N), N)
            lcopy(probs.at[h, rows, :], probs_o.at[h, rows, :], pouts(tag, h)).wait()

    @pl.when(mine)
    def _():
        for a in range(4):
            for r in range(1, Z):
                w_z(a, r).wait_send()
        for t in range(3):
            c_sib(t).wait_send()
    for j in range(B):
        @pl.when(B * c + j != z)
        def _():
            for a in range(4):
                for k in range(1, Q):
                    w_p(a, j, k, q).wait_send()
    for r in range(1, Z):
        for t in range(3):
            c_fwd(t, lax.rem(z + r, Z), c).wait_send()
        for i in range(2):
            x_z(i, r).wait_send()
    for s in range(B):
        @pl.when(jnp.logical_not((B * c + s == z) & mine))
        def _():
            t_z(s).wait_send()
    for x in (tgat, agat, gsum):
        x.drain()
    for k in range(Q):
        s_x(k).wait_send()
    h_x.wait_send()
    for p in range(per):
        here = (c * per + p == z) & mine

        @pl.when(here)
        def _():
            for i in range(2):
                row_l(i, p).wait()

        @pl.when(jnp.logical_not(here))
        def _():
            for i in range(2):
                row_x(i, p).wait_send()
    for s in range(B):
        @pl.when(jnp.logical_not((B * c + s == z) & mine))
        def _():
            for i in range(2):
                rcopy(rows_out[i].at[s], rows_out[i].at[s], ms(i, 0), mr(i, s), (dp, z)).wait_recv()
    near.wait()
    far.wait()
    assert al.used <= FRONT_SEMS


def front(Q, Z, comp, mem, tok, cot, wq, wk, wv, wo, up, down, ub, vc, sq, g1, b1, g2, b2):
    B, R, D = tok.shape
    H = wq.shape[1]
    S = R * Z
    N = S // 2
    W = B * H
    heads = W // HEAD_DIM
    F = up.shape[1] // 2 // Q * Z
    rows = 2 * Q * N
    vm = pltpu.VMEM
    return pl.pallas_call(
        functools.partial(front_kernel, Q, Z),
        out_shape=[
            sds((S, D), BF), sds((3 * S, D), BF), sds((S, W), BF), sds((3 * S, W), BF), sds((3 * S, W), BF),
            sds((heads, S, 3 * S), BF), sds((S, W), BF), sds((D, W), BF), sds((D, W), BF), sds((D, W), BF), sds((W, D), BF),
            sds((N, D), F32), sds((N, D), F32), sds((S, D), BF), sds((D, F), BF), sds((F, D), BF), sds((rows, D), BF),
            sds((8, D), F32), sds((B, R, D), BF), sds((B, R, D), BF),
        ],
        in_specs=[ANY] * 11 + [VM] + [ANY] + [VM] * 4,
        out_specs=[ANY] * 17 + [VM] + [ANY] * 2,
        scratch_shapes=[
            vm((3, S, D), BF), vm((3 * S, D), BF), vm((D, W), BF), vm((D, W), BF), vm((D, W), BF), vm((W, D), BF),
            vm((S, W), BF), vm((3 * S, W), BF), vm((3 * S, W), BF), vm((heads, S, 3 * S), BF), vm((S, W), BF),
            vm((N, D), F32), vm((N, D), F32), vm((N, D), F32), vm((rows, D), BF), vm((rows, D), BF), vm((D, F), BF), vm((F, D), BF),
            vm((Z, 1, F // Z), F32), vm(vc.shape, jnp.int32), vm((rows, F), BF), vm((rows, F), BF), vm((rows, D), BF),
            vm((Q, N, D), BF), vm((2, N // 2, D), BF), vm((2, N, D), BF), vm((N, D), BF),
            vm((N, D), BF), vm((N, D), BF), vm((D, F), BF), vm((F, D), BF), vm((rows, D), BF),
            DMA((FRONT_SEMS,)),
        ],
        compiler_params=pltpu.CompilerParams(collective_id=1, has_side_effects=True, vmem_limit_bytes=63 << 20),
        name="front",
    )(comp, mem, tok, cot, wq, wk, wv, wo, up, down, ub, vc, sq, g1, b1, g2, b2)


BACK_SEMS = 300


def back_kernel(Q, Z, B, tok, normed_i, q_i, k_i, v_i, probs_i, mixed_i, wq_i, wk_i, wv_i, wo_i, resid_i, gresid_i, glow_i,
                gu, gd, down_i, ffs, cot, g1, b1, db,
                aw, ago, afu, afd, aub, small_o, out_o, tg_o,
                normed, qs, ks, vs, probs, mixed, wqs, wks, wvs, wos, toks, resid, gresid, glow, gms,
                xu, xd, xb, fus, fds, fbs, dgot, dnb, dh, dg, gkv, gqs, gos, gwb, gh, gg, oh, og,
                wdone, odone, zb, zo, wfin, ofin, ghalf, ggot, cots, arow, sums, sgot, srow, pgot, zgot, outs, tgs, sems):
    dp, c, q, z = where_am_i(Q, Z)
    sib = (dp + 1 - 2 * c, z)
    partners = [sib]
    for r in range(1, Z):
        for d in (dp, dp + 1 - 2 * c):
            partners.append((d, lax.rem(z + r, Z)))

    def peer(k):
        return (2 * across(q, k) + c, z)

    for k in range(1, Q):
        partners.append(peer(k))
    enter(partners)
    S, D = glow.shape
    N = S // 2
    W = qs.shape[1]
    H = W // B
    F = gd.shape[0]
    E = F // Z
    R = S // Z
    heads = W // HEAD_DIM
    hj = H // HEAD_DIM
    mine = c == z // B
    jz = lax.rem(z, B)
    al = Slots(sems)

    def dev(k, core):
        return 2 * across(q, k) + core

    def up_to_z(r):
        return (dp, lax.rem(z + Z - r, Z))

    xs, xr = al.take(3, Z), al.take(3, Z)

    def x_z(i, r):
        if i == 0:
            return rcopy(gu.at[:, pl.ds(r * E, E)], xu.at[r], xs(0, r), xr(0, r), up_to_z(r))
        if i == 1:
            return rcopy(gd.at[pl.ds(r * E, E), :], xd.at[r], xs(1, r), xr(1, r), up_to_z(r))
        return rcopy(ffs.at[pl.ds(2, 1), pl.ds(r * E, E)], xb.at[r], xs(2, r), xr(2, r), up_to_z(r))

    ss, sr = al.take(Q), al.take(Q)

    def d_x(k):
        return rcopy(down_i.at[pl.ds(pl.multiple_of(dev(k, 1 - c) * N, N), N), :], dgot.at[k], ss(k), sr(k), sib)

    ld = al.take(30)
    pairs = [(wo_i, wos), (glow_i, glow), (mixed_i, mixed), (probs_i, probs), (v_i, vs), (k_i, ks), (q_i, qs),
             (normed_i, normed), (wq_i, wqs), (wk_i, wks), (wv_i, wvs), (gresid_i, gresid), (resid_i, resid),
             (tok.at[pl.ds(pl.multiple_of(c * N, N), N), :], toks), (cot, cots),
             (gu.at[:, pl.ds(0, E)], xu.at[0]), (gd.at[pl.ds(0, E), :], xd.at[0])]
    pairs += [(down_i.at[pl.ds(pl.multiple_of(dev(k, c) * N, N), N), :], dnb.at[k]) for k in range(Q)]
    loads = [lcopy(src, dst, ld(i)) for i, (src, dst) in enumerate(pairs)]
    for x in loads[:3] + loads[17:]:
        x.start()
    for k in (3, 1, 2, 0):
        d_x(k).start()
    for x in loads[3:17]:
        x.start()
    for r in range(1, Z):
        for i in range(3):
            x_z(i, r).start()

    for x in loads[:3]:
        x.wait()
    T = 256

    def mix_rows(i, carry):
        at = pl.ds(pl.multiple_of(i * T, T), T)
        gms[at, :] = nt_dot(glow[at, :], wos[...]).astype(BF)
        gos[at, :] = tn_dot(mixed[:, at], glow[...]).astype(BF)
        return carry

    lax.fori_loop(0, S // T, mix_rows, 0)
    OR = H // Q
    M = D // Q

    def o_blk(j):
        def blk(k, lo, n):
            return gos.at[pl.ds(pl.multiple_of(j * H + across(q, k) * OR + lo, n), n), :]
        return blk

    def w_blk(j):
        def blk(k, lo, n):
            return gwb.at[j, pl.ds(pl.multiple_of(across(q, k) * M + lo, n), n), :]
        return blk

    osum = [PlaneSum(al, peer, o_blk(j), OR, oh.at[j], og.at[j]) for j in range(B)]
    wsum = [PlaneSum(al, peer, w_blk(j), M, gh.at[j], gg.at[j]) for j in range(B)]
    dsum = PlaneSum(al, peer, lambda k, lo, n: dnb.at[k, pl.ds(lo, n), :], N, dh, dg)
    for x in osum:
        x.start()
    for x in loads[17:]:
        x.wait()
    for k in (3, 1, 2, 0):
        d_x(k).wait_recv()
        dnb[k] = (dnb[k].astype(F32) + dgot[k].astype(F32)).astype(BF)
        if k == 3:
            dsum.start()
    sums[...] = jnp.zeros_like(sums)
    arow[...] = jnp.zeros_like(arow)
    scale = HEAD_DIM ** (-0.5)

    def head(h, hh):
        hd = pl.ds(h * HEAD_DIM, HEAD_DIM)
        ko = pl.ds(hh * HEAD_DIM, HEAD_DIM)
        vo = pl.ds(H + hh * HEAD_DIM, HEAD_DIM)
        p = probs[h]
        gm = gms[:, hd]
        gp = nt_dot(gm, vs[:, hd])
        delta = jnp.sum(gm.astype(F32) * mixed[:, hd].astype(F32), axis=-1, keepdims=True)
        gs = (p.astype(F32) * (gp - delta)).astype(BF)
        gqs[:, hd] = (scale * nn_dot(gs, ks[:, hd])).astype(BF)
        gkv[:, ko] = (scale * tn_dot(gs, qs[:, hd])).astype(BF)
        gkv[:, vo] = tn_dot(p, gm).astype(BF)

    def split_rows(v):
        hi = v.astype(BF)
        rest = v - hi.astype(F32)
        mid = rest.astype(BF)
        low = (rest - mid.astype(F32)).astype(BF)
        return jnp.concatenate([hi, mid, low, jnp.zeros((5, v.shape[1]), BF)], axis=0)

    def weights(j):
        js = pl.ds(j * H, H)

        def rows(i, carry):
            at = pl.ds(pl.multiple_of(i * T, T), T)
            kv = tn_dot(normed[:, at], gkv[...])
            gq = tn_dot(normed[pl.ds(2 * S, S), at], gqs[:, js])
            gwb[j, at, pl.ds(0, 2 * H)] = kv.astype(BF)
            gwb[j, at, pl.ds(2 * H, H)] = gq.astype(BF)
            t = (kv[:, :H] * wks[at, js].astype(F32) + kv[:, H:] * wvs[at, js].astype(F32) + gq * wqs[at, js].astype(F32))
            arow[at, :] = arow[at, :] + jnp.broadcast_to(jnp.sum(t, axis=-1, keepdims=True), (T, 128))
            return carry

        lax.fori_loop(0, D // T, rows, 0)
        wsum[j].start()
        skv = split_rows(jnp.sum(gkv[...].astype(F32), axis=0, keepdims=True))
        sq_ = split_rows(jnp.sum(gqs[:, js].astype(F32), axis=0, keepdims=True))
        b = nt_dot(skv[:, :H], wks[:, js]) + nt_dot(skv[:, H:], wvs[:, js]) + nt_dot(sq_, wqs[:, js])
        sums[1:2, :] = sums[1:2, :] + jnp.sum(b, axis=0, keepdims=True)

    for x in loads[3:7]:
        x.wait()
    for h in range(hj):
        head(h, h)
    for x in loads[7:11]:
        x.wait()
    H2 = pl.ds(2 * S, S)

    def token_rows(j, half):
        js = pl.ds(j * H, H)
        rows = pl.ds(pl.multiple_of(half * N, N), N)
        krows = pl.ds(pl.multiple_of(2 * S + half * N, N), N)
        return (nt_dot(gkv[krows, pl.ds(0, H)], wks[:, js]) + nt_dot(gkv[krows, pl.ds(H, H)], wvs[:, js])
                + nt_dot(gqs[rows, js], wqs[:, js]))

    for x in osum:
        x.middle()
    weights(0)
    dsum.middle()
    ghalf[...] = token_rows(0, 1 - c)
    srow[...] = token_rows(0, c)
    for h in range(hj, 2 * hj):
        head(h, h - hj)
    wsum[0].middle()
    weights(1)
    ghalf[...] = ghalf[...] + token_rows(1, 1 - c)
    ts_, tr_ = al.take(1), al.take(1)
    t_x = rcopy(ghalf, ggot, ts_(0), tr_(0), sib)
    t_x.start()
    srow[...] = srow[...] + token_rows(1, c)

    for x in loads[11:17]:
        x.wait()
    acol = jnp.swapaxes(arow[...], 0, 1)[0:1, :]
    bsum = sums[1:2, :]
    sums[0:1, :] = (acol - b1[...] * bsum) / g1[...]
    sums[2:3, :] = ffs[0:1, :]
    sums[3:4, :] = ffs[1:2, :]
    sums[4:5, :] = jnp.sum(cots[...].astype(F32), axis=(0, 1)).reshape(1, D)
    n1, n2 = al.take(1), al.take(1)
    v_x = rcopy(sums, sgot, n1(0), n2(0), sib)
    v_x.start()
    osums = []
    ozs, ozr = al.take(2, B), al.take(2, Z)

    def z_x(i, j):
        src, dst = ((wdone, zb), (odone, zo))[i]
        return rcopy(src.at[j], dst.at[z], ozs(i, j), ozr(i, z), (dp, B * c + j))

    def z_arrive(i, zz):
        dst = (zb, zo)[i]
        return rcopy(dst.at[zz], dst.at[zz], ozs(i, 0), ozr(i, zz), (dp, z))

    def to_plane(i, j):
        ((wdone, odone)[i])[j] = ((wsum, osum)[i])[j].total().astype(BF)

        @pl.when(B * c + j != z)
        def _():
            z_x(i, j).start()

    wsum[1].middle()
    for j in range(B):
        to_plane(1, j)
    t_x.wait_recv()
    C = 64

    def norm_rows(i, carry):
        at = pl.ds(pl.multiple_of(i * C, C), C)
        gn = srow[at, :] + ggot[at, :]
        xhat, inv = layer_norm_rows(toks[at, :].astype(F32))
        e = gn * g1[...]
        m1 = jnp.mean(e, axis=-1, keepdims=True)
        m2 = jnp.mean(e * xhat, axis=-1, keepdims=True)
        tgs[at, :] = (gresid[at, :] + inv * (e - m1 - xhat * m2)).astype(BF)
        return carry

    lax.fori_loop(0, N // C, norm_rows, 0)
    per = N // R
    rs, rr, rl = al.take(2, 2), al.take(2, B), al.take(2)
    rows_in = [tgs, outs]
    rows_out = [tg_o, out_o]

    def row_x(i, p):
        return rcopy(rows_in[i].at[pl.ds(p * R, R), :], rows_out[i].at[jz], rs(i, p), rr(i, jz), (2 * q + z // B, c * per + p))

    def row_l(i, p):
        return lcopy(rows_in[i].at[pl.ds(p * R, R), :], rows_out[i].at[jz], rl(i))

    def send_rows(i):
        for p in range(per):
            here = (c * per + p == z) & mine

            @pl.when(here)
            def _():
                row_l(i, p).start()

            @pl.when(jnp.logical_not(here))
            def _():
                row_x(i, p).start()

    send_rows(0)
    for r in range(1, Z):
        for i in range(3):
            x_z(i, r).wait_recv()
    fu, fd, fb = xu[0].astype(F32), xd[0].astype(F32), ffs[2:3, 0:E]
    for r in range(1, Z):
        fu = fu + xu[r].astype(F32)
        fd = fd + xd[r].astype(F32)
        fb = fb + xb[r]
    fus[...] = fu.astype(BF)
    fds[...] = fd.astype(BF)
    fbs[...] = fb

    def u_loc(core):
        def loc(k, lo, n):
            return afu.at[pl.ds(lo, n), pl.ds(pl.multiple_of(dev(k, core) * E, E), E)]
        return loc

    def d_loc(core):
        def loc(k, lo, n):
            return afd.at[pl.ds(pl.multiple_of(dev(k, core) * E + lo, n), n), :]
        return loc

    ugat = PlaneGather(al, peer, sib, u_loc(c), D, own=fus)
    dgat = PlaneGather(al, peer, sib, d_loc(c), E, own=fds)
    fl = al.take(3)
    f_l = [lcopy(fus, u_loc(c)(0, 0, D), fl(0)), lcopy(fds, d_loc(c)(0, 0, E), fl(1))]
    bs, br, bfs, bfr = al.take(Q), al.take(Q), al.take(Q), al.take(Q)

    def b_x(k):
        return rcopy(fbs, aub.at[dp], bs(k), br(k), peer(k))

    def b_arrive(k):
        return rcopy(aub.at[dev(k, c)], aub.at[dev(k, c)], bs(k), br(k), peer(k))

    def b_f(k):
        src = fbs if k == 0 else aub.at[dev(k, c)]
        return rcopy(src, aub.at[dev(k, c)], bfs(k), bfr(k), sib)

    b_l = lcopy(fbs, aub.at[dp], fl(2))
    ugat.start()
    dgat.start()
    for x in f_l:
        x.start()
    b_l.start()
    for k in range(1, Q):
        b_x(k).start()
    b_f(0).start()
    v_x.wait()
    srow[0:8, :] = sums[...] + sgot[...]
    pgot[q] = srow[0:8, :]
    vps, vpr, vzs, vzr = al.take(Q), al.take(Q), al.take(Z), al.take(Z)

    def vp_x(k):
        return rcopy(srow.at[pl.ds(0, 8), :], pgot.at[q], vps(k), vpr(k), peer(k))

    def vp_arrive(k):
        return rcopy(pgot.at[across(q, k)], pgot.at[across(q, k)], vps(k), vpr(k), peer(k))

    def vz_x(r):
        return rcopy(srow.at[pl.ds(8, 8), :], zgot.at[z], vzs(r), vzr(r), (dp, lax.rem(z + r, Z)))

    def vz_arrive(r):
        zz = lax.rem(z + Z - r, Z)
        return rcopy(zgot.at[zz], zgot.at[zz], vzs(r), vzr(r), (dp, z))

    for k in range(1, Q):
        vp_x(k).start()
    for i in range(2):
        pass
    outs[...] = (resid[...] + dsum.total() + db[...]).astype(BF)
    send_rows(1)
    to_plane(0, 0)
    for k in range(1, Q):
        vp_arrive(k).wait_recv()
    psum = pgot[0]
    for k in range(1, Q):
        psum = psum + pgot[k]
    srow[8:16, :] = psum
    zgot[z] = psum
    for r in range(1, Z):
        vz_x(r).start()
    to_plane(0, 1)

    def a_loc(ref, n_rows):
        def loc(k, lo, n):
            return ref.at[pl.ds(pl.multiple_of(across(q, k) * n_rows + lo, n), n), :]
        return loc

    wgat = PlaneGather(al, peer, sib, a_loc(aw, M), M, own=wfin)
    ogat = PlaneGather(al, peer, sib, a_loc(ago, OR), OR, own=ofin)
    gl = al.take(2)
    g_l = [lcopy(wfin, a_loc(aw, M)(0, 0, M), gl(0)), lcopy(ofin, a_loc(ago, OR)(0, 0, OR), gl(1))]

    @pl.when(mine)
    def _():
        for i, (fin, done, buf, gat) in ((1, (ofin, odone, zo, ogat)), (0, (wfin, wdone, zb, wgat))):
            for zz in range(Z):
                @pl.when(zz != z)
                def _():
                    z_arrive(i, zz).wait_recv()
            buf[z] = done[jz]
            t = buf[0].astype(F32)
            for zz in range(1, Z):
                t = t + buf[zz].astype(F32)
            fin[...] = t.astype(BF)
            gat.start()
            g_l[1 if i == 1 else 0].start()
    for gat in (ugat, dgat):
        gat.middle()
    for k in range(1, Q):
        b_arrive(k).wait_recv()
        b_f(k).start()
    for r in range(1, Z):
        vz_arrive(r).wait_recv()
    zsum = zgot[0]
    for zz in range(1, Z):
        zsum = zsum + zgot[zz]
    small_o[...] = zsum

    @pl.when(mine)
    def _():
        for gat in (ogat, wgat):
            gat.middle()
    for gat in (ugat, dgat):
        gat.last()

    @pl.when(mine)
    def _():
        for gat in (ogat, wgat):
            gat.last()
    ugat.arrivals(u_loc(1 - c))
    dgat.arrivals(d_loc(1 - c))

    @pl.when(jnp.logical_not(mine))
    def _():
        ogat.arrivals(a_loc(ago, OR))
        wgat.arrivals(a_loc(aw, M))

    for k in range(Q):
        rcopy(aub.at[dev(k, 1 - c)], aub.at[dev(k, 1 - c)], bfs(k), bfr(k), sib).wait_recv()
        b_f(k).wait_send()
        d_x(k).wait_send()
    for k in range(1, Q):
        b_x(k).wait_send()
        vp_x(k).wait_send()
    b_l.wait()
    for x in f_l:
        x.wait()
    for r in range(1, Z):
        vz_x(r).wait_send()
        for i in range(3):
            x_z(i, r).wait_send()
    for x in osum + wsum + [dsum, ugat, dgat]:
        x.drain()

    @pl.when(mine)
    def _():
        for x in (ogat, wgat):
            x.drain()
        for x in g_l:
            x.wait()
    t_x.wait_send()
    for j in range(B):
        @pl.when(B * c + j != z)
        def _():
            for i in range(2):
                z_x(i, j).wait_send()
    for p in range(per):
        here = (c * per + p == z) & mine

        @pl.when(here)
        def _():
            for i in range(2):
                row_l(i, p).wait()

        @pl.when(jnp.logical_not(here))
        def _():
            for i in range(2):
                row_x(i, p).wait_send()
    for s in range(B):
        @pl.when(jnp.logical_not((B * c + s == z) & mine))
        def _():
            for i in range(2):
                rcopy(rows_out[i].at[s], rows_out[i].at[s], rs(i, 0), rr(i, s), (dp, z)).wait_recv()
    assert al.used <= BACK_SEMS


def back(Q, Z, B, tok, normed, q_, k_, v_, probs, mixed, wq, wk, wv, wo, resid, gresid, glow, gu, gd, down, ffs, cot, g1, b1, db):
    S, D = glow.shape
    N, R = S // 2, S // Z
    W = q_.shape[1]
    H = W // B
    F = gd.shape[0]
    E = F // Z
    heads = W // HEAD_DIM
    M, OR = D // Q, H // Q
    vm = pltpu.VMEM
    return pl.pallas_call(
        functools.partial(back_kernel, Q, Z, B),
        out_shape=[
            sds((D, 3 * H), BF), sds((H, D), BF), sds((D, 2 * Q * E), BF), sds((2 * Q * E, D), BF), sds((2 * Q, 1, E), F32),
            sds((8, D), F32), sds((B, R, D), BF), sds((B, R, D), BF),
        ],
        in_specs=[ANY] * 17 + [VM] + [ANY] + [VM] * 3,
        out_specs=[ANY] * 5 + [VM] + [ANY] * 2,
        scratch_shapes=[
            vm((3 * S, D), BF), vm((S, W), BF), vm((3 * S, W), BF), vm((3 * S, W), BF), vm((heads, S, 3 * S), BF), vm((S, W), BF),
            vm((D, W), BF), vm((D, W), BF), vm((D, W), BF), vm((W, D), BF),
            vm((N, D), BF), vm((N, D), F32), vm((N, D), F32), vm((S, D), BF), vm((S, W), BF),
            vm((Z, D, E), BF), vm((Z, E, D), BF), vm((Z, 1, E), F32), vm((D, E), BF), vm((E, D), BF), vm((1, E), F32),
            vm((Q, N, D), BF), vm((Q, N, D), BF), vm((2, N // 2, D), BF), vm((2, N, D), BF),
            vm((3 * S, 2 * H), BF), vm((S, W), BF), vm((W, D), BF), vm((B, D, 3 * H), BF),
            vm((B, 2, M // 2, 3 * H), BF), vm((B, 2, M, 3 * H), BF), vm((B, 2, OR // 2, D), BF), vm((B, 2, OR, D), BF),
            vm((B, M, 3 * H), BF), vm((B, OR, D), BF), vm((Z, M, 3 * H), BF), vm((Z, OR, D), BF), vm((M, 3 * H), BF), vm((OR, D), BF),
            vm((N, D), F32), vm((N, D), F32), vm(cot.shape, BF), vm((D, 128), F32),
            vm((8, D), F32), vm((8, D), F32), vm((N, D), F32), vm((Q, 8, D), F32), vm((Z, 8, D), F32), vm((N, D), BF), vm((N, D), BF),
            DMA((BACK_SEMS,)),
        ],
        compiler_params=pltpu.CompilerParams(collective_id=2, has_side_effects=True, vmem_limit_bytes=63 << 20),
        name="back",
    )(tok, normed, q_, k_, v_, probs, mixed, wq, wk, wv, wo, resid, gresid, glow, gu, gd, down, ffs, cot, g1, b1, db)


def chip_device(Q, Z, tokens, memory, compressed, valid_counts, attention_norm_gain, attention_norm_bias,
                query_projection, key_projection, value_projection, out_weight, feedforward_norm_gain,
                feedforward_norm_bias, up_weight, up_bias, down_weight, down_bias, squeeze_weight, cotangent):
    B, R, D = tokens.shape
    H = query_projection.shape[1]
    FL = up_weight.shape[1]
    E = FL // (2 * Q)
    (tok_all, normed, q_, k_, v_, probs, mixed, wqg, wkg, wvg, wog, resid, g_resid, g_low, up_low, down_g_low, down,
     ff_small, o_nm, o_nc) = front(
        Q, Z, compressed, memory, tokens, cotangent, query_projection, key_projection, value_projection, out_weight,
        up_weight, down_weight, up_bias.reshape(2 * Q, 1, E), jnp.broadcast_to(valid_counts[:, None, None], (B, 8, 128)),
        squeeze_weight, attention_norm_gain.reshape(1, D), attention_norm_bias.reshape(1, D),
        feedforward_norm_gain.reshape(1, D), feedforward_norm_bias.reshape(1, D),
    )
    aw, ago, afu, afd, aub, small, o_out, o_tg = back(
        Q, Z, B, tok_all, normed, q_, k_, v_, probs, mixed, wqg, wkg, wvg, wog, resid, g_resid, g_low, up_low, down_g_low, down,
        ff_small, cotangent, attention_norm_gain.reshape(1, D), attention_norm_bias.reshape(1, D), down_bias.reshape(1, D),
    )
    aw = aw.astype(F32)
    return (
        o_out, o_tg.astype(F32), small[0], small[1], aw[:, 2 * H:], aw[:, :H], aw[:, H:2 * H], ago.astype(F32),
        small[2], small[3], afu.astype(F32), aub.reshape(FL), afd.astype(F32), small[4], o_nm, o_nc,
    )


def solution(mesh):
    in_specs = (
        P("dp", "mp", None),
        P("dp", "mp", None),
        P("dp", "mp", None),
        P("dp"),
        P(),
        P(),
        P(None, "mp"),
        P(None, "mp"),
        P(None, "mp"),
        P("mp", None),
        P(),
        P(),
        P(None, "mp"),
        P("mp"),
        P("mp", None),
        P(),
        P(),
        P("dp", "mp", None),
    )
    out_specs = (
        P("dp", "mp", None),
        P("dp", "mp", None),
        P(),
        P(),
        P(None, "mp"),
        P(None, "mp"),
        P(None, "mp"),
        P("mp", None),
        P(),
        P(),
        P(None, "mp"),
        P("mp"),
        P("mp", None),
        P(),
        P("dp", "mp", None),
        P("dp", "mp", None),
    )
    Q, Z = mesh.shape["dp"] // 2, mesh.shape["mp"]

    def per_device(*args):
        B, R, D = args[0].shape
        H, FL = args[6].shape[1], args[12].shape[1]
        whole = Q == 4 and B == 2 and 2 * B == Z and H % HEAD_DIM == 0 and D % (16 * Q) == 0 and H % (16 * Q) == 0
        if whole and R % 32 == 0 and FL % (256 * Q) == 0:
            return chip_device(Q, Z, *args)
        return general_device(*args)

    return jax.shard_map(
        per_device, mesh=mesh, in_specs=in_specs, out_specs=out_specs, check_vma=False
    )
```

```python
import functools

import jax
import jax.numpy as jnp
from jax import lax
from jax.experimental import pallas as pl
from jax.experimental.pallas import tpu as pltpu
from jax.sharding import PartitionSpec as P

HEAD_DIM = 128
RATE = 3


def apply_layer_norm(rows):
    center = jnp.mean(rows, axis=-1, keepdims=True)
    centered = rows - center
    spread = jnp.mean(centered * centered, axis=-1, keepdims=True)
    inverse_deviation = lax.rsqrt(spread + 1e-05)
    return (centered * inverse_deviation, inverse_deviation)


def norm_backward_pass(input_gradient, standardized_rows, inverse_deviation, scale_factor):
    scaled_rows = input_gradient * scale_factor
    attention_norm_mean = jnp.mean(scaled_rows, axis=-1, keepdims=True)
    feedforward_norm_mean = jnp.mean(scaled_rows * standardized_rows, axis=-1, keepdims=True)
    return inverse_deviation * (
        scaled_rows - attention_norm_mean - standardized_rows * feedforward_norm_mean
    )


def squeeze_rows(old_comp, old_mem, fresh, valid_count, offset, own_rows, squeeze_weight):
    features = old_mem.shape[1]
    joined = jnp.concatenate([old_mem, fresh], axis=0)
    new_memory = lax.dynamic_slice_in_dim(joined, valid_count + offset, own_rows, 0)
    comp_len = old_comp.shape[0]
    evicted = valid_count // RATE
    first_row = evicted + offset
    window_start = jnp.maximum(first_row - comp_len, 0)
    padded = jnp.concatenate(
        [old_mem, jnp.zeros((RATE * own_rows, features), jnp.bfloat16)], axis=0
    )
    window = lax.dynamic_slice_in_dim(padded, window_start * RATE, RATE * own_rows, 0)
    squeezed = jnp.dot(
        window.reshape(own_rows, RATE * features),
        squeeze_weight,
        preferred_element_type=jnp.float32,
    ).astype(jnp.bfloat16)
    positions = first_row + jnp.arange(own_rows)
    from_old = jnp.take(old_comp, jnp.clip(positions, 0, comp_len - 1), axis=0)
    from_new = jnp.take(
        squeezed, jnp.clip(positions - comp_len - window_start, 0, own_rows - 1), axis=0
    )
    new_compressed = jnp.where((positions < comp_len)[:, None], from_old, from_new)
    return (new_memory, new_compressed)


def general_device(
    tokens,
    memory,
    compressed,
    valid_counts,
    attention_norm_gain,
    attention_norm_bias,
    query_projection,
    key_projection,
    value_projection,
    out_weight,
    feedforward_norm_gain,
    feedforward_norm_bias,
    up_weight,
    up_bias,
    down_weight,
    down_bias,
    squeeze_weight,
    cotangent,
):
    batch_segs, own_rows, features = tokens.shape
    offset = lax.axis_index("mp") * own_rows
    old_comp, old_mem, fresh = (
        lax.all_gather(compressed, "mp", axis=1, tiled=True),
        lax.all_gather(memory, "mp", axis=1, tiled=True),
        lax.all_gather(tokens, "mp", axis=1, tiled=True),
    )
    seg_len = fresh.shape[1]
    prior_rows = old_comp.shape[1] + old_mem.shape[1]
    context_tokens = jnp.concatenate([old_comp, old_mem, fresh], axis=1).astype(jnp.float32)
    ctx_len = context_tokens.shape[1]
    standardized_full, inverse_deviation_full = apply_layer_norm(context_tokens)
    normed_rows = (standardized_full * attention_norm_gain + attention_norm_bias).astype(
        jnp.bfloat16
    )
    token_rows_normed = normed_rows[:, prior_rows:]
    queries = jnp.einsum(
        "xhp,pj->xhj", token_rows_normed, query_projection, preferred_element_type=jnp.float32
    ).astype(jnp.bfloat16)
    key_rows = jnp.einsum(
        "xhp,pj->xhj", normed_rows, key_projection, preferred_element_type=jnp.float32
    ).astype(jnp.bfloat16)
    values = jnp.einsum(
        "xhp,pj->xhj", normed_rows, value_projection, preferred_element_type=jnp.float32
    ).astype(jnp.bfloat16)
    local_heads = query_projection.shape[1] // HEAD_DIM
    score_scale = HEAD_DIM ** (-0.5)

    def by_heads(matrix):
        return matrix.reshape(matrix.shape[0], matrix.shape[1], local_heads, HEAD_DIM)

    query_pos = jnp.arange(seg_len)[:, None]
    key_pos = jnp.arange(ctx_len)[None, :] - prior_rows
    allowed = (key_pos[None] < 0) | (key_pos <= query_pos)[None] & (
        key_pos[None] < valid_counts[:, None, None]
    )

    def scores_of(query_in, key_in):
        raw = (
            jnp.einsum(
                "gqhe,gkhe->ghqk",
                by_heads(query_in),
                by_heads(key_in),
                preferred_element_type=jnp.float32,
            )
            * score_scale
        )
        return jnp.where(allowed[:, None], raw, -1e30)

    scores = scores_of(queries, key_rows)
    peak_score = jnp.max(scores, axis=-1, keepdims=True)
    exponent = jnp.exp(scores - peak_score)
    exp_total = jnp.sum(exponent, axis=-1, keepdims=True)
    log_total = peak_score + jnp.log(exp_total)
    probs_low = (exponent / exp_total).astype(jnp.bfloat16)
    mixed_heads = jnp.einsum(
        "ghqk,gkhe->gqhe", probs_low, by_heads(values), preferred_element_type=jnp.float32
    ).astype(jnp.bfloat16)
    mixed_heads = mixed_heads.reshape(batch_segs, seg_len, local_heads * HEAD_DIM)
    partial_attn = jnp.einsum(
        "gsc,cd->gsd", mixed_heads, out_weight, preferred_element_type=jnp.float32
    )
    attention = lax.psum_scatter(partial_attn, "mp", scatter_dimension=1, tiled=True)
    residual_stream = tokens.astype(jnp.float32) + attention
    standardized_feedforward, inverse_deviation_feedforward = apply_layer_norm(residual_stream)
    feedforward_input = (
        standardized_feedforward * feedforward_norm_gain + feedforward_norm_bias
    ).astype(jnp.bfloat16)
    second_all = lax.all_gather(feedforward_input, "mp", axis=1, tiled=True)
    upper_in = (
        jnp.einsum("gsd,df->gsf", second_all, up_weight, preferred_element_type=jnp.float32)
        + up_bias
    )
    active, gelu_back = jax.vjp(jax.nn.gelu, upper_in)
    active_low = active.astype(jnp.bfloat16)
    partial_ffn = jnp.einsum(
        "gsf,fd->gsd", active_low, down_weight, preferred_element_type=jnp.float32
    )
    down_out = lax.psum_scatter(
        partial_ffn.astype(jnp.bfloat16), "mp", scatter_dimension=1, tiled=True
    ).astype(jnp.float32)
    output = (residual_stream + down_out + down_bias).astype(jnp.bfloat16)

    def update_one(comp_seg, mem_seg, fresh_seg, valid_count):
        return squeeze_rows(
            comp_seg, mem_seg, fresh_seg, valid_count, offset, own_rows, squeeze_weight
        )

    new_memory, new_compressed = jax.vmap(update_one)(old_comp, old_mem, fresh, valid_counts)
    output_gradient = cotangent.astype(jnp.float32)
    down_bias_grad = jnp.sum(output_gradient, axis=(0, 1))
    grad_all = lax.all_gather(cotangent, "mp", axis=1, tiled=True)
    down_weight_grad = jnp.einsum(
        "gsf,gsd->fd", active_low, grad_all, preferred_element_type=jnp.float32
    )
    grad_active = jnp.einsum(
        "gsd,fd->gsf", grad_all, down_weight, preferred_element_type=jnp.float32
    )
    grad_upper = gelu_back(grad_active)[0].astype(jnp.bfloat16)
    up_weight_grad = jnp.einsum(
        "gsd,gsf->df", second_all, grad_upper, preferred_element_type=jnp.float32
    )
    up_bias_grad = jnp.sum(grad_upper.astype(jnp.float32), axis=(0, 1))
    partial_second = jnp.einsum(
        "gsf,df->gsd", grad_upper, up_weight, preferred_element_type=jnp.float32
    )
    feedforward_gradient = lax.psum_scatter(partial_second, "mp", scatter_dimension=1, tiled=True)
    feedforward_gain_gradient = jnp.sum(
        feedforward_gradient * standardized_feedforward, axis=(0, 1)
    )
    second_bias_grad = jnp.sum(feedforward_gradient, axis=(0, 1))
    residual_gradient = output_gradient + norm_backward_pass(
        feedforward_gradient,
        standardized_feedforward,
        inverse_deviation_feedforward,
        feedforward_norm_gain,
    )
    grad_resid_all = lax.all_gather(
        residual_gradient.astype(jnp.bfloat16), "mp", axis=1, tiled=True
    )
    out_weight_grad = jnp.einsum(
        "gsc,gsd->cd", mixed_heads, grad_resid_all, preferred_element_type=jnp.float32
    )
    grad_mixed = jnp.einsum(
        "gsd,cd->gsc", grad_resid_all, out_weight, preferred_element_type=jnp.float32
    ).astype(jnp.bfloat16)
    probs_again = jnp.exp(scores_of(queries, key_rows) - log_total)
    grad_probs = jnp.einsum(
        "gqhe,gkhe->ghqk",
        by_heads(grad_mixed),
        by_heads(values),
        preferred_element_type=jnp.float32,
    )
    row_dot = jnp.sum(probs_again * grad_probs, axis=-1, keepdims=True)
    grad_scores = (probs_again * (grad_probs - row_dot)).astype(jnp.bfloat16)
    query_gradient = (
        score_scale
        * jnp.einsum(
            "ghqk,gkhe->gqhe", grad_scores, by_heads(key_rows), preferred_element_type=jnp.float32
        )
    ).astype(jnp.bfloat16)
    key_gradient = (
        score_scale
        * jnp.einsum(
            "ghqk,gqhe->gkhe", grad_scores, by_heads(queries), preferred_element_type=jnp.float32
        )
    ).astype(jnp.bfloat16)
    value_gradient = jnp.einsum(
        "ghqk,gqhe->gkhe",
        probs_again.astype(jnp.bfloat16),
        by_heads(grad_mixed),
        preferred_element_type=jnp.float32,
    ).astype(jnp.bfloat16)
    query_gradient = query_gradient.reshape(batch_segs, seg_len, -1)
    key_gradient = key_gradient.reshape(batch_segs, ctx_len, -1)
    value_gradient = value_gradient.reshape(batch_segs, ctx_len, -1)
    query_weight_grad = jnp.einsum(
        "nja,njr->ar", token_rows_normed, query_gradient, preferred_element_type=jnp.float32
    )
    key_weight_grad = jnp.einsum(
        "nja,njr->ar", normed_rows, key_gradient, preferred_element_type=jnp.float32
    )
    value_weight_grad = jnp.einsum(
        "nja,njr->ar", normed_rows, value_gradient, preferred_element_type=jnp.float32
    )
    partial_normed = jnp.einsum(
        "xmo,qo->xmq", key_gradient, key_projection, preferred_element_type=jnp.float32
    )
    partial_normed = partial_normed + jnp.einsum(
        "xmo,qo->xmq", value_gradient, value_projection, preferred_element_type=jnp.float32
    )
    partial_normed = partial_normed.at[:, prior_rows:].add(
        jnp.einsum(
            "xmo,qo->xmq", query_gradient, query_projection, preferred_element_type=jnp.float32
        )
    )
    partial_normed = partial_normed.reshape(batch_segs, 3, seg_len, features)
    normed_gradient = lax.psum_scatter(
        partial_normed.astype(jnp.bfloat16), "mp", scatter_dimension=2, tiled=True
    ).astype(jnp.float32)
    segment_context = jnp.stack([compressed, memory, tokens], axis=1).astype(jnp.float32)
    standardized_segment, inverse_deviation_segment = apply_layer_norm(segment_context)
    attention_gain_gradient = jnp.sum(normed_gradient * standardized_segment, axis=(0, 1, 2))
    first_bias_grad = jnp.sum(normed_gradient, axis=(0, 1, 2))
    tokens_grad = residual_gradient + norm_backward_pass(
        normed_gradient[:, 2],
        standardized_segment[:, 2],
        inverse_deviation_segment[:, 2],
        attention_norm_gain,
    )
    summed = (
        lax.psum(query_weight_grad.astype(jnp.bfloat16), "dp").astype(jnp.float32),
        lax.psum(key_weight_grad.astype(jnp.bfloat16), "dp").astype(jnp.float32),
        lax.psum(value_weight_grad.astype(jnp.bfloat16), "dp").astype(jnp.float32),
        lax.psum(out_weight_grad.astype(jnp.bfloat16), "dp").astype(jnp.float32),
        lax.psum(up_weight_grad.astype(jnp.bfloat16), "dp").astype(jnp.float32),
        lax.psum(up_bias_grad.astype(jnp.bfloat16), "dp").astype(jnp.float32),
        lax.psum(down_weight_grad.astype(jnp.bfloat16), "dp").astype(jnp.float32),
    )
    norms = lax.psum(
        (
            attention_gain_gradient,
            first_bias_grad,
            feedforward_gain_gradient,
            second_bias_grad,
            down_bias_grad,
        ),
        ("dp", "mp"),
    )
    return (
        output,
        tokens_grad,
        norms[0],
        norms[1],
        summed[0],
        summed[1],
        summed[2],
        summed[3],
        norms[2],
        norms[3],
        summed[4],
        summed[5],
        summed[6],
        norms[4],
        new_memory,
        new_compressed,
    )


BF = jnp.bfloat16
F32 = jnp.float32
MESH = pl.DeviceIdType.MESH
ANY = pl.BlockSpec(memory_space=pl.ANY)
VM = pl.BlockSpec(memory_space=pltpu.VMEM)
DMA = pltpu.SemaphoreType.DMA


def sds(shape, dtype):
    return jax.ShapeDtypeStruct(shape, dtype)


def where_am_i(chips, depth):
    dp = lax.axis_index("dp")
    return dp, lax.rem(dp, 2), dp // 2, lax.axis_index("mp")


def rcopy(src, dst, send, recv, device):
    return pltpu.make_async_remote_copy(
        src_ref=src,
        dst_ref=dst,
        send_sem=send,
        recv_sem=recv,
        device_id=device,
        device_id_type=MESH,
    )


def lcopy(src, dst, sem):
    return pltpu.make_async_copy(src, dst, sem)


def enter(partners):
    barrier = pltpu.get_barrier_semaphore()
    for p in partners:
        pl.semaphore_signal(barrier, inc=1, device_id=p, device_id_type=MESH)
    pl.semaphore_wait(barrier, len(partners))


def across(q, k):
    if k == 0:
        return q
    if k == 1:
        return q + 1 - 2 * lax.rem(q, 2)
    if k == 2:
        return lax.rem(q + 2, 4)
    return 3 - q


def layer_norm_rows(rows):
    center = jnp.mean(rows, axis=-1, keepdims=True)
    centered = rows - center
    spread = jnp.mean(centered * centered, axis=-1, keepdims=True)
    inv = lax.rsqrt(spread + 1e-05)
    return centered * inv, inv


class Slots:
    def __init__(self, ref):
        self.ref = ref
        self.used = 0

    def take(self, *shape):
        base = self.used
        size = 1
        for n in shape:
            size *= n
        self.used += size

        def at(*index):
            flat = 0
            for n, i in zip(shape, index):
                flat = flat * n + i
            return self.ref.at[base + flat]

        return at


def nt_dot(a, b):
    return lax.dot_general(a, b, (((1,), (1,)), ((), ())), preferred_element_type=F32)


def tn_dot(a, b):
    return lax.dot_general(a, b, (((0,), (0,)), ((), ())), preferred_element_type=F32)


def nn_dot(a, b):
    return jnp.dot(a, b, preferred_element_type=F32)


def one_hot(shape, offset):
    row = lax.broadcasted_iota(jnp.int32, shape, 0)
    col = lax.broadcasted_iota(jnp.int32, shape, 1)
    return jnp.where(col == row + offset, 1.0, 0.0).astype(BF)


def stack(ref, offset, rows, width=None):
    width = ref.shape[-1] if width is None else width

    def view(i):
        return ref.at[pl.ds(pl.multiple_of(offset + i * rows, rows), rows), pl.ds(0, width)]

    return view


class PlaneSum:
    def __init__(self, al, peer, blk, rows, h, g):
        self.peer, self.blk, self.half, self.rows, self.h, self.g = peer, blk, rows // 2, rows, h, g
        self.hs, self.hr, self.gs, self.gr = al.take(2), al.take(2), al.take(2), al.take(2)

    def h_x(self, i):
        return rcopy(self.blk(3, i * self.half, self.half), self.h(i), self.hs(i), self.hr(i), self.peer(i + 1))

    def g_x(self, i):
        return rcopy(self.blk(i + 1, 0, self.rows), self.g(i), self.gs(i), self.gr(i), self.peer(i + 1))

    def start(self):
        for i in range(2):
            self.h_x(i).start()

    def middle(self):
        for i in range(2):
            self.h_x(i).wait_recv()
            mine = self.blk(2 - i, i * self.half, self.half)
            mine[...] = (mine[...].astype(F32) + self.h(i)[...].astype(F32)).astype(BF)
            self.g_x(1 - i).start()

    def arrive(self):
        for i in range(2):
            self.g_x(i).wait_recv()

    def total(self):
        self.arrive()
        own = self.blk(0, 0, self.rows)
        return own[...].astype(F32) + (self.g(0)[...].astype(F32) + self.g(1)[...].astype(F32))

    def drain(self):
        for i in range(2):
            self.h_x(i).wait_send()
            self.g_x(i).wait_send()


class PlaneGather:
    def __init__(self, al, peer, sib, loc, rows, own=None):
        self.peer, self.sib, self.loc, self.half, self.rows = peer, sib, loc, rows // 2, rows
        self.own = own
        self.as_, self.ar, self.hs, self.hr = al.take(2), al.take(2), al.take(2), al.take(2)
        self.fs, self.fr = al.take(4), al.take(4)

    def a_x(self, i, k=0):
        src = self.loc(0, 0, self.rows) if self.own is None else self.own
        return rcopy(src, self.loc(k, 0, self.rows), self.as_(i), self.ar(i), self.peer(i + 1))

    def h_x(self, i, k=None):
        k = 2 - (1 - i) if k is None else k
        rows = self.loc(k, i * self.half, self.half)
        return rcopy(rows, rows, self.hs(i), self.hr(i), self.peer(2 - i))

    def f_x(self, k, other=None):
        src = self.loc(k, 0, self.rows)
        if k == 0 and self.own is not None:
            src = self.own
        dst = self.loc(k, 0, self.rows) if other is None else other(k, 0, self.rows)
        return rcopy(src, dst, self.fs(k), self.fr(k), self.sib)

    def start(self):
        for i in range(2):
            self.a_x(i).start()
        self.f_x(0).start()

    def middle(self):
        for i in range(2):
            rcopy(self.loc(i + 1, 0, self.rows), self.loc(i + 1, 0, self.rows), self.as_(i), self.ar(i), self.peer(1)).wait_recv()
            self.h_x(i).start()
            self.f_x(i + 1).start()

    def last(self):
        for i in range(2):
            self.h_x(i, 3).wait_recv()
        self.f_x(3).start()

    def drain(self):
        for i in range(2):
            self.a_x(i).wait_send()
            self.h_x(i).wait_send()
        for k in range(4):
            self.f_x(k).wait_send()

    def arrivals(self, other):
        for k in range(4):
            rcopy(other(k, 0, self.rows), other(k, 0, self.rows), self.fs(k), self.fr(k), self.sib).wait_recv()


LAYER_SEMS = 600


def layer_kernel(Q, Z, comp, mem, tok, cot, wq, wk, wv, wo, up, down, ub, vc, sq, g1, b1, g2, b2, db,
                 aw, ago, afu, afd, aub, small_o, out_o, tg_o, nm_o, nc_o,
                 ctx, normed, wqs, wks, wvs, wos, qs, ks, vs, probs, mixed, phalf, got, resid, sec, cots, ups, downs,
                 ubs, vco, act, gup, gbuf, got1, gh, gg, glow, nms, ncs, gus, gds, dgot, dh, dg, ggot, srow,
                 xu, xd, xb, fbs, arow, ffs, sums, sgot, pgot, zgot, sems, ready):
    dp, c, q, z = where_am_i(Q, Z)
    sd = dp + 1 - 2 * c
    sib = (sd, z)
    partners = [sib]
    for r in range(1, Z):
        for d in (dp, sd):
            partners.append((d, lax.rem(z + r, Z)))
    for k in range(1, Q):
        partners.append((2 * across(q, k) + c, z))
    enter(partners)
    B, R, D = tok.shape
    H = wq.shape[1]
    QR = D // Q
    OR = H // Q
    HR = R // 2
    S = R * Z
    N = S // 2
    E = up.shape[1] // (2 * Q)
    heads = B * H // HEAD_DIM
    mine = c == z // B
    jz = lax.rem(z, B)
    al = Slots(sems)

    def peer(k):
        return (2 * across(q, k) + c, z)

    wins = [wq, wk, wv, wo]
    wss = [wqs, wks, wvs, wos]

    def piece(a):
        if a < 3:
            return wins[a].at[pl.ds(q * QR, QR), :]
        return wo.at[pl.ds(q * OR, OR), :]

    def place(a, j, qq):
        if a < 3:
            return wss[a].at[pl.ds(pl.multiple_of(qq * QR, QR), QR), pl.ds(pl.multiple_of(j * H, H), H)]
        return wos.at[pl.ds(pl.multiple_of(j * H + qq * OR, OR), OR), :]

    def place_whole(a, j):
        if a < 3:
            return wss[a].at[:, pl.ds(pl.multiple_of(j * H, H), H)]
        return wos.at[pl.ds(pl.multiple_of(j * H, H), H), :]

    ws, wr = al.take(4, Z - 1), al.take(4, B)
    ps, pr = al.take(4, B, Q - 1), al.take(4, B, Q - 1)
    wl = al.take(4)

    def w_z(a, r):
        return rcopy(piece(a), place(a, jz, q), ws(a, r - 1), wr(a, jz), (dp, lax.rem(z + r, Z)))

    def w_arrive(a, j):
        return rcopy(place(a, j, q), place(a, j, q), ws(a, 0), wr(a, j), (dp, z))

    def w_p(a, j, k, qq):
        return rcopy(place(a, j, qq), place(a, j, qq), ps(a, j, k - 1), pr(a, j, k - 1), peer(k))

    def w_l(a):
        return lcopy(wins[a], place_whole(a, jz), wl(a))

    acts = [comp, mem, tok]
    cs, cr = al.take(3, B, 2), al.take(3, Z)
    fs, fr = al.take(3, Z), al.take(3, Z)
    cl = al.take(3)

    def c_rows(t, zs):
        return ctx.at[t, pl.ds(pl.multiple_of(zs * R, R), R), :]

    def c_half(t, zs, h):
        return ctx.at[t, pl.ds(pl.multiple_of(zs * R + HR * h, HR), HR), :]

    def c_l(t):
        return lcopy(acts[t].at[jz], c_rows(t, z), cl(t))

    def c_sib(t):
        return rcopy(acts[t].at[jz], c_rows(t, z), fs(t, z), fr(t, z), sib)

    def c_z(t, s, h):
        return rcopy(acts[t].at[s, pl.ds(HR * h, HR), :], c_half(t, z, h), cs(t, s, h), cr(t, z), (2 * q + h, B * c + s))

    def c_arrive(t, zs):
        return rcopy(c_half(t, zs, c), c_half(t, zs, c), cs(t, 0, 0), cr(t, zs), (dp, z))

    def c_fwd(t, zs, half):
        return rcopy(c_half(t, zs, half), c_half(t, zs, half), fs(t, zs), fr(t, zs), sib)

    us, ur, ul = al.take(Z - 1), al.take(Z - 1), al.take(1)
    vs_, vr_ = al.take(1), al.take(1)

    def u_z(r):
        return rcopy(ub.at[dp], ubs.at[r], us(r - 1), ur(r - 1), (dp, lax.rem(z + r, Z)))

    u_l = lcopy(ub.at[dp], ubs.at[0], ul(0))
    v_s = rcopy(vc, vco, vs_(0), vr_(0), sib)

    ts, tr, tl = al.take(B), al.take(B), al.take(1)

    def dev(k, core):
        return 2 * across(q, k) + core

    def t_rows(d, i):
        return cots.at[pl.ds(pl.multiple_of(d * N + i * R, R), R), :]

    def t_z(s):
        to = 2 * q + z // B
        return rcopy(cot.at[s], t_rows(to, jz), ts(s), tr(jz), (to, B * c + s))

    def t_l():
        return lcopy(cot.at[jz], t_rows(dp, jz), tl(0))

    def t_arrive(i):
        return rcopy(t_rows(dp, i), t_rows(dp, i), ts(0), tr(i), (dp, z))

    def rows_at(ref, core):
        def loc(k, lo, n):
            return ref.at[pl.ds(pl.multiple_of(dev(k, core) * N + lo, n), n), :]
        return loc

    tgat = PlaneGather(al, peer, sib, rows_at(cots, c), N)
    agat = PlaneGather(al, peer, sib, rows_at(sec, c), N)

    xs, xr_, xl, xf = al.take(2, Z), al.take(2, Z), al.take(2), al.take(2, 2)
    is_end = lax.rem(z, Z - 1) == 0

    def x_place(i, r):
        if i == 0:
            return ups.at[:, pl.ds(r * E, E)]
        return downs.at[pl.ds(r * E, E), :]

    def x_z(i, r):
        src = up.at[:, pl.ds(pl.multiple_of(dp * E, E), E)] if i == 0 else down.at[pl.ds(pl.multiple_of(dp * E, E), E), :]
        return rcopy(src, x_place(i, r), xs(i, r), xr_(i, r), (dp, lax.rem(z + r, Z)))

    def x_direct(r):
        return (z < Z - 1, is_end, z > 0)[r - 1]

    def x_start(i):
        for r in range(1, Z):
            @pl.when(x_direct(r))
            def _():
                x_z(i, r).start()

    onward = ((2, 3, ((2, 3), (1, 2)), 3), (1, 0, ((2, 1), (3, 2)), 1))

    def x_onward(i, n, to, a, b):
        return rcopy(x_place(i, a), x_place(i, b), xf(i, n), xr_(i, b), (dp, to))

    def x_forward(i):
        for at, to, pairs, rest in onward:
            @pl.when(z == at)
            def _():
                for n, (a, b) in enumerate(pairs):
                    x_z(i, a).wait_recv()
                    x_onward(i, n, to, a, b).start()

    def x_rest(i):
        for at, to, pairs, rest in onward:
            @pl.when(z == at)
            def _():
                x_z(i, rest).wait_recv()

        @pl.when(is_end)
        def _():
            for r in range(1, Z):
                x_z(i, r).wait_recv()

    def x_drain(i):
        for r in range(1, Z):
            @pl.when(x_direct(r))
            def _():
                x_z(i, r).wait_send()
        for at, to, pairs, rest in onward:
            @pl.when(z == at)
            def _():
                for n, (a, b) in enumerate(pairs):
                    x_onward(i, n, to, a, b).wait_send()

    x_l = [lcopy(up.at[:, pl.ds(pl.multiple_of(dp * E, E), E)], ups.at[:, pl.ds(0, E)], xl(0)),
           lcopy(down.at[pl.ds(pl.multiple_of(dp * E, E), E), :], downs.at[pl.ds(0, E), :], xl(1))]

    c_sem = al.take(B)
    c_in = [lcopy(cot.at[i], nms.at[pl.ds(i * R, R), :], c_sem(i)) for i in range(B)]

    for x in c_in:
        x.start()
    sums[...] = jnp.zeros_like(sums)
    @pl.when(mine)
    def _():
        for a in range(4):
            for r in range(1, Z):
                w_z(a, r).start()
        for a in range(4):
            w_l(a).start()
        for t in range(3):
            c_l(t).start()
            c_sib(t).start()
    for r in range(1, Z):
        u_z(r).start()
    v_s.start()
    u_l.start()
    for x in x_l:
        x.start()
    for j in range(B):
        @pl.when(B * c + j != z)
        def _():
            for a in range(4):
                w_arrive(a, j).wait_recv()
                for k in range(1, Q):
                    w_p(a, j, k, q).start()
    for s in range(B):
        @pl.when(B * c + s != z)
        def _():
            for t in range(3):
                for h in range(2):
                    c_z(t, s, h).start()

    def norm_block(t, zs):
        at = pl.ds(pl.multiple_of(zs * R, R), R)
        to = pl.ds(pl.multiple_of(t * S + zs * R, R), R)
        xhat, _ = layer_norm_rows(ctx[t, at, :].astype(F32))
        normed[to, :] = (xhat * g1[...] + b1[...]).astype(BF)

    @pl.when(mine)
    def _():
        for t in range(3):
            c_l(t).wait()

    @pl.when(jnp.logical_not(mine))
    def _():
        for t in range(3):
            rcopy(c_rows(t, z), c_rows(t, z), fs(t, z), fr(t, z), sib).wait_recv()

    def norm_own(t, carry):
        norm_block(t, z)
        return carry

    lax.fori_loop(0, 3, norm_own, 0)
    for x in c_in:
        x.wait()
    sums[4:5, :] = jnp.sum(nms[...].astype(F32), axis=0, keepdims=True)
    for r in range(1, Z):
        zs = lax.rem(z + r, Z)
        for t in range(3):
            c_arrive(t, zs).wait_recv()
            c_fwd(t, zs, c).start()
    for s in range(B):
        @pl.when(B * c + s != z)
        def _():
            for t in range(3):
                for h in range(2):
                    c_z(t, s, h).wait_send()
    for s in range(B):
        here = (B * c + s == z) & mine

        @pl.when(here)
        def _():
            t_l().start()

        @pl.when(jnp.logical_not(here))
        def _():
            t_z(s).start()
    for r in range(1, Z):
        zs = lax.rem(z + r, Z)
        for t in range(3):
            c_fwd(t, zs, 1 - c).wait_recv()

        def norm_one(t, carry, zs=zs):
            norm_block(t, zs)
            return carry

        lax.fori_loop(0, 3, norm_one, 0)
    for j in range(B):
        @pl.when(B * c + j != z)
        def _():
            for a in range(4):
                for k in range(1, Q):
                    w_p(a, j, k, across(q, k)).wait_recv()

    @pl.when(mine)
    def _():
        for a in range(4):
            w_l(a).wait()

    T = 256

    def project(i, carry):
        at = pl.ds(pl.multiple_of(i * T, T), T)
        ks[at, :] = nn_dot(normed[at, :], wks[...]).astype(BF)
        vs[at, :] = nn_dot(normed[at, :], wvs[...]).astype(BF)
        return carry

    lax.fori_loop(0, 3 * S // T, project, 0)

    def project_q(i, carry):
        at = pl.ds(pl.multiple_of(i * T, T), T)
        qs[at, :] = nn_dot(normed[pl.ds(pl.multiple_of(2 * S + i * T, T), T), :], wqs[...]).astype(BF)
        return carry

    lax.fori_loop(0, S // T, project_q, 0)
    x_start(0)

    v_s.wait()
    counts = jnp.where(mine, vc[jz], vco[jz])
    count = counts[0:1, 0:1]
    scale = HEAD_DIM ** (-0.5)
    P2 = 2 * S

    def attend(half, tag):
        r0 = pl.multiple_of(half * N, N)

        def head(h, carry):
            hd = pl.ds(pl.multiple_of(h * HEAD_DIM, HEAD_DIM), HEAD_DIM)
            qh = qs[pl.ds(r0, N), hd]
            s1 = nt_dot(qh, ks[pl.ds(0, P2), hd])
            s2 = nt_dot(qh, ks[pl.ds(P2, S), hd])
            row = lax.broadcasted_iota(jnp.int32, (N, S), 0) + half * N
            col = lax.broadcasted_iota(jnp.int32, (N, S), 1)
            s2 = jnp.where((col <= row) & (col < count), s2, -1e30)
            top = jnp.maximum(jnp.max(s1, axis=-1, keepdims=True), jnp.max(s2, axis=-1, keepdims=True))
            p1 = jnp.exp((s1 - top) * scale)
            p2 = jnp.exp((s2 - top) * scale)
            inv = 1.0 / (jnp.sum(p1, axis=-1, keepdims=True) + jnp.sum(p2, axis=-1, keepdims=True))
            p1 = (p1 * inv).astype(BF)
            p2 = (p2 * inv).astype(BF)
            probs[h, pl.ds(r0, N), pl.ds(0, P2)] = p1
            probs[h, pl.ds(r0, N), pl.ds(P2, S)] = p2
            mix = nn_dot(p1, vs[pl.ds(0, P2), hd]) + nn_dot(p2, vs[pl.ds(P2, S), hd])
            mixed[pl.ds(r0, N), hd] = mix.astype(BF)
            return carry

        lax.fori_loop(0, heads, head, 0)

    hs, hr = al.take(1), al.take(1)
    h_x = rcopy(phalf, got, hs(0), hr(0), sib)
    attend(1 - c, 0)
    phalf[...] = nn_dot(mixed[pl.ds(pl.multiple_of((1 - c) * N, N), N), :], wos[...])
    h_x.start()
    x_start(1)
    for i in range(B):
        @pl.when(jnp.logical_not((B * c + i == z) & mine))
        def _():
            t_arrive(i).wait_recv()

        @pl.when((B * c + i == z) & mine)
        def _():
            t_l().wait()
    tgat.start()
    attend(c, 1)
    own_part = nn_dot(mixed[pl.ds(pl.multiple_of(c * N, N), N), :], wos[...])
    h_x.wait_recv()
    resid[...] = ctx[2, pl.ds(pl.multiple_of(c * N, N), N), :].astype(F32) + (own_part + got[...])
    xhat2, _ = layer_norm_rows(resid[...])
    sec[pl.ds(pl.multiple_of(dp * N, N), N), :] = (xhat2 * g2[...] + b2[...]).astype(BF)

    agat.start()
    sqc = al.take(RATE)
    sqs = [gbuf.at[pl.ds(0, D), :], gbuf.at[pl.ds(D, D), :], dgot]
    sq_x = [lcopy(sq.at[pl.ds(r * D, D), :], sqs[r], sqc(r)) for r in range(RATE)]
    for x in sq_x:
        x.start()
    ss, sr = al.take(Q), al.take(Q)

    def s_x(k):
        return rcopy(rows_at(gbuf, 1 - c)(k, 0, N), stack(got1, 0, N)(k), ss(k), sr(k), sib)

    gsum = PlaneSum(al, peer, rows_at(gbuf, c), N, stack(gh, 0, N // 2), stack(gg, 0, N))
    ffs[...] = jnp.zeros_like(ffs)

    def forward_block(b, bias_row):
        at = pl.ds(pl.multiple_of(b * N, N), N)
        x = nn_dot(sec[at, :], ups[...]) + bias_row
        ga = nt_dot(cots[at, :], downs[...])
        x2 = x * x
        root = 0.7978845608028654
        th = jnp.tanh(root * (x + 0.044715 * (x2 * x)))
        act[at, :] = (0.5 * x * (1.0 + th)).astype(BF)
        slope = 0.5 * (1.0 + th) + 0.5 * x * (1.0 - th * th) * (root * (1.0 + 0.134145 * x2))
        gu = (ga * slope).astype(BF)
        gup[at, :] = gu
        ffs[2:3, pl.ds(0, Z * E)] = ffs[2:3, pl.ds(0, Z * E)] + jnp.sum(gu.astype(F32), axis=0, keepdims=True)
        gbuf[at, :] = nt_dot(gu, ups[...]).astype(BF)
        return bias_row

    def feed(k, bias_row):
        lax.fori_loop(dev(k, 0), dev(k, 0) + 2, forward_block, bias_row)
        s_x(k).start()

    def combine(k):
        s_x(k).wait_recv()
        rows = rows_at(gbuf, c)(k, 0, N)
        rows[...] = (rows[...].astype(F32) + stack(got1, 0, N)(k)[...].astype(F32)).astype(BF)

    groups = S // RATE
    squeezed = None
    for r in range(RATE):
        sq_x[r].wait()
        row = lax.broadcasted_iota(jnp.int32, (ncs.shape[0], S), 0)
        col = lax.broadcasted_iota(jnp.int32, (ncs.shape[0], S), 1)
        pick = jnp.where((col == row * RATE + r) & (row < groups), 1.0, 0.0).astype(BF)
        picked = nn_dot(pick, ctx[1]).astype(BF)
        term = nn_dot(picked, sqs[r][...])
        squeezed = term if squeezed is None else squeezed + term
    ncs[...] = squeezed.astype(BF)
    shift = count + c * N
    new_mem = nn_dot(one_hot((N, S), shift), ctx[1]) + nn_dot(one_hot((N, S), shift - S), ctx[2])
    nms[...] = new_mem.astype(BF)
    third = lax.shift_right_logical(count * 21846, 16)
    shift = third + c * N
    new_comp = nn_dot(one_hot((N, S), shift), ctx[0]) + nn_dot(one_hot((N, ncs.shape[0]), shift - S), ncs[...])
    ncs[pl.ds(0, N), :] = new_comp.astype(BF)
    per = N // R
    ms, mr, ml = al.take(2, 2), al.take(2, B), al.take(2)
    kept_in = [nms, ncs]
    kept_out = [nm_o, nc_o]

    def keep_x(i, p):
        return rcopy(kept_in[i].at[pl.ds(p * R, R), :], kept_out[i].at[jz], ms(i, p), mr(i, jz), (2 * q + z // B, c * per + p))

    def keep_l(i, p):
        return lcopy(kept_in[i].at[pl.ds(p * R, R), :], kept_out[i].at[jz], ml(i))

    x_forward(0)
    tgat.middle()
    agat.middle()
    tgat.last()
    x_forward(1)
    agat.last()
    for r in range(1, Z):
        u_z(r).wait()
    for i in range(2):
        x_rest(i)
    u_l.wait()
    for x in x_l:
        x.wait()
    tgat.arrivals(rows_at(cots, 1 - c))
    agat.arrivals(rows_at(sec, 1 - c))
    for p in range(per):
        here = (c * per + p == z) & mine

        @pl.when(here)
        def _():
            for i in range(2):
                keep_l(i, p).start()

        @pl.when(jnp.logical_not(here))
        def _():
            for i in range(2):
                keep_x(i, p).start()

    bias = jnp.concatenate([ubs[r] for r in range(Z)], axis=1)
    feed(3, bias)
    feed(1, bias)
    combine(3)
    gsum.start()
    feed(2, bias)
    combine(1)
    feed(0, bias)
    combine(2)
    gsum.middle()

    def up_grad(i, carry):
        at = pl.ds(pl.multiple_of(i * T, T), T)
        gus[at, :] = tn_dot(sec[:, at], gup[...]).astype(BF)
        return carry

    lax.fori_loop(0, D // T, up_grad, 0)
    ys, yr = al.take(2, 6), al.take(2, 4)
    near_r, near_z = 3 - 2 * lax.rem(z, 2), z + 1 - 2 * lax.rem(z, 2)

    def y_own(i, r):
        if i == 0:
            return gus.at[:, pl.ds(pl.multiple_of(r * E, E), E)]
        return gds.at[pl.ds(pl.multiple_of(r * E, E), E), :]

    def y_buf(i, n):
        return (xu, xd)[i].at[n]

    def y_near(i):
        return rcopy(y_own(i, near_r), y_buf(i, 0), ys(i, 0), yr(i, 0), (dp, near_z))

    def y_hand(i, n):
        r = 2 if n == 0 else 1 + 2 * (z // 3)
        return rcopy(y_own(i, r), y_buf(i, 2 + n), ys(i, 2 + n), yr(i, 2 + n), (dp, 1 + z // 3))

    def y_far(i, n):
        r = 5 - 2 * z if n == 0 else 2
        return rcopy(y_own(i, r), y_buf(i, 1), ys(i, 4 + n), yr(i, 1), (dp, lax.rem(z + Z - r, Z)))

    def y_start(i):
        @pl.when(is_end)
        def _():
            for n in range(2):
                y_hand(i, n).start()
        y_near(i).start()

    def y_middle(i):
        @pl.when(jnp.logical_not(is_end))
        def _():
            for n in range(2):
                rcopy(y_buf(i, 2 + n), y_buf(i, 2 + n), ys(i, 2 + n), yr(i, 2 + n), (dp, z)).wait_recv()
                mine_ = y_own(i, 5 - 2 * z if n == 0 else 2)
                mine_[...] = (mine_[...].astype(F32) + y_buf(i, 2 + n)[...].astype(F32)).astype(BF)
                y_far(i, n).start()

    def y_arrive(i):
        for n in range(2):
            rcopy(y_buf(i, n), y_buf(i, n), ys(i, 0), yr(i, n), (dp, z)).wait_recv()

    def y_drain(i):
        y_near(i).wait_send()

        @pl.when(is_end)
        def _():
            for n in range(2):
                y_hand(i, n).wait_send()

        @pl.when(jnp.logical_not(is_end))
        def _():
            for n in range(2):
                y_far(i, n).wait_send()

    ubs_, ubr = al.take(Z), al.take(Z)

    def ub_x(r):
        return rcopy(ffs.at[pl.ds(2, 1), pl.ds(r * E, E)], xb.at[r], ubs_(r), ubr(r), (dp, lax.rem(z + Z - r, Z)))

    y_start(0)
    for r in range(1, Z):
        ub_x(r).start()
    agat.drain()

    def down_rows(b, carry):
        at = pl.ds(pl.multiple_of(b * N, N), N)
        sec[at, :] = nn_dot(act[at, :], downs[...]).astype(BF)
        return carry

    lax.fori_loop(0, 2 * Q, down_rows, 0)
    dss, dsr = al.take(Q), al.take(Q)

    def d_x(k):
        return rcopy(rows_at(sec, 1 - c)(k, 0, N), stack(dgot, 0, N)(k), dss(k), dsr(k), sib)

    dsum = PlaneSum(al, peer, rows_at(sec, c), N, stack(dh, 0, N // 2), stack(dg, 0, N))
    for k in (3, 1, 2, 0):
        d_x(k).start()

    def down_grad(i, carry):
        at = pl.ds(pl.multiple_of(i * T, T), T)
        gds[at, :] = tn_dot(act[:, at], cots[...]).astype(BF)
        return carry

    lax.fori_loop(0, Z * E // T, down_grad, 0)

    y_start(1)
    for k in (3, 1, 2, 0):
        d_x(k).wait_recv()
        rows = rows_at(sec, c)(k, 0, N)
        rows[...] = (rows[...].astype(F32) + stack(dgot, 0, N)(k)[...].astype(F32)).astype(BF)
        if k == 3:
            dsum.start()

    combine(0)
    gsum.arrive()
    C = 64

    def back_rows(i, carry):
        at = pl.ds(pl.multiple_of(i * C, C), C)
        own = pl.ds(pl.multiple_of(dp * N + i * C, C), C)
        gs = gbuf[own, :].astype(F32) + (gg[at, :].astype(F32) + gg[pl.ds(pl.multiple_of(N + i * C, C), C), :].astype(F32))
        xhat, inv = layer_norm_rows(resid[at, :])
        ffs[0:1, :] = ffs[0:1, :] + jnp.sum(gs * xhat, axis=0, keepdims=True)
        ffs[1:2, :] = ffs[1:2, :] + jnp.sum(gs, axis=0, keepdims=True)
        e = gs * g2[...]
        m1 = jnp.mean(e, axis=-1, keepdims=True)
        m2 = jnp.mean(e * xhat, axis=-1, keepdims=True)
        gr = cots[own, :].astype(F32) + inv * (e - m1 - xhat * m2)
        got[at, :] = gr
        glow[pl.ds(pl.multiple_of(c * N + i * C, C), C), :] = gr.astype(BF)
        return carry

    lax.fori_loop(0, N // C, back_rows, 0)
    ls_, lr_ = al.take(1), al.take(1)

    def far_x(half):
        rows = glow.at[pl.ds(pl.multiple_of(half * N, N), N), :]
        return rcopy(rows, rows, ls_(0), lr_(0), sib)

    far_x(c).start()
    for x in (tgat, gsum):
        x.drain()
    for k in range(Q):
        s_x(k).wait_send()
    h_x.wait_send()

    @pl.when(mine)
    def _():
        for t in range(3):
            c_sib(t).wait_send()
    for r in range(1, Z):
        for t in range(3):
            c_fwd(t, lax.rem(z + r, Z), c).wait_send()
    for i in range(2):
        x_drain(i)
    for p in partners:
        pl.semaphore_signal(ready, inc=1, device_id=p, device_id_type=MESH)
    far_x(1 - c).wait_recv()

    W = B * H
    hj = H // HEAD_DIM
    M = D // Q
    gms, gqs, gkv = gup.at[pl.ds(0, S), :], gup.at[pl.ds(S, S), :], act.at[pl.ds(0, 3 * S), :]
    gos = gbuf.at[pl.ds(0, W), :]
    tgs, outs = ctx.at[0, pl.ds(0, N), :], ctx.at[0, pl.ds(N, N), :]
    small1 = ctx.at[1]
    odone = stack(small1, 2 * S // 2 - B * OR, OR)
    wdone = stack(downs, 0, M, 3 * H)
    zb, zo = stack(got1, 0, M, 3 * H), stack(gg, 0, OR)
    wfin, ofin = gg.at[pl.ds(N, M), pl.ds(0, 3 * H)], gh.at[pl.ds(0, OR), :]

    def mix_rows(i, carry):
        at = pl.ds(pl.multiple_of(i * T, T), T)
        gms[at, :] = nt_dot(glow[at, :], wos[...]).astype(BF)
        gos[at, :] = tn_dot(mixed[:, at], glow[...]).astype(BF)
        return carry

    lax.fori_loop(0, S // T, mix_rows, 0)

    def o_blk(j):
        def blk(k, lo, n):
            return gos.at[pl.ds(pl.multiple_of(j * H + across(q, k) * OR + lo, n), n), :]
        return blk

    def w_blk(j):
        def blk(k, lo, n):
            return cots.at[pl.ds(pl.multiple_of(j * D + across(q, k) * M + lo, n), n), pl.ds(0, 3 * H)]
        return blk

    osum = [
        PlaneSum(al, peer, o_blk(j), OR, stack(small1, j * OR, OR // 2), stack(small1, B * OR + 2 * j * OR, OR)) for j in range(B)
    ]
    wsum = [
        PlaneSum(al, peer, w_blk(j), M, stack(gbuf, W + 2 * B * M + j * M, M // 2, 3 * H), stack(gbuf, W + 2 * j * M, M, 3 * H))
        for j in range(B)
    ]
    pl.semaphore_wait(ready, len(partners))
    for x in osum:
        x.start()
    arow[...] = jnp.zeros_like(arow)

    def back_head(h, hh):
        hd = pl.ds(h * HEAD_DIM, HEAD_DIM)
        ko = pl.ds(hh * HEAD_DIM, HEAD_DIM)
        vo = pl.ds(H + hh * HEAD_DIM, HEAD_DIM)
        p = probs[h]
        gm = gms[:, hd]
        gp = nt_dot(gm, vs[:, hd])
        delta = jnp.sum(gm.astype(F32) * mixed[:, hd].astype(F32), axis=-1, keepdims=True)
        gs = (p.astype(F32) * (gp - delta)).astype(BF)
        gqs[:, hd] = (scale * nn_dot(gs, ks[:, hd])).astype(BF)
        gkv[:, ko] = (scale * tn_dot(gs, qs[:, hd])).astype(BF)
        gkv[:, vo] = tn_dot(p, gm).astype(BF)

    def split_rows(v):
        hi = v.astype(BF)
        rest = v - hi.astype(F32)
        mid = rest.astype(BF)
        low = (rest - mid.astype(F32)).astype(BF)
        return jnp.concatenate([hi, mid, low, jnp.zeros((5, v.shape[1]), BF)], axis=0)

    def weights(j):
        js = pl.ds(j * H, H)

        def rows(i, carry):
            at = pl.ds(pl.multiple_of(i * T, T), T)
            kv = tn_dot(normed[:, at], gkv[...])
            gq = tn_dot(normed[pl.ds(2 * S, S), at], gqs[:, js])
            to = pl.ds(pl.multiple_of(j * D + i * T, T), T)
            cots[to, pl.ds(0, 2 * H)] = kv.astype(BF)
            cots[to, pl.ds(2 * H, H)] = gq.astype(BF)
            t = (kv[:, :H] * wks[at, js].astype(F32) + kv[:, H:] * wvs[at, js].astype(F32) + gq * wqs[at, js].astype(F32))
            arow[at, :] = arow[at, :] + jnp.broadcast_to(jnp.sum(t, axis=-1, keepdims=True), (T, 128))
            return carry

        lax.fori_loop(0, D // T, rows, 0)
        wsum[j].start()
        skv = split_rows(jnp.sum(gkv[...].astype(F32), axis=0, keepdims=True))
        sq_ = split_rows(jnp.sum(gqs[:, js].astype(F32), axis=0, keepdims=True))
        b = nt_dot(skv[:, :H], wks[:, js]) + nt_dot(skv[:, H:], wvs[:, js]) + nt_dot(sq_, wqs[:, js])
        sums[1:2, :] = sums[1:2, :] + jnp.sum(b, axis=0, keepdims=True)

    for h in range(hj):
        back_head(h, h)

    def token_rows(j, half):
        js = pl.ds(j * H, H)
        rows = pl.ds(pl.multiple_of(half * N, N), N)
        krows = pl.ds(pl.multiple_of(2 * S + half * N, N), N)
        return (nt_dot(gkv[krows, pl.ds(0, H)], wks[:, js]) + nt_dot(gkv[krows, pl.ds(H, H)], wvs[:, js])
                + nt_dot(gqs[rows, js], wqs[:, js]))

    for x in osum:
        x.middle()
    weights(0)
    dsum.middle()
    y_middle(0)
    phalf[...] = token_rows(0, 1 - c)
    srow[...] = token_rows(0, c)
    for h in range(hj, 2 * hj):
        back_head(h, h - hj)
    wsum[0].middle()
    y_middle(1)
    weights(1)
    phalf[...] = phalf[...] + token_rows(1, 1 - c)
    ts_, tr_ = al.take(1), al.take(1)
    t_x = rcopy(phalf, ggot, ts_(0), tr_(0), sib)
    t_x.start()
    srow[...] = srow[...] + token_rows(1, c)

    acol = jnp.swapaxes(arow[...], 0, 1)[0:1, :]
    bsum = sums[1:2, :]
    sums[0:1, :] = (acol - b1[...] * bsum) / g1[...]
    sums[2:3, :] = ffs[0:1, :]
    sums[3:4, :] = ffs[1:2, :]
    n1, n2 = al.take(1), al.take(1)
    v_x = rcopy(sums, sgot, n1(0), n2(0), sib)
    v_x.start()
    ozs, ozr = al.take(2, B), al.take(2, Z)

    def z_x(i, j):
        src, dst = ((wdone, zb), (odone, zo))[i]
        return rcopy(src(j), dst(z), ozs(i, j), ozr(i, z), (dp, B * c + j))

    def z_arrive(i, zz):
        dst = (zb, zo)[i]
        return rcopy(dst(zz), dst(zz), ozs(i, 0), ozr(i, zz), (dp, z))

    def to_plane(i, j):
        (wdone, odone)[i](j)[...] = (wsum, osum)[i][j].total().astype(BF)

        @pl.when(B * c + j != z)
        def _():
            z_x(i, j).start()

    wsum[1].middle()
    for j in range(B):
        to_plane(1, j)
    t_x.wait_recv()
    def norm_rows(i, carry):
        at = pl.ds(pl.multiple_of(i * C, C), C)
        gn = srow[at, :] + ggot[at, :]
        xhat, inv = layer_norm_rows(ctx[2, pl.ds(pl.multiple_of(c * N + i * C, C), C), :].astype(F32))
        e = gn * g1[...]
        m1 = jnp.mean(e, axis=-1, keepdims=True)
        m2 = jnp.mean(e * xhat, axis=-1, keepdims=True)
        tgs[at, :] = (got[at, :] + inv * (e - m1 - xhat * m2)).astype(BF)
        return carry

    lax.fori_loop(0, N // C, norm_rows, 0)
    rs, rr, rl = al.take(2, 2), al.take(2, B), al.take(2)
    rows_in = [tgs, outs]
    rows_out = [tg_o, out_o]

    def row_x(i, p):
        return rcopy(rows_in[i].at[pl.ds(p * R, R), :], rows_out[i].at[jz], rs(i, p), rr(i, jz), (2 * q + z // B, c * per + p))

    def row_l(i, p):
        return lcopy(rows_in[i].at[pl.ds(p * R, R), :], rows_out[i].at[jz], rl(i))

    def send_rows(i):
        for p in range(per):
            here = (c * per + p == z) & mine

            @pl.when(here)
            def _():
                row_l(i, p).start()

            @pl.when(jnp.logical_not(here))
            def _():
                row_x(i, p).start()

    send_rows(0)
    for i in range(2):
        y_arrive(i)
    fu = y_own(0, 0)[...].astype(F32) + (xu[0].astype(F32) + xu[1].astype(F32))
    fd = y_own(1, 0)[...].astype(F32) + (xd[0].astype(F32) + xd[1].astype(F32))
    fb = ffs[2:3, 0:E]
    for r in range(1, Z):
        ub_x(r).wait_recv()
        fb = fb + xb[r]
    fus, fds = xu.at[2], xd.at[2]
    fus[...] = fu.astype(BF)
    fds[...] = fd.astype(BF)
    fbs[...] = fb

    def u_loc(core):
        def loc(k, lo, n):
            return afu.at[pl.ds(lo, n), pl.ds(pl.multiple_of(dev(k, core) * E, E), E)]
        return loc

    def d_loc(core):
        def loc(k, lo, n):
            return afd.at[pl.ds(pl.multiple_of(dev(k, core) * E + lo, n), n), :]
        return loc

    ugat = PlaneGather(al, peer, sib, u_loc(c), D, own=fus)
    dgat = PlaneGather(al, peer, sib, d_loc(c), E, own=fds)
    fl = al.take(3)
    f_l = [lcopy(fus, u_loc(c)(0, 0, D), fl(0)), lcopy(fds, d_loc(c)(0, 0, E), fl(1))]
    bs, br, bfs, bfr = al.take(Q), al.take(Q), al.take(Q), al.take(Q)

    def b_x(k):
        return rcopy(fbs, aub.at[dp], bs(k), br(k), peer(k))

    def b_arrive(k):
        return rcopy(aub.at[dev(k, c)], aub.at[dev(k, c)], bs(k), br(k), peer(k))

    def b_f(k):
        src = fbs if k == 0 else aub.at[dev(k, c)]
        return rcopy(src, aub.at[dev(k, c)], bfs(k), bfr(k), sib)

    b_l = lcopy(fbs, aub.at[dp], fl(2))
    ugat.start()
    dgat.start()
    for x in f_l:
        x.start()
    b_l.start()
    for k in range(1, Q):
        b_x(k).start()
    b_f(0).start()
    v_x.wait()
    srow[0:8, :] = sums[...] + sgot[...]
    pgot[q] = srow[0:8, :]
    vps, vpr, vzs, vzr = al.take(Q), al.take(Q), al.take(Z), al.take(Z)

    def vp_x(k):
        return rcopy(srow.at[pl.ds(0, 8), :], pgot.at[q], vps(k), vpr(k), peer(k))

    def vp_arrive(k):
        return rcopy(pgot.at[across(q, k)], pgot.at[across(q, k)], vps(k), vpr(k), peer(k))

    def vz_x(r):
        return rcopy(srow.at[pl.ds(8, 8), :], zgot.at[z], vzs(r), vzr(r), (dp, lax.rem(z + r, Z)))

    def vz_arrive(r):
        zz = lax.rem(z + Z - r, Z)
        return rcopy(zgot.at[zz], zgot.at[zz], vzs(r), vzr(r), (dp, z))

    for k in range(1, Q):
        vp_x(k).start()
    outs[...] = (resid[...] + dsum.total() + db[...]).astype(BF)
    send_rows(1)
    to_plane(0, 0)
    for k in range(1, Q):
        vp_arrive(k).wait_recv()
    psum = pgot[0]
    for k in range(1, Q):
        psum = psum + pgot[k]
    srow[8:16, :] = psum
    zgot[z] = psum
    for r in range(1, Z):
        vz_x(r).start()
    to_plane(0, 1)

    def a_loc(ref, n_rows):
        def loc(k, lo, n):
            return ref.at[pl.ds(pl.multiple_of(across(q, k) * n_rows + lo, n), n), :]
        return loc

    wgat = PlaneGather(al, peer, sib, a_loc(aw, M), M, own=wfin)
    ogat = PlaneGather(al, peer, sib, a_loc(ago, OR), OR, own=ofin)
    gl = al.take(2)
    g_l = [lcopy(wfin, a_loc(aw, M)(0, 0, M), gl(0)), lcopy(ofin, a_loc(ago, OR)(0, 0, OR), gl(1))]

    @pl.when(mine)
    def _():
        for i, (fin, done, buf, gat) in ((1, (ofin, odone, zo, ogat)), (0, (wfin, wdone, zb, wgat))):
            for zz in range(Z):
                @pl.when(zz != z)
                def _():
                    z_arrive(i, zz).wait_recv()
            buf(z)[...] = done(jz)[...]
            t = buf(0)[...].astype(F32)
            for zz in range(1, Z):
                t = t + buf(zz)[...].astype(F32)
            fin[...] = t.astype(BF)
            gat.start()
            g_l[1 if i == 1 else 0].start()
    for gat in (ugat, dgat):
        gat.middle()
    for k in range(1, Q):
        b_arrive(k).wait_recv()
        b_f(k).start()
    for r in range(1, Z):
        vz_arrive(r).wait_recv()
    zsum = zgot[0]
    for zz in range(1, Z):
        zsum = zsum + zgot[zz]
    small_o[...] = zsum

    @pl.when(mine)
    def _():
        for gat in (ogat, wgat):
            gat.middle()
    for gat in (ugat, dgat):
        gat.last()

    @pl.when(mine)
    def _():
        for gat in (ogat, wgat):
            gat.last()
    ugat.arrivals(u_loc(1 - c))
    dgat.arrivals(d_loc(1 - c))

    @pl.when(jnp.logical_not(mine))
    def _():
        ogat.arrivals(a_loc(ago, OR))
        wgat.arrivals(a_loc(aw, M))

    for k in range(Q):
        rcopy(aub.at[dev(k, 1 - c)], aub.at[dev(k, 1 - c)], bfs(k), bfr(k), sib).wait_recv()
        b_f(k).wait_send()
        d_x(k).wait_send()
    for k in range(1, Q):
        b_x(k).wait_send()
        vp_x(k).wait_send()
    b_l.wait()
    for x in f_l:
        x.wait()
    for r in range(1, Z):
        vz_x(r).wait_send()
        ub_x(r).wait_send()
    for i in range(2):
        y_drain(i)
    for x in osum + wsum + [dsum, ugat, dgat]:
        x.drain()

    @pl.when(mine)
    def _():
        for x in (ogat, wgat):
            x.drain()
        for x in g_l:
            x.wait()
    t_x.wait_send()
    for j in range(B):
        @pl.when(B * c + j != z)
        def _():
            for i in range(2):
                z_x(i, j).wait_send()
    for p in range(per):
        here = (c * per + p == z) & mine

        @pl.when(here)
        def _():
            for i in range(2):
                row_l(i, p).wait()

        @pl.when(jnp.logical_not(here))
        def _():
            for i in range(2):
                row_x(i, p).wait_send()
    for s in range(B):
        @pl.when(jnp.logical_not((B * c + s == z) & mine))
        def _():
            for i in range(2):
                rcopy(rows_out[i].at[s], rows_out[i].at[s], rs(i, 0), rr(i, s), (dp, z)).wait_recv()
    far_x(c).wait_send()

    @pl.when(mine)
    def _():
        for a in range(4):
            for r in range(1, Z):
                w_z(a, r).wait_send()
    for j in range(B):
        @pl.when(B * c + j != z)
        def _():
            for a in range(4):
                for k in range(1, Q):
                    w_p(a, j, k, q).wait_send()
    for s in range(B):
        @pl.when(jnp.logical_not((B * c + s == z) & mine))
        def _():
            t_z(s).wait_send()
    for p in range(per):
        here = (c * per + p == z) & mine

        @pl.when(here)
        def _():
            for i in range(2):
                keep_l(i, p).wait()

        @pl.when(jnp.logical_not(here))
        def _():
            for i in range(2):
                keep_x(i, p).wait_send()
    for s in range(B):
        @pl.when(jnp.logical_not((B * c + s == z) & mine))
        def _():
            for i in range(2):
                rcopy(kept_out[i].at[s], kept_out[i].at[s], ms(i, 0), mr(i, s), (dp, z)).wait_recv()
    assert al.used <= LAYER_SEMS


def layer(Q, Z, comp, mem, tok, cot, wq, wk, wv, wo, up, down, ub, vc, sq, g1, b1, g2, b2, db):
    B, R, D = tok.shape
    H = wq.shape[1]
    S = R * Z
    N = S // 2
    W = B * H
    heads = W // HEAD_DIM
    E = up.shape[1] // (2 * Q)
    F = E * Z
    rows = 2 * Q * N
    vm = pltpu.VMEM
    return pl.pallas_call(
        functools.partial(layer_kernel, Q, Z),
        out_shape=[
            sds((D, 3 * H), BF), sds((H, D), BF), sds((D, 2 * Q * E), BF), sds((2 * Q * E, D), BF), sds((2 * Q, 1, E), F32),
            sds((8, D), F32), sds((B, R, D), BF), sds((B, R, D), BF), sds((B, R, D), BF), sds((B, R, D), BF),
        ],
        in_specs=[ANY] * 11 + [VM] + [ANY] + [VM] * 5,
        out_specs=[ANY] * 5 + [VM] + [ANY] * 4,
        scratch_shapes=[
            vm((3, S, D), BF), vm((3 * S, D), BF), vm((D, W), BF), vm((D, W), BF), vm((D, W), BF), vm((W, D), BF),
            vm((S, W), BF), vm((3 * S, W), BF), vm((3 * S, W), BF), vm((heads, S, 3 * S), BF), vm((S, W), BF),
            vm((N, D), F32), vm((N, D), F32), vm((N, D), F32), vm((rows, D), BF), vm((rows, D), BF), vm((D, F), BF), vm((F, D), BF),
            vm((Z, 1, E), F32), vm(vc.shape, jnp.int32), vm((rows, F), BF), vm((rows, F), BF), vm((rows, D), BF),
            vm((Q * N, D), BF), vm((N, D), BF), vm((2 * N, D), BF), vm((S, D), BF),
            vm((N, D), BF), vm((N, D), BF), vm((D, F), BF), vm((F, D), BF), vm((Q * N, D), BF), vm((N, D), BF), vm((2 * N, D), BF),
            vm((N, D), F32), vm((N, D), F32),
            vm((4, D, E), BF), vm((4, E, D), BF), vm((Z, 1, E), F32), vm((1, E), F32),
            vm((D, 128), F32), vm((8, D), F32), vm((8, D), F32), vm((8, D), F32),
            vm((Q, 8, D), F32), vm((Z, 8, D), F32),
            DMA((LAYER_SEMS,)), pltpu.SemaphoreType.REGULAR,
        ],
        compiler_params=pltpu.CompilerParams(collective_id=1, has_side_effects=True, vmem_limit_bytes=63 << 20),
        name="layer",
    )(comp, mem, tok, cot, wq, wk, wv, wo, up, down, ub, vc, sq, g1, b1, g2, b2, db)


def chip_device(Q, Z, tokens, memory, compressed, valid_counts, attention_norm_gain, attention_norm_bias,
                query_projection, key_projection, value_projection, out_weight, feedforward_norm_gain,
                feedforward_norm_bias, up_weight, up_bias, down_weight, down_bias, squeeze_weight, cotangent):
    B, R, D = tokens.shape
    H = query_projection.shape[1]
    FL = up_weight.shape[1]
    E = FL // (2 * Q)
    aw, ago, afu, afd, aub, small, o_out, o_tg, o_nm, o_nc = layer(
        Q, Z, compressed, memory, tokens, cotangent, query_projection, key_projection, value_projection, out_weight,
        up_weight, down_weight, up_bias.reshape(2 * Q, 1, E), jnp.broadcast_to(valid_counts[:, None, None], (B, 8, 128)),
        squeeze_weight, attention_norm_gain.reshape(1, D), attention_norm_bias.reshape(1, D),
        feedforward_norm_gain.reshape(1, D), feedforward_norm_bias.reshape(1, D), down_bias.reshape(1, D),
    )
    aw = aw.astype(F32)
    return (
        o_out, o_tg.astype(F32), small[0], small[1], aw[:, 2 * H:], aw[:, :H], aw[:, H:2 * H], ago.astype(F32),
        small[2], small[3], afu.astype(F32), aub.reshape(FL), afd.astype(F32), small[4], o_nm, o_nc,
    )


def solution(mesh):
    in_specs = (
        P("dp", "mp", None),
        P("dp", "mp", None),
        P("dp", "mp", None),
        P("dp"),
        P(),
        P(),
        P(None, "mp"),
        P(None, "mp"),
        P(None, "mp"),
        P("mp", None),
        P(),
        P(),
        P(None, "mp"),
        P("mp"),
        P("mp", None),
        P(),
        P(),
        P("dp", "mp", None),
    )
    out_specs = (
        P("dp", "mp", None),
        P("dp", "mp", None),
        P(),
        P(),
        P(None, "mp"),
        P(None, "mp"),
        P(None, "mp"),
        P("mp", None),
        P(),
        P(),
        P(None, "mp"),
        P("mp"),
        P("mp", None),
        P(),
        P("dp", "mp", None),
        P("dp", "mp", None),
    )
    Q, Z = mesh.shape["dp"] // 2, mesh.shape["mp"]

    def per_device(*args):
        B, R, D = args[0].shape
        H, FL = args[6].shape[1], args[12].shape[1]
        whole = Q == 4 and B == 2 and 2 * B == Z and H % HEAD_DIM == 0 and D % (16 * Q) == 0 and H % (16 * Q) == 0
        if whole and R % 32 == 0 and FL % (256 * Q) == 0:
            return chip_device(Q, Z, *args)
        return general_device(*args)

    return jax.shard_map(
        per_device, mesh=mesh, in_specs=in_specs, out_specs=out_specs, check_vma=False
    )
```

```python
import functools

import jax
import jax.numpy as jnp
from jax import lax
from jax.experimental import pallas as pl
from jax.experimental.pallas import tpu as pltpu
from jax.sharding import PartitionSpec as P

HEAD_DIM = 128
RATE = 3


def apply_layer_norm(rows):
    center = jnp.mean(rows, axis=-1, keepdims=True)
    centered = rows - center
    spread = jnp.mean(centered * centered, axis=-1, keepdims=True)
    inverse_deviation = lax.rsqrt(spread + 1e-05)
    return (centered * inverse_deviation, inverse_deviation)


def norm_backward_pass(input_gradient, standardized_rows, inverse_deviation, scale_factor):
    scaled_rows = input_gradient * scale_factor
    attention_norm_mean = jnp.mean(scaled_rows, axis=-1, keepdims=True)
    feedforward_norm_mean = jnp.mean(scaled_rows * standardized_rows, axis=-1, keepdims=True)
    return inverse_deviation * (
        scaled_rows - attention_norm_mean - standardized_rows * feedforward_norm_mean
    )


def squeeze_rows(old_comp, old_mem, fresh, valid_count, offset, own_rows, squeeze_weight):
    features = old_mem.shape[1]
    joined = jnp.concatenate([old_mem, fresh], axis=0)
    new_memory = lax.dynamic_slice_in_dim(joined, valid_count + offset, own_rows, 0)
    comp_len = old_comp.shape[0]
    evicted = valid_count // RATE
    first_row = evicted + offset
    window_start = jnp.maximum(first_row - comp_len, 0)
    padded = jnp.concatenate(
        [old_mem, jnp.zeros((RATE * own_rows, features), jnp.bfloat16)], axis=0
    )
    window = lax.dynamic_slice_in_dim(padded, window_start * RATE, RATE * own_rows, 0)
    squeezed = jnp.dot(
        window.reshape(own_rows, RATE * features),
        squeeze_weight,
        preferred_element_type=jnp.float32,
    ).astype(jnp.bfloat16)
    positions = first_row + jnp.arange(own_rows)
    from_old = jnp.take(old_comp, jnp.clip(positions, 0, comp_len - 1), axis=0)
    from_new = jnp.take(
        squeezed, jnp.clip(positions - comp_len - window_start, 0, own_rows - 1), axis=0
    )
    new_compressed = jnp.where((positions < comp_len)[:, None], from_old, from_new)
    return (new_memory, new_compressed)


def general_device(
    tokens,
    memory,
    compressed,
    valid_counts,
    attention_norm_gain,
    attention_norm_bias,
    query_projection,
    key_projection,
    value_projection,
    out_weight,
    feedforward_norm_gain,
    feedforward_norm_bias,
    up_weight,
    up_bias,
    down_weight,
    down_bias,
    squeeze_weight,
    cotangent,
):
    batch_segs, own_rows, features = tokens.shape
    offset = lax.axis_index("mp") * own_rows
    old_comp, old_mem, fresh = (
        lax.all_gather(compressed, "mp", axis=1, tiled=True),
        lax.all_gather(memory, "mp", axis=1, tiled=True),
        lax.all_gather(tokens, "mp", axis=1, tiled=True),
    )
    seg_len = fresh.shape[1]
    prior_rows = old_comp.shape[1] + old_mem.shape[1]
    context_tokens = jnp.concatenate([old_comp, old_mem, fresh], axis=1).astype(jnp.float32)
    ctx_len = context_tokens.shape[1]
    standardized_full, inverse_deviation_full = apply_layer_norm(context_tokens)
    normed_rows = (standardized_full * attention_norm_gain + attention_norm_bias).astype(
        jnp.bfloat16
    )
    token_rows_normed = normed_rows[:, prior_rows:]
    queries = jnp.einsum(
        "xhp,pj->xhj", token_rows_normed, query_projection, preferred_element_type=jnp.float32
    ).astype(jnp.bfloat16)
    key_rows = jnp.einsum(
        "xhp,pj->xhj", normed_rows, key_projection, preferred_element_type=jnp.float32
    ).astype(jnp.bfloat16)
    values = jnp.einsum(
        "xhp,pj->xhj", normed_rows, value_projection, preferred_element_type=jnp.float32
    ).astype(jnp.bfloat16)
    local_heads = query_projection.shape[1] // HEAD_DIM
    score_scale = HEAD_DIM ** (-0.5)

    def by_heads(matrix):
        return matrix.reshape(matrix.shape[0], matrix.shape[1], local_heads, HEAD_DIM)

    query_pos = jnp.arange(seg_len)[:, None]
    key_pos = jnp.arange(ctx_len)[None, :] - prior_rows
    allowed = (key_pos[None] < 0) | (key_pos <= query_pos)[None] & (
        key_pos[None] < valid_counts[:, None, None]
    )

    def scores_of(query_in, key_in):
        raw = (
            jnp.einsum(
                "gqhe,gkhe->ghqk",
                by_heads(query_in),
                by_heads(key_in),
                preferred_element_type=jnp.float32,
            )
            * score_scale
        )
        return jnp.where(allowed[:, None], raw, -1e30)

    scores = scores_of(queries, key_rows)
    peak_score = jnp.max(scores, axis=-1, keepdims=True)
    exponent = jnp.exp(scores - peak_score)
    exp_total = jnp.sum(exponent, axis=-1, keepdims=True)
    log_total = peak_score + jnp.log(exp_total)
    probs_low = (exponent / exp_total).astype(jnp.bfloat16)
    mixed_heads = jnp.einsum(
        "ghqk,gkhe->gqhe", probs_low, by_heads(values), preferred_element_type=jnp.float32
    ).astype(jnp.bfloat16)
    mixed_heads = mixed_heads.reshape(batch_segs, seg_len, local_heads * HEAD_DIM)
    partial_attn = jnp.einsum(
        "gsc,cd->gsd", mixed_heads, out_weight, preferred_element_type=jnp.float32
    )
    attention = lax.psum_scatter(partial_attn, "mp", scatter_dimension=1, tiled=True)
    residual_stream = tokens.astype(jnp.float32) + attention
    standardized_feedforward, inverse_deviation_feedforward = apply_layer_norm(residual_stream)
    feedforward_input = (
        standardized_feedforward * feedforward_norm_gain + feedforward_norm_bias
    ).astype(jnp.bfloat16)
    second_all = lax.all_gather(feedforward_input, "mp", axis=1, tiled=True)
    upper_in = (
        jnp.einsum("gsd,df->gsf", second_all, up_weight, preferred_element_type=jnp.float32)
        + up_bias
    )
    active, gelu_back = jax.vjp(jax.nn.gelu, upper_in)
    active_low = active.astype(jnp.bfloat16)
    partial_ffn = jnp.einsum(
        "gsf,fd->gsd", active_low, down_weight, preferred_element_type=jnp.float32
    )
    down_out = lax.psum_scatter(
        partial_ffn.astype(jnp.bfloat16), "mp", scatter_dimension=1, tiled=True
    ).astype(jnp.float32)
    output = (residual_stream + down_out + down_bias).astype(jnp.bfloat16)

    def update_one(comp_seg, mem_seg, fresh_seg, valid_count):
        return squeeze_rows(
            comp_seg, mem_seg, fresh_seg, valid_count, offset, own_rows, squeeze_weight
        )

    new_memory, new_compressed = jax.vmap(update_one)(old_comp, old_mem, fresh, valid_counts)
    output_gradient = cotangent.astype(jnp.float32)
    down_bias_grad = jnp.sum(output_gradient, axis=(0, 1))
    grad_all = lax.all_gather(cotangent, "mp", axis=1, tiled=True)
    down_weight_grad = jnp.einsum(
        "gsf,gsd->fd", active_low, grad_all, preferred_element_type=jnp.float32
    )
    grad_active = jnp.einsum(
        "gsd,fd->gsf", grad_all, down_weight, preferred_element_type=jnp.float32
    )
    grad_upper = gelu_back(grad_active)[0].astype(jnp.bfloat16)
    up_weight_grad = jnp.einsum(
        "gsd,gsf->df", second_all, grad_upper, preferred_element_type=jnp.float32
    )
    up_bias_grad = jnp.sum(grad_upper.astype(jnp.float32), axis=(0, 1))
    partial_second = jnp.einsum(
        "gsf,df->gsd", grad_upper, up_weight, preferred_element_type=jnp.float32
    )
    feedforward_gradient = lax.psum_scatter(partial_second, "mp", scatter_dimension=1, tiled=True)
    feedforward_gain_gradient = jnp.sum(
        feedforward_gradient * standardized_feedforward, axis=(0, 1)
    )
    second_bias_grad = jnp.sum(feedforward_gradient, axis=(0, 1))
    residual_gradient = output_gradient + norm_backward_pass(
        feedforward_gradient,
        standardized_feedforward,
        inverse_deviation_feedforward,
        feedforward_norm_gain,
    )
    grad_resid_all = lax.all_gather(
        residual_gradient.astype(jnp.bfloat16), "mp", axis=1, tiled=True
    )
    out_weight_grad = jnp.einsum(
        "gsc,gsd->cd", mixed_heads, grad_resid_all, preferred_element_type=jnp.float32
    )
    grad_mixed = jnp.einsum(
        "gsd,cd->gsc", grad_resid_all, out_weight, preferred_element_type=jnp.float32
    ).astype(jnp.bfloat16)
    probs_again = jnp.exp(scores_of(queries, key_rows) - log_total)
    grad_probs = jnp.einsum(
        "gqhe,gkhe->ghqk",
        by_heads(grad_mixed),
        by_heads(values),
        preferred_element_type=jnp.float32,
    )
    row_dot = jnp.sum(probs_again * grad_probs, axis=-1, keepdims=True)
    grad_scores = (probs_again * (grad_probs - row_dot)).astype(jnp.bfloat16)
    query_gradient = (
        score_scale
        * jnp.einsum(
            "ghqk,gkhe->gqhe", grad_scores, by_heads(key_rows), preferred_element_type=jnp.float32
        )
    ).astype(jnp.bfloat16)
    key_gradient = (
        score_scale
        * jnp.einsum(
            "ghqk,gqhe->gkhe", grad_scores, by_heads(queries), preferred_element_type=jnp.float32
        )
    ).astype(jnp.bfloat16)
    value_gradient = jnp.einsum(
        "ghqk,gqhe->gkhe",
        probs_again.astype(jnp.bfloat16),
        by_heads(grad_mixed),
        preferred_element_type=jnp.float32,
    ).astype(jnp.bfloat16)
    query_gradient = query_gradient.reshape(batch_segs, seg_len, -1)
    key_gradient = key_gradient.reshape(batch_segs, ctx_len, -1)
    value_gradient = value_gradient.reshape(batch_segs, ctx_len, -1)
    query_weight_grad = jnp.einsum(
        "nja,njr->ar", token_rows_normed, query_gradient, preferred_element_type=jnp.float32
    )
    key_weight_grad = jnp.einsum(
        "nja,njr->ar", normed_rows, key_gradient, preferred_element_type=jnp.float32
    )
    value_weight_grad = jnp.einsum(
        "nja,njr->ar", normed_rows, value_gradient, preferred_element_type=jnp.float32
    )
    partial_normed = jnp.einsum(
        "xmo,qo->xmq", key_gradient, key_projection, preferred_element_type=jnp.float32
    )
    partial_normed = partial_normed + jnp.einsum(
        "xmo,qo->xmq", value_gradient, value_projection, preferred_element_type=jnp.float32
    )
    partial_normed = partial_normed.at[:, prior_rows:].add(
        jnp.einsum(
            "xmo,qo->xmq", query_gradient, query_projection, preferred_element_type=jnp.float32
        )
    )
    partial_normed = partial_normed.reshape(batch_segs, 3, seg_len, features)
    normed_gradient = lax.psum_scatter(
        partial_normed.astype(jnp.bfloat16), "mp", scatter_dimension=2, tiled=True
    ).astype(jnp.float32)
    segment_context = jnp.stack([compressed, memory, tokens], axis=1).astype(jnp.float32)
    standardized_segment, inverse_deviation_segment = apply_layer_norm(segment_context)
    attention_gain_gradient = jnp.sum(normed_gradient * standardized_segment, axis=(0, 1, 2))
    first_bias_grad = jnp.sum(normed_gradient, axis=(0, 1, 2))
    tokens_grad = residual_gradient + norm_backward_pass(
        normed_gradient[:, 2],
        standardized_segment[:, 2],
        inverse_deviation_segment[:, 2],
        attention_norm_gain,
    )
    summed = (
        lax.psum(query_weight_grad.astype(jnp.bfloat16), "dp").astype(jnp.float32),
        lax.psum(key_weight_grad.astype(jnp.bfloat16), "dp").astype(jnp.float32),
        lax.psum(value_weight_grad.astype(jnp.bfloat16), "dp").astype(jnp.float32),
        lax.psum(out_weight_grad.astype(jnp.bfloat16), "dp").astype(jnp.float32),
        lax.psum(up_weight_grad.astype(jnp.bfloat16), "dp").astype(jnp.float32),
        lax.psum(up_bias_grad.astype(jnp.bfloat16), "dp").astype(jnp.float32),
        lax.psum(down_weight_grad.astype(jnp.bfloat16), "dp").astype(jnp.float32),
    )
    norms = lax.psum(
        (
            attention_gain_gradient,
            first_bias_grad,
            feedforward_gain_gradient,
            second_bias_grad,
            down_bias_grad,
        ),
        ("dp", "mp"),
    )
    return (
        output,
        tokens_grad,
        norms[0],
        norms[1],
        summed[0],
        summed[1],
        summed[2],
        summed[3],
        norms[2],
        norms[3],
        summed[4],
        summed[5],
        summed[6],
        norms[4],
        new_memory,
        new_compressed,
    )


BF = jnp.bfloat16
F32 = jnp.float32
MESH = pl.DeviceIdType.MESH
ANY = pl.BlockSpec(memory_space=pl.ANY)
VM = pl.BlockSpec(memory_space=pltpu.VMEM)
DMA = pltpu.SemaphoreType.DMA


def sds(shape, dtype):
    return jax.ShapeDtypeStruct(shape, dtype)


def where_am_i(chips, depth):
    dp = lax.axis_index("dp")
    return dp, lax.rem(dp, 2), dp // 2, lax.axis_index("mp")


def rcopy(src, dst, send, recv, device):
    return pltpu.make_async_remote_copy(
        src_ref=src,
        dst_ref=dst,
        send_sem=send,
        recv_sem=recv,
        device_id=device,
        device_id_type=MESH,
    )


def lcopy(src, dst, sem):
    return pltpu.make_async_copy(src, dst, sem)


def enter(partners):
    barrier = pltpu.get_barrier_semaphore()
    for p in partners:
        pl.semaphore_signal(barrier, inc=1, device_id=p, device_id_type=MESH)
    pl.semaphore_wait(barrier, len(partners))


def across(q, k):
    if k == 0:
        return q
    if k == 1:
        return q + 1 - 2 * lax.rem(q, 2)
    if k == 2:
        return lax.rem(q + 2, 4)
    return 3 - q


def across_by(q, i):
    x, y = lax.rem(q, 2), q // 2
    dx, dy = 1 - lax.rem(i, 2), 1 - i // 2
    return (x + dx - 2 * x * dx) + 2 * (y + dy - 2 * y * dy)


def layer_norm_rows(rows):
    center = jnp.mean(rows, axis=-1, keepdims=True)
    centered = rows - center
    spread = jnp.mean(centered * centered, axis=-1, keepdims=True)
    inv = lax.rsqrt(spread + 1e-05)
    return centered * inv, inv


class Slots:
    def __init__(self, ref):
        self.ref = ref
        self.used = 0

    def take(self, *shape):
        base = self.used
        size = 1
        for n in shape:
            size *= n
        self.used += size

        def at(*index):
            flat = 0
            for n, i in zip(shape, index):
                flat = flat * n + i
            return self.ref.at[base + flat]

        return at


def nt_dot(a, b):
    return lax.dot_general(a, b, (((1,), (1,)), ((), ())), preferred_element_type=F32)


def tn_dot(a, b):
    return lax.dot_general(a, b, (((0,), (0,)), ((), ())), preferred_element_type=F32)


def nn_dot(a, b):
    return jnp.dot(a, b, preferred_element_type=F32)


def one_hot(shape, offset):
    row = lax.broadcasted_iota(jnp.int32, shape, 0)
    col = lax.broadcasted_iota(jnp.int32, shape, 1)
    return jnp.where(col == row + offset, 1.0, 0.0).astype(BF)


def stack(ref, offset, rows, width=None):
    width = ref.shape[-1] if width is None else width

    def view(i):
        return ref.at[pl.ds(pl.multiple_of(offset + i * rows, rows), rows), pl.ds(0, width)]

    return view


class PlaneSum:
    def __init__(self, al, peer, blk, rows, h, g):
        self.peer, self.blk, self.half, self.rows, self.h, self.g = peer, blk, rows // 2, rows, h, g
        self.hs, self.hr, self.gs, self.gr = al.take(2), al.take(2), al.take(2), al.take(2)

    def h_x(self, i):
        return rcopy(self.blk(3, i * self.half, self.half), self.h(i), self.hs(i), self.hr(i), self.peer(i + 1))

    def g_x(self, i):
        return rcopy(self.blk(i + 1, 0, self.rows), self.g(i), self.gs(i), self.gr(i), self.peer(i + 1))

    def start(self):
        for i in range(2):
            self.h_x(i).start()

    def middle(self):
        for i in range(2):
            self.h_x(i).wait_recv()
            mine = self.blk(2 - i, i * self.half, self.half)
            mine[...] = (mine[...].astype(F32) + self.h(i)[...].astype(F32)).astype(BF)
            self.g_x(1 - i).start()

    def arrive(self):
        for i in range(2):
            self.g_x(i).wait_recv()

    def total(self):
        self.arrive()
        own = self.blk(0, 0, self.rows)
        return own[...].astype(F32) + (self.g(0)[...].astype(F32) + self.g(1)[...].astype(F32))

    def drain(self):
        for i in range(2):
            self.h_x(i).wait_send()
            self.g_x(i).wait_send()


class PlaneGather:
    def __init__(self, al, peer, sib, loc, rows, own=None):
        self.peer, self.sib, self.loc, self.half, self.rows = peer, sib, loc, rows // 2, rows
        self.own = own
        self.as_, self.ar, self.hs, self.hr = al.take(2), al.take(2), al.take(2), al.take(2)
        self.fs, self.fr = al.take(4), al.take(4)

    def a_x(self, i, k=0):
        src = self.loc(0, 0, self.rows) if self.own is None else self.own
        return rcopy(src, self.loc(k, 0, self.rows), self.as_(i), self.ar(i), self.peer(i + 1))

    def h_x(self, i, k=None):
        k = 2 - (1 - i) if k is None else k
        rows = self.loc(k, i * self.half, self.half)
        return rcopy(rows, rows, self.hs(i), self.hr(i), self.peer(2 - i))

    def f_x(self, k, other=None):
        src = self.loc(k, 0, self.rows)
        if k == 0 and self.own is not None:
            src = self.own
        dst = self.loc(k, 0, self.rows) if other is None else other(k, 0, self.rows)
        return rcopy(src, dst, self.fs(k), self.fr(k), self.sib)

    def start(self):
        for i in range(2):
            self.a_x(i).start()
        self.f_x(0).start()

    def middle(self):
        for i in range(2):
            rcopy(self.loc(i + 1, 0, self.rows), self.loc(i + 1, 0, self.rows), self.as_(i), self.ar(i), self.peer(1)).wait_recv()
            self.h_x(i).start()
            self.f_x(i + 1).start()

    def last(self):
        for i in range(2):
            self.h_x(i, 3).wait_recv()
        self.f_x(3).start()

    def drain(self):
        for i in range(2):
            self.a_x(i).wait_send()
            self.h_x(i).wait_send()
        for k in range(4):
            self.f_x(k).wait_send()

    def arrivals(self, other):
        for k in range(4):
            rcopy(other(k, 0, self.rows), other(k, 0, self.rows), self.fs(k), self.fr(k), self.sib).wait_recv()


LAYER_SEMS = 600


def layer_kernel(Q, Z, comp, mem, tok, cot, wq, wk, wv, wo, up, down, ub, vc, sq, g1, b1, g2, b2, db,
                 aw, ago, afu, afd, aub, small_o, out_o, tg_o, nm_o, nc_o,
                 ctx, normed, wqs, wks, wvs, wos, qs, ks, vs, probs, mixed, phalf, got, resid, sec, cots, ups, downs,
                 ubs, vco, act, gup, gbuf, got1, gh, gg, glow, nms, ncs, gus, gds, dgot, dh, dg, ggot, srow,
                 xu, xd, xb, fbs, arow, ffs, sums, sgot, pgot, zgot, sems, ready):
    dp, c, q, z = where_am_i(Q, Z)
    sd = dp + 1 - 2 * c
    sib = (sd, z)
    partners = [sib]
    for r in range(1, Z):
        for d in (dp, sd):
            partners.append((d, lax.rem(z + r, Z)))
    for k in range(1, Q):
        partners.append((2 * across(q, k) + c, z))
    enter(partners)
    B, R, D = tok.shape
    H = wq.shape[1]
    QR = D // Q
    OR = H // Q
    HR = R // 2
    S = R * Z
    N = S // 2
    E = up.shape[1] // (2 * Q)
    heads = B * H // HEAD_DIM
    mine = c == z // B
    jz = lax.rem(z, B)
    al = Slots(sems)

    def peer(k):
        return (2 * across(q, k) + c, z)

    wins = [wq, wk, wv, wo]
    wss = [wqs, wks, wvs, wos]

    def piece(a):
        if a < 3:
            return wins[a].at[pl.ds(q * QR, QR), :]
        return wo.at[pl.ds(q * OR, OR), :]

    def place(a, j, qq):
        if a < 3:
            return wss[a].at[pl.ds(pl.multiple_of(qq * QR, QR), QR), pl.ds(pl.multiple_of(j * H, H), H)]
        return wos.at[pl.ds(pl.multiple_of(j * H + qq * OR, OR), OR), :]

    def place_whole(a, j):
        if a < 3:
            return wss[a].at[:, pl.ds(pl.multiple_of(j * H, H), H)]
        return wos.at[pl.ds(pl.multiple_of(j * H, H), H), :]

    ws, wr = al.take(4, Z - 1), al.take(4, B)
    ps, pr = al.take(4, B, Q - 1), al.take(4, B, Q - 1)
    wl = al.take(4)

    def w_z(a, r):
        return rcopy(piece(a), place(a, jz, q), ws(a, r - 1), wr(a, jz), (dp, lax.rem(z + r, Z)))

    def w_direct(r):
        zt = lax.rem(z + r, Z)
        return jnp.logical_not((lax.rem(zt, Z - 1) == 0) & (zt // B != z // B))

    wf = al.take(4, B)

    def w_onward(a, j):
        return rcopy(place(a, j, q), place(a, j, q), wf(a, j), wr(a, j), (dp, (Z - 1) * (1 - c)))

    def w_arrive(a, j):
        return rcopy(place(a, j, q), place(a, j, q), ws(a, 0), wr(a, j), (dp, z))

    def w_p(a, j, k, qq):
        return rcopy(place(a, j, qq), place(a, j, qq), ps(a, j, k - 1), pr(a, j, k - 1), peer(k))

    relay = z == 2 - c

    def w_l(a):
        return lcopy(wins[a], place_whole(a, jz), wl(a))

    acts = [comp, mem, tok]
    cs, cr = al.take(3, B, 2), al.take(3, Z)
    fs, fr = al.take(3, Z), al.take(3, Z)
    cl = al.take(3)

    def c_rows(t, zs):
        return ctx.at[t, pl.ds(pl.multiple_of(zs * R, R), R), :]

    def c_half(t, zs, h):
        return ctx.at[t, pl.ds(pl.multiple_of(zs * R + HR * h, HR), HR), :]

    def c_l(t):
        return lcopy(acts[t].at[jz], c_rows(t, z), cl(t))

    def c_sib(t):
        return rcopy(acts[t].at[jz], c_rows(t, z), fs(t, z), fr(t, z), sib)

    def c_z(t, s, h):
        return rcopy(acts[t].at[s, pl.ds(HR * h, HR), :], c_half(t, z, h), cs(t, s, h), cr(t, z), (2 * q + h, B * c + s))

    def c_arrive(t, zs):
        return rcopy(c_half(t, zs, c), c_half(t, zs, c), cs(t, 0, 0), cr(t, zs), (dp, z))

    def c_fwd(t, zs, half):
        return rcopy(c_half(t, zs, half), c_half(t, zs, half), fs(t, zs), fr(t, zs), sib)

    us, ur, ul = al.take(Z - 1), al.take(Z - 1), al.take(1)
    vs_, vr_ = al.take(1), al.take(1)

    def u_z(r):
        return rcopy(ub.at[dp], ubs.at[r], us(r - 1), ur(r - 1), (dp, lax.rem(z + r, Z)))

    u_l = lcopy(ub.at[dp], ubs.at[0], ul(0))
    v_s = rcopy(vc, vco, vs_(0), vr_(0), sib)

    ts, tr, tl = al.take(B), al.take(B), al.take(1)

    def dev(k, core):
        return 2 * across(q, k) + core

    def t_rows(d, i):
        return cots.at[pl.ds(pl.multiple_of(d * N + i * R, R), R), :]

    def t_z(s):
        to = 2 * q + z // B
        return rcopy(cot.at[s], t_rows(to, jz), ts(s), tr(jz), (to, B * c + s))

    def t_l():
        return lcopy(cot.at[jz], t_rows(dp, jz), tl(0))

    def t_arrive(i):
        return rcopy(t_rows(dp, i), t_rows(dp, i), ts(0), tr(i), (dp, z))

    def rows_at(ref, core):
        def loc(k, lo, n):
            return ref.at[pl.ds(pl.multiple_of(dev(k, core) * N + lo, n), n), :]
        return loc

    tgat = PlaneGather(al, peer, sib, rows_at(cots, c), N)
    agat = PlaneGather(al, peer, sib, rows_at(sec, c), N)

    xs, xr_, xl, xf = al.take(2, Z), al.take(2, Z), al.take(2), al.take(2, 2)
    is_end = lax.rem(z, Z - 1) == 0

    def x_place(i, r):
        if i == 0:
            return ups.at[:, pl.ds(r * E, E)]
        return downs.at[pl.ds(r * E, E), :]

    def x_z(i, r):
        src = up.at[:, pl.ds(pl.multiple_of(dp * E, E), E)] if i == 0 else down.at[pl.ds(pl.multiple_of(dp * E, E), E), :]
        return rcopy(src, x_place(i, r), xs(i, r), xr_(i, r), (dp, lax.rem(z + r, Z)))

    def x_direct(r):
        return (z < Z - 1, is_end, z > 0)[r - 1]

    def x_start(i):
        for r in range(1, Z):
            @pl.when(x_direct(r))
            def _():
                x_z(i, r).start()

    onward = ((2, 3, ((2, 3), (1, 2)), 3), (1, 0, ((2, 1), (3, 2)), 1))

    def x_onward(i, n, to, a, b):
        return rcopy(x_place(i, a), x_place(i, b), xf(i, n), xr_(i, b), (dp, to))

    def x_forward(i):
        for at, to, pairs, rest in onward:
            @pl.when(z == at)
            def _():
                for n, (a, b) in enumerate(pairs):
                    x_z(i, a).wait_recv()
                    x_onward(i, n, to, a, b).start()

    def x_rest(i):
        for at, to, pairs, rest in onward:
            @pl.when(z == at)
            def _():
                x_z(i, rest).wait_recv()

        @pl.when(is_end)
        def _():
            for r in range(1, Z):
                x_z(i, r).wait_recv()

    def x_drain(i):
        for r in range(1, Z):
            @pl.when(x_direct(r))
            def _():
                x_z(i, r).wait_send()
        for at, to, pairs, rest in onward:
            @pl.when(z == at)
            def _():
                for n, (a, b) in enumerate(pairs):
                    x_onward(i, n, to, a, b).wait_send()

    x_l = [lcopy(up.at[:, pl.ds(pl.multiple_of(dp * E, E), E)], ups.at[:, pl.ds(0, E)], xl(0)),
           lcopy(down.at[pl.ds(pl.multiple_of(dp * E, E), E), :], downs.at[pl.ds(0, E), :], xl(1))]

    c_sem = al.take(B)
    c_in = [lcopy(cot.at[i], nms.at[pl.ds(i * R, R), :], c_sem(i)) for i in range(B)]

    for x in c_in:
        x.start()
    sums[...] = jnp.zeros_like(sums)
    @pl.when(mine)
    def _():
        for r in range(1, Z):
            @pl.when(w_direct(r))
            def _():
                for a in range(4):
                    w_z(a, r).start()
        for a in range(4):
            w_l(a).start()
        for t in range(3):
            c_l(t).start()
            c_sib(t).start()
    for r in range(1, Z):
        u_z(r).start()
    v_s.start()
    u_l.start()
    for x in x_l:
        x.start()
    for j in range(B):
        @pl.when(B * c + j != z)
        def _():
            for a in range(4):
                w_arrive(a, j).wait_recv()

                @pl.when(relay)
                def _():
                    w_onward(a, j).start()
                for k in range(1, Q):
                    w_p(a, j, k, q).start()
    for s in range(B):
        @pl.when(B * c + s != z)
        def _():
            for t in range(3):
                for h in range(2):
                    c_z(t, s, h).start()

    def norm_block(t, zs):
        at = pl.ds(pl.multiple_of(zs * R, R), R)
        to = pl.ds(pl.multiple_of(t * S + zs * R, R), R)
        xhat, _ = layer_norm_rows(ctx[t, at, :].astype(F32))
        normed[to, :] = (xhat * g1[...] + b1[...]).astype(BF)

    @pl.when(mine)
    def _():
        for t in range(3):
            c_l(t).wait()

    @pl.when(jnp.logical_not(mine))
    def _():
        for t in range(3):
            rcopy(c_rows(t, z), c_rows(t, z), fs(t, z), fr(t, z), sib).wait_recv()

    def norm_own(t, carry):
        norm_block(t, z)
        return carry

    lax.fori_loop(0, 3, norm_own, 0)
    for x in c_in:
        x.wait()
    sums[4:5, :] = jnp.sum(nms[...].astype(F32), axis=0, keepdims=True)
    for r in range(1, Z):
        zs = lax.rem(z + r, Z)
        for t in range(3):
            c_arrive(t, zs).wait_recv()
            c_fwd(t, zs, c).start()
    for s in range(B):
        @pl.when(B * c + s != z)
        def _():
            for t in range(3):
                for h in range(2):
                    c_z(t, s, h).wait_send()
    for s in range(B):
        here = (B * c + s == z) & mine

        @pl.when(here)
        def _():
            t_l().start()

        @pl.when(jnp.logical_not(here))
        def _():
            t_z(s).start()
    x_start(0)
    for r in range(1, Z):
        zs = lax.rem(z + r, Z)
        for t in range(3):
            c_fwd(t, zs, 1 - c).wait_recv()

        def norm_one(t, carry, zs=zs):
            norm_block(t, zs)
            return carry

        lax.fori_loop(0, 3, norm_one, 0)
    for j in range(B):
        @pl.when(B * c + j != z)
        def _():
            for a in range(4):
                for k in range(1, Q):
                    w_p(a, j, k, across(q, k)).wait_recv()

    @pl.when(mine)
    def _():
        for a in range(4):
            w_l(a).wait()

    T = 256

    def project(i, carry):
        at = pl.ds(pl.multiple_of(i * T, T), T)
        ks[at, :] = nn_dot(normed[at, :], wks[...]).astype(BF)
        vs[at, :] = nn_dot(normed[at, :], wvs[...]).astype(BF)
        return carry

    lax.fori_loop(0, 3 * S // T, project, 0)

    def project_q(i, carry):
        at = pl.ds(pl.multiple_of(i * T, T), T)
        qs[at, :] = nn_dot(normed[pl.ds(pl.multiple_of(2 * S + i * T, T), T), :], wqs[...]).astype(BF)
        return carry

    lax.fori_loop(0, S // T, project_q, 0)
    x_start(1)

    v_s.wait()
    counts = jnp.where(mine, vc[jz], vco[jz])
    count = counts[0:1, 0:1]
    scale = HEAD_DIM ** (-0.5)
    P2 = 2 * S

    def attend(half, tag):
        r0 = pl.multiple_of(half * N, N)

        def head(h, carry):
            hd = pl.ds(pl.multiple_of(h * HEAD_DIM, HEAD_DIM), HEAD_DIM)
            qh = qs[pl.ds(r0, N), hd]
            s1 = nt_dot(qh, ks[pl.ds(0, P2), hd])
            s2 = nt_dot(qh, ks[pl.ds(P2, S), hd])
            row = lax.broadcasted_iota(jnp.int32, (N, S), 0) + half * N
            col = lax.broadcasted_iota(jnp.int32, (N, S), 1)
            s2 = jnp.where((col <= row) & (col < count), s2, -1e30)
            top = jnp.maximum(jnp.max(s1, axis=-1, keepdims=True), jnp.max(s2, axis=-1, keepdims=True))
            p1 = jnp.exp((s1 - top) * scale)
            p2 = jnp.exp((s2 - top) * scale)
            inv = 1.0 / (jnp.sum(p1, axis=-1, keepdims=True) + jnp.sum(p2, axis=-1, keepdims=True))
            p1 = (p1 * inv).astype(BF)
            p2 = (p2 * inv).astype(BF)
            probs[h, pl.ds(r0, N), pl.ds(0, P2)] = p1
            probs[h, pl.ds(r0, N), pl.ds(P2, S)] = p2
            mix = nn_dot(p1, vs[pl.ds(0, P2), hd]) + nn_dot(p2, vs[pl.ds(P2, S), hd])
            mixed[pl.ds(r0, N), hd] = mix.astype(BF)
            return carry

        lax.fori_loop(0, heads, head, 0)

    hs, hr = al.take(1), al.take(1)
    h_x = rcopy(phalf, got, hs(0), hr(0), sib)
    attend(1 - c, 0)
    phalf[...] = nn_dot(mixed[pl.ds(pl.multiple_of((1 - c) * N, N), N), :], wos[...])
    h_x.start()
    for i in range(B):
        @pl.when(jnp.logical_not((B * c + i == z) & mine))
        def _():
            t_arrive(i).wait_recv()

        @pl.when((B * c + i == z) & mine)
        def _():
            t_l().wait()
    tgat.start()
    attend(c, 1)
    own_part = nn_dot(mixed[pl.ds(pl.multiple_of(c * N, N), N), :], wos[...])
    x_forward(0)
    h_x.wait_recv()
    resid[...] = ctx[2, pl.ds(pl.multiple_of(c * N, N), N), :].astype(F32) + (own_part + got[...])
    xhat2, _ = layer_norm_rows(resid[...])
    sec[pl.ds(pl.multiple_of(dp * N, N), N), :] = (xhat2 * g2[...] + b2[...]).astype(BF)

    agat.start()
    sqc = al.take(RATE)
    sqs = [gbuf.at[pl.ds(0, D), :], gbuf.at[pl.ds(D, D), :], dgot]
    sq_x = [lcopy(sq.at[pl.ds(r * D, D), :], sqs[r], sqc(r)) for r in range(RATE)]
    for x in sq_x:
        x.start()
    ss, sr = al.take(Q), al.take(Q)

    def s_x(k):
        return rcopy(rows_at(gbuf, 1 - c)(k, 0, N), stack(got1, 0, N)(k), ss(k), sr(k), sib)

    gsum = PlaneSum(al, peer, rows_at(gbuf, c), N, stack(gh, 0, N // 2), stack(gg, 0, N))
    ffs[...] = jnp.zeros_like(ffs)

    def slope_at(b):
        return (b // 4, pl.ds(pl.multiple_of(lax.rem(b // 2, 2) * N, N), N), pl.ds(pl.multiple_of(lax.rem(b, 2) * Z * E, Z * E), Z * E))

    def up_block(b, bias_row):
        at = pl.ds(pl.multiple_of(b * N, N), N)
        x = nn_dot(sec[at, :], ups[...]) + bias_row
        x2 = x * x
        root = 0.7978845608028654
        th = jnp.tanh(root * (x + 0.044715 * (x2 * x)))
        act[at, :] = (0.5 * x * (1.0 + th)).astype(BF)
        slope = 0.5 * (1.0 + th) + 0.5 * x * (1.0 - th * th) * (root * (1.0 + 0.134145 * x2))
        ctx[slope_at(b)] = slope.astype(BF)
        return bias_row

    def back_block(b):
        at = pl.ds(pl.multiple_of(b * N, N), N)
        ga = nt_dot(cots[at, :], downs[...])
        gu = (ga * ctx[slope_at(b)].astype(F32)).astype(BF)
        gup[at, :] = gu
        ffs[2:3, pl.ds(0, Z * E)] = ffs[2:3, pl.ds(0, Z * E)] + jnp.sum(gu.astype(F32), axis=0, keepdims=True)
        gbuf[at, :] = nt_dot(gu, ups[...]).astype(BF)

    def feed(k):
        def half(i, carry):
            back_block(dev(k, 1 - c) + i * (2 * c - 1))

            @pl.when(i == 0)
            def _():
                s_x(k).start()
            return carry

        lax.fori_loop(0, 2, half, 0)

    def combine(k):
        s_x(k).wait_recv()
        rows = rows_at(gbuf, c)(k, 0, N)
        rows[...] = (rows[...].astype(F32) + stack(got1, 0, N)(k)[...].astype(F32)).astype(BF)

    groups = S // RATE
    squeezed = None
    for r in range(RATE):
        sq_x[r].wait()
        row = lax.broadcasted_iota(jnp.int32, (ncs.shape[0], S), 0)
        col = lax.broadcasted_iota(jnp.int32, (ncs.shape[0], S), 1)
        pick = jnp.where((col == row * RATE + r) & (row < groups), 1.0, 0.0).astype(BF)
        picked = nn_dot(pick, ctx[1]).astype(BF)
        term = nn_dot(picked, sqs[r][...])
        squeezed = term if squeezed is None else squeezed + term
    ncs[...] = squeezed.astype(BF)
    shift = count + c * N
    new_mem = nn_dot(one_hot((N, S), shift), ctx[1]) + nn_dot(one_hot((N, S), shift - S), ctx[2])
    nms[...] = new_mem.astype(BF)
    third = lax.shift_right_logical(count * 21846, 16)
    shift = third + c * N
    new_comp = nn_dot(one_hot((N, S), shift), ctx[0]) + nn_dot(one_hot((N, ncs.shape[0]), shift - S), ncs[...])
    ncs[pl.ds(0, N), :] = new_comp.astype(BF)
    per = N // R
    ms, mr, ml = al.take(2, 2), al.take(2, B), al.take(2)
    kept_in = [nms, ncs]
    kept_out = [nm_o, nc_o]

    def keep_x(i, p):
        return rcopy(kept_in[i].at[pl.ds(p * R, R), :], kept_out[i].at[jz], ms(i, p), mr(i, jz), (2 * q + z // B, c * per + p))

    def keep_l(i, p):
        return lcopy(kept_in[i].at[pl.ds(p * R, R), :], kept_out[i].at[jz], ml(i))

    x_forward(1)
    tgat.middle()
    agat.middle()
    tgat.last()
    agat.last()
    for r in range(1, Z):
        u_z(r).wait()
    u_l.wait()

    @pl.when(mine)
    def _():
        for t in range(3):
            c_sib(t).wait_send()
    for r in range(1, Z):
        for t in range(3):
            c_fwd(t, lax.rem(z + r, Z), c).wait_send()
    x_rest(0)
    for x in x_l:
        x.wait()
    agat.arrivals(rows_at(sec, 1 - c))
    lax.fori_loop(0, 2 * Q, up_block, jnp.concatenate([ubs[r] for r in range(Z)], axis=1))
    x_rest(1)
    tgat.arrivals(rows_at(cots, 1 - c))
    for p in range(per):
        here = (c * per + p == z) & mine

        @pl.when(here)
        def _():
            for i in range(2):
                keep_l(i, p).start()

        @pl.when(jnp.logical_not(here))
        def _():
            for i in range(2):
                keep_x(i, p).start()


    feed(3)
    combine(3)
    gsum.start()
    feed(1)
    feed(2)
    combine(1)
    combine(2)
    gsum.middle()
    feed(0)

    def up_grad(i, carry):
        at = pl.ds(pl.multiple_of(i * T, T), T)
        gus[at, :] = tn_dot(sec[:, at], gup[...]).astype(BF)
        return carry

    lax.fori_loop(0, D // T, up_grad, 0)
    ys, yr = al.take(2, 6), al.take(2, 4)
    near_r, near_z = 3 - 2 * lax.rem(z, 2), z + 1 - 2 * lax.rem(z, 2)

    def y_own(i, r):
        if i == 0:
            return gus.at[:, pl.ds(pl.multiple_of(r * E, E), E)]
        return gds.at[pl.ds(pl.multiple_of(r * E, E), E), :]

    def y_buf(i, n):
        return (xu, xd)[i].at[n]

    def y_near(i):
        return rcopy(y_own(i, near_r), y_buf(i, 0), ys(i, 0), yr(i, 0), (dp, near_z))

    def y_hand(i, n):
        r = 2 if n == 0 else 1 + 2 * (z // 3)
        return rcopy(y_own(i, r), y_buf(i, 2 + n), ys(i, 2 + n), yr(i, 2 + n), (dp, 1 + z // 3))

    def y_far(i, n):
        r = 5 - 2 * z if n == 0 else 2
        return rcopy(y_own(i, r), y_buf(i, 1), ys(i, 4 + n), yr(i, 1), (dp, lax.rem(z + Z - r, Z)))

    def y_start(i):
        @pl.when(is_end)
        def _():
            for n in range(2):
                y_hand(i, n).start()
        y_near(i).start()

    def y_middle(i):
        @pl.when(jnp.logical_not(is_end))
        def _():
            for n in range(2):
                rcopy(y_buf(i, 2 + n), y_buf(i, 2 + n), ys(i, 2 + n), yr(i, 2 + n), (dp, z)).wait_recv()
                mine_ = y_own(i, 5 - 2 * z if n == 0 else 2)
                mine_[...] = (mine_[...].astype(F32) + y_buf(i, 2 + n)[...].astype(F32)).astype(BF)
                y_far(i, n).start()

    def y_arrive(i):
        for n in range(2):
            rcopy(y_buf(i, n), y_buf(i, n), ys(i, 0), yr(i, n), (dp, z)).wait_recv()

    def y_drain(i):
        y_near(i).wait_send()

        @pl.when(is_end)
        def _():
            for n in range(2):
                y_hand(i, n).wait_send()

        @pl.when(jnp.logical_not(is_end))
        def _():
            for n in range(2):
                y_far(i, n).wait_send()

    ubs_, ubr = al.take(Z), al.take(Z)

    def ub_x(r):
        return rcopy(ffs.at[pl.ds(2, 1), pl.ds(r * E, E)], xb.at[r], ubs_(r), ubr(r), (dp, lax.rem(z + Z - r, Z)))

    y_start(0)
    for r in range(1, Z):
        ub_x(r).start()
    agat.drain()

    def down_rows(b, carry):
        at = pl.ds(pl.multiple_of(b * N, N), N)
        sec[at, :] = nn_dot(act[at, :], downs[...]).astype(BF)
        return carry

    lax.fori_loop(0, 2 * Q, down_rows, 0)
    dss, dsr = al.take(Q), al.take(Q)

    def d_x(k):
        return rcopy(rows_at(sec, 1 - c)(k, 0, N), stack(dgot, 0, N)(k), dss(k), dsr(k), sib)

    dsum = PlaneSum(al, peer, rows_at(sec, c), N, stack(dh, 0, N // 2), stack(dg, 0, N))
    for k in (3, 1, 2, 0):
        d_x(k).start()

    def down_grad(i, carry):
        at = pl.ds(pl.multiple_of(i * T, T), T)
        gds[at, :] = tn_dot(act[:, at], cots[...]).astype(BF)
        return carry

    lax.fori_loop(0, Z * E // T, down_grad, 0)

    y_start(1)
    for k in (3, 1, 2, 0):
        d_x(k).wait_recv()
        rows = rows_at(sec, c)(k, 0, N)
        rows[...] = (rows[...].astype(F32) + stack(dgot, 0, N)(k)[...].astype(F32)).astype(BF)
    combine(0)
    gsum.arrive()
    dsum.start()
    C = 64

    def back_rows(i, carry):
        at = pl.ds(pl.multiple_of(i * C, C), C)
        own = pl.ds(pl.multiple_of(dp * N + i * C, C), C)
        gs = gbuf[own, :].astype(F32) + (gg[at, :].astype(F32) + gg[pl.ds(pl.multiple_of(N + i * C, C), C), :].astype(F32))
        xhat, inv = layer_norm_rows(resid[at, :])
        ffs[0:1, :] = ffs[0:1, :] + jnp.sum(gs * xhat, axis=0, keepdims=True)
        ffs[1:2, :] = ffs[1:2, :] + jnp.sum(gs, axis=0, keepdims=True)
        e = gs * g2[...]
        m1 = jnp.mean(e, axis=-1, keepdims=True)
        m2 = jnp.mean(e * xhat, axis=-1, keepdims=True)
        gr = cots[own, :].astype(F32) + inv * (e - m1 - xhat * m2)
        got[at, :] = gr
        glow[pl.ds(pl.multiple_of(c * N + i * C, C), C), :] = gr.astype(BF)
        return carry

    lax.fori_loop(0, N // C, back_rows, 0)
    ls_, lr_ = al.take(1), al.take(1)

    def far_x(half):
        rows = glow.at[pl.ds(pl.multiple_of(half * N, N), N), :]
        return rcopy(rows, rows, ls_(0), lr_(0), sib)

    far_x(c).start()
    for x in (tgat, gsum):
        x.drain()
    for k in range(Q):
        s_x(k).wait_send()
    h_x.wait_send()
    for i in range(2):
        x_drain(i)
    for p in partners:
        pl.semaphore_signal(ready, inc=1, device_id=p, device_id_type=MESH)
    far_x(1 - c).wait_recv()

    W = B * H
    hj = H // HEAD_DIM
    M = D // Q
    gms, gqs, gkv = gup.at[pl.ds(0, S), :], gup.at[pl.ds(S, S), :], act.at[pl.ds(0, 3 * S), :]
    gos = gbuf.at[pl.ds(0, W), :]
    tgs, outs = ctx.at[0, pl.ds(0, N), :], ctx.at[0, pl.ds(N, N), :]
    small1 = ctx.at[1]
    odone = stack(small1, 2 * S // 2 - B * OR, OR)
    zo = stack(gg, 0, OR)
    wfin, ofin = gg.at[pl.ds(N, M), pl.ds(0, 3 * H)], gh.at[pl.ds(0, OR), :]

    def mix_rows(i, carry):
        at = pl.ds(pl.multiple_of(i * T, T), T)
        gms[at, :] = nt_dot(glow[at, :], wos[...]).astype(BF)
        gos[at, :] = tn_dot(mixed[:, at], glow[...]).astype(BF)
        return carry

    lax.fori_loop(0, S // T, mix_rows, 0)

    def o_blk(j):
        def blk(k, lo, n):
            return gos.at[pl.ds(pl.multiple_of(j * H + across(q, k) * OR + lo, n), n), :]
        return blk

    M2 = M // 2

    def w_blk(j, half):
        def blk(k, lo, n):
            return cots.at[pl.ds(pl.multiple_of(j * D + across(q, k) * M + half * M2 + lo, n), n), pl.ds(0, 3 * H)]
        return blk

    osum = [
        PlaneSum(al, peer, o_blk(j), OR, stack(small1, j * OR, OR // 2), stack(small1, B * OR + 2 * j * OR, OR)) for j in range(B)
    ]
    wsum = [
        [
            PlaneSum(
                al, peer, w_blk(j, half), M2,
                stack(gbuf, W + 2 * B * M + j * M + half * M2, M2 // 2, 3 * H), stack(gbuf, W + 2 * j * M + half * M, M2, 3 * H),
            )
            for half in range(2)
        ]
        for j in range(B)
    ]
    pl.semaphore_wait(ready, len(partners))
    for x in osum:
        x.start()
    arow[...] = jnp.zeros_like(arow)

    def back_head(h, hh):
        hd = pl.ds(h * HEAD_DIM, HEAD_DIM)
        ko = pl.ds(hh * HEAD_DIM, HEAD_DIM)
        vo = pl.ds(H + hh * HEAD_DIM, HEAD_DIM)
        p = probs[h]
        gm = gms[:, hd]
        gp = nt_dot(gm, vs[:, hd])
        delta = jnp.sum(gm.astype(F32) * mixed[:, hd].astype(F32), axis=-1, keepdims=True)
        gs = (p.astype(F32) * (gp - delta)).astype(BF)
        gqs[:, hd] = (scale * nn_dot(gs, ks[:, hd])).astype(BF)
        gkv[:, ko] = (scale * tn_dot(gs, qs[:, hd])).astype(BF)
        gkv[:, vo] = tn_dot(p, gm).astype(BF)

    def split_rows(v):
        hi = v.astype(BF)
        rest = v - hi.astype(F32)
        mid = rest.astype(BF)
        low = (rest - mid.astype(F32)).astype(BF)
        return jnp.concatenate([hi, mid, low, jnp.zeros((5, v.shape[1]), BF)], axis=0)

    def weights(j):
        js = pl.ds(j * H, H)

        def rows(i, carry):
            to_chip = across_by(q, i)
            at = pl.ds(pl.multiple_of(to_chip * M, M), M)
            kv = tn_dot(normed[:, at], gkv[...])
            gq = tn_dot(normed[pl.ds(2 * S, S), at], gqs[:, js])
            to = pl.ds(pl.multiple_of(j * D + to_chip * M, M), M)
            cots[to, pl.ds(0, 2 * H)] = kv.astype(BF)
            cots[to, pl.ds(2 * H, H)] = gq.astype(BF)
            t = (kv[:, :H] * wks[at, js].astype(F32) + kv[:, H:] * wvs[at, js].astype(F32) + gq * wqs[at, js].astype(F32))
            arow[at, :] = arow[at, :] + jnp.broadcast_to(jnp.sum(t, axis=-1, keepdims=True), (M, 128))

            @pl.when(i == 0)
            def _():
                for x in wsum[j]:
                    x.start()
            return carry

        lax.fori_loop(0, Q, rows, 0)
        skv = split_rows(jnp.sum(gkv[...].astype(F32), axis=0, keepdims=True))
        sq_ = split_rows(jnp.sum(gqs[:, js].astype(F32), axis=0, keepdims=True))
        b = nt_dot(skv[:, :H], wks[:, js]) + nt_dot(skv[:, H:], wvs[:, js]) + nt_dot(sq_, wqs[:, js])
        sums[1:2, :] = sums[1:2, :] + jnp.sum(b, axis=0, keepdims=True)

    for h in range(hj):
        back_head(h, h)

    def token_rows(j, half):
        js = pl.ds(j * H, H)
        rows = pl.ds(pl.multiple_of(half * N, N), N)
        krows = pl.ds(pl.multiple_of(2 * S + half * N, N), N)
        return (nt_dot(gkv[krows, pl.ds(0, H)], wks[:, js]) + nt_dot(gkv[krows, pl.ds(H, H)], wvs[:, js])
                + nt_dot(gqs[rows, js], wqs[:, js]))

    for x in osum:
        x.middle()
    weights(0)
    dsum.middle()
    y_middle(0)
    phalf[...] = token_rows(0, 1 - c)
    srow[...] = token_rows(0, c)
    for h in range(hj, 2 * hj):
        back_head(h, h - hj)
    for x in wsum[0]:
        x.middle()
    y_middle(1)
    weights(1)
    phalf[...] = phalf[...] + token_rows(1, 1 - c)
    ts_, tr_ = al.take(1), al.take(1)
    t_x = rcopy(phalf, ggot, ts_(0), tr_(0), sib)
    t_x.start()
    srow[...] = srow[...] + token_rows(1, c)
    rs, rr, rl = al.take(2, 2), al.take(2, B), al.take(2)
    rows_in = [tgs, outs]
    rows_out = [tg_o, out_o]

    def row_x(i, p):
        return rcopy(rows_in[i].at[pl.ds(p * R, R), :], rows_out[i].at[jz], rs(i, p), rr(i, jz), (2 * q + z // B, c * per + p))

    def row_l(i, p):
        return lcopy(rows_in[i].at[pl.ds(p * R, R), :], rows_out[i].at[jz], rl(i))

    def send_rows(i):
        for p in range(per):
            here = (c * per + p == z) & mine

            @pl.when(here)
            def _():
                row_l(i, p).start()

            @pl.when(jnp.logical_not(here))
            def _():
                row_x(i, p).start()

    outs[...] = (resid[...] + dsum.total() + db[...]).astype(BF)
    send_rows(1)
    ozs, ozr = al.take(3, B), al.take(3, Z)

    def z_buf(i, zz):
        if i == 2:
            return zo(zz)
        return got1.at[pl.ds(pl.multiple_of(zz * M + i * M2, M2), M2), pl.ds(0, 3 * H)]

    def z_done(i, j):
        if i == 2:
            return odone(j)
        return downs.at[pl.ds(pl.multiple_of(j * M + i * M2, M2), M2), pl.ds(0, 3 * H)]

    def z_x(i, j):
        return rcopy(z_done(i, j), z_buf(i, z), ozs(i, j), ozr(i, z), (dp, B * c + j))

    def z_arrive(i, zz):
        return rcopy(z_buf(i, zz), z_buf(i, zz), ozs(i, 0), ozr(i, zz), (dp, z))

    def to_plane(i, j):
        z_done(i, j)[...] = (osum[j] if i == 2 else wsum[j][i]).total().astype(BF)

        @pl.when(B * c + j != z)
        def _():
            z_x(i, j).start()

    for j in range(B):
        to_plane(2, j)
    for x in wsum[1]:
        x.middle()
    for half in range(2):
        to_plane(half, 0)
    acol = jnp.swapaxes(arow[...], 0, 1)[0:1, :]
    bsum = sums[1:2, :]
    sums[0:1, :] = (acol - b1[...] * bsum) / g1[...]
    sums[2:3, :] = ffs[0:1, :]
    sums[3:4, :] = ffs[1:2, :]
    n1, n2 = al.take(1), al.take(1)
    v_x = rcopy(sums, sgot, n1(0), n2(0), sib)
    v_x.start()
    t_x.wait_recv()
    def norm_rows(i, carry):
        at = pl.ds(pl.multiple_of(i * C, C), C)
        gn = srow[at, :] + ggot[at, :]
        xhat, inv = layer_norm_rows(ctx[2, pl.ds(pl.multiple_of(c * N + i * C, C), C), :].astype(F32))
        e = gn * g1[...]
        m1 = jnp.mean(e, axis=-1, keepdims=True)
        m2 = jnp.mean(e * xhat, axis=-1, keepdims=True)
        tgs[at, :] = (got[at, :] + inv * (e - m1 - xhat * m2)).astype(BF)
        return carry

    lax.fori_loop(0, N // C, norm_rows, 0)
    for i in range(2):
        y_arrive(i)
    fu = y_own(0, 0)[...].astype(F32) + (xu[0].astype(F32) + xu[1].astype(F32))
    fd = y_own(1, 0)[...].astype(F32) + (xd[0].astype(F32) + xd[1].astype(F32))
    fb = ffs[2:3, 0:E]
    for r in range(1, Z):
        ub_x(r).wait_recv()
        fb = fb + xb[r]
    fus, fds = xu.at[2], xd.at[2]
    fus[...] = fu.astype(BF)
    fds[...] = fd.astype(BF)
    fbs[...] = fb

    def u_loc(core):
        def loc(k, lo, n):
            return afu.at[pl.ds(lo, n), pl.ds(pl.multiple_of(dev(k, core) * E, E), E)]
        return loc

    def d_loc(core):
        def loc(k, lo, n):
            return afd.at[pl.ds(pl.multiple_of(dev(k, core) * E + lo, n), n), :]
        return loc

    ugat = PlaneGather(al, peer, sib, u_loc(c), D, own=fus)
    dgat = PlaneGather(al, peer, sib, d_loc(c), E, own=fds)
    fl = al.take(3)
    f_l = [lcopy(fus, u_loc(c)(0, 0, D), fl(0)), lcopy(fds, d_loc(c)(0, 0, E), fl(1))]
    bs, br, bfs, bfr = al.take(Q), al.take(Q), al.take(Q), al.take(Q)

    def b_x(k):
        return rcopy(fbs, aub.at[dp], bs(k), br(k), peer(k))

    def b_arrive(k):
        return rcopy(aub.at[dev(k, c)], aub.at[dev(k, c)], bs(k), br(k), peer(k))

    def b_f(k):
        src = fbs if k == 0 else aub.at[dev(k, c)]
        return rcopy(src, aub.at[dev(k, c)], bfs(k), bfr(k), sib)

    b_l = lcopy(fbs, aub.at[dp], fl(2))
    v_x.wait()
    srow[0:8, :] = sums[...] + sgot[...]
    pgot[q] = srow[0:8, :]
    vps, vpr, vzs, vzr = al.take(Q), al.take(Q), al.take(Z), al.take(Z)

    def vp_x(k):
        return rcopy(srow.at[pl.ds(0, 8), :], pgot.at[q], vps(k), vpr(k), peer(k))

    def vp_arrive(k):
        return rcopy(pgot.at[across(q, k)], pgot.at[across(q, k)], vps(k), vpr(k), peer(k))

    def vz_x(r):
        return rcopy(srow.at[pl.ds(8, 8), :], zgot.at[z], vzs(r), vzr(r), (dp, lax.rem(z + r, Z)))

    def vz_arrive(r):
        zz = lax.rem(z + Z - r, Z)
        return rcopy(zgot.at[zz], zgot.at[zz], vzs(r), vzr(r), (dp, z))

    for k in range(1, Q):
        vp_x(k).start()
    for k in range(1, Q):
        vp_arrive(k).wait_recv()
    psum = pgot[0]
    for k in range(1, Q):
        psum = psum + pgot[k]
    srow[8:16, :] = psum
    zgot[z] = psum
    for r in range(1, Z):
        vz_x(r).start()
    for half in range(2):
        to_plane(half, 1)
    ugat.start()
    dgat.start()
    for x in f_l:
        x.start()
    b_l.start()
    for k in range(1, Q):
        b_x(k).start()
    b_f(0).start()

    def a_loc(ref, n_rows):
        def loc(k, lo, n):
            return ref.at[pl.ds(pl.multiple_of(across(q, k) * n_rows + lo, n), n), :]
        return loc

    fins = [wfin.at[pl.ds(0, M2), :], wfin.at[pl.ds(M2, M2), :], ofin]

    def half_loc(half):
        def loc(k, lo, n):
            return aw.at[pl.ds(pl.multiple_of(across(q, k) * M + half * M2 + lo, n), n), :]
        return loc

    locs = [half_loc(0), half_loc(1), a_loc(ago, OR)]
    gats = [PlaneGather(al, peer, sib, locs[i], OR if i == 2 else M2, own=fins[i]) for i in range(3)]
    gl = al.take(3)
    g_l = [lcopy(fins[i], locs[i](0, 0, OR if i == 2 else M2), gl(i)) for i in range(3)]
    for gat in (ugat, dgat):
        gat.middle()
    send_rows(0)
    for k in range(1, Q):
        b_arrive(k).wait_recv()
        b_f(k).start()

    @pl.when(mine)
    def _():
        for i in (2, 0, 1):
            for zz in range(Z):
                @pl.when(zz != z)
                def _():
                    z_arrive(i, zz).wait_recv()
            z_buf(i, z)[...] = z_done(i, jz)[...]
            t = z_buf(i, 0)[...].astype(F32)
            for zz in range(1, Z):
                t = t + z_buf(i, zz)[...].astype(F32)
            fins[i][...] = t.astype(BF)
            gats[i].start()
            g_l[i].start()
    for r in range(1, Z):
        vz_arrive(r).wait_recv()
    zsum = zgot[0]
    for zz in range(1, Z):
        zsum = zsum + zgot[zz]
    small_o[...] = zsum

    @pl.when(mine)
    def _():
        for i in (2, 0, 1):
            gats[i].middle()
    for gat in (ugat, dgat):
        gat.last()

    @pl.when(mine)
    def _():
        for i in (2, 0, 1):
            gats[i].last()
    ugat.arrivals(u_loc(1 - c))
    dgat.arrivals(d_loc(1 - c))

    @pl.when(jnp.logical_not(mine))
    def _():
        for i in range(3):
            gats[i].arrivals(locs[i])

    for k in range(Q):
        rcopy(aub.at[dev(k, 1 - c)], aub.at[dev(k, 1 - c)], bfs(k), bfr(k), sib).wait_recv()
        b_f(k).wait_send()
        d_x(k).wait_send()
    for k in range(1, Q):
        b_x(k).wait_send()
        vp_x(k).wait_send()
    b_l.wait()
    for x in f_l:
        x.wait()
    for r in range(1, Z):
        vz_x(r).wait_send()
        ub_x(r).wait_send()
    for i in range(2):
        y_drain(i)
    for x in osum + wsum[0] + wsum[1] + [dsum, ugat, dgat]:
        x.drain()

    @pl.when(mine)
    def _():
        for x in gats:
            x.drain()
        for x in g_l:
            x.wait()
    t_x.wait_send()
    for j in range(B):
        @pl.when(B * c + j != z)
        def _():
            for i in range(3):
                z_x(i, j).wait_send()
    for p in range(per):
        here = (c * per + p == z) & mine

        @pl.when(here)
        def _():
            for i in range(2):
                row_l(i, p).wait()

        @pl.when(jnp.logical_not(here))
        def _():
            for i in range(2):
                row_x(i, p).wait_send()
    for s in range(B):
        @pl.when(jnp.logical_not((B * c + s == z) & mine))
        def _():
            for i in range(2):
                rcopy(rows_out[i].at[s], rows_out[i].at[s], rs(i, 0), rr(i, s), (dp, z)).wait_recv()
    far_x(c).wait_send()

    @pl.when(mine)
    def _():
        for r in range(1, Z):
            @pl.when(w_direct(r))
            def _():
                for a in range(4):
                    w_z(a, r).wait_send()
    for j in range(B):
        @pl.when(B * c + j != z)
        def _():
            for a in range(4):
                @pl.when(relay)
                def _():
                    w_onward(a, j).wait_send()
                for k in range(1, Q):
                    w_p(a, j, k, q).wait_send()
    for s in range(B):
        @pl.when(jnp.logical_not((B * c + s == z) & mine))
        def _():
            t_z(s).wait_send()
    for p in range(per):
        here = (c * per + p == z) & mine

        @pl.when(here)
        def _():
            for i in range(2):
                keep_l(i, p).wait()

        @pl.when(jnp.logical_not(here))
        def _():
            for i in range(2):
                keep_x(i, p).wait_send()
    for s in range(B):
        @pl.when(jnp.logical_not((B * c + s == z) & mine))
        def _():
            for i in range(2):
                rcopy(kept_out[i].at[s], kept_out[i].at[s], ms(i, 0), mr(i, s), (dp, z)).wait_recv()
    assert al.used <= LAYER_SEMS


def layer(Q, Z, comp, mem, tok, cot, wq, wk, wv, wo, up, down, ub, vc, sq, g1, b1, g2, b2, db):
    B, R, D = tok.shape
    H = wq.shape[1]
    S = R * Z
    N = S // 2
    W = B * H
    heads = W // HEAD_DIM
    E = up.shape[1] // (2 * Q)
    F = E * Z
    rows = 2 * Q * N
    vm = pltpu.VMEM
    return pl.pallas_call(
        functools.partial(layer_kernel, Q, Z),
        out_shape=[
            sds((D, 3 * H), BF), sds((H, D), BF), sds((D, 2 * Q * E), BF), sds((2 * Q * E, D), BF), sds((2 * Q, 1, E), F32),
            sds((8, D), F32), sds((B, R, D), BF), sds((B, R, D), BF), sds((B, R, D), BF), sds((B, R, D), BF),
        ],
        in_specs=[ANY] * 11 + [VM] + [ANY] + [VM] * 5,
        out_specs=[ANY] * 5 + [VM] + [ANY] * 4,
        scratch_shapes=[
            vm((3, S, D), BF), vm((3 * S, D), BF), vm((D, W), BF), vm((D, W), BF), vm((D, W), BF), vm((W, D), BF),
            vm((S, W), BF), vm((3 * S, W), BF), vm((3 * S, W), BF), vm((heads, S, 3 * S), BF), vm((S, W), BF),
            vm((N, D), F32), vm((N, D), F32), vm((N, D), F32), vm((rows, D), BF), vm((rows, D), BF), vm((D, F), BF), vm((F, D), BF),
            vm((Z, 1, E), F32), vm(vc.shape, jnp.int32), vm((rows, F), BF), vm((rows, F), BF), vm((rows, D), BF),
            vm((Q * N, D), BF), vm((N, D), BF), vm((2 * N, D), BF), vm((S, D), BF),
            vm((N, D), BF), vm((N, D), BF), vm((D, F), BF), vm((F, D), BF), vm((Q * N, D), BF), vm((N, D), BF), vm((2 * N, D), BF),
            vm((N, D), F32), vm((N, D), F32),
            vm((4, D, E), BF), vm((4, E, D), BF), vm((Z, 1, E), F32), vm((1, E), F32),
            vm((D, 128), F32), vm((8, D), F32), vm((8, D), F32), vm((8, D), F32),
            vm((Q, 8, D), F32), vm((Z, 8, D), F32),
            DMA((LAYER_SEMS,)), pltpu.SemaphoreType.REGULAR,
        ],
        compiler_params=pltpu.CompilerParams(collective_id=1, has_side_effects=True, vmem_limit_bytes=63 << 20),
        name="layer",
    )(comp, mem, tok, cot, wq, wk, wv, wo, up, down, ub, vc, sq, g1, b1, g2, b2, db)


def convert_kernel(w, wo, u, d, t, a0, a1, a2, gk, gv, gq, go, gu, gd, gt, b0, b1, b2):
    h = gk.shape[1]
    for i, out in enumerate((gk, gv, gq)):
        out[...] = w[:, i * h:(i + 1) * h].astype(F32)
    for src, out in ((wo, go), (u, gu), (d, gd), (t, gt)):
        out[...] = src[...].astype(F32)
    for src, out in ((a0, b0), (a1, b1), (a2, b2)):
        out[...] = src[...]


def convert(w, wo, u, d, *rows):
    steps = 8
    H = w.shape[1] // 3
    D = rows[0].shape[2]
    flat = [r.reshape(-1, D) for r in rows]

    def spec(a, cols=None):
        return pl.BlockSpec((a.shape[0] // steps, a.shape[1] if cols is None else cols), lambda i: (i, 0))

    ins = [w, wo, u, d] + flat
    shapes = [sds((w.shape[0], H), F32)] * 3 + [sds(a.shape, F32) for a in (wo, u, d, flat[0])] + [sds(a.shape, BF) for a in flat[1:]]
    out = pl.pallas_call(
        convert_kernel,
        grid=(steps,),
        out_shape=shapes,
        in_specs=[spec(a) for a in ins],
        out_specs=[spec(a) for a in shapes],
        compiler_params=pltpu.CompilerParams(vmem_limit_bytes=63 << 20),
        name="convert",
    )(*ins)
    return list(out[:6]) + [o.reshape(rows[0].shape) for o in out[6:]]


def chip_device(Q, Z, tokens, memory, compressed, valid_counts, attention_norm_gain, attention_norm_bias,
                query_projection, key_projection, value_projection, out_weight, feedforward_norm_gain,
                feedforward_norm_bias, up_weight, up_bias, down_weight, down_bias, squeeze_weight, cotangent):
    B, R, D = tokens.shape
    H = query_projection.shape[1]
    FL = up_weight.shape[1]
    E = FL // (2 * Q)
    aw, ago, afu, afd, aub, small, o_out, o_tg, o_nm, o_nc = layer(
        Q, Z, compressed, memory, tokens, cotangent, query_projection, key_projection, value_projection, out_weight,
        up_weight, down_weight, up_bias.reshape(2 * Q, 1, E), jnp.broadcast_to(valid_counts[:, None, None], (B, 8, 128)),
        squeeze_weight, attention_norm_gain.reshape(1, D), attention_norm_bias.reshape(1, D),
        feedforward_norm_gain.reshape(1, D), feedforward_norm_bias.reshape(1, D), down_bias.reshape(1, D),
    )
    gk, gv, gq, go, gu, gd, g_tokens, out, new_mem, new_comp = convert(aw, ago, afu, afd, o_tg, o_out, o_nm, o_nc)
    return (
        out, g_tokens, small[0], small[1], gq, gk, gv, go, small[2], small[3], gu, aub.reshape(FL), gd, small[4], new_mem, new_comp,
    )


def solution(mesh):
    in_specs = (
        P("dp", "mp", None),
        P("dp", "mp", None),
        P("dp", "mp", None),
        P("dp"),
        P(),
        P(),
        P(None, "mp"),
        P(None, "mp"),
        P(None, "mp"),
        P("mp", None),
        P(),
        P(),
        P(None, "mp"),
        P("mp"),
        P("mp", None),
        P(),
        P(),
        P("dp", "mp", None),
    )
    out_specs = (
        P("dp", "mp", None),
        P("dp", "mp", None),
        P(),
        P(),
        P(None, "mp"),
        P(None, "mp"),
        P(None, "mp"),
        P("mp", None),
        P(),
        P(),
        P(None, "mp"),
        P("mp"),
        P("mp", None),
        P(),
        P("dp", "mp", None),
        P("dp", "mp", None),
    )
    Q, Z = mesh.shape["dp"] // 2, mesh.shape["mp"]

    def per_device(*args):
        B, R, D = args[0].shape
        H, FL = args[6].shape[1], args[12].shape[1]
        whole = Q == 4 and B == 2 and 2 * B == Z and H % HEAD_DIM == 0 and D % (16 * Q) == 0 and H % (16 * Q) == 0
        if whole and R % 32 == 0 and FL % (256 * Q) == 0:
            return chip_device(Q, Z, *args)
        return general_device(*args)

    return jax.shard_map(
        per_device, mesh=mesh, in_specs=in_specs, out_specs=out_specs, check_vma=False
    )
```

```python
import functools

import jax
import jax.numpy as jnp
from jax import lax
from jax.experimental import pallas as pl
from jax.experimental.pallas import tpu as pltpu
from jax.sharding import PartitionSpec as P

HEAD_DIM = 128
RATE = 3


def apply_layer_norm(rows):
    center = jnp.mean(rows, axis=-1, keepdims=True)
    centered = rows - center
    spread = jnp.mean(centered * centered, axis=-1, keepdims=True)
    inverse_deviation = lax.rsqrt(spread + 1e-05)
    return (centered * inverse_deviation, inverse_deviation)


def norm_backward_pass(input_gradient, standardized_rows, inverse_deviation, scale_factor):
    scaled_rows = input_gradient * scale_factor
    attention_norm_mean = jnp.mean(scaled_rows, axis=-1, keepdims=True)
    feedforward_norm_mean = jnp.mean(scaled_rows * standardized_rows, axis=-1, keepdims=True)
    return inverse_deviation * (
        scaled_rows - attention_norm_mean - standardized_rows * feedforward_norm_mean
    )


def squeeze_rows(old_comp, old_mem, fresh, valid_count, offset, own_rows, squeeze_weight):
    features = old_mem.shape[1]
    joined = jnp.concatenate([old_mem, fresh], axis=0)
    new_memory = lax.dynamic_slice_in_dim(joined, valid_count + offset, own_rows, 0)
    comp_len = old_comp.shape[0]
    evicted = valid_count // RATE
    first_row = evicted + offset
    window_start = jnp.maximum(first_row - comp_len, 0)
    padded = jnp.concatenate(
        [old_mem, jnp.zeros((RATE * own_rows, features), jnp.bfloat16)], axis=0
    )
    window = lax.dynamic_slice_in_dim(padded, window_start * RATE, RATE * own_rows, 0)
    squeezed = jnp.dot(
        window.reshape(own_rows, RATE * features),
        squeeze_weight,
        preferred_element_type=jnp.float32,
    ).astype(jnp.bfloat16)
    positions = first_row + jnp.arange(own_rows)
    from_old = jnp.take(old_comp, jnp.clip(positions, 0, comp_len - 1), axis=0)
    from_new = jnp.take(
        squeezed, jnp.clip(positions - comp_len - window_start, 0, own_rows - 1), axis=0
    )
    new_compressed = jnp.where((positions < comp_len)[:, None], from_old, from_new)
    return (new_memory, new_compressed)


def general_device(
    tokens,
    memory,
    compressed,
    valid_counts,
    attention_norm_gain,
    attention_norm_bias,
    query_projection,
    key_projection,
    value_projection,
    out_weight,
    feedforward_norm_gain,
    feedforward_norm_bias,
    up_weight,
    up_bias,
    down_weight,
    down_bias,
    squeeze_weight,
    cotangent,
):
    batch_segs, own_rows, features = tokens.shape
    offset = lax.axis_index("mp") * own_rows
    old_comp, old_mem, fresh = (
        lax.all_gather(compressed, "mp", axis=1, tiled=True),
        lax.all_gather(memory, "mp", axis=1, tiled=True),
        lax.all_gather(tokens, "mp", axis=1, tiled=True),
    )
    seg_len = fresh.shape[1]
    prior_rows = old_comp.shape[1] + old_mem.shape[1]
    context_tokens = jnp.concatenate([old_comp, old_mem, fresh], axis=1).astype(jnp.float32)
    ctx_len = context_tokens.shape[1]
    standardized_full, inverse_deviation_full = apply_layer_norm(context_tokens)
    normed_rows = (standardized_full * attention_norm_gain + attention_norm_bias).astype(
        jnp.bfloat16
    )
    token_rows_normed = normed_rows[:, prior_rows:]
    queries = jnp.einsum(
        "xhp,pj->xhj", token_rows_normed, query_projection, preferred_element_type=jnp.float32
    ).astype(jnp.bfloat16)
    key_rows = jnp.einsum(
        "xhp,pj->xhj", normed_rows, key_projection, preferred_element_type=jnp.float32
    ).astype(jnp.bfloat16)
    values = jnp.einsum(
        "xhp,pj->xhj", normed_rows, value_projection, preferred_element_type=jnp.float32
    ).astype(jnp.bfloat16)
    local_heads = query_projection.shape[1] // HEAD_DIM
    score_scale = HEAD_DIM ** (-0.5)

    def by_heads(matrix):
        return matrix.reshape(matrix.shape[0], matrix.shape[1], local_heads, HEAD_DIM)

    query_pos = jnp.arange(seg_len)[:, None]
    key_pos = jnp.arange(ctx_len)[None, :] - prior_rows
    allowed = (key_pos[None] < 0) | (key_pos <= query_pos)[None] & (
        key_pos[None] < valid_counts[:, None, None]
    )

    def scores_of(query_in, key_in):
        raw = (
            jnp.einsum(
                "gqhe,gkhe->ghqk",
                by_heads(query_in),
                by_heads(key_in),
                preferred_element_type=jnp.float32,
            )
            * score_scale
        )
        return jnp.where(allowed[:, None], raw, -1e30)

    scores = scores_of(queries, key_rows)
    peak_score = jnp.max(scores, axis=-1, keepdims=True)
    exponent = jnp.exp(scores - peak_score)
    exp_total = jnp.sum(exponent, axis=-1, keepdims=True)
    log_total = peak_score + jnp.log(exp_total)
    probs_low = (exponent / exp_total).astype(jnp.bfloat16)
    mixed_heads = jnp.einsum(
        "ghqk,gkhe->gqhe", probs_low, by_heads(values), preferred_element_type=jnp.float32
    ).astype(jnp.bfloat16)
    mixed_heads = mixed_heads.reshape(batch_segs, seg_len, local_heads * HEAD_DIM)
    partial_attn = jnp.einsum(
        "gsc,cd->gsd", mixed_heads, out_weight, preferred_element_type=jnp.float32
    )
    attention = lax.psum_scatter(partial_attn, "mp", scatter_dimension=1, tiled=True)
    residual_stream = tokens.astype(jnp.float32) + attention
    standardized_feedforward, inverse_deviation_feedforward = apply_layer_norm(residual_stream)
    feedforward_input = (
        standardized_feedforward * feedforward_norm_gain + feedforward_norm_bias
    ).astype(jnp.bfloat16)
    second_all = lax.all_gather(feedforward_input, "mp", axis=1, tiled=True)
    upper_in = (
        jnp.einsum("gsd,df->gsf", second_all, up_weight, preferred_element_type=jnp.float32)
        + up_bias
    )
    active, gelu_back = jax.vjp(jax.nn.gelu, upper_in)
    active_low = active.astype(jnp.bfloat16)
    partial_ffn = jnp.einsum(
        "gsf,fd->gsd", active_low, down_weight, preferred_element_type=jnp.float32
    )
    down_out = lax.psum_scatter(
        partial_ffn.astype(jnp.bfloat16), "mp", scatter_dimension=1, tiled=True
    ).astype(jnp.float32)
    output = (residual_stream + down_out + down_bias).astype(jnp.bfloat16)

    def update_one(comp_seg, mem_seg, fresh_seg, valid_count):
        return squeeze_rows(
            comp_seg, mem_seg, fresh_seg, valid_count, offset, own_rows, squeeze_weight
        )

    new_memory, new_compressed = jax.vmap(update_one)(old_comp, old_mem, fresh, valid_counts)
    output_gradient = cotangent.astype(jnp.float32)
    down_bias_grad = jnp.sum(output_gradient, axis=(0, 1))
    grad_all = lax.all_gather(cotangent, "mp", axis=1, tiled=True)
    down_weight_grad = jnp.einsum(
        "gsf,gsd->fd", active_low, grad_all, preferred_element_type=jnp.float32
    )
    grad_active = jnp.einsum(
        "gsd,fd->gsf", grad_all, down_weight, preferred_element_type=jnp.float32
    )
    grad_upper = gelu_back(grad_active)[0].astype(jnp.bfloat16)
    up_weight_grad = jnp.einsum(
        "gsd,gsf->df", second_all, grad_upper, preferred_element_type=jnp.float32
    )
    up_bias_grad = jnp.sum(grad_upper.astype(jnp.float32), axis=(0, 1))
    partial_second = jnp.einsum(
        "gsf,df->gsd", grad_upper, up_weight, preferred_element_type=jnp.float32
    )
    feedforward_gradient = lax.psum_scatter(partial_second, "mp", scatter_dimension=1, tiled=True)
    feedforward_gain_gradient = jnp.sum(
        feedforward_gradient * standardized_feedforward, axis=(0, 1)
    )
    second_bias_grad = jnp.sum(feedforward_gradient, axis=(0, 1))
    residual_gradient = output_gradient + norm_backward_pass(
        feedforward_gradient,
        standardized_feedforward,
        inverse_deviation_feedforward,
        feedforward_norm_gain,
    )
    grad_resid_all = lax.all_gather(
        residual_gradient.astype(jnp.bfloat16), "mp", axis=1, tiled=True
    )
    out_weight_grad = jnp.einsum(
        "gsc,gsd->cd", mixed_heads, grad_resid_all, preferred_element_type=jnp.float32
    )
    grad_mixed = jnp.einsum(
        "gsd,cd->gsc", grad_resid_all, out_weight, preferred_element_type=jnp.float32
    ).astype(jnp.bfloat16)
    probs_again = jnp.exp(scores_of(queries, key_rows) - log_total)
    grad_probs = jnp.einsum(
        "gqhe,gkhe->ghqk",
        by_heads(grad_mixed),
        by_heads(values),
        preferred_element_type=jnp.float32,
    )
    row_dot = jnp.sum(probs_again * grad_probs, axis=-1, keepdims=True)
    grad_scores = (probs_again * (grad_probs - row_dot)).astype(jnp.bfloat16)
    query_gradient = (
        score_scale
        * jnp.einsum(
            "ghqk,gkhe->gqhe", grad_scores, by_heads(key_rows), preferred_element_type=jnp.float32
        )
    ).astype(jnp.bfloat16)
    key_gradient = (
        score_scale
        * jnp.einsum(
            "ghqk,gqhe->gkhe", grad_scores, by_heads(queries), preferred_element_type=jnp.float32
        )
    ).astype(jnp.bfloat16)
    value_gradient = jnp.einsum(
        "ghqk,gqhe->gkhe",
        probs_again.astype(jnp.bfloat16),
        by_heads(grad_mixed),
        preferred_element_type=jnp.float32,
    ).astype(jnp.bfloat16)
    query_gradient = query_gradient.reshape(batch_segs, seg_len, -1)
    key_gradient = key_gradient.reshape(batch_segs, ctx_len, -1)
    value_gradient = value_gradient.reshape(batch_segs, ctx_len, -1)
    query_weight_grad = jnp.einsum(
        "nja,njr->ar", token_rows_normed, query_gradient, preferred_element_type=jnp.float32
    )
    key_weight_grad = jnp.einsum(
        "nja,njr->ar", normed_rows, key_gradient, preferred_element_type=jnp.float32
    )
    value_weight_grad = jnp.einsum(
        "nja,njr->ar", normed_rows, value_gradient, preferred_element_type=jnp.float32
    )
    partial_normed = jnp.einsum(
        "xmo,qo->xmq", key_gradient, key_projection, preferred_element_type=jnp.float32
    )
    partial_normed = partial_normed + jnp.einsum(
        "xmo,qo->xmq", value_gradient, value_projection, preferred_element_type=jnp.float32
    )
    partial_normed = partial_normed.at[:, prior_rows:].add(
        jnp.einsum(
            "xmo,qo->xmq", query_gradient, query_projection, preferred_element_type=jnp.float32
        )
    )
    partial_normed = partial_normed.reshape(batch_segs, 3, seg_len, features)
    normed_gradient = lax.psum_scatter(
        partial_normed.astype(jnp.bfloat16), "mp", scatter_dimension=2, tiled=True
    ).astype(jnp.float32)
    segment_context = jnp.stack([compressed, memory, tokens], axis=1).astype(jnp.float32)
    standardized_segment, inverse_deviation_segment = apply_layer_norm(segment_context)
    attention_gain_gradient = jnp.sum(normed_gradient * standardized_segment, axis=(0, 1, 2))
    first_bias_grad = jnp.sum(normed_gradient, axis=(0, 1, 2))
    tokens_grad = residual_gradient + norm_backward_pass(
        normed_gradient[:, 2],
        standardized_segment[:, 2],
        inverse_deviation_segment[:, 2],
        attention_norm_gain,
    )
    summed = (
        lax.psum(query_weight_grad.astype(jnp.bfloat16), "dp").astype(jnp.float32),
        lax.psum(key_weight_grad.astype(jnp.bfloat16), "dp").astype(jnp.float32),
        lax.psum(value_weight_grad.astype(jnp.bfloat16), "dp").astype(jnp.float32),
        lax.psum(out_weight_grad.astype(jnp.bfloat16), "dp").astype(jnp.float32),
        lax.psum(up_weight_grad.astype(jnp.bfloat16), "dp").astype(jnp.float32),
        lax.psum(up_bias_grad.astype(jnp.bfloat16), "dp").astype(jnp.float32),
        lax.psum(down_weight_grad.astype(jnp.bfloat16), "dp").astype(jnp.float32),
    )
    norms = lax.psum(
        (
            attention_gain_gradient,
            first_bias_grad,
            feedforward_gain_gradient,
            second_bias_grad,
            down_bias_grad,
        ),
        ("dp", "mp"),
    )
    return (
        output,
        tokens_grad,
        norms[0],
        norms[1],
        summed[0],
        summed[1],
        summed[2],
        summed[3],
        norms[2],
        norms[3],
        summed[4],
        summed[5],
        summed[6],
        norms[4],
        new_memory,
        new_compressed,
    )


BF = jnp.bfloat16
F32 = jnp.float32
MESH = pl.DeviceIdType.MESH
ANY = pl.BlockSpec(memory_space=pl.ANY)
VM = pl.BlockSpec(memory_space=pltpu.VMEM)
DMA = pltpu.SemaphoreType.DMA


def sds(shape, dtype):
    return jax.ShapeDtypeStruct(shape, dtype)


def where_am_i(chips, depth):
    dp = lax.axis_index("dp")
    return dp, lax.rem(dp, 2), dp // 2, lax.axis_index("mp")


def rcopy(src, dst, send, recv, device):
    return pltpu.make_async_remote_copy(
        src_ref=src,
        dst_ref=dst,
        send_sem=send,
        recv_sem=recv,
        device_id=device,
        device_id_type=MESH,
    )


def lcopy(src, dst, sem):
    return pltpu.make_async_copy(src, dst, sem)


def enter(partners):
    barrier = pltpu.get_barrier_semaphore()
    for p in partners:
        pl.semaphore_signal(barrier, inc=1, device_id=p, device_id_type=MESH)
    pl.semaphore_wait(barrier, len(partners))


def across(q, k):
    if k == 0:
        return q
    if k == 1:
        return q + 1 - 2 * lax.rem(q, 2)
    if k == 2:
        return lax.rem(q + 2, 4)
    return 3 - q


def across_by(q, i):
    x, y = lax.rem(q, 2), q // 2
    dx, dy = 1 - lax.rem(i, 2), 1 - i // 2
    return (x + dx - 2 * x * dx) + 2 * (y + dy - 2 * y * dy)


def layer_norm_rows(rows):
    center = jnp.mean(rows, axis=-1, keepdims=True)
    centered = rows - center
    spread = jnp.mean(centered * centered, axis=-1, keepdims=True)
    inv = lax.rsqrt(spread + 1e-05)
    return centered * inv, inv


class Slots:
    def __init__(self, ref):
        self.ref = ref
        self.used = 0

    def take(self, *shape):
        base = self.used
        size = 1
        for n in shape:
            size *= n
        self.used += size

        def at(*index):
            flat = 0
            for n, i in zip(shape, index):
                flat = flat * n + i
            return self.ref.at[base + flat]

        return at


def nt_dot(a, b):
    return lax.dot_general(a, b, (((1,), (1,)), ((), ())), preferred_element_type=F32)


def tn_dot(a, b):
    return lax.dot_general(a, b, (((0,), (0,)), ((), ())), preferred_element_type=F32)


def nn_dot(a, b):
    return jnp.dot(a, b, preferred_element_type=F32)


def one_hot(shape, offset):
    row = lax.broadcasted_iota(jnp.int32, shape, 0)
    col = lax.broadcasted_iota(jnp.int32, shape, 1)
    return jnp.where(col == row + offset, 1.0, 0.0).astype(BF)


def stack(ref, offset, rows, width=None):
    width = ref.shape[-1] if width is None else width

    def view(i):
        return ref.at[pl.ds(pl.multiple_of(offset + i * rows, rows), rows), pl.ds(0, width)]

    return view


class PlaneSum:
    def __init__(self, al, peer, blk, rows, h, g):
        self.peer, self.blk, self.half, self.rows, self.h, self.g = peer, blk, rows // 2, rows, h, g
        self.hs, self.hr, self.gs, self.gr = al.take(2), al.take(2), al.take(2), al.take(2)

    def h_x(self, i):
        return rcopy(self.blk(3, i * self.half, self.half), self.h(i), self.hs(i), self.hr(i), self.peer(i + 1))

    def g_x(self, i):
        return rcopy(self.blk(i + 1, 0, self.rows), self.g(i), self.gs(i), self.gr(i), self.peer(i + 1))

    def start(self):
        for i in range(2):
            self.h_x(i).start()

    def middle(self):
        for i in range(2):
            self.h_x(i).wait_recv()
            mine = self.blk(2 - i, i * self.half, self.half)
            mine[...] = (mine[...].astype(F32) + self.h(i)[...].astype(F32)).astype(BF)
            self.g_x(1 - i).start()

    def arrive(self):
        for i in range(2):
            self.g_x(i).wait_recv()

    def total(self):
        self.arrive()
        own = self.blk(0, 0, self.rows)
        return own[...].astype(F32) + (self.g(0)[...].astype(F32) + self.g(1)[...].astype(F32))

    def drain(self):
        for i in range(2):
            self.h_x(i).wait_send()
            self.g_x(i).wait_send()


class PlaneGather:
    def __init__(self, al, peer, sib, loc, rows, own=None):
        self.peer, self.sib, self.loc, self.half, self.rows = peer, sib, loc, rows // 2, rows
        self.own = own
        self.as_, self.ar, self.hs, self.hr = al.take(2), al.take(2), al.take(2), al.take(2)
        self.fs, self.fr = al.take(4), al.take(4)

    def a_x(self, i, k=0):
        src = self.loc(0, 0, self.rows) if self.own is None else self.own
        return rcopy(src, self.loc(k, 0, self.rows), self.as_(i), self.ar(i), self.peer(i + 1))

    def h_x(self, i, k=None):
        k = 2 - (1 - i) if k is None else k
        rows = self.loc(k, i * self.half, self.half)
        return rcopy(rows, rows, self.hs(i), self.hr(i), self.peer(2 - i))

    def f_x(self, k, other=None):
        src = self.loc(k, 0, self.rows)
        if k == 0 and self.own is not None:
            src = self.own
        dst = self.loc(k, 0, self.rows) if other is None else other(k, 0, self.rows)
        return rcopy(src, dst, self.fs(k), self.fr(k), self.sib)

    def start(self):
        for i in range(2):
            self.a_x(i).start()
        self.f_x(0).start()

    def middle(self):
        for i in range(2):
            rcopy(self.loc(i + 1, 0, self.rows), self.loc(i + 1, 0, self.rows), self.as_(i), self.ar(i), self.peer(1)).wait_recv()
            self.h_x(i).start()
            self.f_x(i + 1).start()

    def last(self):
        for i in range(2):
            self.h_x(i, 3).wait_recv()
        self.f_x(3).start()

    def drain(self):
        for i in range(2):
            self.a_x(i).wait_send()
            self.h_x(i).wait_send()
        for k in range(4):
            self.f_x(k).wait_send()

    def arrivals(self, other):
        for k in range(4):
            rcopy(other(k, 0, self.rows), other(k, 0, self.rows), self.fs(k), self.fr(k), self.sib).wait_recv()


LAYER_SEMS = 600


def layer_kernel(Q, Z, comp, mem, tok, cot, wq, wk, wv, wo, up, down, ub, vc, sq, g1, b1, g2, b2, db,
                 aw, ago, afu, afd, aub, small_o, out_o, tg_o, nm_o, nc_o,
                 ctx, normed, wqs, wks, wvs, wos, qs, ks, vs, probs, mixed, phalf, got, resid, sec, cots, ups, downs,
                 ubs, vco, act, gup, gbuf, got1, gh, gg, glow, nms, ncs, gus, gds, dgot, dh, dg, ggot, srow,
                 xu, xd, xb, fbs, arow, ffs, sums, sgot, pgot, zgot, sems, ready):
    dp, c, q, z = where_am_i(Q, Z)
    sd = dp + 1 - 2 * c
    sib = (sd, z)
    partners = [sib]
    for r in range(1, Z):
        for d in (dp, sd):
            partners.append((d, lax.rem(z + r, Z)))
    for k in range(1, Q):
        partners.append((2 * across(q, k) + c, z))
    enter(partners)
    B, R, D = tok.shape
    H = wq.shape[1]
    QR = D // Q
    OR = H // Q
    HR = R // 2
    S = R * Z
    N = S // 2
    E = up.shape[1] // (2 * Q)
    heads = B * H // HEAD_DIM
    mine = c == z // B
    jz = lax.rem(z, B)
    al = Slots(sems)

    def peer(k):
        return (2 * across(q, k) + c, z)

    wins = [wq, wk, wv, wo]
    wss = [wqs, wks, wvs, wos]

    def piece(a):
        if a < 3:
            return wins[a].at[pl.ds(q * QR, QR), :]
        return wo.at[pl.ds(q * OR, OR), :]

    def place(a, j, qq):
        if a < 3:
            return wss[a].at[pl.ds(pl.multiple_of(qq * QR, QR), QR), pl.ds(pl.multiple_of(j * H, H), H)]
        return wos.at[pl.ds(pl.multiple_of(j * H + qq * OR, OR), OR), :]

    def place_whole(a, j):
        if a < 3:
            return wss[a].at[:, pl.ds(pl.multiple_of(j * H, H), H)]
        return wos.at[pl.ds(pl.multiple_of(j * H, H), H), :]

    ws, wr = al.take(4, Z - 1), al.take(4, B)
    ps, pr = al.take(4, B, Q - 1), al.take(4, B, Q - 1)
    wl = al.take(4)

    def w_z(a, r):
        return rcopy(piece(a), place(a, jz, q), ws(a, r - 1), wr(a, jz), (dp, lax.rem(z + r, Z)))

    def w_direct(r):
        zt = lax.rem(z + r, Z)
        return jnp.logical_not((lax.rem(zt, Z - 1) == 0) & (zt // B != z // B))

    wf = al.take(4, B)

    def w_onward(a, j):
        return rcopy(place(a, j, q), place(a, j, q), wf(a, j), wr(a, j), (dp, (Z - 1) * (1 - c)))

    def w_arrive(a, j):
        return rcopy(place(a, j, q), place(a, j, q), ws(a, 0), wr(a, j), (dp, z))

    def w_p(a, j, k, qq):
        return rcopy(place(a, j, qq), place(a, j, qq), ps(a, j, k - 1), pr(a, j, k - 1), peer(k))

    relay = z == 2 - c

    def w_l(a):
        return lcopy(wins[a], place_whole(a, jz), wl(a))

    acts = [comp, mem, tok]
    cs, cr = al.take(3, B, 2), al.take(3, Z)
    fs, fr = al.take(3, Z), al.take(3, Z)
    cl = al.take(3)

    def c_rows(t, zs):
        return ctx.at[t, pl.ds(pl.multiple_of(zs * R, R), R), :]

    def c_half(t, zs, h):
        return ctx.at[t, pl.ds(pl.multiple_of(zs * R + HR * h, HR), HR), :]

    def c_l(t):
        return lcopy(acts[t].at[jz], c_rows(t, z), cl(t))

    def c_sib(t):
        return rcopy(acts[t].at[jz], c_rows(t, z), fs(t, z), fr(t, z), sib)

    def c_z(t, s, h):
        return rcopy(acts[t].at[s, pl.ds(HR * h, HR), :], c_half(t, z, h), cs(t, s, h), cr(t, z), (2 * q + h, B * c + s))

    def c_arrive(t, zs):
        return rcopy(c_half(t, zs, c), c_half(t, zs, c), cs(t, 0, 0), cr(t, zs), (dp, z))

    def c_fwd(t, zs, half):
        return rcopy(c_half(t, zs, half), c_half(t, zs, half), fs(t, zs), fr(t, zs), sib)

    us, ur, ul = al.take(Z - 1), al.take(Z - 1), al.take(1)
    vs_, vr_ = al.take(1), al.take(1)

    def u_z(r):
        return rcopy(ub.at[dp], ubs.at[r], us(r - 1), ur(r - 1), (dp, lax.rem(z + r, Z)))

    u_l = lcopy(ub.at[dp], ubs.at[0], ul(0))
    v_s = rcopy(vc, vco, vs_(0), vr_(0), sib)

    ts, tr, tl = al.take(B), al.take(B), al.take(1)

    def dev(k, core):
        return 2 * across(q, k) + core

    def t_rows(d, i):
        return cots.at[pl.ds(pl.multiple_of(d * N + i * R, R), R), :]

    def t_z(s):
        to = 2 * q + z // B
        return rcopy(cot.at[s], t_rows(to, jz), ts(s), tr(jz), (to, B * c + s))

    def t_l():
        return lcopy(cot.at[jz], t_rows(dp, jz), tl(0))

    def t_arrive(i):
        return rcopy(t_rows(dp, i), t_rows(dp, i), ts(0), tr(i), (dp, z))

    def rows_at(ref, core):
        def loc(k, lo, n):
            return ref.at[pl.ds(pl.multiple_of(dev(k, core) * N + lo, n), n), :]
        return loc

    tgat = PlaneGather(al, peer, sib, rows_at(cots, c), N)
    agat = PlaneGather(al, peer, sib, rows_at(sec, c), N)

    xs, xr_, xl, xf = al.take(2, Z), al.take(2, Z), al.take(2), al.take(2, 2)
    is_end = lax.rem(z, Z - 1) == 0

    def x_place(i, r):
        if i == 0:
            return ups.at[:, pl.ds(r * E, E)]
        return downs.at[pl.ds(r * E, E), :]

    def x_z(i, r):
        src = up.at[:, pl.ds(pl.multiple_of(dp * E, E), E)] if i == 0 else down.at[pl.ds(pl.multiple_of(dp * E, E), E), :]
        return rcopy(src, x_place(i, r), xs(i, r), xr_(i, r), (dp, lax.rem(z + r, Z)))

    def x_direct(r):
        return (z < Z - 1, is_end, z > 0)[r - 1]

    def x_start(i):
        for r in range(1, Z):
            @pl.when(x_direct(r))
            def _():
                x_z(i, r).start()

    onward = ((2, 3, ((2, 3), (1, 2)), 3), (1, 0, ((2, 1), (3, 2)), 1))

    def x_onward(i, n, to, a, b):
        return rcopy(x_place(i, a), x_place(i, b), xf(i, n), xr_(i, b), (dp, to))

    def x_forward(i):
        for at, to, pairs, rest in onward:
            @pl.when(z == at)
            def _():
                for n, (a, b) in enumerate(pairs):
                    x_z(i, a).wait_recv()
                    x_onward(i, n, to, a, b).start()

    def x_rest(i):
        for at, to, pairs, rest in onward:
            @pl.when(z == at)
            def _():
                x_z(i, rest).wait_recv()

        @pl.when(is_end)
        def _():
            for r in range(1, Z):
                x_z(i, r).wait_recv()

    def x_drain(i):
        for r in range(1, Z):
            @pl.when(x_direct(r))
            def _():
                x_z(i, r).wait_send()
        for at, to, pairs, rest in onward:
            @pl.when(z == at)
            def _():
                for n, (a, b) in enumerate(pairs):
                    x_onward(i, n, to, a, b).wait_send()

    x_l = [lcopy(up.at[:, pl.ds(pl.multiple_of(dp * E, E), E)], ups.at[:, pl.ds(0, E)], xl(0)),
           lcopy(down.at[pl.ds(pl.multiple_of(dp * E, E), E), :], downs.at[pl.ds(0, E), :], xl(1))]

    c_sem = al.take(B)
    c_in = [lcopy(cot.at[i], nms.at[pl.ds(i * R, R), :], c_sem(i)) for i in range(B)]

    for x in c_in:
        x.start()
    sums[...] = jnp.zeros_like(sums)
    @pl.when(mine)
    def _():
        for r in range(1, Z):
            @pl.when(w_direct(r))
            def _():
                for a in range(4):
                    w_z(a, r).start()
        for a in range(4):
            w_l(a).start()
        for t in range(3):
            c_l(t).start()
            c_sib(t).start()
    for r in range(1, Z):
        u_z(r).start()
    v_s.start()
    u_l.start()
    for x in x_l:
        x.start()
    for j in range(B):
        @pl.when(B * c + j != z)
        def _():
            for a in range(4):
                w_arrive(a, j).wait_recv()

                @pl.when(relay)
                def _():
                    w_onward(a, j).start()
                for k in range(1, Q):
                    w_p(a, j, k, q).start()
    def c_start(t):
        for s in range(B):
            @pl.when(B * c + s != z)
            def _():
                for h in range(2):
                    c_z(t, s, h).start()

    def c_sent(t):
        for s in range(B):
            @pl.when(B * c + s != z)
            def _():
                for h in range(2):
                    c_z(t, s, h).wait_send()

    for t in range(3):
        c_start(t)

    def norm_block(t, zs):
        at = pl.ds(pl.multiple_of(zs * R, R), R)
        to = pl.ds(pl.multiple_of(t * S + zs * R, R), R)
        xhat, _ = layer_norm_rows(ctx[t, at, :].astype(F32))
        normed[to, :] = (xhat * g1[...] + b1[...]).astype(BF)

    @pl.when(mine)
    def _():
        for t in range(3):
            c_l(t).wait()

    @pl.when(jnp.logical_not(mine))
    def _():
        for t in range(3):
            rcopy(c_rows(t, z), c_rows(t, z), fs(t, z), fr(t, z), sib).wait_recv()

    def norm_own(t, carry):
        norm_block(t, z)
        return carry

    lax.fori_loop(0, 3, norm_own, 0)
    for x in c_in:
        x.wait()
    sums[4:5, :] = jnp.sum(nms[...].astype(F32), axis=0, keepdims=True)
    T = 256

    def project(i, carry):
        at = pl.ds(pl.multiple_of(i * T, T), T)
        ks[at, :] = nn_dot(normed[at, :], wks[...]).astype(BF)
        vs[at, :] = nn_dot(normed[at, :], wvs[...]).astype(BF)
        return carry

    def project_q(i, carry):
        at = pl.ds(pl.multiple_of(i * T, T), T)
        qs[at, :] = nn_dot(normed[pl.ds(pl.multiple_of(2 * S + i * T, T), T), :], wqs[...]).astype(BF)
        return carry

    for t in range(3):
        for r in range(1, Z):
            zs = lax.rem(z + r, Z)
            c_arrive(t, zs).wait_recv()
            c_fwd(t, zs, c).start()
        if t == 2:
            for u in range(3):
                c_sent(u)
            for s in range(B):
                here = (B * c + s == z) & mine

                @pl.when(here)
                def _():
                    t_l().start()

                @pl.when(jnp.logical_not(here))
                def _():
                    t_z(s).start()
            x_start(0)
        for r in range(1, Z):
            c_fwd(t, lax.rem(z + r, Z), 1 - c).wait_recv()

        def norm_one(r, carry, t=t):
            norm_block(t, lax.rem(z + r, Z))
            return carry

        lax.fori_loop(1, Z, norm_one, 0)
        if t == 0:
            for j in range(B):
                @pl.when(B * c + j != z)
                def _():
                    for a in range(4):
                        for k in range(1, Q):
                            w_p(a, j, k, across(q, k)).wait_recv()

            @pl.when(mine)
            def _():
                for a in range(4):
                    w_l(a).wait()
        lax.fori_loop(t * S // T, (t + 1) * S // T, project, 0)
    lax.fori_loop(0, S // T, project_q, 0)
    x_start(1)

    v_s.wait()
    counts = jnp.where(mine, vc[jz], vco[jz])
    count = counts[0:1, 0:1]
    scale = HEAD_DIM ** (-0.5)
    P2 = 2 * S

    def attend(half, tag):
        r0 = pl.multiple_of(half * N, N)

        def head(h, carry):
            hd = pl.ds(pl.multiple_of(h * HEAD_DIM, HEAD_DIM), HEAD_DIM)
            qh = qs[pl.ds(r0, N), hd]
            s1 = nt_dot(qh, ks[pl.ds(0, P2), hd])
            s2 = nt_dot(qh, ks[pl.ds(P2, S), hd])
            row = lax.broadcasted_iota(jnp.int32, (N, S), 0) + half * N
            col = lax.broadcasted_iota(jnp.int32, (N, S), 1)
            s2 = jnp.where((col <= row) & (col < count), s2, -1e30)
            top = jnp.maximum(jnp.max(s1, axis=-1, keepdims=True), jnp.max(s2, axis=-1, keepdims=True))
            p1 = jnp.exp((s1 - top) * scale)
            p2 = jnp.exp((s2 - top) * scale)
            inv = 1.0 / (jnp.sum(p1, axis=-1, keepdims=True) + jnp.sum(p2, axis=-1, keepdims=True))
            p1 = (p1 * inv).astype(BF)
            p2 = (p2 * inv).astype(BF)
            probs[h, pl.ds(r0, N), pl.ds(0, P2)] = p1
            probs[h, pl.ds(r0, N), pl.ds(P2, S)] = p2
            mix = nn_dot(p1, vs[pl.ds(0, P2), hd]) + nn_dot(p2, vs[pl.ds(P2, S), hd])
            mixed[pl.ds(r0, N), hd] = mix.astype(BF)
            return carry

        lax.fori_loop(0, heads, head, 0)

    hs, hr = al.take(1), al.take(1)
    h_x = rcopy(phalf, got, hs(0), hr(0), sib)
    attend(1 - c, 0)
    phalf[...] = nn_dot(mixed[pl.ds(pl.multiple_of((1 - c) * N, N), N), :], wos[...])
    h_x.start()
    for i in range(B):
        @pl.when(jnp.logical_not((B * c + i == z) & mine))
        def _():
            t_arrive(i).wait_recv()

        @pl.when((B * c + i == z) & mine)
        def _():
            t_l().wait()
    tgat.start()
    attend(c, 1)
    own_part = nn_dot(mixed[pl.ds(pl.multiple_of(c * N, N), N), :], wos[...])
    x_forward(0)
    h_x.wait_recv()
    resid[...] = ctx[2, pl.ds(pl.multiple_of(c * N, N), N), :].astype(F32) + (own_part + got[...])
    xhat2, _ = layer_norm_rows(resid[...])
    sec[pl.ds(pl.multiple_of(dp * N, N), N), :] = (xhat2 * g2[...] + b2[...]).astype(BF)

    agat.start()
    sqc = al.take(RATE)
    sqs = [gbuf.at[pl.ds(0, D), :], gbuf.at[pl.ds(D, D), :], dgot]
    sq_x = [lcopy(sq.at[pl.ds(r * D, D), :], sqs[r], sqc(r)) for r in range(RATE)]
    for x in sq_x:
        x.start()
    ss, sr = al.take(Q), al.take(Q)

    def s_x(k):
        return rcopy(rows_at(gbuf, 1 - c)(k, 0, N), stack(got1, 0, N)(k), ss(k), sr(k), sib)

    gsum = PlaneSum(al, peer, rows_at(gbuf, c), N, stack(gh, 0, N // 2), stack(gg, 0, N))
    ffs[...] = jnp.zeros_like(ffs)

    def slope_at(b):
        return (b // 4, pl.ds(pl.multiple_of(lax.rem(b // 2, 2) * N, N), N), pl.ds(pl.multiple_of(lax.rem(b, 2) * Z * E, Z * E), Z * E))

    def up_block(b, bias_row):
        at = pl.ds(pl.multiple_of(b * N, N), N)
        x = nn_dot(sec[at, :], ups[...]) + bias_row
        x2 = x * x
        root = 0.7978845608028654
        th = jnp.tanh(root * (x + 0.044715 * (x2 * x)))
        act[at, :] = (0.5 * x * (1.0 + th)).astype(BF)
        slope = 0.5 * (1.0 + th) + 0.5 * x * (1.0 - th * th) * (root * (1.0 + 0.134145 * x2))
        ctx[slope_at(b)] = slope.astype(BF)
        return bias_row

    def back_block(b):
        at = pl.ds(pl.multiple_of(b * N, N), N)
        ga = nt_dot(cots[at, :], downs[...])
        gu = (ga * ctx[slope_at(b)].astype(F32)).astype(BF)
        gup[at, :] = gu
        ffs[2:3, pl.ds(0, Z * E)] = ffs[2:3, pl.ds(0, Z * E)] + jnp.sum(gu.astype(F32), axis=0, keepdims=True)
        gbuf[at, :] = nt_dot(gu, ups[...]).astype(BF)

    def feed(k):
        def half(i, carry):
            back_block(dev(k, 1 - c) + i * (2 * c - 1))

            @pl.when(i == 0)
            def _():
                s_x(k).start()
            return carry

        lax.fori_loop(0, 2, half, 0)

    def combine(k):
        s_x(k).wait_recv()
        rows = rows_at(gbuf, c)(k, 0, N)
        rows[...] = (rows[...].astype(F32) + stack(got1, 0, N)(k)[...].astype(F32)).astype(BF)

    groups = S // RATE
    squeezed = None
    for r in range(RATE):
        sq_x[r].wait()
        row = lax.broadcasted_iota(jnp.int32, (ncs.shape[0], S), 0)
        col = lax.broadcasted_iota(jnp.int32, (ncs.shape[0], S), 1)
        pick = jnp.where((col == row * RATE + r) & (row < groups), 1.0, 0.0).astype(BF)
        picked = nn_dot(pick, ctx[1]).astype(BF)
        term = nn_dot(picked, sqs[r][...])
        squeezed = term if squeezed is None else squeezed + term
    ncs[...] = squeezed.astype(BF)
    shift = count + c * N
    new_mem = nn_dot(one_hot((N, S), shift), ctx[1]) + nn_dot(one_hot((N, S), shift - S), ctx[2])
    nms[...] = new_mem.astype(BF)
    third = lax.shift_right_logical(count * 21846, 16)
    shift = third + c * N
    new_comp = nn_dot(one_hot((N, S), shift), ctx[0]) + nn_dot(one_hot((N, ncs.shape[0]), shift - S), ncs[...])
    ncs[pl.ds(0, N), :] = new_comp.astype(BF)
    per = N // R
    ms, mr, ml = al.take(2, 2), al.take(2, B), al.take(2)
    kept_in = [nms, ncs]
    kept_out = [nm_o, nc_o]

    def keep_x(i, p):
        return rcopy(kept_in[i].at[pl.ds(p * R, R), :], kept_out[i].at[jz], ms(i, p), mr(i, jz), (2 * q + z // B, c * per + p))

    def keep_l(i, p):
        return lcopy(kept_in[i].at[pl.ds(p * R, R), :], kept_out[i].at[jz], ml(i))

    x_forward(1)
    tgat.middle()
    agat.middle()
    tgat.last()
    agat.last()
    for r in range(1, Z):
        u_z(r).wait()
    u_l.wait()

    @pl.when(mine)
    def _():
        for t in range(3):
            c_sib(t).wait_send()
    for r in range(1, Z):
        for t in range(3):
            c_fwd(t, lax.rem(z + r, Z), c).wait_send()
    x_rest(0)
    for x in x_l:
        x.wait()
    agat.arrivals(rows_at(sec, 1 - c))
    lax.fori_loop(0, 2 * Q, up_block, jnp.concatenate([ubs[r] for r in range(Z)], axis=1))
    x_rest(1)
    tgat.arrivals(rows_at(cots, 1 - c))
    for p in range(per):
        here = (c * per + p == z) & mine

        @pl.when(here)
        def _():
            for i in range(2):
                keep_l(i, p).start()

        @pl.when(jnp.logical_not(here))
        def _():
            for i in range(2):
                keep_x(i, p).start()


    feed(3)
    combine(3)
    gsum.start()
    feed(1)
    feed(2)
    combine(1)
    combine(2)
    gsum.middle()
    feed(0)

    def up_grad(i, carry):
        at = pl.ds(pl.multiple_of(i * T, T), T)
        gus[at, :] = tn_dot(sec[:, at], gup[...]).astype(BF)
        return carry

    lax.fori_loop(0, D // T, up_grad, 0)
    ys, yr = al.take(2, 6), al.take(2, 4)
    near_r, near_z = 3 - 2 * lax.rem(z, 2), z + 1 - 2 * lax.rem(z, 2)

    def y_own(i, r):
        if i == 0:
            return gus.at[:, pl.ds(pl.multiple_of(r * E, E), E)]
        return gds.at[pl.ds(pl.multiple_of(r * E, E), E), :]

    def y_buf(i, n):
        return (xu, xd)[i].at[n]

    def y_near(i):
        return rcopy(y_own(i, near_r), y_buf(i, 0), ys(i, 0), yr(i, 0), (dp, near_z))

    def y_hand(i, n):
        r = 2 if n == 0 else 1 + 2 * (z // 3)
        return rcopy(y_own(i, r), y_buf(i, 2 + n), ys(i, 2 + n), yr(i, 2 + n), (dp, 1 + z // 3))

    def y_far(i, n):
        r = 5 - 2 * z if n == 0 else 2
        return rcopy(y_own(i, r), y_buf(i, 1), ys(i, 4 + n), yr(i, 1), (dp, lax.rem(z + Z - r, Z)))

    def y_start(i):
        @pl.when(is_end)
        def _():
            for n in range(2):
                y_hand(i, n).start()
        y_near(i).start()

    def y_middle(i):
        @pl.when(jnp.logical_not(is_end))
        def _():
            for n in range(2):
                rcopy(y_buf(i, 2 + n), y_buf(i, 2 + n), ys(i, 2 + n), yr(i, 2 + n), (dp, z)).wait_recv()
                mine_ = y_own(i, 5 - 2 * z if n == 0 else 2)
                mine_[...] = (mine_[...].astype(F32) + y_buf(i, 2 + n)[...].astype(F32)).astype(BF)
                y_far(i, n).start()

    def y_arrive(i):
        for n in range(2):
            rcopy(y_buf(i, n), y_buf(i, n), ys(i, 0), yr(i, n), (dp, z)).wait_recv()

    def y_drain(i):
        y_near(i).wait_send()

        @pl.when(is_end)
        def _():
            for n in range(2):
                y_hand(i, n).wait_send()

        @pl.when(jnp.logical_not(is_end))
        def _():
            for n in range(2):
                y_far(i, n).wait_send()

    ubs_, ubr = al.take(Z), al.take(Z)

    def ub_x(r):
        return rcopy(ffs.at[pl.ds(2, 1), pl.ds(r * E, E)], xb.at[r], ubs_(r), ubr(r), (dp, lax.rem(z + Z - r, Z)))

    y_start(0)
    for r in range(1, Z):
        ub_x(r).start()
    agat.drain()

    def down_rows(b, carry):
        at = pl.ds(pl.multiple_of(b * N, N), N)
        sec[at, :] = nn_dot(act[at, :], downs[...]).astype(BF)
        return carry

    lax.fori_loop(0, 2 * Q, down_rows, 0)
    dss, dsr = al.take(Q), al.take(Q)

    def d_x(k):
        return rcopy(rows_at(sec, 1 - c)(k, 0, N), stack(dgot, 0, N)(k), dss(k), dsr(k), sib)

    dsum = PlaneSum(al, peer, rows_at(sec, c), N, stack(dh, 0, N // 2), stack(dg, 0, N))
    for k in (3, 1, 2, 0):
        d_x(k).start()

    def down_grad(i, carry):
        at = pl.ds(pl.multiple_of(i * T, T), T)
        gds[at, :] = tn_dot(act[:, at], cots[...]).astype(BF)
        return carry

    lax.fori_loop(0, Z * E // T, down_grad, 0)

    y_start(1)
    for k in (3, 1, 2, 0):
        d_x(k).wait_recv()
        rows = rows_at(sec, c)(k, 0, N)
        rows[...] = (rows[...].astype(F32) + stack(dgot, 0, N)(k)[...].astype(F32)).astype(BF)
    combine(0)
    gsum.arrive()
    dsum.start()
    C = 64

    def back_rows(i, carry):
        at = pl.ds(pl.multiple_of(i * C, C), C)
        own = pl.ds(pl.multiple_of(dp * N + i * C, C), C)
        gs = gbuf[own, :].astype(F32) + (gg[at, :].astype(F32) + gg[pl.ds(pl.multiple_of(N + i * C, C), C), :].astype(F32))
        xhat, inv = layer_norm_rows(resid[at, :])
        ffs[0:1, :] = ffs[0:1, :] + jnp.sum(gs * xhat, axis=0, keepdims=True)
        ffs[1:2, :] = ffs[1:2, :] + jnp.sum(gs, axis=0, keepdims=True)
        e = gs * g2[...]
        m1 = jnp.mean(e, axis=-1, keepdims=True)
        m2 = jnp.mean(e * xhat, axis=-1, keepdims=True)
        gr = cots[own, :].astype(F32) + inv * (e - m1 - xhat * m2)
        got[at, :] = gr
        glow[pl.ds(pl.multiple_of(c * N + i * C, C), C), :] = gr.astype(BF)
        return carry

    lax.fori_loop(0, N // C, back_rows, 0)
    ls_, lr_ = al.take(1), al.take(1)

    def far_x(half):
        rows = glow.at[pl.ds(pl.multiple_of(half * N, N), N), :]
        return rcopy(rows, rows, ls_(0), lr_(0), sib)

    far_x(c).start()
    for x in (tgat, gsum):
        x.drain()
    for k in range(Q):
        s_x(k).wait_send()
    h_x.wait_send()
    for i in range(2):
        x_drain(i)
    for p in partners:
        pl.semaphore_signal(ready, inc=1, device_id=p, device_id_type=MESH)
    far_x(1 - c).wait_recv()

    W = B * H
    hj = H // HEAD_DIM
    M = D // Q
    gms, gqs, gkv = gup.at[pl.ds(0, S), :], gup.at[pl.ds(S, S), :], act.at[pl.ds(0, 3 * S), :]
    gos = gbuf.at[pl.ds(0, W), :]
    tgs, outs = ctx.at[0, pl.ds(0, N), :], ctx.at[0, pl.ds(N, N), :]
    small1 = ctx.at[1]
    odone = stack(small1, 2 * S // 2 - B * OR, OR)
    zo = stack(gg, 0, OR)
    wfin, ofin = gg.at[pl.ds(N, M), pl.ds(0, 3 * H)], gh.at[pl.ds(0, OR), :]

    def mix_rows(i, carry):
        at = pl.ds(pl.multiple_of(i * T, T), T)
        gms[at, :] = nt_dot(glow[at, :], wos[...]).astype(BF)
        gos[at, :] = tn_dot(mixed[:, at], glow[...]).astype(BF)
        return carry

    lax.fori_loop(0, S // T, mix_rows, 0)

    def o_blk(j):
        def blk(k, lo, n):
            return gos.at[pl.ds(pl.multiple_of(j * H + across(q, k) * OR + lo, n), n), :]
        return blk

    M2 = M // 2

    def w_blk(j, half):
        def blk(k, lo, n):
            return cots.at[pl.ds(pl.multiple_of(j * D + across(q, k) * M + half * M2 + lo, n), n), pl.ds(0, 3 * H)]
        return blk

    osum = [
        PlaneSum(al, peer, o_blk(j), OR, stack(small1, j * OR, OR // 2), stack(small1, B * OR + 2 * j * OR, OR)) for j in range(B)
    ]
    wsum = [
        [
            PlaneSum(
                al, peer, w_blk(j, half), M2,
                stack(gbuf, W + 2 * B * M + j * M + half * M2, M2 // 2, 3 * H), stack(gbuf, W + 2 * j * M + half * M, M2, 3 * H),
            )
            for half in range(2)
        ]
        for j in range(B)
    ]
    pl.semaphore_wait(ready, len(partners))
    for x in osum:
        x.start()
    arow[...] = jnp.zeros_like(arow)

    def back_head(h, hh):
        hd = pl.ds(h * HEAD_DIM, HEAD_DIM)
        ko = pl.ds(hh * HEAD_DIM, HEAD_DIM)
        vo = pl.ds(H + hh * HEAD_DIM, HEAD_DIM)
        p = probs[h]
        gm = gms[:, hd]
        gp = nt_dot(gm, vs[:, hd])
        delta = jnp.sum(gm.astype(F32) * mixed[:, hd].astype(F32), axis=-1, keepdims=True)
        gs = (p.astype(F32) * (gp - delta)).astype(BF)
        gqs[:, hd] = (scale * nn_dot(gs, ks[:, hd])).astype(BF)
        gkv[:, ko] = (scale * tn_dot(gs, qs[:, hd])).astype(BF)
        gkv[:, vo] = tn_dot(p, gm).astype(BF)

    def split_rows(v):
        hi = v.astype(BF)
        rest = v - hi.astype(F32)
        mid = rest.astype(BF)
        low = (rest - mid.astype(F32)).astype(BF)
        return jnp.concatenate([hi, mid, low, jnp.zeros((5, v.shape[1]), BF)], axis=0)

    def weights(j):
        js = pl.ds(j * H, H)

        def rows(i, carry):
            to_chip = across_by(q, i)
            at = pl.ds(pl.multiple_of(to_chip * M, M), M)
            kv = tn_dot(normed[:, at], gkv[...])
            gq = tn_dot(normed[pl.ds(2 * S, S), at], gqs[:, js])
            to = pl.ds(pl.multiple_of(j * D + to_chip * M, M), M)
            cots[to, pl.ds(0, 2 * H)] = kv.astype(BF)
            cots[to, pl.ds(2 * H, H)] = gq.astype(BF)
            t = (kv[:, :H] * wks[at, js].astype(F32) + kv[:, H:] * wvs[at, js].astype(F32) + gq * wqs[at, js].astype(F32))
            arow[at, :] = arow[at, :] + jnp.broadcast_to(jnp.sum(t, axis=-1, keepdims=True), (M, 128))

            @pl.when(i == 0)
            def _():
                for x in wsum[j]:
                    x.start()
            return carry

        lax.fori_loop(0, Q, rows, 0)
        skv = split_rows(jnp.sum(gkv[...].astype(F32), axis=0, keepdims=True))
        sq_ = split_rows(jnp.sum(gqs[:, js].astype(F32), axis=0, keepdims=True))
        b = nt_dot(skv[:, :H], wks[:, js]) + nt_dot(skv[:, H:], wvs[:, js]) + nt_dot(sq_, wqs[:, js])
        sums[1:2, :] = sums[1:2, :] + jnp.sum(b, axis=0, keepdims=True)

    for h in range(hj):
        back_head(h, h)

    def token_rows(j, half):
        js = pl.ds(j * H, H)
        rows = pl.ds(pl.multiple_of(half * N, N), N)
        krows = pl.ds(pl.multiple_of(2 * S + half * N, N), N)
        return (nt_dot(gkv[krows, pl.ds(0, H)], wks[:, js]) + nt_dot(gkv[krows, pl.ds(H, H)], wvs[:, js])
                + nt_dot(gqs[rows, js], wqs[:, js]))

    for x in osum:
        x.middle()
    weights(0)
    dsum.middle()
    y_middle(0)
    phalf[...] = token_rows(0, 1 - c)
    srow[...] = token_rows(0, c)
    for h in range(hj, 2 * hj):
        back_head(h, h - hj)
    for x in wsum[0]:
        x.middle()
    y_middle(1)
    weights(1)
    phalf[...] = phalf[...] + token_rows(1, 1 - c)
    ts_, tr_ = al.take(1), al.take(1)
    t_x = rcopy(phalf, ggot, ts_(0), tr_(0), sib)
    t_x.start()
    srow[...] = srow[...] + token_rows(1, c)
    rs, rr, rl = al.take(2, 2), al.take(2, B), al.take(2)
    rows_in = [tgs, outs]
    rows_out = [tg_o, out_o]

    def row_x(i, p):
        return rcopy(rows_in[i].at[pl.ds(p * R, R), :], rows_out[i].at[jz], rs(i, p), rr(i, jz), (2 * q + z // B, c * per + p))

    def row_l(i, p):
        return lcopy(rows_in[i].at[pl.ds(p * R, R), :], rows_out[i].at[jz], rl(i))

    def send_rows(i):
        for p in range(per):
            here = (c * per + p == z) & mine

            @pl.when(here)
            def _():
                row_l(i, p).start()

            @pl.when(jnp.logical_not(here))
            def _():
                row_x(i, p).start()

    outs[...] = (resid[...] + dsum.total() + db[...]).astype(BF)
    send_rows(1)
    ozs, ozr = al.take(3, B), al.take(3, Z)

    def z_buf(i, zz):
        if i == 2:
            return zo(zz)
        return got1.at[pl.ds(pl.multiple_of(zz * M + i * M2, M2), M2), pl.ds(0, 3 * H)]

    def z_done(i, j):
        if i == 2:
            return odone(j)
        return downs.at[pl.ds(pl.multiple_of(j * M + i * M2, M2), M2), pl.ds(0, 3 * H)]

    def z_x(i, j):
        return rcopy(z_done(i, j), z_buf(i, z), ozs(i, j), ozr(i, z), (dp, B * c + j))

    def z_arrive(i, zz):
        return rcopy(z_buf(i, zz), z_buf(i, zz), ozs(i, 0), ozr(i, zz), (dp, z))

    def to_plane(i, j):
        z_done(i, j)[...] = (osum[j] if i == 2 else wsum[j][i]).total().astype(BF)

        @pl.when(B * c + j != z)
        def _():
            z_x(i, j).start()

    for j in range(B):
        to_plane(2, j)
    for x in wsum[1]:
        x.middle()
    for half in range(2):
        to_plane(half, 0)
    acol = jnp.swapaxes(arow[...], 0, 1)[0:1, :]
    bsum = sums[1:2, :]
    sums[0:1, :] = (acol - b1[...] * bsum) / g1[...]
    sums[2:3, :] = ffs[0:1, :]
    sums[3:4, :] = ffs[1:2, :]
    n1, n2 = al.take(1), al.take(1)
    v_x = rcopy(sums, sgot, n1(0), n2(0), sib)
    v_x.start()
    t_x.wait_recv()
    def norm_rows(i, carry):
        at = pl.ds(pl.multiple_of(i * C, C), C)
        gn = srow[at, :] + ggot[at, :]
        xhat, inv = layer_norm_rows(ctx[2, pl.ds(pl.multiple_of(c * N + i * C, C), C), :].astype(F32))
        e = gn * g1[...]
        m1 = jnp.mean(e, axis=-1, keepdims=True)
        m2 = jnp.mean(e * xhat, axis=-1, keepdims=True)
        tgs[at, :] = (got[at, :] + inv * (e - m1 - xhat * m2)).astype(BF)
        return carry

    lax.fori_loop(0, N // C, norm_rows, 0)
    for i in range(2):
        y_arrive(i)
    fu = y_own(0, 0)[...].astype(F32) + (xu[0].astype(F32) + xu[1].astype(F32))
    fd = y_own(1, 0)[...].astype(F32) + (xd[0].astype(F32) + xd[1].astype(F32))
    fb = ffs[2:3, 0:E]
    for r in range(1, Z):
        ub_x(r).wait_recv()
        fb = fb + xb[r]
    fus, fds = xu.at[2], xd.at[2]
    fus[...] = fu.astype(BF)
    fds[...] = fd.astype(BF)
    fbs[...] = fb

    def u_loc(core):
        def loc(k, lo, n):
            return afu.at[pl.ds(lo, n), pl.ds(pl.multiple_of(dev(k, core) * E, E), E)]
        return loc

    def d_loc(core):
        def loc(k, lo, n):
            return afd.at[pl.ds(pl.multiple_of(dev(k, core) * E + lo, n), n), :]
        return loc

    ugat = PlaneGather(al, peer, sib, u_loc(c), D, own=fus)
    dgat = PlaneGather(al, peer, sib, d_loc(c), E, own=fds)
    fl = al.take(3)
    f_l = [lcopy(fus, u_loc(c)(0, 0, D), fl(0)), lcopy(fds, d_loc(c)(0, 0, E), fl(1))]
    bs, br, bfs, bfr = al.take(Q), al.take(Q), al.take(Q), al.take(Q)

    def b_x(k):
        return rcopy(fbs, aub.at[dp], bs(k), br(k), peer(k))

    def b_arrive(k):
        return rcopy(aub.at[dev(k, c)], aub.at[dev(k, c)], bs(k), br(k), peer(k))

    def b_f(k):
        src = fbs if k == 0 else aub.at[dev(k, c)]
        return rcopy(src, aub.at[dev(k, c)], bfs(k), bfr(k), sib)

    b_l = lcopy(fbs, aub.at[dp], fl(2))
    v_x.wait()
    srow[0:8, :] = sums[...] + sgot[...]
    pgot[q] = srow[0:8, :]
    vps, vpr, vzs, vzr = al.take(Q), al.take(Q), al.take(Z), al.take(Z)

    def vp_x(k):
        return rcopy(srow.at[pl.ds(0, 8), :], pgot.at[q], vps(k), vpr(k), peer(k))

    def vp_arrive(k):
        return rcopy(pgot.at[across(q, k)], pgot.at[across(q, k)], vps(k), vpr(k), peer(k))

    def vz_x(r):
        return rcopy(srow.at[pl.ds(8, 8), :], zgot.at[z], vzs(r), vzr(r), (dp, lax.rem(z + r, Z)))

    def vz_arrive(r):
        zz = lax.rem(z + Z - r, Z)
        return rcopy(zgot.at[zz], zgot.at[zz], vzs(r), vzr(r), (dp, z))

    for k in range(1, Q):
        vp_x(k).start()
    for k in range(1, Q):
        vp_arrive(k).wait_recv()
    psum = pgot[0]
    for k in range(1, Q):
        psum = psum + pgot[k]
    srow[8:16, :] = psum
    zgot[z] = psum
    for r in range(1, Z):
        vz_x(r).start()
    for half in range(2):
        to_plane(half, 1)
    ugat.start()
    dgat.start()
    for x in f_l:
        x.start()
    b_l.start()
    for k in range(1, Q):
        b_x(k).start()
    b_f(0).start()

    def a_loc(ref, n_rows):
        def loc(k, lo, n):
            return ref.at[pl.ds(pl.multiple_of(across(q, k) * n_rows + lo, n), n), :]
        return loc

    fins = [wfin.at[pl.ds(0, M2), :], wfin.at[pl.ds(M2, M2), :], ofin]

    def half_loc(half):
        def loc(k, lo, n):
            return aw.at[pl.ds(pl.multiple_of(across(q, k) * M + half * M2 + lo, n), n), :]
        return loc

    locs = [half_loc(0), half_loc(1), a_loc(ago, OR)]
    gats = [PlaneGather(al, peer, sib, locs[i], OR if i == 2 else M2, own=fins[i]) for i in range(3)]
    gl = al.take(3)
    g_l = [lcopy(fins[i], locs[i](0, 0, OR if i == 2 else M2), gl(i)) for i in range(3)]
    for gat in (ugat, dgat):
        gat.middle()
    send_rows(0)
    for k in range(1, Q):
        b_arrive(k).wait_recv()
        b_f(k).start()

    @pl.when(mine)
    def _():
        for i in (2, 0, 1):
            for zz in range(Z):
                @pl.when(zz != z)
                def _():
                    z_arrive(i, zz).wait_recv()
            z_buf(i, z)[...] = z_done(i, jz)[...]
            t = z_buf(i, 0)[...].astype(F32)
            for zz in range(1, Z):
                t = t + z_buf(i, zz)[...].astype(F32)
            fins[i][...] = t.astype(BF)
            gats[i].start()
            g_l[i].start()
    for r in range(1, Z):
        vz_arrive(r).wait_recv()
    zsum = zgot[0]
    for zz in range(1, Z):
        zsum = zsum + zgot[zz]
    small_o[...] = zsum

    @pl.when(mine)
    def _():
        for i in (2, 0, 1):
            gats[i].middle()
    for gat in (ugat, dgat):
        gat.last()

    @pl.when(mine)
    def _():
        for i in (2, 0, 1):
            gats[i].last()
    ugat.arrivals(u_loc(1 - c))
    dgat.arrivals(d_loc(1 - c))

    @pl.when(jnp.logical_not(mine))
    def _():
        for i in range(3):
            gats[i].arrivals(locs[i])

    for k in range(Q):
        rcopy(aub.at[dev(k, 1 - c)], aub.at[dev(k, 1 - c)], bfs(k), bfr(k), sib).wait_recv()
        b_f(k).wait_send()
        d_x(k).wait_send()
    for k in range(1, Q):
        b_x(k).wait_send()
        vp_x(k).wait_send()
    b_l.wait()
    for x in f_l:
        x.wait()
    for r in range(1, Z):
        vz_x(r).wait_send()
        ub_x(r).wait_send()
    for i in range(2):
        y_drain(i)
    for x in osum + wsum[0] + wsum[1] + [dsum, ugat, dgat]:
        x.drain()

    @pl.when(mine)
    def _():
        for x in gats:
            x.drain()
        for x in g_l:
            x.wait()
    t_x.wait_send()
    for j in range(B):
        @pl.when(B * c + j != z)
        def _():
            for i in range(3):
                z_x(i, j).wait_send()
    for p in range(per):
        here = (c * per + p == z) & mine

        @pl.when(here)
        def _():
            for i in range(2):
                row_l(i, p).wait()

        @pl.when(jnp.logical_not(here))
        def _():
            for i in range(2):
                row_x(i, p).wait_send()
    for s in range(B):
        @pl.when(jnp.logical_not((B * c + s == z) & mine))
        def _():
            for i in range(2):
                rcopy(rows_out[i].at[s], rows_out[i].at[s], rs(i, 0), rr(i, s), (dp, z)).wait_recv()
    far_x(c).wait_send()

    @pl.when(mine)
    def _():
        for r in range(1, Z):
            @pl.when(w_direct(r))
            def _():
                for a in range(4):
                    w_z(a, r).wait_send()
    for j in range(B):
        @pl.when(B * c + j != z)
        def _():
            for a in range(4):
                @pl.when(relay)
                def _():
                    w_onward(a, j).wait_send()
                for k in range(1, Q):
                    w_p(a, j, k, q).wait_send()
    for s in range(B):
        @pl.when(jnp.logical_not((B * c + s == z) & mine))
        def _():
            t_z(s).wait_send()
    for p in range(per):
        here = (c * per + p == z) & mine

        @pl.when(here)
        def _():
            for i in range(2):
                keep_l(i, p).wait()

        @pl.when(jnp.logical_not(here))
        def _():
            for i in range(2):
                keep_x(i, p).wait_send()
    for s in range(B):
        @pl.when(jnp.logical_not((B * c + s == z) & mine))
        def _():
            for i in range(2):
                rcopy(kept_out[i].at[s], kept_out[i].at[s], ms(i, 0), mr(i, s), (dp, z)).wait_recv()
    assert al.used <= LAYER_SEMS


def layer(Q, Z, comp, mem, tok, cot, wq, wk, wv, wo, up, down, ub, vc, sq, g1, b1, g2, b2, db):
    B, R, D = tok.shape
    H = wq.shape[1]
    S = R * Z
    N = S // 2
    W = B * H
    heads = W // HEAD_DIM
    E = up.shape[1] // (2 * Q)
    F = E * Z
    rows = 2 * Q * N
    vm = pltpu.VMEM
    return pl.pallas_call(
        functools.partial(layer_kernel, Q, Z),
        out_shape=[
            sds((D, 3 * H), BF), sds((H, D), BF), sds((D, 2 * Q * E), BF), sds((2 * Q * E, D), BF), sds((2 * Q, 1, E), F32),
            sds((8, D), F32), sds((B, R, D), BF), sds((B, R, D), BF), sds((B, R, D), BF), sds((B, R, D), BF),
        ],
        in_specs=[ANY] * 11 + [VM] + [ANY] + [VM] * 5,
        out_specs=[ANY] * 5 + [VM] + [ANY] * 4,
        scratch_shapes=[
            vm((3, S, D), BF), vm((3 * S, D), BF), vm((D, W), BF), vm((D, W), BF), vm((D, W), BF), vm((W, D), BF),
            vm((S, W), BF), vm((3 * S, W), BF), vm((3 * S, W), BF), vm((heads, S, 3 * S), BF), vm((S, W), BF),
            vm((N, D), F32), vm((N, D), F32), vm((N, D), F32), vm((rows, D), BF), vm((rows, D), BF), vm((D, F), BF), vm((F, D), BF),
            vm((Z, 1, E), F32), vm(vc.shape, jnp.int32), vm((rows, F), BF), vm((rows, F), BF), vm((rows, D), BF),
            vm((Q * N, D), BF), vm((N, D), BF), vm((2 * N, D), BF), vm((S, D), BF),
            vm((N, D), BF), vm((N, D), BF), vm((D, F), BF), vm((F, D), BF), vm((Q * N, D), BF), vm((N, D), BF), vm((2 * N, D), BF),
            vm((N, D), F32), vm((N, D), F32),
            vm((4, D, E), BF), vm((4, E, D), BF), vm((Z, 1, E), F32), vm((1, E), F32),
            vm((D, 128), F32), vm((8, D), F32), vm((8, D), F32), vm((8, D), F32),
            vm((Q, 8, D), F32), vm((Z, 8, D), F32),
            DMA((LAYER_SEMS,)), pltpu.SemaphoreType.REGULAR,
        ],
        compiler_params=pltpu.CompilerParams(collective_id=1, has_side_effects=True, vmem_limit_bytes=63 << 20),
        name="layer",
    )(comp, mem, tok, cot, wq, wk, wv, wo, up, down, ub, vc, sq, g1, b1, g2, b2, db)


def convert_kernel(w, wo, u, d, t, a0, a1, a2, v, gk, gv, gq, go, gu, gd, gt, b0, b1, b2, *vecs):
    for i, out in enumerate(vecs):
        out[...] = v[i, :]
    h = gk.shape[1]
    for i, out in enumerate((gk, gv, gq)):
        out[...] = w[:, i * h:(i + 1) * h].astype(F32)
    for src, out in ((wo, go), (u, gu), (d, gd), (t, gt)):
        out[...] = src[...].astype(F32)
    for src, out in ((a0, b0), (a1, b1), (a2, b2)):
        out[...] = src[...]


def convert(small, w, wo, u, d, *rows):
    steps = 2
    H = w.shape[1] // 3
    D = rows[0].shape[2]
    flat = [r.reshape(-1, D) for r in rows]

    def spec(a, cols=None):
        return pl.BlockSpec((a.shape[0] // steps, a.shape[1] if cols is None else cols), lambda i: (i, 0))

    ins = [w, wo, u, d] + flat
    shapes = [sds((w.shape[0], H), F32)] * 3 + [sds(a.shape, F32) for a in (wo, u, d, flat[0])] + [sds(a.shape, BF) for a in flat[1:]]
    out = pl.pallas_call(
        convert_kernel,
        grid=(steps,),
        out_shape=shapes + [sds((D,), F32)] * 5,
        in_specs=[spec(a) for a in ins] + [pl.BlockSpec(small.shape, lambda i: (0, 0))],
        out_specs=[spec(a) for a in shapes] + [pl.BlockSpec((D,), lambda i: (0,))] * 5,
        compiler_params=pltpu.CompilerParams(vmem_limit_bytes=63 << 20),
        name="convert",
    )(*ins, small)
    return list(out[:6]) + [o.reshape(rows[0].shape) for o in out[6:10]] + list(out[10:])


def chip_device(Q, Z, tokens, memory, compressed, valid_counts, attention_norm_gain, attention_norm_bias,
                query_projection, key_projection, value_projection, out_weight, feedforward_norm_gain,
                feedforward_norm_bias, up_weight, up_bias, down_weight, down_bias, squeeze_weight, cotangent):
    B, R, D = tokens.shape
    H = query_projection.shape[1]
    FL = up_weight.shape[1]
    E = FL // (2 * Q)
    aw, ago, afu, afd, aub, small, o_out, o_tg, o_nm, o_nc = layer(
        Q, Z, compressed, memory, tokens, cotangent, query_projection, key_projection, value_projection, out_weight,
        up_weight, down_weight, up_bias.reshape(2 * Q, 1, E), jnp.broadcast_to(valid_counts[:, None, None], (B, 8, 128)),
        squeeze_weight, attention_norm_gain.reshape(1, D), attention_norm_bias.reshape(1, D),
        feedforward_norm_gain.reshape(1, D), feedforward_norm_bias.reshape(1, D), down_bias.reshape(1, D),
    )
    gk, gv, gq, go, gu, gd, g_tokens, out, new_mem, new_comp, *vecs = convert(small, aw, ago, afu, afd, o_tg, o_out, o_nm, o_nc)
    return (
        out, g_tokens, vecs[0], vecs[1], gq, gk, gv, go, vecs[2], vecs[3], gu, aub.reshape(FL), gd, vecs[4], new_mem, new_comp,
    )


def solution(mesh):
    in_specs = (
        P("dp", "mp", None),
        P("dp", "mp", None),
        P("dp", "mp", None),
        P("dp"),
        P(),
        P(),
        P(None, "mp"),
        P(None, "mp"),
        P(None, "mp"),
        P("mp", None),
        P(),
        P(),
        P(None, "mp"),
        P("mp"),
        P("mp", None),
        P(),
        P(),
        P("dp", "mp", None),
    )
    out_specs = (
        P("dp", "mp", None),
        P("dp", "mp", None),
        P(),
        P(),
        P(None, "mp"),
        P(None, "mp"),
        P(None, "mp"),
        P("mp", None),
        P(),
        P(),
        P(None, "mp"),
        P("mp"),
        P("mp", None),
        P(),
        P("dp", "mp", None),
        P("dp", "mp", None),
    )
    Q, Z = mesh.shape["dp"] // 2, mesh.shape["mp"]

    def per_device(*args):
        B, R, D = args[0].shape
        H, FL = args[6].shape[1], args[12].shape[1]
        whole = Q == 4 and B == 2 and 2 * B == Z and H % HEAD_DIM == 0 and D % (16 * Q) == 0 and H % (16 * Q) == 0
        if whole and R % 32 == 0 and FL % (256 * Q) == 0:
            return chip_device(Q, Z, *args)
        return general_device(*args)

    return jax.shard_map(
        per_device, mesh=mesh, in_specs=in_specs, out_specs=out_specs, check_vma=False
    )
```

```python
import functools

import jax
import jax.numpy as jnp
from jax import lax
from jax.experimental import pallas as pl
from jax.experimental.pallas import tpu as pltpu
from jax.sharding import PartitionSpec as P

HEAD_DIM = 128
RATE = 3


def apply_layer_norm(rows):
    center = jnp.mean(rows, axis=-1, keepdims=True)
    centered = rows - center
    spread = jnp.mean(centered * centered, axis=-1, keepdims=True)
    inverse_deviation = lax.rsqrt(spread + 1e-05)
    return (centered * inverse_deviation, inverse_deviation)


def norm_backward_pass(input_gradient, standardized_rows, inverse_deviation, scale_factor):
    scaled_rows = input_gradient * scale_factor
    attention_norm_mean = jnp.mean(scaled_rows, axis=-1, keepdims=True)
    feedforward_norm_mean = jnp.mean(scaled_rows * standardized_rows, axis=-1, keepdims=True)
    return inverse_deviation * (
        scaled_rows - attention_norm_mean - standardized_rows * feedforward_norm_mean
    )


def squeeze_rows(old_comp, old_mem, fresh, valid_count, offset, own_rows, squeeze_weight):
    features = old_mem.shape[1]
    joined = jnp.concatenate([old_mem, fresh], axis=0)
    new_memory = lax.dynamic_slice_in_dim(joined, valid_count + offset, own_rows, 0)
    comp_len = old_comp.shape[0]
    evicted = valid_count // RATE
    first_row = evicted + offset
    window_start = jnp.maximum(first_row - comp_len, 0)
    padded = jnp.concatenate(
        [old_mem, jnp.zeros((RATE * own_rows, features), jnp.bfloat16)], axis=0
    )
    window = lax.dynamic_slice_in_dim(padded, window_start * RATE, RATE * own_rows, 0)
    squeezed = jnp.dot(
        window.reshape(own_rows, RATE * features),
        squeeze_weight,
        preferred_element_type=jnp.float32,
    ).astype(jnp.bfloat16)
    positions = first_row + jnp.arange(own_rows)
    from_old = jnp.take(old_comp, jnp.clip(positions, 0, comp_len - 1), axis=0)
    from_new = jnp.take(
        squeezed, jnp.clip(positions - comp_len - window_start, 0, own_rows - 1), axis=0
    )
    new_compressed = jnp.where((positions < comp_len)[:, None], from_old, from_new)
    return (new_memory, new_compressed)


def general_device(
    tokens,
    memory,
    compressed,
    valid_counts,
    attention_norm_gain,
    attention_norm_bias,
    query_projection,
    key_projection,
    value_projection,
    out_weight,
    feedforward_norm_gain,
    feedforward_norm_bias,
    up_weight,
    up_bias,
    down_weight,
    down_bias,
    squeeze_weight,
    cotangent,
):
    batch_segs, own_rows, features = tokens.shape
    offset = lax.axis_index("mp") * own_rows
    old_comp, old_mem, fresh = (
        lax.all_gather(compressed, "mp", axis=1, tiled=True),
        lax.all_gather(memory, "mp", axis=1, tiled=True),
        lax.all_gather(tokens, "mp", axis=1, tiled=True),
    )
    seg_len = fresh.shape[1]
    prior_rows = old_comp.shape[1] + old_mem.shape[1]
    context_tokens = jnp.concatenate([old_comp, old_mem, fresh], axis=1).astype(jnp.float32)
    ctx_len = context_tokens.shape[1]
    standardized_full, inverse_deviation_full = apply_layer_norm(context_tokens)
    normed_rows = (standardized_full * attention_norm_gain + attention_norm_bias).astype(
        jnp.bfloat16
    )
    token_rows_normed = normed_rows[:, prior_rows:]
    queries = jnp.einsum(
        "xhp,pj->xhj", token_rows_normed, query_projection, preferred_element_type=jnp.float32
    ).astype(jnp.bfloat16)
    key_rows = jnp.einsum(
        "xhp,pj->xhj", normed_rows, key_projection, preferred_element_type=jnp.float32
    ).astype(jnp.bfloat16)
    values = jnp.einsum(
        "xhp,pj->xhj", normed_rows, value_projection, preferred_element_type=jnp.float32
    ).astype(jnp.bfloat16)
    local_heads = query_projection.shape[1] // HEAD_DIM
    score_scale = HEAD_DIM ** (-0.5)

    def by_heads(matrix):
        return matrix.reshape(matrix.shape[0], matrix.shape[1], local_heads, HEAD_DIM)

    query_pos = jnp.arange(seg_len)[:, None]
    key_pos = jnp.arange(ctx_len)[None, :] - prior_rows
    allowed = (key_pos[None] < 0) | (key_pos <= query_pos)[None] & (
        key_pos[None] < valid_counts[:, None, None]
    )

    def scores_of(query_in, key_in):
        raw = (
            jnp.einsum(
                "gqhe,gkhe->ghqk",
                by_heads(query_in),
                by_heads(key_in),
                preferred_element_type=jnp.float32,
            )
            * score_scale
        )
        return jnp.where(allowed[:, None], raw, -1e30)

    scores = scores_of(queries, key_rows)
    peak_score = jnp.max(scores, axis=-1, keepdims=True)
    exponent = jnp.exp(scores - peak_score)
    exp_total = jnp.sum(exponent, axis=-1, keepdims=True)
    log_total = peak_score + jnp.log(exp_total)
    probs_low = (exponent / exp_total).astype(jnp.bfloat16)
    mixed_heads = jnp.einsum(
        "ghqk,gkhe->gqhe", probs_low, by_heads(values), preferred_element_type=jnp.float32
    ).astype(jnp.bfloat16)
    mixed_heads = mixed_heads.reshape(batch_segs, seg_len, local_heads * HEAD_DIM)
    partial_attn = jnp.einsum(
        "gsc,cd->gsd", mixed_heads, out_weight, preferred_element_type=jnp.float32
    )
    attention = lax.psum_scatter(partial_attn, "mp", scatter_dimension=1, tiled=True)
    residual_stream = tokens.astype(jnp.float32) + attention
    standardized_feedforward, inverse_deviation_feedforward = apply_layer_norm(residual_stream)
    feedforward_input = (
        standardized_feedforward * feedforward_norm_gain + feedforward_norm_bias
    ).astype(jnp.bfloat16)
    second_all = lax.all_gather(feedforward_input, "mp", axis=1, tiled=True)
    upper_in = (
        jnp.einsum("gsd,df->gsf", second_all, up_weight, preferred_element_type=jnp.float32)
        + up_bias
    )
    active, gelu_back = jax.vjp(jax.nn.gelu, upper_in)
    active_low = active.astype(jnp.bfloat16)
    partial_ffn = jnp.einsum(
        "gsf,fd->gsd", active_low, down_weight, preferred_element_type=jnp.float32
    )
    down_out = lax.psum_scatter(
        partial_ffn.astype(jnp.bfloat16), "mp", scatter_dimension=1, tiled=True
    ).astype(jnp.float32)
    output = (residual_stream + down_out + down_bias).astype(jnp.bfloat16)

    def update_one(comp_seg, mem_seg, fresh_seg, valid_count):
        return squeeze_rows(
            comp_seg, mem_seg, fresh_seg, valid_count, offset, own_rows, squeeze_weight
        )

    new_memory, new_compressed = jax.vmap(update_one)(old_comp, old_mem, fresh, valid_counts)
    output_gradient = cotangent.astype(jnp.float32)
    down_bias_grad = jnp.sum(output_gradient, axis=(0, 1))
    grad_all = lax.all_gather(cotangent, "mp", axis=1, tiled=True)
    down_weight_grad = jnp.einsum(
        "gsf,gsd->fd", active_low, grad_all, preferred_element_type=jnp.float32
    )
    grad_active = jnp.einsum(
        "gsd,fd->gsf", grad_all, down_weight, preferred_element_type=jnp.float32
    )
    grad_upper = gelu_back(grad_active)[0].astype(jnp.bfloat16)
    up_weight_grad = jnp.einsum(
        "gsd,gsf->df", second_all, grad_upper, preferred_element_type=jnp.float32
    )
    up_bias_grad = jnp.sum(grad_upper.astype(jnp.float32), axis=(0, 1))
    partial_second = jnp.einsum(
        "gsf,df->gsd", grad_upper, up_weight, preferred_element_type=jnp.float32
    )
    feedforward_gradient = lax.psum_scatter(partial_second, "mp", scatter_dimension=1, tiled=True)
    feedforward_gain_gradient = jnp.sum(
        feedforward_gradient * standardized_feedforward, axis=(0, 1)
    )
    second_bias_grad = jnp.sum(feedforward_gradient, axis=(0, 1))
    residual_gradient = output_gradient + norm_backward_pass(
        feedforward_gradient,
        standardized_feedforward,
        inverse_deviation_feedforward,
        feedforward_norm_gain,
    )
    grad_resid_all = lax.all_gather(
        residual_gradient.astype(jnp.bfloat16), "mp", axis=1, tiled=True
    )
    out_weight_grad = jnp.einsum(
        "gsc,gsd->cd", mixed_heads, grad_resid_all, preferred_element_type=jnp.float32
    )
    grad_mixed = jnp.einsum(
        "gsd,cd->gsc", grad_resid_all, out_weight, preferred_element_type=jnp.float32
    ).astype(jnp.bfloat16)
    probs_again = jnp.exp(scores_of(queries, key_rows) - log_total)
    grad_probs = jnp.einsum(
        "gqhe,gkhe->ghqk",
        by_heads(grad_mixed),
        by_heads(values),
        preferred_element_type=jnp.float32,
    )
    row_dot = jnp.sum(probs_again * grad_probs, axis=-1, keepdims=True)
    grad_scores = (probs_again * (grad_probs - row_dot)).astype(jnp.bfloat16)
    query_gradient = (
        score_scale
        * jnp.einsum(
            "ghqk,gkhe->gqhe", grad_scores, by_heads(key_rows), preferred_element_type=jnp.float32
        )
    ).astype(jnp.bfloat16)
    key_gradient = (
        score_scale
        * jnp.einsum(
            "ghqk,gqhe->gkhe", grad_scores, by_heads(queries), preferred_element_type=jnp.float32
        )
    ).astype(jnp.bfloat16)
    value_gradient = jnp.einsum(
        "ghqk,gqhe->gkhe",
        probs_again.astype(jnp.bfloat16),
        by_heads(grad_mixed),
        preferred_element_type=jnp.float32,
    ).astype(jnp.bfloat16)
    query_gradient = query_gradient.reshape(batch_segs, seg_len, -1)
    key_gradient = key_gradient.reshape(batch_segs, ctx_len, -1)
    value_gradient = value_gradient.reshape(batch_segs, ctx_len, -1)
    query_weight_grad = jnp.einsum(
        "nja,njr->ar", token_rows_normed, query_gradient, preferred_element_type=jnp.float32
    )
    key_weight_grad = jnp.einsum(
        "nja,njr->ar", normed_rows, key_gradient, preferred_element_type=jnp.float32
    )
    value_weight_grad = jnp.einsum(
        "nja,njr->ar", normed_rows, value_gradient, preferred_element_type=jnp.float32
    )
    partial_normed = jnp.einsum(
        "xmo,qo->xmq", key_gradient, key_projection, preferred_element_type=jnp.float32
    )
    partial_normed = partial_normed + jnp.einsum(
        "xmo,qo->xmq", value_gradient, value_projection, preferred_element_type=jnp.float32
    )
    partial_normed = partial_normed.at[:, prior_rows:].add(
        jnp.einsum(
            "xmo,qo->xmq", query_gradient, query_projection, preferred_element_type=jnp.float32
        )
    )
    partial_normed = partial_normed.reshape(batch_segs, 3, seg_len, features)
    normed_gradient = lax.psum_scatter(
        partial_normed.astype(jnp.bfloat16), "mp", scatter_dimension=2, tiled=True
    ).astype(jnp.float32)
    segment_context = jnp.stack([compressed, memory, tokens], axis=1).astype(jnp.float32)
    standardized_segment, inverse_deviation_segment = apply_layer_norm(segment_context)
    attention_gain_gradient = jnp.sum(normed_gradient * standardized_segment, axis=(0, 1, 2))
    first_bias_grad = jnp.sum(normed_gradient, axis=(0, 1, 2))
    tokens_grad = residual_gradient + norm_backward_pass(
        normed_gradient[:, 2],
        standardized_segment[:, 2],
        inverse_deviation_segment[:, 2],
        attention_norm_gain,
    )
    summed = (
        lax.psum(query_weight_grad.astype(jnp.bfloat16), "dp").astype(jnp.float32),
        lax.psum(key_weight_grad.astype(jnp.bfloat16), "dp").astype(jnp.float32),
        lax.psum(value_weight_grad.astype(jnp.bfloat16), "dp").astype(jnp.float32),
        lax.psum(out_weight_grad.astype(jnp.bfloat16), "dp").astype(jnp.float32),
        lax.psum(up_weight_grad.astype(jnp.bfloat16), "dp").astype(jnp.float32),
        lax.psum(up_bias_grad.astype(jnp.bfloat16), "dp").astype(jnp.float32),
        lax.psum(down_weight_grad.astype(jnp.bfloat16), "dp").astype(jnp.float32),
    )
    norms = lax.psum(
        (
            attention_gain_gradient,
            first_bias_grad,
            feedforward_gain_gradient,
            second_bias_grad,
            down_bias_grad,
        ),
        ("dp", "mp"),
    )
    return (
        output,
        tokens_grad,
        norms[0],
        norms[1],
        summed[0],
        summed[1],
        summed[2],
        summed[3],
        norms[2],
        norms[3],
        summed[4],
        summed[5],
        summed[6],
        norms[4],
        new_memory,
        new_compressed,
    )


BF = jnp.bfloat16
F32 = jnp.float32
MESH = pl.DeviceIdType.MESH
ANY = pl.BlockSpec(memory_space=pl.ANY)
VM = pl.BlockSpec(memory_space=pltpu.VMEM)
DMA = pltpu.SemaphoreType.DMA


def sds(shape, dtype):
    return jax.ShapeDtypeStruct(shape, dtype)


def where_am_i(chips, depth):
    dp = lax.axis_index("dp")
    return dp, lax.rem(dp, 2), dp // 2, lax.axis_index("mp")


def rcopy(src, dst, send, recv, device):
    return pltpu.make_async_remote_copy(
        src_ref=src,
        dst_ref=dst,
        send_sem=send,
        recv_sem=recv,
        device_id=device,
        device_id_type=MESH,
    )


def lcopy(src, dst, sem):
    return pltpu.make_async_copy(src, dst, sem)


def enter(partners):
    barrier = pltpu.get_barrier_semaphore()
    for p in partners:
        pl.semaphore_signal(barrier, inc=1, device_id=p, device_id_type=MESH)
    pl.semaphore_wait(barrier, len(partners))


def across(q, k):
    if k == 0:
        return q
    if k == 1:
        return q + 1 - 2 * lax.rem(q, 2)
    if k == 2:
        return lax.rem(q + 2, 4)
    return 3 - q


def across_by(q, i):
    x, y = lax.rem(q, 2), q // 2
    dx, dy = 1 - lax.rem(i, 2), 1 - i // 2
    return (x + dx - 2 * x * dx) + 2 * (y + dy - 2 * y * dy)


def layer_norm_rows(rows):
    center = jnp.mean(rows, axis=-1, keepdims=True)
    centered = rows - center
    spread = jnp.mean(centered * centered, axis=-1, keepdims=True)
    inv = lax.rsqrt(spread + 1e-05)
    return centered * inv, inv


class Slots:
    def __init__(self, ref):
        self.ref = ref
        self.used = 0

    def take(self, *shape):
        base = self.used
        size = 1
        for n in shape:
            size *= n
        self.used += size

        def at(*index):
            flat = 0
            for n, i in zip(shape, index):
                flat = flat * n + i
            return self.ref.at[base + flat]

        return at


def nt_dot(a, b):
    return lax.dot_general(a, b, (((1,), (1,)), ((), ())), preferred_element_type=F32)


def tn_dot(a, b):
    return lax.dot_general(a, b, (((0,), (0,)), ((), ())), preferred_element_type=F32)


def nn_dot(a, b):
    return jnp.dot(a, b, preferred_element_type=F32)


def one_hot(shape, offset):
    row = lax.broadcasted_iota(jnp.int32, shape, 0)
    col = lax.broadcasted_iota(jnp.int32, shape, 1)
    return jnp.where(col == row + offset, 1.0, 0.0).astype(BF)


def stack(ref, offset, rows, width=None):
    width = ref.shape[-1] if width is None else width

    def view(i):
        return ref.at[pl.ds(pl.multiple_of(offset + i * rows, rows), rows), pl.ds(0, width)]

    return view


class PlaneSum:
    def __init__(self, al, peer, blk, rows, h, g):
        self.peer, self.blk, self.half, self.rows, self.h, self.g = peer, blk, rows // 2, rows, h, g
        self.hs, self.hr, self.gs, self.gr = al.take(2), al.take(2), al.take(2), al.take(2)

    def h_x(self, i):
        return rcopy(self.blk(3, i * self.half, self.half), self.h(i), self.hs(i), self.hr(i), self.peer(i + 1))

    def g_x(self, i):
        return rcopy(self.blk(i + 1, 0, self.rows), self.g(i), self.gs(i), self.gr(i), self.peer(i + 1))

    def start(self):
        for i in range(2):
            self.h_x(i).start()

    def middle(self):
        for i in range(2):
            self.h_x(i).wait_recv()
            mine = self.blk(2 - i, i * self.half, self.half)
            mine[...] = (mine[...].astype(F32) + self.h(i)[...].astype(F32)).astype(BF)
            self.g_x(1 - i).start()

    def arrive(self):
        for i in range(2):
            self.g_x(i).wait_recv()

    def total(self):
        self.arrive()
        own = self.blk(0, 0, self.rows)
        return own[...].astype(F32) + (self.g(0)[...].astype(F32) + self.g(1)[...].astype(F32))

    def drain(self):
        for i in range(2):
            self.h_x(i).wait_send()
            self.g_x(i).wait_send()


class PlaneGather:
    def __init__(self, al, peer, sib, loc, rows, own=None):
        self.peer, self.sib, self.loc, self.half, self.rows = peer, sib, loc, rows // 2, rows
        self.own = own
        self.as_, self.ar, self.hs, self.hr = al.take(2), al.take(2), al.take(2), al.take(2)
        self.fs, self.fr = al.take(4), al.take(4)

    def a_x(self, i, k=0):
        src = self.loc(0, 0, self.rows) if self.own is None else self.own
        return rcopy(src, self.loc(k, 0, self.rows), self.as_(i), self.ar(i), self.peer(i + 1))

    def h_x(self, i, k=None):
        k = 2 - (1 - i) if k is None else k
        rows = self.loc(k, i * self.half, self.half)
        return rcopy(rows, rows, self.hs(i), self.hr(i), self.peer(2 - i))

    def f_x(self, k, other=None):
        src = self.loc(k, 0, self.rows)
        if k == 0 and self.own is not None:
            src = self.own
        dst = self.loc(k, 0, self.rows) if other is None else other(k, 0, self.rows)
        return rcopy(src, dst, self.fs(k), self.fr(k), self.sib)

    def start(self):
        for i in range(2):
            self.a_x(i).start()
        self.f_x(0).start()

    def middle(self):
        for i in range(2):
            rcopy(self.loc(i + 1, 0, self.rows), self.loc(i + 1, 0, self.rows), self.as_(i), self.ar(i), self.peer(1)).wait_recv()
            self.h_x(i).start()
            self.f_x(i + 1).start()

    def last(self):
        for i in range(2):
            self.h_x(i, 3).wait_recv()
        self.f_x(3).start()

    def drain(self):
        for i in range(2):
            self.a_x(i).wait_send()
            self.h_x(i).wait_send()
        for k in range(4):
            self.f_x(k).wait_send()

    def arrivals(self, other):
        for k in range(4):
            rcopy(other(k, 0, self.rows), other(k, 0, self.rows), self.fs(k), self.fr(k), self.sib).wait_recv()


LAYER_SEMS = 600


def layer_kernel(Q, Z, comp, mem, tok, cot, wq, wk, wv, wo, up, down, ub, vc, sq, g1, b1, g2, b2, db,
                 aw, ago, afu, afd, aub, small_o, out_o, tg_o, nm_o, nc_o,
                 ctx, normed, wqs, wks, wvs, wos, qs, ks, vs, probs, mixed, phalf, got, resid, sec, cots, ups, downs,
                 ubs, vco, act, gup, gbuf, got1, gh, gg, glow, nms, ncs, gus, gds, dgot, dh, dg, ggot, srow,
                 xu, xd, xb, fbs, arow, ffs, sums, sgot, pgot, zgot, sems, ready):
    dp, c, q, z = where_am_i(Q, Z)
    sd = dp + 1 - 2 * c
    sib = (sd, z)
    partners = [sib]
    for r in range(1, Z):
        for d in (dp, sd):
            partners.append((d, lax.rem(z + r, Z)))
    for k in range(1, Q):
        partners.append((2 * across(q, k) + c, z))
    enter(partners)
    B, R, D = tok.shape
    H = wq.shape[1]
    QR = D // Q
    OR = H // Q
    HR = R // 2
    S = R * Z
    N = S // 2
    E = up.shape[1] // (2 * Q)
    heads = B * H // HEAD_DIM
    mine = c == z // B
    jz = lax.rem(z, B)
    al = Slots(sems)

    def peer(k):
        return (2 * across(q, k) + c, z)

    wins = [wq, wk, wv, wo]
    wss = [wqs, wks, wvs, wos]

    def piece(a):
        if a < 3:
            return wins[a].at[pl.ds(q * QR, QR), :]
        return wo.at[pl.ds(q * OR, OR), :]

    def place(a, j, qq):
        if a < 3:
            return wss[a].at[pl.ds(pl.multiple_of(qq * QR, QR), QR), pl.ds(pl.multiple_of(j * H, H), H)]
        return wos.at[pl.ds(pl.multiple_of(j * H + qq * OR, OR), OR), :]

    def place_whole(a, j):
        if a < 3:
            return wss[a].at[:, pl.ds(pl.multiple_of(j * H, H), H)]
        return wos.at[pl.ds(pl.multiple_of(j * H, H), H), :]

    ws, wr = al.take(4, Z - 1), al.take(4, B)
    ps, pr = al.take(4, B, Q - 1), al.take(4, B, Q - 1)
    wl = al.take(4)

    def w_z(a, r):
        return rcopy(piece(a), place(a, jz, q), ws(a, r - 1), wr(a, jz), (dp, lax.rem(z + r, Z)))

    def w_direct(r):
        zt = lax.rem(z + r, Z)
        return jnp.logical_not((lax.rem(zt, Z - 1) == 0) & (zt // B != z // B))

    wf = al.take(4, B)

    def w_onward(a, j):
        return rcopy(place(a, j, q), place(a, j, q), wf(a, j), wr(a, j), (dp, (Z - 1) * (1 - c)))

    def w_arrive(a, j):
        return rcopy(place(a, j, q), place(a, j, q), ws(a, 0), wr(a, j), (dp, z))

    def w_p(a, j, k, qq):
        return rcopy(place(a, j, qq), place(a, j, qq), ps(a, j, k - 1), pr(a, j, k - 1), peer(k))

    relay = z == 2 - c

    def w_l(a):
        return lcopy(wins[a], place_whole(a, jz), wl(a))

    acts = [comp, mem, tok]
    cs, cr = al.take(3, B, 2), al.take(3, Z)
    fs, fr = al.take(3, Z), al.take(3, Z)
    cl = al.take(3)

    def c_rows(t, zs):
        return ctx.at[t, pl.ds(pl.multiple_of(zs * R, R), R), :]

    def c_half(t, zs, h):
        return ctx.at[t, pl.ds(pl.multiple_of(zs * R + HR * h, HR), HR), :]

    def c_l(t):
        return lcopy(acts[t].at[jz], c_rows(t, z), cl(t))

    def c_sib(t):
        return rcopy(acts[t].at[jz], c_rows(t, z), fs(t, z), fr(t, z), sib)

    def c_z(t, s, h):
        return rcopy(acts[t].at[s, pl.ds(HR * h, HR), :], c_half(t, z, h), cs(t, s, h), cr(t, z), (2 * q + h, B * c + s))

    def c_arrive(t, zs):
        return rcopy(c_half(t, zs, c), c_half(t, zs, c), cs(t, 0, 0), cr(t, zs), (dp, z))

    def c_fwd(t, zs, half):
        return rcopy(c_half(t, zs, half), c_half(t, zs, half), fs(t, zs), fr(t, zs), sib)

    us, ur, ul = al.take(Z - 1), al.take(Z - 1), al.take(1)
    vs_, vr_ = al.take(1), al.take(1)

    def u_z(r):
        return rcopy(ub.at[dp], ubs.at[r], us(r - 1), ur(r - 1), (dp, lax.rem(z + r, Z)))

    u_l = lcopy(ub.at[dp], ubs.at[0], ul(0))
    v_s = rcopy(vc, vco, vs_(0), vr_(0), sib)

    ts, tr, tl = al.take(B), al.take(B), al.take(1)

    def dev(k, core):
        return 2 * across(q, k) + core

    def t_rows(d, i):
        return cots.at[pl.ds(pl.multiple_of(d * N + i * R, R), R), :]

    def t_z(s):
        to = 2 * q + z // B
        return rcopy(cot.at[s], t_rows(to, jz), ts(s), tr(jz), (to, B * c + s))

    def t_l():
        return lcopy(cot.at[jz], t_rows(dp, jz), tl(0))

    def t_arrive(i):
        return rcopy(t_rows(dp, i), t_rows(dp, i), ts(0), tr(i), (dp, z))

    def rows_at(ref, core):
        def loc(k, lo, n):
            return ref.at[pl.ds(pl.multiple_of(dev(k, core) * N + lo, n), n), :]
        return loc

    tgat = PlaneGather(al, peer, sib, rows_at(cots, c), N)
    agat = PlaneGather(al, peer, sib, rows_at(sec, c), N)

    xs, xr_, xl, xf = al.take(2, Z), al.take(2, Z), al.take(2), al.take(2, 2)
    is_end = lax.rem(z, Z - 1) == 0

    def x_place(i, r):
        if i == 0:
            return ups.at[:, pl.ds(r * E, E)]
        return downs.at[pl.ds(r * E, E), :]

    def x_z(i, r):
        src = up.at[:, pl.ds(pl.multiple_of(dp * E, E), E)] if i == 0 else down.at[pl.ds(pl.multiple_of(dp * E, E), E), :]
        return rcopy(src, x_place(i, r), xs(i, r), xr_(i, r), (dp, lax.rem(z + r, Z)))

    def x_direct(r):
        return (z < Z - 1, is_end, z > 0)[r - 1]

    def x_start(i):
        for r in range(1, Z):
            @pl.when(x_direct(r))
            def _():
                x_z(i, r).start()

    onward = ((2, 3, ((2, 3), (1, 2)), 3), (1, 0, ((2, 1), (3, 2)), 1))

    def x_onward(i, n, to, a, b):
        return rcopy(x_place(i, a), x_place(i, b), xf(i, n), xr_(i, b), (dp, to))

    def x_forward(i):
        for at, to, pairs, rest in onward:
            @pl.when(z == at)
            def _():
                for n, (a, b) in enumerate(pairs):
                    x_z(i, a).wait_recv()
                    x_onward(i, n, to, a, b).start()

    def x_rest(i):
        for at, to, pairs, rest in onward:
            @pl.when(z == at)
            def _():
                x_z(i, rest).wait_recv()

        @pl.when(is_end)
        def _():
            for r in range(1, Z):
                x_z(i, r).wait_recv()

    def x_drain(i):
        for r in range(1, Z):
            @pl.when(x_direct(r))
            def _():
                x_z(i, r).wait_send()
        for at, to, pairs, rest in onward:
            @pl.when(z == at)
            def _():
                for n, (a, b) in enumerate(pairs):
                    x_onward(i, n, to, a, b).wait_send()

    x_l = [lcopy(up.at[:, pl.ds(pl.multiple_of(dp * E, E), E)], ups.at[:, pl.ds(0, E)], xl(0)),
           lcopy(down.at[pl.ds(pl.multiple_of(dp * E, E), E), :], downs.at[pl.ds(0, E), :], xl(1))]

    c_sem = al.take(B)
    c_in = [lcopy(cot.at[i], nms.at[pl.ds(i * R, R), :], c_sem(i)) for i in range(B)]

    for x in c_in:
        x.start()
    sums[...] = jnp.zeros_like(sums)
    @pl.when(mine)
    def _():
        for r in range(1, Z):
            @pl.when(w_direct(r))
            def _():
                for a in range(4):
                    w_z(a, r).start()
        for a in range(4):
            w_l(a).start()
        for t in range(3):
            c_l(t).start()
            c_sib(t).start()
    for r in range(1, Z):
        u_z(r).start()
    v_s.start()
    u_l.start()
    for x in x_l:
        x.start()
    for j in range(B):
        @pl.when(B * c + j != z)
        def _():
            for a in range(4):
                w_arrive(a, j).wait_recv()

                @pl.when(relay)
                def _():
                    w_onward(a, j).start()
                for k in range(1, Q):
                    w_p(a, j, k, q).start()
    def c_start(t):
        for s in range(B):
            @pl.when(B * c + s != z)
            def _():
                for h in range(2):
                    c_z(t, s, h).start()

    def c_sent(t):
        for s in range(B):
            @pl.when(B * c + s != z)
            def _():
                for h in range(2):
                    c_z(t, s, h).wait_send()

    for t in range(3):
        c_start(t)

    def norm_block(t, zs):
        at = pl.ds(pl.multiple_of(zs * R, R), R)
        to = pl.ds(pl.multiple_of(t * S + zs * R, R), R)
        xhat, _ = layer_norm_rows(ctx[t, at, :].astype(F32))
        normed[to, :] = (xhat * g1[...] + b1[...]).astype(BF)

    @pl.when(mine)
    def _():
        for t in range(3):
            c_l(t).wait()

    @pl.when(jnp.logical_not(mine))
    def _():
        for t in range(3):
            rcopy(c_rows(t, z), c_rows(t, z), fs(t, z), fr(t, z), sib).wait_recv()

    def norm_own(t, carry):
        norm_block(t, z)
        return carry

    lax.fori_loop(0, 3, norm_own, 0)
    for x in c_in:
        x.wait()
    sums[4:5, :] = jnp.sum(nms[...].astype(F32), axis=0, keepdims=True)
    T = 256

    def project(i, carry):
        at = pl.ds(pl.multiple_of(i * T, T), T)
        ks[at, :] = nn_dot(normed[at, :], wks[...]).astype(BF)
        vs[at, :] = nn_dot(normed[at, :], wvs[...]).astype(BF)
        return carry

    def project_q(i, carry):
        at = pl.ds(pl.multiple_of(i * T, T), T)
        qs[at, :] = nn_dot(normed[pl.ds(pl.multiple_of(2 * S + i * T, T), T), :], wqs[...]).astype(BF)
        return carry

    for t in range(3):
        for r in range(1, Z):
            zs = lax.rem(z + r, Z)
            c_arrive(t, zs).wait_recv()
            c_fwd(t, zs, c).start()
        if t == 2:
            for u in range(3):
                c_sent(u)
            for s in range(B):
                here = (B * c + s == z) & mine

                @pl.when(here)
                def _():
                    t_l().start()

                @pl.when(jnp.logical_not(here))
                def _():
                    t_z(s).start()
            x_start(0)
        for r in range(1, Z):
            c_fwd(t, lax.rem(z + r, Z), 1 - c).wait_recv()

        def norm_one(r, carry, t=t):
            norm_block(t, lax.rem(z + r, Z))
            return carry

        lax.fori_loop(1, Z, norm_one, 0)
        if t == 0:
            for j in range(B):
                @pl.when(B * c + j != z)
                def _():
                    for a in range(4):
                        for k in range(1, Q):
                            w_p(a, j, k, across(q, k)).wait_recv()

            @pl.when(mine)
            def _():
                for a in range(4):
                    w_l(a).wait()
        lax.fori_loop(t * S // T, (t + 1) * S // T, project, 0)
    lax.fori_loop(0, S // T, project_q, 0)
    x_start(1)

    v_s.wait()
    counts = jnp.where(mine, vc[jz], vco[jz])
    count = counts[0:1, 0:1]
    scale = HEAD_DIM ** (-0.5)
    P2 = 2 * S

    def attend(half, tag):
        r0 = pl.multiple_of(half * N, N)

        def head(h, carry):
            hd = pl.ds(pl.multiple_of(h * HEAD_DIM, HEAD_DIM), HEAD_DIM)
            qh = qs[pl.ds(r0, N), hd]
            s1 = nt_dot(qh, ks[pl.ds(0, P2), hd])
            s2 = nt_dot(qh, ks[pl.ds(P2, S), hd])
            row = lax.broadcasted_iota(jnp.int32, (N, S), 0) + half * N
            col = lax.broadcasted_iota(jnp.int32, (N, S), 1)
            s2 = jnp.where((col <= row) & (col < count), s2, -1e30)
            top = jnp.maximum(jnp.max(s1, axis=-1, keepdims=True), jnp.max(s2, axis=-1, keepdims=True))
            p1 = jnp.exp((s1 - top) * scale)
            p2 = jnp.exp((s2 - top) * scale)
            inv = 1.0 / (jnp.sum(p1, axis=-1, keepdims=True) + jnp.sum(p2, axis=-1, keepdims=True))
            p1 = (p1 * inv).astype(BF)
            p2 = (p2 * inv).astype(BF)
            probs[h, pl.ds(r0, N), pl.ds(0, P2)] = p1
            probs[h, pl.ds(r0, N), pl.ds(P2, S)] = p2
            mix = nn_dot(p1, vs[pl.ds(0, P2), hd]) + nn_dot(p2, vs[pl.ds(P2, S), hd])
            mixed[pl.ds(r0, N), hd] = mix.astype(BF)
            return carry

        lax.fori_loop(0, heads, head, 0)

    hs, hr = al.take(1), al.take(1)
    h_x = rcopy(phalf, got, hs(0), hr(0), sib)
    attend(1 - c, 0)
    phalf[...] = nn_dot(mixed[pl.ds(pl.multiple_of((1 - c) * N, N), N), :], wos[...])
    h_x.start()
    for i in range(B):
        @pl.when(jnp.logical_not((B * c + i == z) & mine))
        def _():
            t_arrive(i).wait_recv()

        @pl.when((B * c + i == z) & mine)
        def _():
            t_l().wait()
    tgat.start()
    attend(c, 1)
    own_part = nn_dot(mixed[pl.ds(pl.multiple_of(c * N, N), N), :], wos[...])
    x_forward(0)
    h_x.wait_recv()
    resid[...] = ctx[2, pl.ds(pl.multiple_of(c * N, N), N), :].astype(F32) + (own_part + got[...])
    xhat2, _ = layer_norm_rows(resid[...])
    sec[pl.ds(pl.multiple_of(dp * N, N), N), :] = (xhat2 * g2[...] + b2[...]).astype(BF)

    agat.start()
    sqc = al.take(RATE)
    sqs = [gbuf.at[pl.ds(0, D), :], gbuf.at[pl.ds(D, D), :], dgot]
    sq_x = [lcopy(sq.at[pl.ds(r * D, D), :], sqs[r], sqc(r)) for r in range(RATE)]
    for x in sq_x:
        x.start()
    ss, sr = al.take(Q), al.take(Q)

    def s_x(k):
        return rcopy(rows_at(gbuf, 1 - c)(k, 0, N), stack(got1, 0, N)(k), ss(k), sr(k), sib)

    gsum = PlaneSum(al, peer, rows_at(gbuf, c), N, stack(gh, 0, N // 2), stack(gg, 0, N))
    ffs[...] = jnp.zeros_like(ffs)

    def slope_at(b):
        return (b // 4, pl.ds(pl.multiple_of(lax.rem(b // 2, 2) * N, N), N), pl.ds(pl.multiple_of(lax.rem(b, 2) * Z * E, Z * E), Z * E))

    def up_block(b, bias_row):
        at = pl.ds(pl.multiple_of(b * N, N), N)
        x = nn_dot(sec[at, :], ups[...]) + bias_row
        x2 = x * x
        root = 0.7978845608028654
        th = jnp.tanh(root * (x + 0.044715 * (x2 * x)))
        act[at, :] = (0.5 * x * (1.0 + th)).astype(BF)
        slope = 0.5 * (1.0 + th) + 0.5 * x * (1.0 - th * th) * (root * (1.0 + 0.134145 * x2))
        ctx[slope_at(b)] = slope.astype(BF)
        return bias_row

    def back_block(b):
        at = pl.ds(pl.multiple_of(b * N, N), N)
        ga = nt_dot(cots[at, :], downs[...])
        gu = (ga * ctx[slope_at(b)].astype(F32)).astype(BF)
        gup[at, :] = gu
        ffs[2:3, pl.ds(0, Z * E)] = ffs[2:3, pl.ds(0, Z * E)] + jnp.sum(gu.astype(F32), axis=0, keepdims=True)
        gbuf[at, :] = nt_dot(gu, ups[...]).astype(BF)

    def feed(k):
        def half(i, carry):
            back_block(dev(k, 1 - c) + i * (2 * c - 1))

            @pl.when(i == 0)
            def _():
                s_x(k).start()
            return carry

        lax.fori_loop(0, 2, half, 0)

    def combine(k):
        s_x(k).wait_recv()
        rows = rows_at(gbuf, c)(k, 0, N)
        rows[...] = (rows[...].astype(F32) + stack(got1, 0, N)(k)[...].astype(F32)).astype(BF)

    groups = S // RATE
    squeezed = None
    for r in range(RATE):
        sq_x[r].wait()
        row = lax.broadcasted_iota(jnp.int32, (ncs.shape[0], S), 0)
        col = lax.broadcasted_iota(jnp.int32, (ncs.shape[0], S), 1)
        pick = jnp.where((col == row * RATE + r) & (row < groups), 1.0, 0.0).astype(BF)
        picked = nn_dot(pick, ctx[1]).astype(BF)
        term = nn_dot(picked, sqs[r][...])
        squeezed = term if squeezed is None else squeezed + term
    ncs[...] = squeezed.astype(BF)
    shift = count + c * N
    new_mem = nn_dot(one_hot((N, S), shift), ctx[1]) + nn_dot(one_hot((N, S), shift - S), ctx[2])
    nms[...] = new_mem.astype(BF)
    third = lax.shift_right_logical(count * 21846, 16)
    shift = third + c * N
    new_comp = nn_dot(one_hot((N, S), shift), ctx[0]) + nn_dot(one_hot((N, ncs.shape[0]), shift - S), ncs[...])
    ncs[pl.ds(0, N), :] = new_comp.astype(BF)
    per = N // R
    ms, mr, ml = al.take(2, 2), al.take(2, B), al.take(2)
    kept_in = [nms, ncs]
    kept_out = [nm_o, nc_o]

    def keep_x(i, p):
        return rcopy(kept_in[i].at[pl.ds(p * R, R), :], kept_out[i].at[jz], ms(i, p), mr(i, jz), (2 * q + z // B, c * per + p))

    def keep_l(i, p):
        return lcopy(kept_in[i].at[pl.ds(p * R, R), :], kept_out[i].at[jz], ml(i))

    x_forward(1)
    tgat.middle()
    agat.middle()
    tgat.last()
    agat.last()
    for r in range(1, Z):
        u_z(r).wait()
    u_l.wait()

    @pl.when(mine)
    def _():
        for t in range(3):
            c_sib(t).wait_send()
    for r in range(1, Z):
        for t in range(3):
            c_fwd(t, lax.rem(z + r, Z), c).wait_send()
    x_rest(0)
    for x in x_l:
        x.wait()
    agat.arrivals(rows_at(sec, 1 - c))
    lax.fori_loop(0, 2 * Q, up_block, jnp.concatenate([ubs[r] for r in range(Z)], axis=1))
    x_rest(1)
    tgat.arrivals(rows_at(cots, 1 - c))
    for p in range(per):
        here = (c * per + p == z) & mine

        @pl.when(here)
        def _():
            for i in range(2):
                keep_l(i, p).start()

        @pl.when(jnp.logical_not(here))
        def _():
            for i in range(2):
                keep_x(i, p).start()


    feed(3)
    combine(3)
    gsum.start()
    feed(1)
    feed(2)
    combine(1)
    combine(2)
    gsum.middle()
    feed(0)

    def up_grad(i, carry):
        at = pl.ds(pl.multiple_of(i * T, T), T)
        gus[at, :] = tn_dot(sec[:, at], gup[...]).astype(BF)
        return carry

    lax.fori_loop(0, D // T, up_grad, 0)
    ys, yr = al.take(2, 6), al.take(2, 4)
    near_r, near_z = 3 - 2 * lax.rem(z, 2), z + 1 - 2 * lax.rem(z, 2)

    def y_own(i, r):
        if i == 0:
            return gus.at[:, pl.ds(pl.multiple_of(r * E, E), E)]
        return gds.at[pl.ds(pl.multiple_of(r * E, E), E), :]

    def y_buf(i, n):
        return (xu, xd)[i].at[n]

    def y_near(i):
        return rcopy(y_own(i, near_r), y_buf(i, 0), ys(i, 0), yr(i, 0), (dp, near_z))

    def y_hand(i, n):
        r = 2 if n == 0 else 1 + 2 * (z // 3)
        return rcopy(y_own(i, r), y_buf(i, 2 + n), ys(i, 2 + n), yr(i, 2 + n), (dp, 1 + z // 3))

    def y_far(i, n):
        r = 5 - 2 * z if n == 0 else 2
        return rcopy(y_own(i, r), y_buf(i, 1), ys(i, 4 + n), yr(i, 1), (dp, lax.rem(z + Z - r, Z)))

    def y_start(i):
        @pl.when(is_end)
        def _():
            for n in range(2):
                y_hand(i, n).start()
        y_near(i).start()

    def y_middle(i):
        @pl.when(jnp.logical_not(is_end))
        def _():
            for n in range(2):
                rcopy(y_buf(i, 2 + n), y_buf(i, 2 + n), ys(i, 2 + n), yr(i, 2 + n), (dp, z)).wait_recv()
                mine_ = y_own(i, 5 - 2 * z if n == 0 else 2)
                mine_[...] = (mine_[...].astype(F32) + y_buf(i, 2 + n)[...].astype(F32)).astype(BF)
                y_far(i, n).start()

    def y_arrive(i):
        for n in range(2):
            rcopy(y_buf(i, n), y_buf(i, n), ys(i, 0), yr(i, n), (dp, z)).wait_recv()

    def y_drain(i):
        y_near(i).wait_send()

        @pl.when(is_end)
        def _():
            for n in range(2):
                y_hand(i, n).wait_send()

        @pl.when(jnp.logical_not(is_end))
        def _():
            for n in range(2):
                y_far(i, n).wait_send()

    ubs_, ubr = al.take(Z), al.take(Z)

    def ub_x(r):
        return rcopy(ffs.at[pl.ds(2, 1), pl.ds(r * E, E)], xb.at[r], ubs_(r), ubr(r), (dp, lax.rem(z + Z - r, Z)))

    y_start(0)
    for r in range(1, Z):
        ub_x(r).start()
    agat.drain()

    def down_rows(b, carry):
        at = pl.ds(pl.multiple_of(b * N, N), N)
        sec[at, :] = nn_dot(act[at, :], downs[...]).astype(BF)
        return carry

    lax.fori_loop(0, 2 * Q, down_rows, 0)
    dss, dsr = al.take(Q), al.take(Q)

    def d_x(k):
        return rcopy(rows_at(sec, 1 - c)(k, 0, N), stack(dgot, 0, N)(k), dss(k), dsr(k), sib)

    dsum = PlaneSum(al, peer, rows_at(sec, c), N, stack(dh, 0, N // 2), stack(dg, 0, N))
    for k in (3, 1, 2, 0):
        d_x(k).start()

    def down_grad(i, carry):
        at = pl.ds(pl.multiple_of(i * T, T), T)
        gds[at, :] = tn_dot(act[:, at], cots[...]).astype(BF)
        return carry

    lax.fori_loop(0, Z * E // T, down_grad, 0)

    y_start(1)
    for k in (3, 1, 2, 0):
        d_x(k).wait_recv()
        rows = rows_at(sec, c)(k, 0, N)
        rows[...] = (rows[...].astype(F32) + stack(dgot, 0, N)(k)[...].astype(F32)).astype(BF)
    combine(0)
    gsum.arrive()
    dsum.start()
    C = 64

    def back_rows(i, carry):
        at = pl.ds(pl.multiple_of(i * C, C), C)
        own = pl.ds(pl.multiple_of(dp * N + i * C, C), C)
        gs = gbuf[own, :].astype(F32) + (gg[at, :].astype(F32) + gg[pl.ds(pl.multiple_of(N + i * C, C), C), :].astype(F32))
        xhat, inv = layer_norm_rows(resid[at, :])
        ffs[0:1, :] = ffs[0:1, :] + jnp.sum(gs * xhat, axis=0, keepdims=True)
        ffs[1:2, :] = ffs[1:2, :] + jnp.sum(gs, axis=0, keepdims=True)
        e = gs * g2[...]
        m1 = jnp.mean(e, axis=-1, keepdims=True)
        m2 = jnp.mean(e * xhat, axis=-1, keepdims=True)
        gr = cots[own, :].astype(F32) + inv * (e - m1 - xhat * m2)
        got[at, :] = gr
        glow[pl.ds(pl.multiple_of(c * N + i * C, C), C), :] = gr.astype(BF)
        return carry

    lax.fori_loop(0, N // C, back_rows, 0)
    ls_, lr_ = al.take(1), al.take(1)

    def far_x(half):
        rows = glow.at[pl.ds(pl.multiple_of(half * N, N), N), :]
        return rcopy(rows, rows, ls_(0), lr_(0), sib)

    far_x(c).start()
    for x in (tgat, gsum):
        x.drain()
    for k in range(Q):
        s_x(k).wait_send()
    h_x.wait_send()
    for i in range(2):
        x_drain(i)
    for p in partners:
        pl.semaphore_signal(ready, inc=1, device_id=p, device_id_type=MESH)
    far_x(1 - c).wait_recv()

    W = B * H
    hj = H // HEAD_DIM
    M = D // Q
    gms, gqs, gkv = gup.at[pl.ds(0, S), :], gup.at[pl.ds(S, S), :], act.at[pl.ds(0, 3 * S), :]
    gos = gbuf.at[pl.ds(0, W), :]
    tgs, outs = ctx.at[0, pl.ds(0, N), :], ctx.at[0, pl.ds(N, N), :]
    small1 = ctx.at[1]
    odone = stack(small1, 2 * S // 2 - B * OR, OR)
    zo = stack(gg, 0, OR)
    wfin, ofin = gg.at[pl.ds(N, M), pl.ds(0, 3 * H)], gh.at[pl.ds(0, OR), :]

    def mix_rows(i, carry):
        at = pl.ds(pl.multiple_of(i * T, T), T)
        gms[at, :] = nt_dot(glow[at, :], wos[...]).astype(BF)
        gos[at, :] = tn_dot(mixed[:, at], glow[...]).astype(BF)
        return carry

    lax.fori_loop(0, S // T, mix_rows, 0)

    def o_blk(j):
        def blk(k, lo, n):
            return gos.at[pl.ds(pl.multiple_of(j * H + across(q, k) * OR + lo, n), n), :]
        return blk

    M2 = M // 2

    def w_blk(j, half):
        def blk(k, lo, n):
            return cots.at[pl.ds(pl.multiple_of(j * D + across(q, k) * M + half * M2 + lo, n), n), pl.ds(0, 3 * H)]
        return blk

    osum = [
        PlaneSum(al, peer, o_blk(j), OR, stack(small1, j * OR, OR // 2), stack(small1, B * OR + 2 * j * OR, OR)) for j in range(B)
    ]
    wsum = [
        [
            PlaneSum(
                al, peer, w_blk(j, half), M2,
                stack(gbuf, W + 2 * B * M + j * M + half * M2, M2 // 2, 3 * H), stack(gbuf, W + 2 * j * M + half * M, M2, 3 * H),
            )
            for half in range(2)
        ]
        for j in range(B)
    ]
    pl.semaphore_wait(ready, len(partners))
    for x in osum:
        x.start()
    arow[...] = jnp.zeros_like(arow)

    def back_head(h, hh):
        hd = pl.ds(h * HEAD_DIM, HEAD_DIM)
        ko = pl.ds(hh * HEAD_DIM, HEAD_DIM)
        vo = pl.ds(H + hh * HEAD_DIM, HEAD_DIM)
        p = probs[h]
        gm = gms[:, hd]
        gp = nt_dot(gm, vs[:, hd])
        delta = jnp.sum(gm.astype(F32) * mixed[:, hd].astype(F32), axis=-1, keepdims=True)
        gs = (p.astype(F32) * (gp - delta)).astype(BF)
        gqs[:, hd] = (scale * nn_dot(gs, ks[:, hd])).astype(BF)
        gkv[:, ko] = (scale * tn_dot(gs, qs[:, hd])).astype(BF)
        gkv[:, vo] = tn_dot(p, gm).astype(BF)

    def split_rows(v):
        hi = v.astype(BF)
        rest = v - hi.astype(F32)
        mid = rest.astype(BF)
        low = (rest - mid.astype(F32)).astype(BF)
        return jnp.concatenate([hi, mid, low, jnp.zeros((5, v.shape[1]), BF)], axis=0)

    def weights(j):
        js = pl.ds(j * H, H)

        def rows(i, carry):
            to_chip = across_by(q, i)
            at = pl.ds(pl.multiple_of(to_chip * M, M), M)
            kv = tn_dot(normed[:, at], gkv[...])
            gq = tn_dot(normed[pl.ds(2 * S, S), at], gqs[:, js])
            to = pl.ds(pl.multiple_of(j * D + to_chip * M, M), M)
            cots[to, pl.ds(0, 2 * H)] = kv.astype(BF)
            cots[to, pl.ds(2 * H, H)] = gq.astype(BF)
            t = (kv[:, :H] * wks[at, js].astype(F32) + kv[:, H:] * wvs[at, js].astype(F32) + gq * wqs[at, js].astype(F32))
            arow[at, :] = arow[at, :] + jnp.broadcast_to(jnp.sum(t, axis=-1, keepdims=True), (M, 128))

            @pl.when(i == 0)
            def _():
                for x in wsum[j]:
                    x.start()
            return carry

        lax.fori_loop(0, Q, rows, 0)
        skv = split_rows(jnp.sum(gkv[...].astype(F32), axis=0, keepdims=True))
        sq_ = split_rows(jnp.sum(gqs[:, js].astype(F32), axis=0, keepdims=True))
        b = nt_dot(skv[:, :H], wks[:, js]) + nt_dot(skv[:, H:], wvs[:, js]) + nt_dot(sq_, wqs[:, js])
        sums[1:2, :] = sums[1:2, :] + jnp.sum(b, axis=0, keepdims=True)

    for h in range(hj):
        back_head(h, h)

    def token_rows(j, half):
        js = pl.ds(j * H, H)
        rows = pl.ds(pl.multiple_of(half * N, N), N)
        krows = pl.ds(pl.multiple_of(2 * S + half * N, N), N)
        return (nt_dot(gkv[krows, pl.ds(0, H)], wks[:, js]) + nt_dot(gkv[krows, pl.ds(H, H)], wvs[:, js])
                + nt_dot(gqs[rows, js], wqs[:, js]))

    for x in osum:
        x.middle()
    weights(0)
    dsum.middle()
    y_middle(0)
    phalf[...] = token_rows(0, 1 - c)
    srow[...] = token_rows(0, c)
    for h in range(hj, 2 * hj):
        back_head(h, h - hj)
    for x in wsum[0]:
        x.middle()
    y_middle(1)
    weights(1)
    phalf[...] = phalf[...] + token_rows(1, 1 - c)
    ts_, tr_ = al.take(1), al.take(1)
    t_x = rcopy(phalf, ggot, ts_(0), tr_(0), sib)
    t_x.start()
    srow[...] = srow[...] + token_rows(1, c)
    rs, rr, rl = al.take(2, 2), al.take(2, B), al.take(2)
    rows_in = [tgs, outs]
    rows_out = [tg_o, out_o]

    def row_x(i, p):
        return rcopy(rows_in[i].at[pl.ds(p * R, R), :], rows_out[i].at[jz], rs(i, p), rr(i, jz), (2 * q + z // B, c * per + p))

    def row_l(i, p):
        return lcopy(rows_in[i].at[pl.ds(p * R, R), :], rows_out[i].at[jz], rl(i))

    def send_rows(i):
        for p in range(per):
            here = (c * per + p == z) & mine

            @pl.when(here)
            def _():
                row_l(i, p).start()

            @pl.when(jnp.logical_not(here))
            def _():
                row_x(i, p).start()

    outs[...] = (resid[...] + dsum.total() + db[...]).astype(BF)
    send_rows(1)
    ozs, ozr = al.take(3, B), al.take(3, Z)

    def z_buf(i, zz):
        if i == 2:
            return zo(zz)
        return got1.at[pl.ds(pl.multiple_of(zz * M + i * M2, M2), M2), pl.ds(0, 3 * H)]

    def z_done(i, j):
        if i == 2:
            return odone(j)
        return downs.at[pl.ds(pl.multiple_of(j * M + i * M2, M2), M2), pl.ds(0, 3 * H)]

    def z_x(i, j):
        return rcopy(z_done(i, j), z_buf(i, z), ozs(i, j), ozr(i, z), (dp, B * c + j))

    def z_arrive(i, zz):
        return rcopy(z_buf(i, zz), z_buf(i, zz), ozs(i, 0), ozr(i, zz), (dp, z))

    def to_plane(i, j):
        z_done(i, j)[...] = (osum[j] if i == 2 else wsum[j][i]).total().astype(BF)

        @pl.when(B * c + j != z)
        def _():
            z_x(i, j).start()

    for j in range(B):
        to_plane(2, j)
    for x in wsum[1]:
        x.middle()
    for half in range(2):
        to_plane(half, 0)
    acol = jnp.swapaxes(arow[...], 0, 1)[0:1, :]
    bsum = sums[1:2, :]
    sums[0:1, :] = (acol - b1[...] * bsum) / g1[...]
    sums[2:3, :] = ffs[0:1, :]
    sums[3:4, :] = ffs[1:2, :]
    n1, n2 = al.take(1), al.take(1)
    v_x = rcopy(sums, sgot, n1(0), n2(0), sib)
    v_x.start()
    t_x.wait_recv()
    def norm_rows(i, carry):
        at = pl.ds(pl.multiple_of(i * C, C), C)
        gn = srow[at, :] + ggot[at, :]
        xhat, inv = layer_norm_rows(ctx[2, pl.ds(pl.multiple_of(c * N + i * C, C), C), :].astype(F32))
        e = gn * g1[...]
        m1 = jnp.mean(e, axis=-1, keepdims=True)
        m2 = jnp.mean(e * xhat, axis=-1, keepdims=True)
        tgs[at, :] = (got[at, :] + inv * (e - m1 - xhat * m2)).astype(BF)
        return carry

    lax.fori_loop(0, N // C, norm_rows, 0)
    for i in range(2):
        y_arrive(i)
    fu = y_own(0, 0)[...].astype(F32) + (xu[0].astype(F32) + xu[1].astype(F32))
    fd = y_own(1, 0)[...].astype(F32) + (xd[0].astype(F32) + xd[1].astype(F32))
    fb = ffs[2:3, 0:E]
    for r in range(1, Z):
        ub_x(r).wait_recv()
        fb = fb + xb[r]
    fus, fds = xu.at[2], xd.at[2]
    fus[...] = fu.astype(BF)
    fds[...] = fd.astype(BF)
    fbs[...] = fb

    def u_loc(core):
        def loc(k, lo, n):
            return afu.at[pl.ds(lo, n), pl.ds(pl.multiple_of(dev(k, core) * E, E), E)]
        return loc

    def d_loc(core):
        def loc(k, lo, n):
            return afd.at[pl.ds(pl.multiple_of(dev(k, core) * E + lo, n), n), :]
        return loc

    ugat = PlaneGather(al, peer, sib, u_loc(c), D, own=fus)
    dgat = PlaneGather(al, peer, sib, d_loc(c), E, own=fds)
    fl = al.take(3)
    f_l = [lcopy(fus, u_loc(c)(0, 0, D), fl(0)), lcopy(fds, d_loc(c)(0, 0, E), fl(1))]
    bs, br, bfs, bfr = al.take(Q), al.take(Q), al.take(Q), al.take(Q)

    def b_x(k):
        return rcopy(fbs, aub.at[dp], bs(k), br(k), peer(k))

    def b_arrive(k):
        return rcopy(aub.at[dev(k, c)], aub.at[dev(k, c)], bs(k), br(k), peer(k))

    def b_f(k):
        src = fbs if k == 0 else aub.at[dev(k, c)]
        return rcopy(src, aub.at[dev(k, c)], bfs(k), bfr(k), sib)

    b_l = lcopy(fbs, aub.at[dp], fl(2))
    v_x.wait()
    srow[0:8, :] = sums[...] + sgot[...]
    pgot[q] = srow[0:8, :]
    vps, vpr, vzs, vzr = al.take(Q), al.take(Q), al.take(Z), al.take(Z)

    def vp_x(k):
        return rcopy(srow.at[pl.ds(0, 8), :], pgot.at[q], vps(k), vpr(k), peer(k))

    def vp_arrive(k):
        return rcopy(pgot.at[across(q, k)], pgot.at[across(q, k)], vps(k), vpr(k), peer(k))

    def vz_x(r):
        return rcopy(srow.at[pl.ds(8, 8), :], zgot.at[z], vzs(r), vzr(r), (dp, lax.rem(z + r, Z)))

    def vz_arrive(r):
        zz = lax.rem(z + Z - r, Z)
        return rcopy(zgot.at[zz], zgot.at[zz], vzs(r), vzr(r), (dp, z))

    for k in range(1, Q):
        vp_x(k).start()
    for k in range(1, Q):
        vp_arrive(k).wait_recv()
    psum = pgot[0]
    for k in range(1, Q):
        psum = psum + pgot[k]
    srow[8:16, :] = psum
    zgot[z] = psum
    for r in range(1, Z):
        vz_x(r).start()
    for half in range(2):
        to_plane(half, 1)
    ugat.start()
    dgat.start()
    for x in f_l:
        x.start()
    b_l.start()
    for k in range(1, Q):
        b_x(k).start()
    b_f(0).start()

    def a_loc(ref, n_rows):
        def loc(k, lo, n):
            return ref.at[pl.ds(pl.multiple_of(across(q, k) * n_rows + lo, n), n), :]
        return loc

    fins = [wfin.at[pl.ds(0, M2), :], wfin.at[pl.ds(M2, M2), :], ofin]

    def half_loc(half):
        def loc(k, lo, n):
            return aw.at[pl.ds(pl.multiple_of(across(q, k) * M + half * M2 + lo, n), n), :]
        return loc

    locs = [half_loc(0), half_loc(1), a_loc(ago, OR)]
    gats = [PlaneGather(al, peer, sib, locs[i], OR if i == 2 else M2, own=fins[i]) for i in range(3)]
    gl = al.take(3)
    g_l = [lcopy(fins[i], locs[i](0, 0, OR if i == 2 else M2), gl(i)) for i in range(3)]
    for gat in (ugat, dgat):
        gat.middle()
    send_rows(0)
    for k in range(1, Q):
        b_arrive(k).wait_recv()
        b_f(k).start()

    @pl.when(mine)
    def _():
        for i in (2, 0, 1):
            for zz in range(Z):
                @pl.when(zz != z)
                def _():
                    z_arrive(i, zz).wait_recv()
            z_buf(i, z)[...] = z_done(i, jz)[...]
            t = z_buf(i, 0)[...].astype(F32)
            for zz in range(1, Z):
                t = t + z_buf(i, zz)[...].astype(F32)
            fins[i][...] = t.astype(BF)
            gats[i].start()
            g_l[i].start()
    for r in range(1, Z):
        vz_arrive(r).wait_recv()
    zsum = zgot[0]
    for zz in range(1, Z):
        zsum = zsum + zgot[zz]
    small_o[...] = zsum

    @pl.when(mine)
    def _():
        for i in (2, 0, 1):
            gats[i].middle()
    for gat in (ugat, dgat):
        gat.last()

    @pl.when(mine)
    def _():
        for i in (2, 0, 1):
            gats[i].last()
    ugat.arrivals(u_loc(1 - c))
    dgat.arrivals(d_loc(1 - c))

    @pl.when(jnp.logical_not(mine))
    def _():
        for i in range(3):
            gats[i].arrivals(locs[i])

    for k in range(Q):
        rcopy(aub.at[dev(k, 1 - c)], aub.at[dev(k, 1 - c)], bfs(k), bfr(k), sib).wait_recv()
        b_f(k).wait_send()
        d_x(k).wait_send()
    for k in range(1, Q):
        b_x(k).wait_send()
        vp_x(k).wait_send()
    b_l.wait()
    for x in f_l:
        x.wait()
    for r in range(1, Z):
        vz_x(r).wait_send()
        ub_x(r).wait_send()
    for i in range(2):
        y_drain(i)
    for x in osum + wsum[0] + wsum[1] + [dsum, ugat, dgat]:
        x.drain()

    @pl.when(mine)
    def _():
        for x in gats:
            x.drain()
        for x in g_l:
            x.wait()
    t_x.wait_send()
    for j in range(B):
        @pl.when(B * c + j != z)
        def _():
            for i in range(3):
                z_x(i, j).wait_send()
    for p in range(per):
        here = (c * per + p == z) & mine

        @pl.when(here)
        def _():
            for i in range(2):
                row_l(i, p).wait()

        @pl.when(jnp.logical_not(here))
        def _():
            for i in range(2):
                row_x(i, p).wait_send()
    for s in range(B):
        @pl.when(jnp.logical_not((B * c + s == z) & mine))
        def _():
            for i in range(2):
                rcopy(rows_out[i].at[s], rows_out[i].at[s], rs(i, 0), rr(i, s), (dp, z)).wait_recv()
    far_x(c).wait_send()

    @pl.when(mine)
    def _():
        for r in range(1, Z):
            @pl.when(w_direct(r))
            def _():
                for a in range(4):
                    w_z(a, r).wait_send()
    for j in range(B):
        @pl.when(B * c + j != z)
        def _():
            for a in range(4):
                @pl.when(relay)
                def _():
                    w_onward(a, j).wait_send()
                for k in range(1, Q):
                    w_p(a, j, k, q).wait_send()
    for s in range(B):
        @pl.when(jnp.logical_not((B * c + s == z) & mine))
        def _():
            t_z(s).wait_send()
    for p in range(per):
        here = (c * per + p == z) & mine

        @pl.when(here)
        def _():
            for i in range(2):
                keep_l(i, p).wait()

        @pl.when(jnp.logical_not(here))
        def _():
            for i in range(2):
                keep_x(i, p).wait_send()
    for s in range(B):
        @pl.when(jnp.logical_not((B * c + s == z) & mine))
        def _():
            for i in range(2):
                rcopy(kept_out[i].at[s], kept_out[i].at[s], ms(i, 0), mr(i, s), (dp, z)).wait_recv()
    assert al.used <= LAYER_SEMS


def layer(Q, Z, comp, mem, tok, cot, wq, wk, wv, wo, up, down, ub, vc, sq, g1, b1, g2, b2, db):
    B, R, D = tok.shape
    H = wq.shape[1]
    S = R * Z
    N = S // 2
    W = B * H
    heads = W // HEAD_DIM
    E = up.shape[1] // (2 * Q)
    F = E * Z
    rows = 2 * Q * N
    vm = pltpu.VMEM
    return pl.pallas_call(
        functools.partial(layer_kernel, Q, Z),
        out_shape=[
            sds((D, 3 * H), BF), sds((H, D), BF), sds((D, 2 * Q * E), BF), sds((2 * Q * E, D), BF), sds((2 * Q, 1, E), F32),
            sds((8, D), F32), sds((B, R, D), BF), sds((B, R, D), BF), sds((B, R, D), BF), sds((B, R, D), BF),
        ],
        in_specs=[ANY] * 11 + [VM] + [ANY] + [VM] * 5,
        out_specs=[ANY] * 5 + [VM] + [ANY] * 4,
        scratch_shapes=[
            vm((3, S, D), BF), vm((3 * S, D), BF), vm((D, W), BF), vm((D, W), BF), vm((D, W), BF), vm((W, D), BF),
            vm((S, W), BF), vm((3 * S, W), BF), vm((3 * S, W), BF), vm((heads, S, 3 * S), BF), vm((S, W), BF),
            vm((N, D), F32), vm((N, D), F32), vm((N, D), F32), vm((rows, D), BF), vm((rows, D), BF), vm((D, F), BF), vm((F, D), BF),
            vm((Z, 1, E), F32), vm(vc.shape, jnp.int32), vm((rows, F), BF), vm((rows, F), BF), vm((rows, D), BF),
            vm((Q * N, D), BF), vm((N, D), BF), vm((2 * N, D), BF), vm((S, D), BF),
            vm((N, D), BF), vm((N, D), BF), vm((D, F), BF), vm((F, D), BF), vm((Q * N, D), BF), vm((N, D), BF), vm((2 * N, D), BF),
            vm((N, D), F32), vm((N, D), F32),
            vm((4, D, E), BF), vm((4, E, D), BF), vm((Z, 1, E), F32), vm((1, E), F32),
            vm((D, 128), F32), vm((8, D), F32), vm((8, D), F32), vm((8, D), F32),
            vm((Q, 8, D), F32), vm((Z, 8, D), F32),
            DMA((LAYER_SEMS,)), pltpu.SemaphoreType.REGULAR,
        ],
        compiler_params=pltpu.CompilerParams(collective_id=1, has_side_effects=True, vmem_limit_bytes=63 << 20),
        name="layer",
    )(comp, mem, tok, cot, wq, wk, wv, wo, up, down, ub, vc, sq, g1, b1, g2, b2, db)


def convert_kernel(w, wo, u, d, t, a0, a1, a2, v, gk, gv, gq, go, gu, gd, gt, b0, b1, b2, *vecs):
    for i, out in enumerate(vecs):
        out[...] = v[i, :]
    h = gk.shape[1]
    for i, out in enumerate((gk, gv, gq)):
        out[...] = w[:, i * h:(i + 1) * h].astype(F32)
    for src, out in ((wo, go), (u, gu), (d, gd), (t, gt)):
        out[...] = src[...].astype(F32)
    for src, out in ((a0, b0), (a1, b1), (a2, b2)):
        out[...] = src[...]


def convert(small, w, wo, u, d, *rows):
    steps = 2
    H = w.shape[1] // 3
    D = rows[0].shape[2]
    flat = [r.reshape(-1, D) for r in rows]

    def spec(a, cols=None):
        return pl.BlockSpec((a.shape[0] // steps, a.shape[1] if cols is None else cols), lambda i: (i, 0))

    ins = [w, wo, u, d] + flat
    shapes = [sds((w.shape[0], H), F32)] * 3 + [sds(a.shape, F32) for a in (wo, u, d, flat[0])] + [sds(a.shape, BF) for a in flat[1:]]
    out = pl.pallas_call(
        convert_kernel,
        grid=(steps,),
        out_shape=shapes + [sds((D,), F32)] * 5,
        in_specs=[spec(a) for a in ins] + [pl.BlockSpec(small.shape, lambda i: (0, 0))],
        out_specs=[spec(a) for a in shapes] + [pl.BlockSpec((D,), lambda i: (0,))] * 5,
        compiler_params=pltpu.CompilerParams(vmem_limit_bytes=63 << 20),
        name="convert",
    )(*ins, small)
    return list(out[:6]) + [o.reshape(rows[0].shape) for o in out[6:10]] + list(out[10:])


def chip_device(Q, Z, tokens, memory, compressed, valid_counts, attention_norm_gain, attention_norm_bias,
                query_projection, key_projection, value_projection, out_weight, feedforward_norm_gain,
                feedforward_norm_bias, up_weight, up_bias, down_weight, down_bias, squeeze_weight, cotangent):
    B, R, D = tokens.shape
    H = query_projection.shape[1]
    FL = up_weight.shape[1]
    E = FL // (2 * Q)
    aw, ago, afu, afd, aub, small, o_out, o_tg, o_nm, o_nc = layer(
        Q, Z, compressed, memory, tokens, cotangent, query_projection, key_projection, value_projection, out_weight,
        up_weight, down_weight, up_bias.reshape(2 * Q, 1, E), valid_counts.reshape(B, 1, 1),
        squeeze_weight, attention_norm_gain.reshape(1, D), attention_norm_bias.reshape(1, D),
        feedforward_norm_gain.reshape(1, D), feedforward_norm_bias.reshape(1, D), down_bias.reshape(1, D),
    )
    gk, gv, gq, go, gu, gd, g_tokens, out, new_mem, new_comp, *vecs = convert(small, aw, ago, afu, afd, o_tg, o_out, o_nm, o_nc)
    return (
        out, g_tokens, vecs[0], vecs[1], gq, gk, gv, go, vecs[2], vecs[3], gu, aub.reshape(FL), gd, vecs[4], new_mem, new_comp,
    )


def solution(mesh):
    in_specs = (
        P("dp", "mp", None),
        P("dp", "mp", None),
        P("dp", "mp", None),
        P("dp"),
        P(),
        P(),
        P(None, "mp"),
        P(None, "mp"),
        P(None, "mp"),
        P("mp", None),
        P(),
        P(),
        P(None, "mp"),
        P("mp"),
        P("mp", None),
        P(),
        P(),
        P("dp", "mp", None),
    )
    out_specs = (
        P("dp", "mp", None),
        P("dp", "mp", None),
        P(),
        P(),
        P(None, "mp"),
        P(None, "mp"),
        P(None, "mp"),
        P("mp", None),
        P(),
        P(),
        P(None, "mp"),
        P("mp"),
        P("mp", None),
        P(),
        P("dp", "mp", None),
        P("dp", "mp", None),
    )
    Q, Z = mesh.shape["dp"] // 2, mesh.shape["mp"]

    def per_device(*args):
        B, R, D = args[0].shape
        H, FL = args[6].shape[1], args[12].shape[1]
        whole = Q == 4 and B == 2 and 2 * B == Z and H % HEAD_DIM == 0 and D % (16 * Q) == 0 and H % (16 * Q) == 0
        if whole and R % 32 == 0 and FL % (256 * Q) == 0:
            return chip_device(Q, Z, *args)
        return general_device(*args)

    return jax.shard_map(
        per_device, mesh=mesh, in_specs=in_specs, out_specs=out_specs, check_vma=False
    )
```
